32 devices in a mesh: dp: 4 (over y, x), ctx: 8 (over z, core).
Axes of the slice: x: 2, y: 2, z: 4, core: 2. Of those that a mesh axis runs over, the one named last changes fastest.
Arguments:
- tokens: bfloat16 [8, 2560, 1024], P('dp', 'ctx'), may hold values from -6 to 6
- cotangent: bfloat16 [8, 2560, 1024], P('dp', 'ctx'), may hold values from -6 to 6
- segment_ids: int32 [8, 2560], P('dp'), may hold values from 0 to 12, as said below
- positions: int32 [8, 2560], P('dp'), may hold values from 0 to 1279, as said below
- parents: int32 [8, 13], P('dp'), may hold values from 0 to 4, as said below
- input_norm: bfloat16 [1024], P(('dp', 'ctx')), may hold values from 0.25 to 1.75
- query_proj: bfloat16 [1024, 2048], P(('dp', 'ctx')), may hold values from -0.1875 to 0.1875
- key_proj: bfloat16 [1024, 1024], P(('dp', 'ctx')), may hold values from -0.1875 to 0.1875
- value_proj: bfloat16 [1024, 1024], P(('dp', 'ctx')), may hold values from -0.1875 to 0.1875
- query_norm: bfloat16 [128], P(('dp', 'ctx')), may hold values from 0.25 to 1.75
- key_norm: bfloat16 [128], P(('dp', 'ctx')), may hold values from 0.25 to 1.75
- out_proj: bfloat16 [2048, 1024], P(None, ('dp', 'ctx')), may hold values from -1 to 1
- post_norm: bfloat16 [1024], P(('dp', 'ctx')), may hold values from 0.25 to 1.75
- gate_proj: bfloat16 [1024, 3072], P(('dp', 'ctx')), may hold values from -0.1875 to 0.1875
- up_proj: bfloat16 [1024, 3072], P(('dp', 'ctx')), may hold values from -0.1875 to 0.1875
- down_proj: bfloat16 [3072, 1024], P(None, ('dp', 'ctx')), may hold values from -0.109375 to 0.109375
Outputs:
- output: bfloat16 [8, 2560, 1024], P('dp', 'ctx')
- input_grad: float32 [8, 2560, 1024], P('dp', 'ctx')
- input_norm_grad: float32 [1024], P(('dp', 'ctx'))
- query_proj_grad: float32 [1024, 2048], P(('dp', 'ctx'))
- key_proj_grad: float32 [1024, 1024], P(('dp', 'ctx'))
- value_proj_grad: float32 [1024, 1024], P(('dp', 'ctx'))
- query_norm_grad: float32 [128], P(('dp', 'ctx'))
- key_norm_grad: float32 [128], P(('dp', 'ctx'))
- out_proj_grad: float32 [2048, 1024], P(None, ('dp', 'ctx'))
- post_norm_grad: float32 [1024], P(('dp', 'ctx'))
- gate_proj_grad: float32 [1024, 3072], P(('dp', 'ctx'))
- up_proj_grad: float32 [1024, 3072], P(('dp', 'ctx'))
- down_proj_grad: float32 [3072, 1024], P(None, ('dp', 'ctx'))
The draws below stay inside these ranges and needn't reach their ends.
Inputs may be any that keep to these rules, and one draw needn't show every extreme that they name: `parents`: in every tree segment 0 is the trunk and its own parent; segments 1 to 4 have parent 0; each later segment has a parent among 1 to 4, and each of these has exactly 2 children. `segment_ids`: in every tree tokens 0 to 1023 are segment 0; the other tokens form aligned runs of 128, one run for each other segment, in an order that varies from tree to tree. `positions`: trunk token t has position t; the k-th token of a branch segment has 1024 + k, of a leaf segment 1024 + 128 + k.
All inputs are finite; a program needn't handle non-finite values.
Results may differ from the reference program's by a relative error of at most 0.018.
Values may be sent and summed in bfloat16 or wider, within the bound.
A program may use at most 448 MiB of HBM per device.

```python
import jax
import jax.numpy as jnp
from jax import lax

D = 1024
HEADS = 16
KV_HEADS = 8
HEAD_DIM = 128
FF = 3072
TRUNK = 1024
SEG = 128
BRANCHES = 4
LEAVES = 2
QD = 2048
KVD = 1024
TREE = 2560
TREES = 8


def tree_layout(key):
    tree_keys = jax.random.split(jax.random.fold_in(key, 7), TREES)

    def one_tree(tree_key):
        order = jax.random.permutation(jax.random.fold_in(tree_key, 1), BRANCHES + BRANCHES * LEAVES).astype(jnp.int32) + 1
        children = jax.random.permutation(jax.random.fold_in(tree_key, 2), BRANCHES * LEAVES).astype(jnp.int32) // LEAVES + 1
        parent_tree = jnp.concatenate([jnp.zeros((1 + BRANCHES,), jnp.int32), children])
        tail_index = jnp.arange(TREE - TRUNK, dtype=jnp.int32)
        tail_seg = order[tail_index // SEG]
        tail_pos = TRUNK + tail_index % SEG + jnp.where(tail_seg > BRANCHES, SEG, 0).astype(jnp.int32)
        seg_tree = jnp.concatenate([jnp.zeros((TRUNK,), jnp.int32), tail_seg])
        pos_tree = jnp.concatenate([jnp.arange(TRUNK, dtype=jnp.int32), tail_pos.astype(jnp.int32)])
        return (seg_tree, pos_tree, parent_tree)
    return jax.vmap(one_tree)(tree_keys)


def draw_segment_ids(key, part):
    return tree_layout(key)[0]


def draw_positions(key, part):
    return tree_layout(key)[1]


def draw_parents(key, part):
    return tree_layout(key)[2]


def level_of(own_key, extent, cuts, least, largest):
    def one(dim, blocks):
        draws = jax.random.uniform(jax.random.fold_in(jax.random.fold_in(own_key, 6), dim), (blocks,), jnp.float32, least / len(cuts), largest / len(cuts))
        return jnp.repeat(jnp.exp(draws), extent[dim] // blocks).reshape((-1,) + (1,) * (len(extent) - dim - 1))

    loudness = one(*cuts[0])
    for cut in cuts[1:]:
        loudness = loudness * one(*cut)
    return loudness


def centred(own_key, dims, width, bound, pieces=(), kind=jnp.bfloat16):
    drawn = jax.random.normal(own_key, dims, jnp.float32) * width
    if len(pieces) > 0:
        drawn = level_of(own_key, dims, pieces, -0.22, 0.18) * drawn
    return jnp.clip(drawn, min=-bound, max=bound).astype(kind)


def setup_inputs(seed: int = 0) -> dict:
    streams_of = jax.random.split(jax.random.key(seed), 17)
    tokens = centred(streams_of[0], (TREES, TREE, D), 1.0, 6.0, ((0, 4), (1, 8)))
    cotangent = centred(streams_of[1], (TREES, TREE, D), 1.0, 6.0, ((0, 4), (1, 8)))
    segment_ids = draw_segment_ids(jax.random.fold_in(streams_of[16], 71), 0)
    positions = draw_positions(jax.random.fold_in(streams_of[16], 71), 0)
    parents = draw_parents(jax.random.fold_in(streams_of[16], 71), 0)
    input_norm = jnp.clip(1.0 + 0.15 * jax.random.normal(streams_of[5], (D,), jnp.float32), 0.25, 1.75).astype(jnp.bfloat16)
    query_proj = centred(streams_of[6], (D, QD), D ** -0.5, 0.1875, ((0, 32),))
    key_proj = centred(streams_of[7], (D, KVD), D ** -0.5, 0.1875, ((0, 32),))
    value_proj = centred(streams_of[8], (D, KVD), D ** -0.5, 0.1875, ((0, 32),))
    query_norm = jnp.clip(1.0 + 0.15 * jax.random.normal(streams_of[9], (HEAD_DIM,), jnp.float32), 0.25, 1.75).astype(jnp.bfloat16)
    key_norm = jnp.clip(1.0 + 0.15 * jax.random.normal(streams_of[10], (HEAD_DIM,), jnp.float32), 0.25, 1.75).astype(jnp.bfloat16)
    out_proj = centred(streams_of[11], (QD, D), (QD // 64) ** -0.5, 1.0, ((1, 32),))
    post_norm = jnp.clip(1.0 + 0.15 * jax.random.normal(streams_of[12], (D,), jnp.float32), 0.25, 1.75).astype(jnp.bfloat16)
    gate_proj = centred(streams_of[13], (D, FF), D ** -0.5, 0.1875, ((0, 32),))
    up_proj = centred(streams_of[14], (D, FF), D ** -0.5, 0.1875, ((0, 32),))
    down_proj = centred(streams_of[15], (FF, D), FF ** -0.5, 0.109375, ((1, 32),))
    return {"tokens": tokens, "cotangent": cotangent, "segment_ids": segment_ids, "positions": positions, "parents": parents, "input_norm": input_norm, "query_proj": query_proj, "key_proj": key_proj, "value_proj": value_proj, "query_norm": query_norm, "key_norm": key_norm, "out_proj": out_proj, "post_norm": post_norm, "gate_proj": gate_proj, "up_proj": up_proj, "down_proj": down_proj}


@jax.custom_vjp
def low(v):
    return lax.optimization_barrier(v.astype(jnp.bfloat16)).astype(jnp.float32)

@jax.custom_vjp
def low_back(v):
    return v

def low_keep(v):
    return (low(v), None)

def low_pass(kept, grad):
    return (grad,)

def back_keep(v):
    return (v, None)

def back_low(kept, grad):
    return (low(grad),)
low.defvjp(low_keep, low_pass)
low_back.defvjp(back_keep, back_low)
eps_norm = 1e-06
rope_base = 1000000.0
path_levels = 3
masked_score = -1e+30
highest = lax.Precision.HIGHEST

def product(left_side, right_side):
    return jnp.dot(left_side, right_side, precision=highest, preferred_element_type=jnp.float32)

def rms_norm(values, weight):
    return values * lax.rsqrt(lax.optimization_barrier(jnp.mean(values * values, axis=-1, keepdims=True)) + eps_norm) * weight

def rotate(values, cosine, sine_table):
    middle = values.shape[-1] // 2
    turned = jnp.concatenate([-values[..., middle:], values[..., :middle]], axis=-1)
    return values * cosine + turned * sine_table

def rope_tables(positions):
    steps_half = jnp.arange(HEAD_DIM // 2, dtype=jnp.float32)
    inverse = rope_base ** (-(steps_half * 2.0 / HEAD_DIM))
    angles = positions.astype(jnp.float32)[:, None] * inverse[None, :]
    angles = jnp.concatenate([angles, angles], axis=-1)
    return (jnp.cos(angles)[:, None, :], jnp.sin(angles)[:, None, :])

def ancestor_table(parent_tree):
    seg_count = parent_tree.shape[0]
    seg_index = jnp.arange(seg_count, dtype=jnp.int32)
    current = seg_index
    ancestry = jnp.zeros((seg_count, seg_count), jnp.float32)
    for level_index in range(path_levels):
        matches = current[:, None] == seg_index[None, :]
        ancestry = jnp.maximum(ancestry, matches.astype(jnp.float32))
        current = lax.optimization_barrier(jnp.sum(jnp.where(matches, parent_tree[None, :], 0), axis=1)).astype(jnp.int32)
    return ancestry

def visible_keys(ancestry, seg_rows, pos_rows, seg_cols, pos_cols):
    seg_count = ancestry.shape[0]
    seg_index = jnp.arange(seg_count, dtype=jnp.int32)
    rows_onehot = (seg_rows[:, None] == seg_index[None, :]).astype(jnp.float32)
    cols_onehot = (seg_cols[:, None] == seg_index[None, :]).astype(jnp.float32)
    reaches = jnp.dot(jnp.dot(rows_onehot, ancestry), cols_onehot.T)
    return (reaches > 0.5) & (pos_cols[None, :] <= pos_rows[:, None])

def layer(tokens, weights, seg_tree, pos_tree, parent_tree):
    input_norm, query_proj, key_proj, value_proj, query_norm, key_norm, out_proj, post_norm, gate_proj, up_proj, down_proj = weights
    length = tokens.shape[0]
    groups = HEADS // KV_HEADS
    normed = low(rms_norm(tokens, input_norm))
    queries = low_back(product(normed, query_proj)).reshape(length, HEADS, HEAD_DIM)
    key_rows = low_back(product(normed, key_proj)).reshape(length, KV_HEADS, HEAD_DIM)
    values = low(low_back(product(normed, value_proj))).reshape(length, KV_HEADS, HEAD_DIM)
    cosine, sine_table = rope_tables(pos_tree)
    queries = low(rotate(rms_norm(queries, query_norm), cosine, sine_table))
    queries = queries.reshape(length, KV_HEADS, groups, HEAD_DIM)
    key_rows = low(rotate(rms_norm(key_rows, key_norm), cosine, sine_table))
    allowed = visible_keys(ancestor_table(parent_tree), seg_tree, pos_tree, seg_tree, pos_tree)
    scores = low_back(jnp.einsum('rkgd,tkd->kgrt', queries, key_rows, precision=highest)) * HEAD_DIM ** (-0.5)
    scores = jnp.where(allowed, scores, masked_score)
    weights_soft = jax.nn.softmax(scores, axis=-1)
    mixed_heads = jnp.einsum('kgrt,tkd->rkgd', low(weights_soft), values, precision=highest)
    mixed_heads = low(low_back(mixed_heads.reshape(length, HEADS * HEAD_DIM)))
    hidden = tokens + low_back(product(mixed_heads, out_proj))
    second = low(rms_norm(hidden, post_norm))
    gate_pre = low_back(product(second, gate_proj))
    up_pre = low_back(product(second, up_proj))
    inner_act = low(jax.nn.silu(gate_pre) * up_pre)
    return hidden + product(inner_act, down_proj)

def reference(tokens, cotangent, segment_ids, positions, parents, input_norm, query_proj, key_proj, value_proj, query_norm, key_norm, out_proj, post_norm, gate_proj, up_proj, down_proj):
    weights = tuple((matrix.astype(jnp.float32) for matrix in (input_norm, query_proj, key_proj, value_proj, query_norm, key_norm, out_proj, post_norm, gate_proj, up_proj, down_proj)))

    def one_tree(totals, tree_item):
        tree_tokens, tree_cot, seg_tree, pos_tree, parent_tree = tree_item

        def forward(inputs, params):
            return layer(inputs, params, seg_tree, pos_tree, parent_tree)
        result, pullback = jax.vjp(forward, tree_tokens.astype(jnp.float32), weights)
        grad_tokens, grad_weights = pullback(tree_cot.astype(jnp.float32))
        totals = tuple((running + gradient for running, gradient in zip(totals, grad_weights)))
        return (totals, (result.astype(jnp.bfloat16), grad_tokens))
    zero_grads = tuple((jnp.zeros(matrix.shape, jnp.float32) for matrix in weights))
    totals, (output, input_grad) = lax.scan(one_tree, zero_grads, (tokens, cotangent, segment_ids, positions, parents))
    return (output, input_grad, totals[0], totals[1], totals[2], totals[3], totals[4], totals[5], totals[6], totals[7], totals[8], totals[9], totals[10])
```

```python
import functools
import math

import jax
import jax.numpy as jnp
from jax import lax
from jax.experimental import pallas as pl
from jax.experimental.pallas import tpu as pltpu
from jax.sharding import PartitionSpec as P

D = 1024
HEADS = 16
KV_HEADS = 8
HEAD_DIM = 128
FF = 3072
TRUNK = 1024
SEG = 128
TREE = 2560
QD = HEADS * HEAD_DIM
KVD = KV_HEADS * HEAD_DIM
SUBS = 5
CHUNK = 256
GAIN_COLS = 128

eps_norm = 1e-06
rope_base = 1000000.0
exp2_scale = math.log2(math.e) / math.sqrt(HEAD_DIM)
score_scale = HEAD_DIM ** (-0.5)

MESH = pl.DeviceIdType.MESH
ANY = pl.BlockSpec(memory_space=pl.ANY)
AXES = ("dp", "ctx")


def matmul(left_side, right_side):
    return jnp.dot(left_side, right_side, preferred_element_type=jnp.float32)


def matmul_t(left_side, right_side):
    return lax.dot_general(
        left_side, right_side, (((1,), (1,)), ((), ())), preferred_element_type=jnp.float32
    )


def contract_rows(left_side, right_side):
    return lax.dot_general(
        left_side, right_side, (((0,), (0,)), ((), ())), preferred_element_type=jnp.float32
    )


def norm_forward(values, weight):
    factor = lax.rsqrt(jnp.mean(values * values, axis=-1, keepdims=True) + eps_norm)
    normed = values * factor
    return (normed * weight, normed, factor)


def norm_backward(grad_out, weight, normed, factor):
    weighted = grad_out * weight
    grad_in = factor * (weighted - normed * jnp.mean(weighted * normed, axis=-1, keepdims=True))
    return (grad_in, grad_out * normed)


def rotate(values, cosine, sine_table):
    middle = values.shape[-1] // 2
    turned = jnp.concatenate([-values[..., middle:], values[..., :middle]], axis=-1)
    return values * cosine + turned * sine_table


def rotate_back(gradient, cosine, sine_table):
    middle = gradient.shape[-1] // 2
    moved = gradient * sine_table
    return gradient * cosine + jnp.concatenate([moved[..., middle:], -moved[..., :middle]], axis=-1)


def rope_tables(positions):
    steps_half = jnp.arange(HEAD_DIM // 2, dtype=jnp.float32)
    inverse = rope_base ** (-(steps_half * 2.0 / HEAD_DIM))
    angles = positions.astype(jnp.float32)[:, None] * inverse[None, :]
    angles = jnp.concatenate([angles, angles], axis=-1)
    return (jnp.cos(angles)[:, None, :], jnp.sin(angles)[:, None, :])


def place(sizes):
    ny, nx, nz = sizes
    dp, ctx = lax.axis_index("dp"), lax.axis_index("ctx")
    me = (dp // nx, lax.rem(dp, nx), ctx // 2, lax.rem(ctx, 2))

    def device(y, x, z, core):
        return (y * nx + x, z * 2 + core)

    return me, device


def meet(partners):
    barrier = pltpu.get_barrier_semaphore()
    for partner in partners:
        pl.semaphore_signal(barrier, inc=1, device_id=partner, device_id_type=MESH)
    pl.semaphore_wait(barrier, len(partners))


def gather_kernel(sizes, orders, *refs):
    count = len(orders)
    shard = refs[:count]
    moved = refs[count : count + 2]
    whole = refs[count + 2 : 2 * count + 2]
    placed = refs[2 * count + 2 : 2 * count + 4]
    send_sem, recv_sem, local_sem = refs[2 * count + 4 :]
    ny, nx, nz = sizes
    (y, x, z, core), device = place(sizes)
    half = z // (nz // 2)
    used = [0]

    def others(axis):
        if axis == "z":
            return [(y, x, lax.rem(z + s, nz), core) for s in range(1, nz)]
        if axis == "x":
            return [(y, lax.rem(x + s, nx), z, core) for s in range(1, nx)]
        return [(lax.rem(y + s, ny), x, z, core) for s in range(1, ny)]

    def senders(axis):
        if axis == "z":
            return [(y, x, lax.rem(z + nz - s, nz), core) for s in range(1, nz)]
        if axis == "x":
            return [(y, lax.rem(x + nx - s, nx), z, core) for s in range(1, nx)]
        return [(lax.rem(y + ny - s, ny), x, z, core) for s in range(1, ny)]

    sibling = device(y, x, z, 1 - core)
    across = device(y, x, lax.rem(z + nz // 2, nz), core)
    meet([device(*o) for a in "zxy" for o in others(a)] + [sibling])

    def send(src, dst, target):
        k = used[0]
        used[0] += 1
        copy = pltpu.make_async_remote_copy(
            src_ref=src,
            dst_ref=dst,
            send_sem=send_sem.at[k],
            recv_sem=recv_sem.at[k],
            device_id=target,
            device_id_type=MESH,
        )
        copy.start()
        return copy

    pending = []
    locals_ = []
    for i in range(count):
        copy = pltpu.make_async_copy(shard[i], whole[i].at[y, x, z, core], local_sem.at[i])
        copy.start()
        locals_.append(copy)
    first = []
    for i in range(count):
        first.append(
            [send(shard[i], whole[i].at[y, x, z, core], device(*o)) for o in others("z")]
        )
        pending.append(send(shard[i], whole[i].at[y, x, z, core], sibling))
    for i in range(2):
        pending.append(send(moved[i].at[1 - half], placed[i].at[half], across))
        copy = pltpu.make_async_copy(
            moved[i].at[half], placed[i].at[half], local_sem.at[count + i]
        )
        copy.start()
        locals_.append(copy)

    def slab(i, stage, py, px, pz):
        order = orders[i]
        if stage == 0:
            return whole[i].at[py, px, pz, core]
        if stage == 1:
            return whole[i].at[py, px, :, core]
        if order[1] == "x":
            return whole[i].at[py, :, :, core]
        return whole[i].at[:, px, :, core]

    second = []
    for i in range(count):
        locals_[i].wait()
        for copy in first[i]:
            copy.wait()
        a = orders[i][1]
        second.append([send(slab(i, 1, y, x, z), slab(i, 1, y, x, z), device(*o)) for o in others(a)])
        for o in senders("z"):
            pending.append(send(slab(i, 0, *o[:3]), slab(i, 0, *o[:3]), sibling))
    third = []
    for i in range(count):
        for copy in second[i]:
            copy.wait()
        a, b = orders[i][1], orders[i][2]
        third.append([send(slab(i, 2, y, x, z), slab(i, 2, y, x, z), device(*o)) for o in others(b)])
        for o in senders(a):
            pending.append(send(slab(i, 1, *o[:3]), slab(i, 1, *o[:3]), sibling))
    for i in range(count):
        for copy in third[i]:
            copy.wait()
        b = orders[i][2]
        for o in senders(b):
            pending.append(send(slab(i, 2, *o[:3]), slab(i, 2, *o[:3]), sibling))
    for copy in pending:
        copy.wait()
    for copy in locals_[count:]:
        copy.wait()


def gather_weights(sizes, orders, shards_, moved, collective_id):
    ny, nx, nz = sizes
    count = len(orders)
    rounds = count * (2 * (nz - 1) + 2 * (nx - 1) + 2 * (ny - 1) + 1) + 2
    results = pl.pallas_call(
        functools.partial(gather_kernel, sizes, orders),
        out_shape=[
            jax.ShapeDtypeStruct((ny, nx, nz, 2) + s.shape, s.dtype) for s in shards_
        ]
        + [jax.ShapeDtypeStruct(s.shape, s.dtype) for s in moved],
        in_specs=[ANY] * (count + 2),
        out_specs=[ANY] * (count + 2),
        scratch_shapes=[
            pltpu.SemaphoreType.DMA((rounds,)),
            pltpu.SemaphoreType.DMA((rounds,)),
            pltpu.SemaphoreType.DMA((count + 2,)),
        ],
        compiler_params=pltpu.CompilerParams(
            collective_id=collective_id, has_side_effects=True
        ),
        name="gather_weights",
    )(*shards_, *moved)
    wholes = [r.reshape(-1, r.shape[-1]) for r in results[:count]]
    return wholes, results[count:]


def group_gather_kernel(sizes, key_ref, value_ref, keys_ref, values_ref, send_sem, recv_sem, local_sem):
    ny, nx, nz = sizes
    chips = nz // 2
    (y, x, z, core), device = place(sizes)
    base = (z // chips) * chips
    here = z - base
    sibling = device(y, x, z, 1 - core)

    def other(s):
        return device(y, x, base + lax.rem(here + s, chips), core)

    meet([other(s) for s in range(1, chips)] + [sibling])
    used = [0]

    def send(src, dst, target):
        k = used[0]
        used[0] += 1
        copy = pltpu.make_async_remote_copy(
            src_ref=src,
            dst_ref=dst,
            send_sem=send_sem.at[k],
            recv_sem=recv_sem.at[k],
            device_id=target,
            device_id_type=MESH,
        )
        copy.start()
        return copy

    mine = here * 2 + core
    pairs = ((key_ref, keys_ref), (value_ref, values_ref))
    first, pending, locals_ = [], [], []
    for src, dst in pairs:
        for s in range(1, chips):
            for half in range(2):
                first.append((s, half, dst, send(src.at[half], dst.at[half, mine], other(s))))
    for i, (src, dst) in enumerate(pairs):
        for half in range(2):
            pending.append(send(src.at[half], dst.at[half, mine], sibling))
            copy = pltpu.make_async_copy(
                src.at[half], dst.at[half, mine], local_sem.at[2 * i + half]
            )
            copy.start()
            locals_.append(copy)
    for s, half, dst, copy in first:
        copy.wait()
        came = lax.rem(here + chips - s, chips) * 2 + core
        pending.append(send(dst.at[half, came], dst.at[half, came], sibling))
    for copy in pending + locals_:
        copy.wait()


def group_gather(sizes, key, value, collective_id):
    chips = sizes[2] // 2
    rounds = 4 * (chips - 1) * 2 + 4
    shape = jax.ShapeDtypeStruct((2, 2 * chips) + key.shape[1:], key.dtype)
    return pl.pallas_call(
        functools.partial(group_gather_kernel, sizes),
        out_shape=[shape, shape],
        in_specs=[ANY] * 2,
        out_specs=[ANY] * 2,
        scratch_shapes=[
            pltpu.SemaphoreType.DMA((rounds,)),
            pltpu.SemaphoreType.DMA((rounds,)),
            pltpu.SemaphoreType.DMA((4,)),
        ],
        compiler_params=pltpu.CompilerParams(
            collective_id=collective_id, has_side_effects=True
        ),
        name="group_gather",
    )(key, value)


def group_scatter(parts, here, core, chips):
    _, _, rows, width = parts.shape
    pieces = parts.reshape(2, chips, 2, rows, width)
    size = 2 * chips
    swap = [(i, i ^ 1) for i in range(2 * size)]
    give = lax.dynamic_index_in_dim(pieces, 1 - core, 2, keepdims=False)
    keep = lax.dynamic_index_in_dim(pieces, core, 2, keepdims=False)
    got = lax.ppermute(give, "ctx", swap)
    both = (keep.astype(jnp.float32) + got.astype(jnp.float32)).astype(jnp.bfloat16)
    total = lax.dynamic_index_in_dim(both, here, 1, keepdims=False).astype(jnp.float32)
    for s in range(1, chips):
        hop = [
            (i, (i // size) * size + ((i % size) // 2 + s) % chips * 2 + i % 2)
            for i in range(2 * size)
        ]
        sent = lax.dynamic_index_in_dim(both, (here + s) % chips, 1, keepdims=False)
        total = total + lax.ppermute(sent, "ctx", hop).astype(jnp.float32)
    return total.reshape(2 * rows, width)


def nt(left_side, right_side):
    return lax.dot_general(
        left_side, right_side, (((1,), (1,)), ((), ())), preferred_element_type=jnp.float32
    )


def stacked(ref, piece, rows, sub):
    return jnp.concatenate(
        [
            ref[piece * rows + sub * s : piece * rows + sub * (s + 1), h * HEAD_DIM : (h + 1) * HEAD_DIM]
            for s in range(SUBS)
            for h in range(2)
        ],
        axis=0,
    )


def unstacked(ref, value, piece, rows, sub):
    for s in range(SUBS):
        for h in range(2):
            start = (2 * s + h) * sub
            ref[piece * rows + sub * s : piece * rows + sub * (s + 1), h * HEAD_DIM : (h + 1) * HEAD_DIM] = (
                value[start : start + sub].astype(ref.dtype)
            )


def attend_forward_kernel(rows, meta, q_ref, k_ref, v_ref, o_ref, l_ref, qs, acc, part):
    sub = rows // SUBS
    head = pl.program_id(0)

    @pl.when(head == 0)
    def _():
        l_ref[...] = jnp.zeros_like(l_ref)

    for piece in range(2):
        qs[...] = stacked(q_ref, piece, rows, sub)
        acc[...] = jnp.zeros_like(acc)
        part[...] = jnp.zeros_like(part)
        base = meta[piece]

        def trunk(step, carry):
            start = pl.multiple_of(step * CHUNK, CHUNK)
            scores = nt(qs[...], k_ref[pl.ds(start, CHUNK), :])
            weights = jnp.exp2(scores * exp2_scale)
            if piece == 0:
                at = lax.broadcasted_iota(jnp.int32, weights.shape, 0)
                at = base + (at // (2 * sub)) * sub + at % sub
                key_at = start + lax.broadcasted_iota(jnp.int32, weights.shape, 1)
                weights = jnp.where(key_at <= at, weights, 0.0)
            part[...] += weights[:, :HEAD_DIM] + weights[:, HEAD_DIM:]
            acc[...] += jnp.dot(
                weights.astype(jnp.bfloat16),
                v_ref[pl.ds(start, CHUNK), :],
                preferred_element_type=jnp.float32,
            )
            return carry

        lax.fori_loop(0, meta[32 + piece], trunk, 0)
        for s in range(SUBS):
            index = piece * SUBS + s
            block = slice(2 * sub * s, 2 * sub * (s + 1))

            def add(start, masked):
                start = pl.multiple_of(start, SEG)
                scores = nt(qs[block], k_ref[pl.ds(start, SEG), :])
                weights = jnp.exp2(scores * exp2_scale)
                if masked:
                    at = lax.broadcasted_iota(jnp.int32, weights.shape, 0)
                    at = lax.rem(base + s * sub, SEG) + at % sub
                    key_at = lax.broadcasted_iota(jnp.int32, weights.shape, 1)
                    weights = jnp.where(key_at <= at, weights, 0.0)
                part[block] += weights
                acc[block] += jnp.dot(
                    weights.astype(jnp.bfloat16),
                    v_ref[pl.ds(start, SEG), :],
                    preferred_element_type=jnp.float32,
                )

            @pl.when(meta[22 + index] > 0)
            def _():
                add(meta[2 + index], True)

            @pl.when(meta[22 + index] > 1)
            def _():
                add(meta[12 + index], False)

        total = jnp.sum(part[...], axis=-1, keepdims=True)
        unstacked(o_ref, acc[...] / total, piece, rows, sub)
        lanes = lax.broadcasted_iota(jnp.int32, (2 * rows, HEAD_DIM), 1)
        region = slice(piece * 2 * rows, (piece + 1) * 2 * rows)
        l_ref[region] = jnp.where(lanes == head, total, l_ref[region])


def attend_forward(meta, queries, keys, values):
    rows = queries.shape[0] // 2
    tree = keys.shape[0]
    return pl.pallas_call(
        functools.partial(attend_forward_kernel, rows),
        out_shape=[
            jax.ShapeDtypeStruct((2 * rows, QD), jnp.bfloat16),
            jax.ShapeDtypeStruct((4 * rows, HEAD_DIM), jnp.float32),
        ],
        grid_spec=pltpu.PrefetchScalarGridSpec(
            num_scalar_prefetch=1,
            grid=(KV_HEADS,),
            in_specs=[
                pl.BlockSpec((2 * rows, 2 * HEAD_DIM), lambda h, meta: (0, h)),
                pl.BlockSpec((tree, HEAD_DIM), lambda h, meta: (0, h)),
                pl.BlockSpec((tree, HEAD_DIM), lambda h, meta: (0, h)),
            ],
            out_specs=[
                pl.BlockSpec((2 * rows, 2 * HEAD_DIM), lambda h, meta: (0, h)),
                pl.BlockSpec((4 * rows, HEAD_DIM), lambda h, meta: (0, 0)),
            ],
            scratch_shapes=[
                pltpu.VMEM((2 * rows, HEAD_DIM), jnp.bfloat16),
                pltpu.VMEM((2 * rows, HEAD_DIM), jnp.float32),
                pltpu.VMEM((2 * rows, HEAD_DIM), jnp.float32),
            ],
        ),
        compiler_params=pltpu.CompilerParams(
            dimension_semantics=("arbitrary",), vmem_limit_bytes=48 * 1024 * 1024
        ),
        cost_estimate=pl.CostEstimate(
            flops=4 * 2 * rows * 1200 * QD, bytes_accessed=20_000_000, transcendentals=0
        ),
        name="attend_forward",
    )(meta, queries, keys, values)


def attend_backward_kernel(
    rows, meta, q_ref, g_ref, k_ref, v_ref, lse_ref, del_ref, lses_ref, dels_ref, dq_ref, dk_ref, dv_ref, qs, gs, dq, dk, dv
):
    sub = rows // SUBS
    dk[...] = jnp.zeros_like(dk)
    dv[...] = jnp.zeros_like(dv)
    for piece in range(2):
        qs[...] = stacked(q_ref, piece, rows, sub)
        gs[...] = stacked(g_ref, piece, rows, sub)
        dq[...] = jnp.zeros_like(dq)
        base = meta[piece]

        def add(start, width, block, lse, delta, mask):
            key = k_ref[pl.ds(start, width), :]
            scores = nt(key, qs[block])
            weights = jnp.exp2(scores * exp2_scale - lse)
            if mask is not None:
                weights = jnp.where(mask, weights, 0.0)
            grads = nt(v_ref[pl.ds(start, width), :], gs[block])
            grads = (weights * (grads - delta)).astype(jnp.bfloat16)
            dv[pl.ds(start, width), :] += jnp.dot(
                weights.astype(jnp.bfloat16), gs[block], preferred_element_type=jnp.float32
            )
            dk[pl.ds(start, width), :] += jnp.dot(
                grads, qs[block], preferred_element_type=jnp.float32
            )
            dq[block] += lax.dot_general(
                grads, key, (((0,), (0,)), ((), ())), preferred_element_type=jnp.float32
            )

        def trunk(step, carry):
            start = pl.multiple_of(step * CHUNK, CHUNK)
            mask = None
            if piece == 0:
                shape = (CHUNK, 2 * rows)
                at = lax.broadcasted_iota(jnp.int32, shape, 1)
                at = base + (at // (2 * sub)) * sub + at % sub
                mask = start + lax.broadcasted_iota(jnp.int32, shape, 0) <= at
            add(start, CHUNK, slice(0, 2 * rows), lse_ref[0, piece], del_ref[0, piece], mask)
            return carry

        lax.fori_loop(0, meta[32 + piece], trunk, 0)
        for s in range(SUBS):
            index = piece * SUBS + s
            block = slice(2 * sub * s, 2 * sub * (s + 1))

            @pl.when(meta[22 + index] > 0)
            def _():
                shape = (SEG, 2 * sub)
                at = lax.rem(base + s * sub, SEG) + lax.broadcasted_iota(jnp.int32, shape, 1) % sub
                mask = lax.broadcasted_iota(jnp.int32, shape, 0) <= at
                start = pl.multiple_of(meta[2 + index], SEG)
                add(start, SEG, block, lses_ref[0, index], dels_ref[0, index], mask)

            @pl.when(meta[22 + index] > 1)
            def _():
                start = pl.multiple_of(meta[12 + index], SEG)
                add(start, SEG, block, lses_ref[0, index], dels_ref[0, index], None)

        unstacked(dq_ref, dq[...] * score_scale, piece, rows, sub)
    dk_ref[...] = (dk[...] * score_scale).astype(dk_ref.dtype)
    dv_ref[...] = dv[...].astype(dv_ref.dtype)


def attend_backward(meta, queries, grads, keys, values, log_total, delta):
    rows = queries.shape[0] // 2
    tree = keys.shape[0]
    sub = rows // SUBS
    wide = pl.BlockSpec((2 * rows, 2 * HEAD_DIM), lambda h, meta: (0, h))
    tall = pl.BlockSpec((tree, HEAD_DIM), lambda h, meta: (0, h))
    line = pl.BlockSpec((1, 2, 1, 2 * rows), lambda h, meta: (h, 0, 0, 0))
    lines = pl.BlockSpec((1, 2 * SUBS, 1, 2 * sub), lambda h, meta: (h, 0, 0, 0))
    return pl.pallas_call(
        functools.partial(attend_backward_kernel, rows),
        out_shape=[
            jax.ShapeDtypeStruct((2 * rows, QD), jnp.float32),
            jax.ShapeDtypeStruct((tree, KVD), jnp.bfloat16),
            jax.ShapeDtypeStruct((tree, KVD), jnp.bfloat16),
        ],
        grid_spec=pltpu.PrefetchScalarGridSpec(
            num_scalar_prefetch=1,
            grid=(KV_HEADS,),
            in_specs=[wide, wide, tall, tall, line, line, lines, lines],
            out_specs=[wide, tall, tall],
            scratch_shapes=[
                pltpu.VMEM((2 * rows, HEAD_DIM), jnp.bfloat16),
                pltpu.VMEM((2 * rows, HEAD_DIM), jnp.bfloat16),
                pltpu.VMEM((2 * rows, HEAD_DIM), jnp.float32),
                pltpu.VMEM((tree, HEAD_DIM), jnp.float32),
                pltpu.VMEM((tree, HEAD_DIM), jnp.float32),
            ],
        ),
        compiler_params=pltpu.CompilerParams(
            dimension_semantics=("arbitrary",), vmem_limit_bytes=48 * 1024 * 1024
        ),
        cost_estimate=pl.CostEstimate(
            flops=10 * 2 * rows * 1200 * QD, bytes_accessed=40_000_000, transcendentals=0
        ),
        name="attend_backward",
    )(
        meta,
        queries,
        grads,
        keys,
        values,
        log_total.reshape(KV_HEADS, 2, 1, 2 * rows),
        delta.reshape(KV_HEADS, 2, 1, 2 * rows),
        log_total.reshape(KV_HEADS, 2 * SUBS, 1, 2 * sub),
        delta.reshape(KV_HEADS, 2 * SUBS, 1, 2 * sub),
    )


def attention_meta(seg_tree, parent_tree, rows, group_size, member):
    sub = rows // SUBS
    run_seg = seg_tree[TRUNK::SEG]
    run_parent = parent_tree[run_seg]
    parent_run = jnp.argmax(run_seg[None, :] == run_parent[:, None], axis=1).astype(jnp.int32)
    bases = jnp.stack([rows * member, rows * (group_size + member)]).astype(jnp.int32)
    starts = (bases[:, None] + sub * jnp.arange(SUBS, dtype=jnp.int32)[None, :]).reshape(-1)
    tail = starts >= TRUNK
    run = jnp.maximum(starts - TRUNK, 0) // SEG
    own = TRUNK + SEG * run
    parent = TRUNK + SEG * parent_run[run]
    kind = jnp.where(tail, jnp.where(run_parent[run] > 0, 2, 1), 0)
    chunks = jnp.minimum((bases + rows + CHUNK - 1) // CHUNK, TRUNK // CHUNK)
    return jnp.concatenate([bases, own, parent, kind, chunks]).astype(jnp.int32)


def shards(
    sizes,
    tokens,
    cotangent,
    segment_ids,
    positions,
    parents,
    input_norm,
    query_proj,
    key_proj,
    value_proj,
    query_norm,
    key_norm,
    out_proj,
    post_norm,
    gate_proj,
    up_proj,
    down_proj,
):
    nz = sizes[2]
    rows = tokens.shape[1]
    shard_rows = query_proj.shape[0]
    gain_rows = query_norm.shape[0]
    group_size = nz
    ctx = lax.axis_index("ctx")
    half = ctx // group_size
    member = ctx % group_size
    here, core = member // 2, member % 2
    count_rows = 2 * rows

    def column(gain):
        return jnp.pad(gain, (0, shard_rows - gain.shape[0]))[:, None]

    gains = jnp.concatenate(
        [column(input_norm), column(post_norm), column(query_norm), column(key_norm)], axis=1
    )
    gains = jnp.pad(gains, ((0, 0), (0, GAIN_COLS - 4)))
    key_value = jnp.concatenate([key_proj, value_proj, gains], axis=1)
    feed_shard = jnp.concatenate([out_proj.T, gate_proj, up_proj, down_proj.T], axis=1)

    (query_full, key_value_full), (inputs_low, grad_out) = gather_weights(
        sizes, ("zxy", "zyx"), [query_proj, key_value], [tokens, cotangent], 1
    )
    feed_full = lax.all_gather(feed_shard, AXES, axis=0, tiled=True)

    gain_block = key_value_full[:, 2 * KVD :].astype(jnp.float32)
    in_weight = gain_block[:, 0]
    post_weight = gain_block[:, 1]
    by_device = gain_block.reshape(-1, shard_rows, GAIN_COLS)
    query_weight = by_device[:, :gain_rows, 2].reshape(HEAD_DIM)
    key_weight = by_device[:, :gain_rows, 3].reshape(HEAD_DIM)

    seg_tree = segment_ids[half]
    pos_tree = positions[half].reshape(2, group_size, rows)
    pos_local = lax.dynamic_index_in_dim(pos_tree, member, 1, keepdims=False).reshape(count_rows)
    meta = attention_meta(seg_tree, parents[half], rows, group_size, member)
    cosine_table, sine_table = rope_tables(pos_local)

    inputs = inputs_low.reshape(count_rows, D).astype(jnp.float32)
    grad_out = grad_out.reshape(count_rows, D)

    normed_in, in_hat, in_factor = norm_forward(inputs, in_weight)
    normed_low = normed_in.astype(jnp.bfloat16)
    query_pre = matmul(normed_low, query_full).reshape(count_rows, HEADS, HEAD_DIM)
    key_pre = matmul(normed_low, key_value_full[:, :KVD]).reshape(count_rows, KV_HEADS, HEAD_DIM)
    value_low = matmul(normed_low, key_value_full[:, KVD : 2 * KVD]).astype(jnp.bfloat16)
    query_normed, query_hat, query_factor = norm_forward(query_pre, query_weight)
    key_normed, key_hat, key_factor = norm_forward(key_pre, key_weight)
    query_low = rotate(query_normed, cosine_table, sine_table).astype(jnp.bfloat16)
    key_low = rotate(key_normed, cosine_table, sine_table).astype(jnp.bfloat16)
    query_low = query_low.reshape(count_rows, QD)
    tree_keys, tree_values = group_gather(
        sizes, key_low.reshape(2, rows, KVD), value_low.reshape(2, rows, KVD), 2
    )
    tree_keys = tree_keys.reshape(TREE, KVD)
    tree_values = tree_values.reshape(TREE, KVD)
    mixed_low, totals = attend_forward(meta, query_low, tree_keys, tree_values)
    log_total = jnp.log2(totals[:, :KV_HEADS]).T

    out_t = feed_full[:, :QD]
    gate_full = feed_full[:, QD : QD + FF]
    up_full = feed_full[:, QD + FF : QD + 2 * FF]
    down_t = feed_full[:, QD + 2 * FF :]
    hidden = inputs + matmul_t(mixed_low, out_t)
    normed_post, post_hat, post_factor = norm_forward(hidden, post_weight)
    second_low = normed_post.astype(jnp.bfloat16)
    gate_pre = matmul(second_low, gate_full)
    up_pre = matmul(second_low, up_full)
    activated = jax.nn.silu(gate_pre)
    inner_low = (activated * up_pre).astype(jnp.bfloat16)
    result = (hidden + matmul_t(inner_low, down_t)).astype(jnp.bfloat16)

    grad_inner = matmul(grad_out, down_t)
    sigmoid_gate = jax.nn.sigmoid(gate_pre)
    grad_gate = (
        grad_inner * up_pre * sigmoid_gate * (1.0 + gate_pre * (1.0 - sigmoid_gate))
    ).astype(jnp.bfloat16)
    grad_up = (grad_inner * activated).astype(jnp.bfloat16)
    grad_second = matmul_t(grad_gate, gate_full) + matmul_t(grad_up, up_full)
    feed_part = jnp.concatenate(
        [
            contract_rows(second_low, grad_gate),
            contract_rows(second_low, grad_up),
            contract_rows(grad_out, inner_low),
        ],
        axis=1,
    ).astype(jnp.bfloat16)
    feed_grad = lax.psum_scatter(feed_part, AXES, scatter_dimension=0, tiled=True)

    grad_post_in, post_part = norm_backward(grad_second, post_weight, post_hat, post_factor)
    grad_hidden = grad_out.astype(jnp.float32) + grad_post_in
    grad_branch = grad_hidden.astype(jnp.bfloat16)
    grad_mixed = matmul(grad_branch, out_t).astype(jnp.bfloat16)
    delta = jnp.sum(
        (grad_mixed.astype(jnp.float32) * mixed_low.astype(jnp.float32)).reshape(
            count_rows, HEADS, HEAD_DIM
        ),
        axis=-1,
    )
    delta = delta.reshape(2, SUBS, rows // SUBS, KV_HEADS, 2).transpose(3, 0, 1, 4, 2)
    grad_queries, grad_keys, grad_values = attend_backward(
        meta, query_low, grad_mixed, tree_keys, tree_values, log_total, delta
    )
    key_grad = group_scatter(grad_keys.reshape(2, group_size, rows, KVD), here, core, nz // 2)
    value_grad = group_scatter(grad_values.reshape(2, group_size, rows, KVD), here, core, nz // 2)

    grad_query_normed = rotate_back(
        grad_queries.reshape(count_rows, HEADS, HEAD_DIM), cosine_table, sine_table
    )
    grad_query_pre, query_part = norm_backward(
        grad_query_normed, query_weight, query_hat, query_factor
    )
    grad_key_normed = rotate_back(
        key_grad.reshape(count_rows, KV_HEADS, HEAD_DIM), cosine_table, sine_table
    )
    grad_key_pre, key_part = norm_backward(grad_key_normed, key_weight, key_hat, key_factor)
    grad_query_low = grad_query_pre.reshape(count_rows, QD).astype(jnp.bfloat16)
    grad_key_low = grad_key_pre.reshape(count_rows, KVD).astype(jnp.bfloat16)
    grad_value_low = value_grad.astype(jnp.bfloat16)
    grad_key_value = jnp.concatenate([grad_key_low, grad_value_low], axis=1)
    grad_normed = matmul_t(grad_query_low, query_full) + matmul_t(
        grad_key_value, key_value_full[:, : 2 * KVD]
    )
    grad_in_norm, in_part = norm_backward(grad_normed, in_weight, in_hat, in_factor)
    input_grad = grad_hidden + grad_in_norm

    def gain_column(values):
        if values.shape[0] == D:
            return values[:, None]
        spread = jnp.pad(values.reshape(-1, gain_rows), ((0, 0), (0, shard_rows - gain_rows)))
        return spread.reshape(D, 1)

    gain_grads = jnp.concatenate(
        [
            gain_column(jnp.sum(in_part, axis=0)),
            gain_column(jnp.sum(post_part, axis=0)),
            gain_column(jnp.sum(query_part, axis=(0, 1))),
            gain_column(jnp.sum(key_part, axis=(0, 1))),
        ],
        axis=1,
    )
    gain_grads = jnp.pad(gain_grads, ((0, 0), (0, GAIN_COLS - 4)))
    attention_part = jnp.concatenate(
        [
            contract_rows(normed_low, grad_query_low),
            contract_rows(normed_low, grad_key_value),
            contract_rows(grad_branch, mixed_low),
            gain_grads,
        ],
        axis=1,
    ).astype(jnp.bfloat16)
    attention_grad = lax.psum_scatter(attention_part, AXES, scatter_dimension=0, tiled=True)

    swap = [(i, (i + group_size) % (2 * group_size)) for i in range(2 * group_size)]

    def send_back(values):
        pieces = values.reshape(2, rows, D)
        keep = pieces[half]
        got = lax.ppermute(pieces[1 - half].astype(jnp.bfloat16), "ctx", swap)
        got = got.astype(values.dtype)
        return jnp.where(half == 0, jnp.stack([keep, got]), jnp.stack([got, keep]))

    attention_grad = attention_grad.astype(jnp.float32)
    feed_grad = feed_grad.astype(jnp.float32)
    gain_grad = attention_grad[:, QD + 2 * KVD + QD :]
    return (
        send_back(result),
        send_back(input_grad),
        gain_grad[:, 0],
        attention_grad[:, :QD],
        attention_grad[:, QD : QD + KVD],
        attention_grad[:, QD + KVD : QD + 2 * KVD],
        gain_grad[:gain_rows, 2],
        gain_grad[:gain_rows, 3],
        attention_grad[:, QD + 2 * KVD : QD + 2 * KVD + QD].T,
        gain_grad[:, 1],
        feed_grad[:, :FF],
        feed_grad[:, FF : 2 * FF],
        feed_grad[:, 2 * FF :].T,
    )


def solution(mesh):
    dp, ctx = mesh.shape["dp"], mesh.shape["ctx"]
    sizes = (2, dp // 2, ctx // 2)
    return jax.shard_map(
        functools.partial(shards, sizes),
        mesh=mesh,
        in_specs=(
            P("dp", "ctx", None),
            P("dp", "ctx", None),
            P("dp", None),
            P("dp", None),
            P("dp", None),
            P(("dp", "ctx")),
            P(("dp", "ctx"), None),
            P(("dp", "ctx"), None),
            P(("dp", "ctx"), None),
            P(("dp", "ctx")),
            P(("dp", "ctx")),
            P(None, ("dp", "ctx")),
            P(("dp", "ctx")),
            P(("dp", "ctx"), None),
            P(("dp", "ctx"), None),
            P(None, ("dp", "ctx")),
        ),
        out_specs=(
            P("dp", "ctx", None),
            P("dp", "ctx", None),
            P(("dp", "ctx")),
            P(("dp", "ctx"), None),
            P(("dp", "ctx"), None),
            P(("dp", "ctx"), None),
            P(("dp", "ctx")),
            P(("dp", "ctx")),
            P(None, ("dp", "ctx")),
            P(("dp", "ctx")),
            P(("dp", "ctx"), None),
            P(("dp", "ctx"), None),
            P(None, ("dp", "ctx")),
        ),
        check_vma=False,
    )
```

```python
import functools
import math

import jax
import jax.numpy as jnp
from jax import lax
from jax.experimental import pallas as pl
from jax.experimental.pallas import tpu as pltpu
from jax.sharding import PartitionSpec as P

D = 1024
HEADS = 16
KV_HEADS = 8
HEAD_DIM = 128
FF = 3072
TRUNK = 1024
SEG = 128
TREE = 2560
QD = HEADS * HEAD_DIM
KVD = KV_HEADS * HEAD_DIM
SUBS = 5
CHUNK = 256
GAIN_COLS = 128
LOCAL_RUNS = 3
MIB = 1024 * 1024

eps_norm = 1e-06
rope_base = 1000000.0
exp2_scale = math.log2(math.e) / math.sqrt(HEAD_DIM)
score_scale = HEAD_DIM ** (-0.5)

MESH = pl.DeviceIdType.MESH
ANY = pl.BlockSpec(memory_space=pl.ANY)
F32 = jnp.float32
BF16 = jnp.bfloat16


def matmul(left_side, right_side):
    return jnp.dot(left_side, right_side, preferred_element_type=F32)


def nt(left_side, right_side):
    return lax.dot_general(
        left_side, right_side, (((1,), (1,)), ((), ())), preferred_element_type=F32
    )


def contract_rows(left_side, right_side):
    return lax.dot_general(
        left_side, right_side, (((0,), (0,)), ((), ())), preferred_element_type=F32
    )


def norm_factor(values):
    return lax.rsqrt(jnp.mean(values * values, axis=-1, keepdims=True) + eps_norm)


def norm_backward(grad_out, weight, normed, factor):
    weighted = grad_out * weight
    grad_in = factor * (weighted - normed * jnp.mean(weighted * normed, axis=-1, keepdims=True))
    return (grad_in, grad_out * normed)


def rope_tables(positions):
    steps_half = jnp.arange(HEAD_DIM // 2, dtype=F32)
    inverse = rope_base ** (-(steps_half * 2.0 / HEAD_DIM))
    angles = positions.astype(F32)[:, None] * inverse[None, :]
    cosine, sine = jnp.cos(angles), jnp.sin(angles)
    return jnp.concatenate([cosine, cosine], axis=-1), jnp.concatenate([-sine, sine], axis=-1)


class Links:
    def __init__(self, sizes, send_sem, recv_sem):
        self.sizes = sizes
        self.send_sem = send_sem
        self.recv_sem = recv_sem
        self.index = {}

    def place(self):
        _, nx, _ = self.sizes
        dp, ctx = lax.axis_index("dp"), lax.axis_index("ctx")
        return dp // nx, lax.rem(dp, nx), ctx // 2, lax.rem(ctx, 2)

    def device(self, y, x, z, core):
        return (y * self.sizes[1] + x, z * 2 + core)

    def peers(self, axis, back=False):
        y, x, z, core = self.place()
        at = {"y": y, "x": x, "z": z}
        n = self.sizes["yxz".index(axis)]
        found = []
        for s in range(1, n):
            moved = dict(at)
            moved[axis] = lax.rem(at[axis] + (n - s if back else s), n)
            found.append((moved["y"], moved["x"], moved["z"], core))
        return found

    def sibling(self):
        y, x, z, core = self.place()
        return self.device(y, x, z, 1 - core)

    def across(self):
        y, x, z, core = self.place()
        nz = self.sizes[2]
        return self.device(y, x, lax.rem(z + nz // 2, nz), core)

    def group(self, back=False):
        y, x, z, core = self.place()
        chips = self.sizes[2] // 2
        base = (z // chips) * chips
        here = z - base
        chosen = [lax.rem(here + (chips - s if back else s), chips) for s in range(1, chips)]
        return [(chip, self.device(y, x, base + chip, core)) for chip in chosen]

    def meet(self):
        barrier = pltpu.get_barrier_semaphore()
        partners = [self.device(*p) for a in "zxy" for p in self.peers(a)] + [self.sibling()]
        for partner in partners:
            pl.semaphore_signal(barrier, inc=1, device_id=partner, device_id_type=MESH)
        pl.semaphore_wait(barrier, len(partners))

    def copy(self, key, src, dst, target):
        k = self.index.setdefault(key, len(self.index))
        return pltpu.make_async_remote_copy(
            src_ref=src,
            dst_ref=dst,
            send_sem=self.send_sem.at[k],
            recv_sem=self.recv_sem.at[k],
            device_id=target,
            device_id_type=MESH,
        )


class Gather:
    def __init__(self, links, tag, shard, whole, order, cols, local_sem):
        self.links = links
        self.tag = tag
        self.shard = shard
        self.whole = whole
        self.order = order
        self.cols = cols
        self.local_sem = local_sem

    def own(self):
        y, x, z, core = self.links.place()
        return self.whole.at[y, x, z, core, :, self.cols]

    def slab(self, stage, at):
        y, x, z, core = at
        if stage == 0:
            return self.whole.at[y, x, z, core, :, self.cols]
        if stage == 1:
            return self.whole.at[y, x, :, core, :, self.cols]
        if self.order[0] == "x":
            return self.whole.at[y, :, :, core, :, self.cols]
        return self.whole.at[:, x, :, core, :, self.cols]

    def axis(self, stage):
        return ("z",) + tuple(self.order)[0:2] if stage is None else ("z", self.order[0], self.order[1])[stage]

    def send(self, stage):
        me = self.links.place()
        src = self.shard.at[:, self.cols] if stage == 0 else self.slab(stage, me)
        dst = self.slab(stage, me)
        return [
            self.links.copy((self.tag, stage, i), src, dst, self.links.device(*p))
            for i, p in enumerate(self.links.peers(self.axis(stage)))
        ]

    def forward(self, stage):
        sibling = self.links.sibling()
        if stage < 0:
            return [self.links.copy((self.tag, "own"), self.shard.at[:, self.cols], self.own(), sibling)]
        return [
            self.links.copy((self.tag, "pass", stage, i), self.slab(stage, p), self.slab(stage, p), sibling)
            for i, p in enumerate(self.links.peers(self.axis(stage), back=True))
        ]

    def local(self):
        return pltpu.make_async_copy(self.shard.at[:, self.cols], self.own(), self.local_sem)

    def start(self):
        self.local().start()
        for copy in self.send(0) + self.forward(-1):
            copy.start()

    def step(self, stage):
        if stage == 1:
            self.local().wait()
        for copy in self.send(stage - 1):
            copy.wait()
        if stage < 3:
            for copy in self.send(stage):
                copy.start()
        for copy in self.forward(stage - 1):
            copy.start()

    def close(self):
        for stage in range(-1, 3):
            for copy in self.forward(stage):
                copy.wait()

    @staticmethod
    def copies(sizes):
        return 2 * sum(n - 1 for n in sizes) + 1


class Scatter:
    def __init__(self, links, tag, part, order, cols, halves, firsts, seconds, thirds, temp, temp_sem, out):
        self.links = links
        self.tag = tag
        self.part = part
        self.order = order
        self.cols = cols
        self.sums = halves
        self.got = (firsts, seconds, thirds)
        self.temp = temp
        self.temp_sem = temp_sem
        self.out = out

    def first(self):
        _, _, _, core = self.links.place()
        return self.links.copy(
            (self.tag, "core"), self.part.at[:, :, :, 1 - core, :, self.cols], self.sums, self.links.sibling()
        )

    def load(self):
        _, _, _, core = self.links.place()
        return pltpu.make_async_copy(
            self.part.at[:, :, :, core, :, self.cols], self.temp, self.temp_sem
        )

    def axis(self, stage):
        return (self.order[0], self.order[1], "z")[stage]

    def at(self, stage, place, rest=None):
        y, x, z, _ = place
        if stage == 0:
            return (y,) if self.order[0] == "y" else (slice(None), x)
        if stage == 1:
            return (y, x)
        return (y, x, z)

    def send(self, stage):
        me = self.links.place()
        found = []
        for i, p in enumerate(self.links.peers(self.axis(stage))):
            index = self.at(stage, p)
            found.append(
                self.links.copy(
                    (self.tag, stage, i), self.sums.at[index], self.got[stage].at[i], self.links.device(*p)
                )
            )
        return found

    def start(self):
        self.first().start()

    def begin(self):
        self.first().wait()
        self.load().wait()
        ny, nx, nz = self.links.sizes

        def add(i, carry):
            a, b, c = i // (nx * nz), lax.rem(i // nz, nx), lax.rem(i, nz)
            self.sums[a, b, c] = (
                self.sums[a, b, c].astype(F32) + self.temp[a, b, c].astype(F32)
            ).astype(BF16)
            return carry

        lax.fori_loop(0, ny * nx * nz, add, 0)
        for copy in self.send(0):
            copy.start()

    def middle(self, stage):
        for copy in self.send(stage):
            copy.wait()
        y, x, z, _ = self.links.place()
        _, _, nz = self.links.sizes
        got = self.got[stage]
        peers = got.shape[0]
        if stage == 0:
            other = got.shape[1]

            def add(i, carry):
                b, c = i // nz, lax.rem(i, nz)
                index = (y, b, c) if self.order[0] == "y" else (b, x, c)
                total = self.sums[index].astype(F32)
                for p in range(peers):
                    total = total + got[p, b, c].astype(F32)
                self.sums[index] = total.astype(BF16)
                return carry

            lax.fori_loop(0, other * nz, add, 0)
        else:

            def add(c, carry):
                total = self.sums[y, x, c].astype(F32)
                for p in range(peers):
                    total = total + got[p, c].astype(F32)
                self.sums[y, x, c] = total.astype(BF16)
                return carry

            lax.fori_loop(0, nz, add, 0)
        for copy in self.send(stage + 1):
            copy.start()

    def finish(self):
        for copy in self.send(2):
            copy.wait()
        y, x, z, _ = self.links.place()
        total = self.sums[y, x, z].astype(F32)
        for p in range(self.got[2].shape[0]):
            total = total + self.got[2][p].astype(F32)
        self.out[:, self.cols] = total

    @staticmethod
    def copies(sizes):
        return sum(n - 1 for n in sizes) + 1

    @staticmethod
    def scratch(sizes, order, rows, width):
        ny, nx, nz = sizes
        na, nb = (ny, nx) if order[0] == "y" else (nx, ny)
        return [
            pltpu.VMEM((ny, nx, nz, rows, width), BF16),
            pltpu.VMEM((na - 1, nb, nz, rows, width), BF16),
            pltpu.VMEM((nb - 1, nz, rows, width), BF16),
            pltpu.VMEM((nz - 1, rows, width), BF16),
        ]


ORDERS = ("xy", "yx")


def halves_of(width):
    return (slice(0, width // 2), slice(width // 2, width)) if width >= 512 else (slice(0, width),)


def gather_kernel(sizes, query_ref, kv_ref, moved_ref, query_whole, kv_whole, placed_ref, send_sem, recv_sem, local_sem):
    links = Links(sizes, send_sem, recv_sem)
    links.meet()
    _, _, z, _ = links.place()
    half = z // (sizes[2] // 2)
    parts = []
    for a, (shard, whole) in enumerate(((query_ref, query_whole), (kv_ref, kv_whole))):
        width = shard.shape[-1]
        for b in range(2):
            edge = width // 2 // HEAD_DIM * HEAD_DIM
            cols = slice(0, edge) if b == 0 else slice(edge, width)
            parts.append(
                Gather(links, (a, b), shard, whole, ORDERS[b], cols, local_sem.at[2 * a + b])
            )
    keep = pltpu.make_async_copy(moved_ref.at[half], placed_ref.at[half], local_sem.at[4])
    give = links.copy("moved", moved_ref.at[1 - half], placed_ref.at[half], links.across())
    for part in parts[:2]:
        part.start()
    keep.start()
    for part in parts[2:]:
        part.start()
    for part in parts[:2]:
        part.step(1)
    give.start()
    for part in parts[2:]:
        part.step(1)
    for part in parts[:2]:
        part.step(2)
    for part in parts[2:]:
        part.step(2)
    for part in parts:
        part.step(3)
    for part in parts:
        part.close()
    keep.wait()
    give.wait()


def gather_start(sizes, query, key_value, moved):
    ny, nx, nz = sizes
    rounds = 4 * Gather.copies(sizes) + 1
    query_whole, kv_whole, placed = pl.pallas_call(
        functools.partial(gather_kernel, sizes),
        out_shape=[
            jax.ShapeDtypeStruct((ny, nx, nz, 2) + query.shape, BF16),
            jax.ShapeDtypeStruct((ny, nx, nz, 2) + key_value.shape, BF16),
            jax.ShapeDtypeStruct(moved.shape, BF16),
        ],
        in_specs=[ANY] * 3,
        out_specs=[ANY] * 3,
        scratch_shapes=[
            pltpu.SemaphoreType.DMA((rounds,)),
            pltpu.SemaphoreType.DMA((rounds,)),
            pltpu.SemaphoreType.DMA((5,)),
        ],
        compiler_params=pltpu.CompilerParams(collective_id=1, has_side_effects=True),
        name="gather_start",
    )(query, key_value, moved)
    return query_whole.reshape(D, -1), kv_whole.reshape(D, -1), placed


def roll_half(values):
    return pltpu.roll(values, HEAD_DIM // 2, 1)


def project_kernel(rows, x_ref, gain_ref, wq_ref, wk_ref, wv_ref, qg_ref, kg_ref, cos_ref, sin_ref, normed_ref, q_ref, kv_ref, pre_ref):
    sub = rows // SUBS

    @pl.when(pl.program_id(0) == 0)
    def _():
        values = x_ref[...].astype(F32)
        normed_ref[...] = (values * norm_factor(values) * gain_ref[...]).astype(BF16)

    normed = normed_ref[...]
    cosine, sine = cos_ref[...], sin_ref[...]

    def turned(pre, gain):
        values = pre * norm_factor(pre) * gain
        return (values * cosine + roll_half(values) * sine).astype(BF16)

    query = matmul(normed, wq_ref[...])
    for h in range(2):
        pre = query[:, h * HEAD_DIM : (h + 1) * HEAD_DIM]
        pre_ref[0, :, h * HEAD_DIM : (h + 1) * HEAD_DIM] = pre
        low = turned(pre, qg_ref[...])
        for s in range(2 * SUBS):
            q_ref[0, (2 * s + h) * sub : (2 * s + h + 1) * sub] = low[s * sub : (s + 1) * sub]
    pre = matmul(normed, wk_ref[...])
    pre_ref[0, :, 2 * HEAD_DIM :] = pre
    kv_ref[0, 0] = turned(pre, kg_ref[...]).reshape(2, rows, HEAD_DIM)
    kv_ref[1, 0] = matmul(normed, wv_ref[...]).astype(BF16).reshape(2, rows, HEAD_DIM)


def project(x, gain, query_full, kv_full, query_gain, key_gain, cosine, sine):
    count = x.shape[0]
    rows = count // 2
    full = pl.BlockSpec((count, D), lambda h: (0, 0))
    row = lambda n: pl.BlockSpec((1, n), lambda h: (0, 0))
    table = pl.BlockSpec((count, HEAD_DIM), lambda h: (0, 0))
    return pl.pallas_call(
        functools.partial(project_kernel, rows),
        grid=(KV_HEADS,),
        out_shape=[
            jax.ShapeDtypeStruct((count, D), BF16),
            jax.ShapeDtypeStruct((KV_HEADS, 2 * count, HEAD_DIM), BF16),
            jax.ShapeDtypeStruct((2, KV_HEADS, 2, rows, HEAD_DIM), BF16),
            jax.ShapeDtypeStruct((KV_HEADS, count, 3 * HEAD_DIM), F32),
        ],
        in_specs=[
            full,
            row(D),
            pl.BlockSpec((D, 2 * HEAD_DIM), lambda h: (0, h)),
            pl.BlockSpec((D, HEAD_DIM), lambda h: (0, h)),
            pl.BlockSpec((D, HEAD_DIM), lambda h: (0, KV_HEADS + h)),
            row(HEAD_DIM),
            row(HEAD_DIM),
            table,
            table,
        ],
        out_specs=[
            full,
            pl.BlockSpec((1, 2 * count, HEAD_DIM), lambda h: (h, 0, 0)),
            pl.BlockSpec((2, 1, 2, rows, HEAD_DIM), lambda h: (0, h, 0, 0, 0)),
            pl.BlockSpec((1, count, 3 * HEAD_DIM), lambda h: (h, 0, 0)),
        ],
        compiler_params=pltpu.CompilerParams(vmem_limit_bytes=40 * MIB),
        name="project",
    )(x, gain, query_full, kv_full, kv_full, query_gain, key_gain, cosine, sine)


def project_back_kernel(
    rows, dq_ref, dkv_ref, pre_ref, normed_ref, x_ref, hid_ref, gain_ref, wq_ref, wk_ref, wv_ref, qg_ref, kg_ref, cos_ref, sin_ref,
    dwq_ref, dwk_ref, dwv_ref, dx_ref, in_ref, qk_ref, normed_t, grads,
):
    sub = rows // SUBS
    head = pl.program_id(0)

    @pl.when(head == 0)
    def _():
        normed_t[...] = normed_ref[...].astype(F32).T.astype(BF16)
        grads[...] = jnp.zeros_like(grads)
        qk_ref[...] = jnp.zeros_like(qk_ref)

    cosine, sine = cos_ref[...], sin_ref[...]

    def back(turned_grad, pre, gain):
        grad = turned_grad * cosine - roll_half(turned_grad) * sine
        factor = norm_factor(pre)
        grad_pre, part = norm_backward(grad, gain, pre * factor, factor)
        return grad_pre.astype(BF16), jnp.sum(part, axis=0, keepdims=True)

    pieces = []
    for h in range(2):
        grad = jnp.concatenate(
            [dq_ref[0, (2 * s + h) * sub : (2 * s + h + 1) * sub] for s in range(2 * SUBS)], axis=0
        )
        low, part = back(grad, pre_ref[0, :, h * HEAD_DIM : (h + 1) * HEAD_DIM], qg_ref[...])
        qk_ref[0:1] += part
        pieces.append(low)
    low, part = back(dkv_ref[0, 0].reshape(2 * rows, HEAD_DIM), pre_ref[0, :, 2 * HEAD_DIM :], kg_ref[...])
    qk_ref[1:2] += part
    pieces.append(low)
    pieces.append(dkv_ref[1, 0].reshape(2 * rows, HEAD_DIM).astype(BF16))
    low = jnp.concatenate(pieces, axis=1)
    weights = jnp.concatenate([wq_ref[...], wk_ref[...], wv_ref[...]], axis=1)
    grads[...] += nt(low, weights)
    part = matmul(normed_t[...], low).astype(BF16)
    dwq_ref[...] = part[:, : 2 * HEAD_DIM]
    dwk_ref[...] = part[:, 2 * HEAD_DIM : 3 * HEAD_DIM]
    dwv_ref[...] = part[:, 3 * HEAD_DIM :]

    @pl.when(head == KV_HEADS - 1)
    def _():
        values = x_ref[...].astype(F32)
        factor = norm_factor(values)
        grad_in, part = norm_backward(grads[...], gain_ref[...], values * factor, factor)
        dx_ref[...] = (hid_ref[...] + grad_in).astype(BF16)
        in_ref[...] = jnp.sum(part, axis=0, keepdims=True)


def project_back(dq, dkv, pre, normed, x, grad_hidden, gain, query_full, kv_full, query_gain, key_gain, cosine, sine):
    count = x.shape[0]
    rows = count // 2
    full = pl.BlockSpec((count, D), lambda h: (0, 0))
    row = lambda n: pl.BlockSpec((1, n), lambda h: (0, 0))
    table = pl.BlockSpec((count, HEAD_DIM), lambda h: (0, 0))
    wide = pl.BlockSpec((D, 2 * HEAD_DIM), lambda h: (0, h))
    thin = pl.BlockSpec((D, HEAD_DIM), lambda h: (0, h))
    return pl.pallas_call(
        functools.partial(project_back_kernel, rows),
        grid=(KV_HEADS,),
        out_shape=[
            jax.ShapeDtypeStruct((D, QD), BF16),
            jax.ShapeDtypeStruct((D, KVD), BF16),
            jax.ShapeDtypeStruct((D, KVD), BF16),
            jax.ShapeDtypeStruct((count, D), BF16),
            jax.ShapeDtypeStruct((1, D), F32),
            jax.ShapeDtypeStruct((8, HEAD_DIM), F32),
        ],
        in_specs=[
            pl.BlockSpec((1, 2 * count, HEAD_DIM), lambda h: (h, 0, 0)),
            pl.BlockSpec((2, 1, 2, rows, HEAD_DIM), lambda h: (0, h, 0, 0, 0)),
            pl.BlockSpec((1, count, 3 * HEAD_DIM), lambda h: (h, 0, 0)),
            full,
            full,
            full,
            row(D),
            wide,
            thin,
            pl.BlockSpec((D, HEAD_DIM), lambda h: (0, KV_HEADS + h)),
            row(HEAD_DIM),
            row(HEAD_DIM),
            table,
            table,
        ],
        out_specs=[wide, thin, thin, full, row(D), pl.BlockSpec((8, HEAD_DIM), lambda h: (0, 0))],
        scratch_shapes=[pltpu.VMEM((D, count), BF16), pltpu.VMEM((count, D), F32)],
        compiler_params=pltpu.CompilerParams(vmem_limit_bytes=48 * MIB),
        name="project_back",
    )(dq, dkv, pre, normed, x, grad_hidden, gain, query_full, kv_full, kv_full, query_gain, key_gain, cosine, sine)


class KeyValues:
    def __init__(self, links, rows, own, held, local_sem):
        self.links = links
        self.rows = rows
        self.own = own
        self.held = held
        self.local_sem = local_sem

    def slab(self, group, piece, member):
        members = self.links.sizes[2]
        start = pl.multiple_of(self.rows * (piece * members + member), self.rows)
        return self.held.at[:, 2 * group : 2 * group + 2, pl.ds(start, self.rows)]

    def mine(self):
        _, _, z, core = self.links.place()
        return lax.rem(z, self.links.sizes[2] // 2) * 2 + core

    def across(self, group):
        found = []
        for piece in range(2):
            src = self.own.at[:, 2 * group : 2 * group + 2, piece]
            dst = self.slab(group, piece, self.mine())
            for i, (_, target) in enumerate(self.links.group()):
                found.append(self.links.copy(("kv", group, piece, i), src, dst, target))
        return found

    def near(self, group):
        found = []
        for piece in range(2):
            src = self.own.at[:, 2 * group : 2 * group + 2, piece]
            dst = self.slab(group, piece, self.mine())
            found.append(self.links.copy(("kv own", group, piece), src, dst, self.links.sibling()))
            found.append(pltpu.make_async_copy(src, dst, self.local_sem.at[2 * group + piece]))
        return found

    def forward(self, group):
        _, _, _, core = self.links.place()
        found = []
        for piece in range(2):
            for i, (chip, _) in enumerate(self.links.group(back=True)):
                slab = self.slab(group, piece, chip * 2 + core)
                found.append(
                    self.links.copy(("kv pass", group, piece, i), slab, slab, self.links.sibling())
                )
        return found

    @staticmethod
    def copies(sizes):
        return 4 * 2 * (2 * (sizes[2] // 2 - 1) + 1)


def run_all(copies, act):
    for copy in copies:
        if act == "start":
            copy.start()
        else:
            copy.wait()


def row_places(shape, dim, sub):
    t = lax.broadcasted_iota(jnp.int32, shape, dim)
    return (t // (2 * sub)) * sub + t % sub


def gather_parents(meta, lead, slot, pairs):
    runs = (TREE - TRUNK) // SEG
    for k in range(LOCAL_RUNS):
        parent = meta[jnp.minimum(lead + k, runs - 1)]
        for read, out in pairs:
            total = None
            for b in range(runs):
                share = (1 - jnp.minimum(jnp.abs(parent - b), 1)).astype(F32).astype(BF16)
                term = read(b) * share
                total = term if total is None else total + term
            out[slot + k] = total


def forward_kernel(sizes, rows, meta, q_ref, kv_ref, *refs):
    shard = refs[:4]
    mixed_ref, l_ref, kv_all = refs[4:7]
    whole = refs[7:11]
    kvs, acc, part, places, kp, vp, send_sem, recv_sem, local_sem = refs[11:]
    members = sizes[2]
    sub = rows // SUBS
    head = pl.program_id(0)
    links = Links(sizes, send_sem, recv_sem)
    kv = KeyValues(links, rows, kv_ref, kvs, local_sem)
    weights_ = []
    for a in range(4):
        for b, cols in enumerate(halves_of(shard[a].shape[-1])):
            weights_.append(
                (a, Gather(links, (a, b), shard[a], whole[a], ORDERS[b], cols, local_sem.at[16 + 2 * a + b]))
            )

    def each(array):
        return [g for a, g in weights_ if a == array]

    def kept(group):
        return pltpu.make_async_copy(
            kvs.at[:, 2 * group : 2 * group + 2],
            kv_all.at[:, 2 * group : 2 * group + 2],
            local_sem.at[8 + group],
        )

    @pl.when(head == 0)
    def _():
        links.meet()
        for group in range(4):
            run_all(kv.across(group), "start")
            run_all(kv.near(group), "start")
            for g in each(group):
                g.start()
        l_ref[...] = jnp.zeros_like(l_ref)
        places[...] = row_places(places.shape, 0, sub)

    for group in range(4):

        @pl.when(head == 2 * group)
        def _():
            run_all(kv.across(group), "wait")
            run_all(kv.forward(group), "start")
            run_all(kv.near(group), "wait")
            run_all(kv.forward(group), "wait")
            kept(group).start()

    _, _, z, core = links.place()
    mine = lax.rem(z, members // 2) * 2 + core
    lane = lax.broadcasted_iota(jnp.int32, (2 * rows, HEAD_DIM), 1)
    for piece in range(2):
        base = rows * (piece * members + mine)
        region = slice(piece * 2 * rows, (piece + 1) * 2 * rows)
        acc[...] = jnp.zeros_like(acc)
        part[...] = jnp.zeros_like(part)

        def trunk(step, masked):
            start = pl.multiple_of(step * CHUNK, CHUNK)
            weights = jnp.exp2(nt(q_ref[0, region], kvs[0, head, pl.ds(start, CHUNK)]) * exp2_scale)
            low, high = weights[:, :HEAD_DIM], weights[:, HEAD_DIM:]
            if masked:
                room = places[...] + (base - start)
                low = jnp.where(lane <= room, low, 0.0)
                high = jnp.where(lane + HEAD_DIM <= room, high, 0.0)
                weights = jnp.concatenate([low, high], axis=1)
            part[...] += low + high
            acc[...] += matmul(weights.astype(BF16), kvs[1, head, pl.ds(start, CHUNK)])
            return masked

        if piece == 0:
            clear = jnp.minimum(base // CHUNK, TRUNK // CHUNK)
            last = jnp.minimum((base + rows + CHUNK - 1) // CHUNK, TRUNK // CHUNK)
            lax.fori_loop(0, clear, lambda i, c: (trunk(i, False), c)[1], 0)
            lax.fori_loop(clear, last, lambda i, c: (trunk(i, True), c)[1], 0)
        else:
            lax.fori_loop(0, TRUNK // CHUNK, lambda i, c: (trunk(i, False), c)[1], 0)

        lead = jnp.maximum(base - TRUNK, 0) // SEG

        def parents_():
            gather_parents(
                meta,
                lead,
                0,
                [
                    (lambda b: kvs[0, head, TRUNK + b * SEG : TRUNK + (b + 1) * SEG], kp),
                    (lambda b: kvs[1, head, TRUNK + b * SEG : TRUNK + (b + 1) * SEG], vp),
                ],
            )

        if piece == 0:
            pl.when(base + rows > TRUNK)(parents_)
        else:
            parents_()
        for s in range(SUBS):
            block = slice(2 * sub * s, 2 * sub * (s + 1))

            def runs():
                row = base + s * sub - TRUNK
                run = row // SEG
                own = pl.multiple_of(TRUNK + run * SEG, SEG)
                flag = jnp.minimum(meta[run] + 1, 1).astype(F32)
                query = q_ref[0, piece * 2 * rows + 2 * sub * s : piece * 2 * rows + 2 * sub * (s + 1)]
                room = places[block] + (lax.rem(row, SEG) - s * sub)
                weights = jnp.exp2(nt(query, kvs[0, head, pl.ds(own, SEG)]) * exp2_scale)
                weights = jnp.where(lane[block] <= room, weights, 0.0)
                above = jnp.exp2(nt(query, kp[run - lead]) * exp2_scale) * flag
                part[block] += weights + above
                acc[block] += matmul(weights.astype(BF16), kvs[1, head, pl.ds(own, SEG)]) + matmul(
                    above.astype(BF16), vp[run - lead]
                )

            if piece == 0:
                pl.when(base + s * sub >= TRUNK)(runs)
            else:
                runs()

        total = jnp.sum(part[...], axis=-1, keepdims=True)
        mixed = (acc[...] / total).astype(BF16)
        for s in range(SUBS):
            for h in range(2):
                row = piece * rows + sub * s
                mixed_ref[row : row + sub, h * HEAD_DIM : (h + 1) * HEAD_DIM] = mixed[
                    (2 * s + h) * sub : (2 * s + h + 1) * sub
                ]
        l_ref[region] = jnp.where(lane == head, total, l_ref[region])

    plan = {
        0: [(0, 1)],
        1: [(1, 1)],
        2: [(0, 2)],
        3: [(2, 1)],
        4: [(1, 2), (0, 3)],
        5: [(3, 1)],
        6: [(2, 2), (1, 3)],
        7: [(3, 2), (2, 3), (3, 3)],
    }
    for at, steps in plan.items():

        @pl.when(head == at)
        def _():
            for array, stage in steps:
                for g in each(array):
                    g.step(stage)
            if at == KV_HEADS - 1:
                for _, g in weights_:
                    g.close()
                for group in range(4):
                    kept(group).wait()


def forward(sizes, meta, queries, kv, shards_):
    ny, nx, nz = sizes
    rows = kv.shape[3]
    rounds = KeyValues.copies(sizes) + 8 * Gather.copies(sizes)
    results = pl.pallas_call(
        functools.partial(forward_kernel, sizes, rows),
        out_shape=[
            jax.ShapeDtypeStruct((2 * rows, QD), BF16),
            jax.ShapeDtypeStruct((4 * rows, HEAD_DIM), F32),
            jax.ShapeDtypeStruct((2, KV_HEADS, TREE, HEAD_DIM), BF16),
        ]
        + [jax.ShapeDtypeStruct((ny, nx, nz, 2) + s.shape, BF16) for s in shards_],
        grid_spec=pltpu.PrefetchScalarGridSpec(
            num_scalar_prefetch=1,
            grid=(KV_HEADS,),
            in_specs=[pl.BlockSpec((1, 4 * rows, HEAD_DIM), lambda h, meta: (h, 0, 0)), ANY] + [ANY] * 4,
            out_specs=[
                pl.BlockSpec((2 * rows, 2 * HEAD_DIM), lambda h, meta: (0, h)),
                pl.BlockSpec((4 * rows, HEAD_DIM), lambda h, meta: (0, 0)),
                ANY,
            ]
            + [ANY] * 4,
            scratch_shapes=[
                pltpu.VMEM((2, KV_HEADS, TREE, HEAD_DIM), BF16),
                pltpu.VMEM((2 * rows, HEAD_DIM), F32),
                pltpu.VMEM((2 * rows, HEAD_DIM), F32),
                pltpu.VMEM((2 * rows, HEAD_DIM), jnp.int32),
                pltpu.VMEM((LOCAL_RUNS, SEG, HEAD_DIM), BF16),
                pltpu.VMEM((LOCAL_RUNS, SEG, HEAD_DIM), BF16),
                pltpu.SemaphoreType.DMA((rounds,)),
                pltpu.SemaphoreType.DMA((rounds,)),
                pltpu.SemaphoreType.DMA((24,)),
            ],
        ),
        compiler_params=pltpu.CompilerParams(
            collective_id=2, has_side_effects=True, vmem_limit_bytes=48 * MIB
        ),
        name="forward",
    )(meta, queries, kv, *shards_)
    return results[:3], [w.reshape(D, -1) for w in results[3:]]


def backward_kernel(sizes, rows, shard_rows, widths, meta, q_ref, g_ref, k_ref, v_ref, lse_ref, del_ref, *refs):
    parts = refs[:4]
    dq_ref, dkv_ref = refs[4:6]
    outs = refs[6:10]
    dq, dk, dv, pk, pv, kp, vp, stage, near, sums, far, last, temp = refs[10:23]
    buffers = refs[23:-3]
    send_sem, recv_sem, local_sem = refs[-3:]
    members = sizes[2]
    chips = members // 2
    sub = rows // SUBS
    head = pl.program_id(0)
    links = Links(sizes, send_sem, recv_sem)
    scatters = []
    for a in range(4):
        for b, cols in enumerate(halves_of(widths[a])):
            k = 4 * len(scatters)
            width = cols.stop - cols.start
            scatters.append(
                (
                    a,
                    Scatter(
                        links,
                        (a, b),
                        parts[a],
                        ORDERS[b],
                        cols,
                        *buffers[k : k + 4],
                        temp.at[b, :, :, :, :, :width],
                        local_sem.at[b],
                        outs[a],
                    ),
                )
            )

    def each(array):
        return [s for a, s in scatters if a == array]

    @pl.when(head == 0)
    def _():
        links.meet()
        for s in each(0):
            s.load().start()
        for _, s in scatters:
            s.start()

    _, _, z, core = links.place()
    here = lax.rem(z, chips)
    mine = here * 2 + core
    dk[...] = jnp.zeros_like(dk)
    dv[...] = jnp.zeros_like(dv)
    pk[...] = jnp.zeros_like(pk)
    pv[...] = jnp.zeros_like(pv)
    for piece in range(2):
        base = rows * (piece * members + mine)
        at = piece * 2 * rows
        region = slice(at, at + 2 * rows)
        dq[...] = jnp.zeros_like(dq)

        def pair(key, value, block, mask):
            spot = slice(at + block.start, at + block.stop)
            weights = jnp.exp2(nt(key, q_ref[0, spot]) * exp2_scale - lse_ref[0, :, spot])
            if mask is not None:
                weights = mask(weights)
            grads = (weights * (nt(value, g_ref[0, spot]) - del_ref[0, :, spot])).astype(BF16)
            weights = weights.astype(BF16)
            dq[block] += contract_rows(grads, key)
            return matmul(grads, q_ref[0, spot]), matmul(weights, g_ref[0, spot])

        everything = slice(0, 2 * rows)

        def trunk(step, masked):
            start = pl.multiple_of(step * CHUNK, CHUNK)

            def mask(weights):
                shape = weights.shape
                room = row_places((1, shape[1]), 1, sub) + (base - start)
                return jnp.where(lax.broadcasted_iota(jnp.int32, shape, 0) <= room, weights, 0.0)

            key_grad, value_grad = pair(
                k_ref[0, 0, pl.ds(start, CHUNK)],
                v_ref[0, 0, pl.ds(start, CHUNK)],
                everything,
                mask if masked else None,
            )
            dk[pl.ds(start, CHUNK)] += key_grad
            dv[pl.ds(start, CHUNK)] += value_grad

        if piece == 0:
            clear = jnp.minimum(base // CHUNK, TRUNK // CHUNK)
            end = jnp.minimum((base + rows + CHUNK - 1) // CHUNK, TRUNK // CHUNK)
            lax.fori_loop(0, clear, lambda i, c: (trunk(i, False), c)[1], 0)
            lax.fori_loop(clear, end, lambda i, c: (trunk(i, True), c)[1], 0)
        else:
            lax.fori_loop(0, TRUNK // CHUNK, lambda i, c: (trunk(i, False), c)[1], 0)

        lead = jnp.maximum(base - TRUNK, 0) // SEG

        def parents_():
            gather_parents(
                meta,
                lead,
                0,
                [
                    (lambda b: k_ref[0, 0, TRUNK + b * SEG : TRUNK + (b + 1) * SEG], kp),
                    (lambda b: v_ref[0, 0, TRUNK + b * SEG : TRUNK + (b + 1) * SEG], vp),
                ],
            )

        if piece == 0:
            pl.when(base + rows > TRUNK)(parents_)
        else:
            parents_()
        for s in range(SUBS):
            block = slice(2 * sub * s, 2 * sub * (s + 1))

            def runs():
                row = base + s * sub - TRUNK
                run = row // SEG
                own = pl.multiple_of(TRUNK + run * SEG, SEG)
                flag = jnp.minimum(meta[run] + 1, 1).astype(F32)

                def mask(weights):
                    shape = weights.shape
                    room = lax.broadcasted_iota(jnp.int32, shape, 1) % sub + lax.rem(row, SEG)
                    return jnp.where(lax.broadcasted_iota(jnp.int32, shape, 0) <= room, weights, 0.0)

                key_grad, value_grad = pair(
                    k_ref[0, 0, pl.ds(own, SEG)], v_ref[0, 0, pl.ds(own, SEG)], block, mask
                )
                dk[pl.ds(own, SEG)] += key_grad
                dv[pl.ds(own, SEG)] += value_grad
                key_grad, value_grad = pair(
                    kp[run - lead], vp[run - lead], block, lambda weights: weights * flag
                )
                slot = LOCAL_RUNS * piece + run - lead
                pk[slot] += key_grad
                pv[slot] += value_grad

            if piece == 0:
                pl.when(base + s * sub >= TRUNK)(runs)
            else:
                runs()

        dq_ref[0, region] = dq[...] * score_scale

        def spread():
            parents = [meta[jnp.minimum(lead + k, TREE // SEG - TRUNK // SEG - 1)] for k in range(LOCAL_RUNS)]

            def place(b, carry):
                start = pl.multiple_of(TRUNK + b * SEG, SEG)
                key_grad, value_grad = dk[pl.ds(start, SEG)], dv[pl.ds(start, SEG)]
                for k in range(LOCAL_RUNS):
                    share = (1 - jnp.minimum(jnp.abs(parents[k] - b), 1)).astype(F32)
                    key_grad += pk[LOCAL_RUNS * piece + k] * share
                    value_grad += pv[LOCAL_RUNS * piece + k] * share
                dk[pl.ds(start, SEG)] = key_grad
                dv[pl.ds(start, SEG)] = value_grad
                return carry

            lax.fori_loop(0, (TREE - TRUNK) // SEG, place, 0)

        if piece == 0:
            pl.when(base + rows > TRUNK)(spread)
        else:
            spread()

    def core_copy(h):
        return links.copy(("kv core", h), stage.at[h % 2, :, 1 - core], near.at[h % 2], links.sibling())

    def far_copies(h):
        return [
            links.copy(("kv z", h, i), sums.at[h, chip], far.at[h, i], target)
            for i, (chip, target) in enumerate(links.group())
        ]

    def pass_on(h):
        core_copy(h).wait()

        def add(i, carry):
            chip, which, piece = i // 4, lax.rem(i // 2, 2), lax.rem(i, 2)
            sums[h, chip, which, piece] = (
                stage[h % 2, chip, core, which, piece].astype(F32) + near[h % 2, chip, which, piece].astype(F32)
            ).astype(BF16)
            return carry

        lax.fori_loop(0, chips * 4, add, 0)
        run_all(far_copies(h), "start")

    for h in range(1, KV_HEADS):
        pl.when(head == h)(functools.partial(pass_on, h - 1))

    for which, grad, scale in ((0, dk, score_scale), (1, dv, 1.0)):
        for piece in range(2):
            for member in range(members):
                start = rows * (piece * members + member)
                stage[lax.rem(head, 2), member // 2, member % 2, which, piece] = (
                    grad[start : start + rows] * scale
                ).astype(BF16)
    for h in range(KV_HEADS):

        @pl.when(head == h)
        def _():
            core_copy(h).start()

    plan = {
        0: [(0, 0)],
        1: [(1, 0)],
        2: [(0, 1)],
        3: [(2, 0), (0, 2)],
        4: [(1, 1)],
        5: [(3, 0), (1, 2)],
        6: [(2, 1)],
        7: [(3, 1), (2, 2), (3, 2)],
    }
    for moment, steps in plan.items():

        @pl.when(head == moment)
        def _():
            if moment == KV_HEADS - 1:
                pass_on(moment)
            for array, step in steps:
                for s in each(array):
                    if step == 0:
                        s.begin()
                    else:
                        s.middle(step - 1)
                if step == 0 and array < 3:
                    for s in each(array + 1):
                        s.load().start()

            def result(h):
                return pltpu.make_async_copy(last.at[h % 2], dkv_ref.at[:, h], local_sem.at[2 + h % 2])

            if moment == KV_HEADS - 1:
                for h in range(KV_HEADS):
                    run_all(far_copies(h), "wait")
                    if h > 1:
                        result(h - 2).wait()
                    for which in range(2):
                        for piece in range(2):
                            total = sums[h, here, which, piece].astype(F32)
                            for i in range(chips - 1):
                                total = total + far[h, i, which, piece].astype(F32)
                            last[h % 2, which, piece] = total
                    result(h).start()
                for _, s in scatters:
                    s.finish()
                for h in (KV_HEADS - 2, KV_HEADS - 1):
                    result(h).wait()


def backward(sizes, meta, queries, grads, kv_all, log_total, delta, parts):
    ny, nx, nz = sizes
    chips = nz // 2
    rows = queries.shape[1] // 4
    widths = tuple(p.shape[-1] for p in parts)
    shard_rows = D // (ny * nx * nz * 2)
    pieces = [p.reshape(ny, nx, nz, 2, shard_rows, p.shape[-1]) for p in parts]
    stack = pl.BlockSpec((1, 4 * rows, HEAD_DIM), lambda h, meta: (h, 0, 0))
    line = pl.BlockSpec((1, 1, 4 * rows), lambda h, meta: (h, 0, 0))
    buffers = []
    for w in widths:
        for b, cols in enumerate(halves_of(w)):
            buffers += Scatter.scratch(sizes, ORDERS[b], shard_rows, cols.stop - cols.start)
    rounds = 8 * Scatter.copies(sizes) + KV_HEADS * chips
    results = pl.pallas_call(
        functools.partial(backward_kernel, sizes, rows, shard_rows, widths),
        out_shape=[
            jax.ShapeDtypeStruct((KV_HEADS, 4 * rows, HEAD_DIM), F32),
            jax.ShapeDtypeStruct((2, KV_HEADS, 2, rows, HEAD_DIM), F32),
        ]
        + [jax.ShapeDtypeStruct((shard_rows, w), F32) for w in widths],
        grid_spec=pltpu.PrefetchScalarGridSpec(
            num_scalar_prefetch=1,
            grid=(KV_HEADS,),
            in_specs=[
                stack,
                stack,
                pl.BlockSpec((1, 1, TREE, HEAD_DIM), lambda h, meta: (0, h, 0, 0)),
                pl.BlockSpec((1, 1, TREE, HEAD_DIM), lambda h, meta: (1, h, 0, 0)),
                line,
                line,
            ]
            + [ANY] * 4,
            out_specs=[stack, ANY] + [pl.BlockSpec((shard_rows, w), lambda h, meta: (0, 0)) for w in widths],
            scratch_shapes=[
                pltpu.VMEM((2 * rows, HEAD_DIM), F32),
                pltpu.VMEM((TREE, HEAD_DIM), F32),
                pltpu.VMEM((TREE, HEAD_DIM), F32),
                pltpu.VMEM((2 * LOCAL_RUNS, SEG, HEAD_DIM), F32),
                pltpu.VMEM((2 * LOCAL_RUNS, SEG, HEAD_DIM), F32),
                pltpu.VMEM((LOCAL_RUNS, SEG, HEAD_DIM), BF16),
                pltpu.VMEM((LOCAL_RUNS, SEG, HEAD_DIM), BF16),
                pltpu.VMEM((2, chips, 2, 2, 2, rows, HEAD_DIM), BF16),
                pltpu.VMEM((2, chips, 2, 2, rows, HEAD_DIM), BF16),
                pltpu.VMEM((KV_HEADS, chips, 2, 2, rows, HEAD_DIM), BF16),
                pltpu.VMEM((KV_HEADS, chips - 1, 2, 2, rows, HEAD_DIM), BF16),
                pltpu.VMEM((2, 2, 2, rows, HEAD_DIM), F32),
                pltpu.VMEM((2, ny, nx, nz, shard_rows, max(widths) // 2), BF16),
            ]
            + buffers
            + [
                pltpu.SemaphoreType.DMA((rounds,)),
                pltpu.SemaphoreType.DMA((rounds,)),
                pltpu.SemaphoreType.DMA((4,)),
            ],
        ),
        compiler_params=pltpu.CompilerParams(
            collective_id=3, has_side_effects=True, vmem_limit_bytes=61 * MIB
        ),
        name="backward",
    )(
        meta,
        queries,
        grads,
        kv_all,
        kv_all,
        log_total.reshape(KV_HEADS, 1, 4 * rows),
        delta.reshape(KV_HEADS, 1, 4 * rows),
        *pieces,
    )
    return results[0], results[1], results[2:]


def scatter_kernel(sizes, widths, *refs):
    count = len(widths)
    parts = refs[:count]
    moved_ref = refs[count]
    outs = refs[count + 1 : 2 * count + 1]
    placed_ref = refs[2 * count + 1]
    rest = refs[2 * count + 2 :]
    send_sem, recv_sem, local_sem = rest[-3:]
    links = Links(sizes, send_sem, recv_sem)
    scatters = []
    used = 0
    for a in range(count):
        for b, cols in enumerate(halves_of(widths[a])):
            k = 5 * used
            scatters.append(
                Scatter(
                    links,
                    (a, b),
                    parts[a],
                    ORDERS[b],
                    cols,
                    *rest[k : k + 4],
                    rest[k + 4],
                    local_sem.at[used],
                    outs[a],
                )
            )
            used += 1
    for s in scatters:
        s.load().start()
    links.meet()
    for s in scatters:
        s.start()
    _, _, z, _ = links.place()
    half = z // (sizes[2] // 2)
    keep = pltpu.make_async_copy(moved_ref.at[half], placed_ref.at[half], local_sem.at[used])
    give = links.copy("moved", moved_ref.at[1 - half], placed_ref.at[half], links.across())
    keep.start()
    give.start()
    depth = 2
    for i, s in enumerate(scatters):
        if i >= depth:
            scatters[i - depth].middle(0)
        s.begin()
    for s in scatters[-depth:]:
        s.middle(0)
    for s in scatters:
        s.middle(1)
    for s in scatters:
        s.finish()
    keep.wait()
    give.wait()


def scatter_end(sizes, parts, moved):
    ny, nx, nz = sizes
    shard_rows = D // (ny * nx * nz * 2)
    widths = tuple(p.shape[-1] for p in parts)
    pieces = [p.reshape(ny, nx, nz, 2, shard_rows, p.shape[-1]) for p in parts]
    buffers, count = [], 0
    for w in widths:
        for b, cols in enumerate(halves_of(w)):
            buffers += Scatter.scratch(sizes, ORDERS[b], shard_rows, cols.stop - cols.start)
            buffers.append(pltpu.VMEM((ny, nx, nz, shard_rows, cols.stop - cols.start), BF16))
            count += 1
    rounds = count * Scatter.copies(sizes) + 1
    results = pl.pallas_call(
        functools.partial(scatter_kernel, sizes, widths),
        out_shape=[jax.ShapeDtypeStruct((shard_rows, w), F32) for w in widths]
        + [jax.ShapeDtypeStruct(moved.shape, BF16)],
        in_specs=[ANY] * (len(widths) + 1),
        out_specs=[pl.BlockSpec(memory_space=pltpu.VMEM)] * len(widths) + [ANY],
        scratch_shapes=buffers
        + [
            pltpu.SemaphoreType.DMA((rounds,)),
            pltpu.SemaphoreType.DMA((rounds,)),
            pltpu.SemaphoreType.DMA((count + 1,)),
        ],
        compiler_params=pltpu.CompilerParams(
            collective_id=4, has_side_effects=True, vmem_limit_bytes=48 * MIB
        ),
        name="scatter_end",
    )(*pieces, moved)
    return results[:-1], results[-1]


def shards(
    sizes,
    tokens,
    cotangent,
    segment_ids,
    positions,
    parents,
    input_norm,
    query_proj,
    key_proj,
    value_proj,
    query_norm,
    key_norm,
    out_proj,
    post_norm,
    gate_proj,
    up_proj,
    down_proj,
):
    nz = sizes[2]
    rows = tokens.shape[1]
    shard_rows = query_proj.shape[0]
    gain_rows = query_norm.shape[0]
    ctx = lax.axis_index("ctx")
    half = ctx // nz
    member = ctx % nz
    count = 2 * rows
    sub = rows // SUBS
    swap = [(i, (i + nz) % (2 * nz)) for i in range(2 * nz)]

    def column(gain):
        return jnp.pad(gain, (0, shard_rows - gain.shape[0]))[:, None]

    gains = jnp.concatenate(
        [column(input_norm), column(post_norm), column(query_norm), column(key_norm)], axis=1
    )
    gains = jnp.pad(gains, ((0, 0), (0, GAIN_COLS - 4)))
    key_value = jnp.concatenate([key_proj, value_proj, gains], axis=1)
    query_full, kv_full, placed = gather_start(sizes, query_proj, key_value, tokens)
    x = placed.reshape(count, D)

    gain_block = kv_full[:, 2 * KVD :].astype(F32)
    in_weight = gain_block[:, 0][None, :]
    post_weight = gain_block[:, 1]
    by_device = gain_block.reshape(-1, shard_rows, GAIN_COLS)
    query_weight = by_device[:, :gain_rows, 2].reshape(1, HEAD_DIM)
    key_weight = by_device[:, :gain_rows, 3].reshape(1, HEAD_DIM)

    run_seg = segment_ids[half][TRUNK::SEG]
    run_parent = parents[half][run_seg]
    parent_run = jnp.argmax(run_seg[None, :] == run_parent[:, None], axis=1).astype(jnp.int32)
    meta = jnp.where(run_parent > 0, parent_run, -1)
    pos_tree = positions[half].reshape(2, nz, rows)
    pos_local = lax.dynamic_index_in_dim(pos_tree, member, 1, keepdims=False).reshape(count)
    cosine, sine = rope_tables(pos_local)

    normed, queries, kv, pre = project(
        x, in_weight, query_full, kv_full, query_weight, key_weight, cosine, sine
    )
    (mixed, totals, kv_all), (out_t, gate_full, up_full, down_t) = forward(
        sizes, meta, queries, kv, [out_proj.T, gate_proj, up_proj, down_proj.T]
    )
    log_total = jnp.log2(totals[:, :KV_HEADS]).T

    mixed, cotangent = lax.optimization_barrier((mixed, cotangent))
    cot_keep = cotangent[half]
    cot_got = lax.ppermute(cotangent[1 - half], "ctx", swap)
    grad_out = jnp.where(
        half == 0, jnp.concatenate([cot_keep, cot_got]), jnp.concatenate([cot_got, cot_keep])
    )

    hidden = x.astype(F32) + nt(mixed, out_t)
    post_factor = norm_factor(hidden)
    post_hat = hidden * post_factor
    second = (post_hat * post_weight).astype(BF16)
    gate_pre = matmul(second, gate_full)
    up_pre = matmul(second, up_full)
    activated = jax.nn.silu(gate_pre)
    inner = (activated * up_pre).astype(BF16)
    result = (hidden + nt(inner, down_t)).astype(BF16).reshape(2, rows, D)
    result_keep = result[half]
    result_got = lax.ppermute(result[1 - half], "ctx", swap)
    output = jnp.where(
        half == 0, jnp.stack([result_keep, result_got]), jnp.stack([result_got, result_keep])
    )

    grad_inner = matmul(grad_out, down_t)
    sigmoid_gate = jax.nn.sigmoid(gate_pre)
    grad_gate = (
        grad_inner * up_pre * sigmoid_gate * (1.0 + gate_pre * (1.0 - sigmoid_gate))
    ).astype(BF16)
    grad_up = (grad_inner * activated).astype(BF16)
    grad_second = nt(grad_gate, gate_full) + nt(grad_up, up_full)
    grad_post_in, post_part = norm_backward(grad_second, post_weight, post_hat, post_factor)
    grad_hidden = grad_out.astype(F32) + grad_post_in
    grad_branch = grad_hidden.astype(BF16)
    grad_mixed = matmul(grad_branch, out_t).astype(BF16)
    parts = [
        contract_rows(grad_branch, mixed).astype(BF16),
        contract_rows(second, grad_gate).astype(BF16),
        contract_rows(second, grad_up).astype(BF16),
        contract_rows(grad_out, inner).astype(BF16),
    ]
    delta = jnp.sum(
        (grad_mixed.astype(F32) * mixed.astype(F32)).reshape(count, HEADS, HEAD_DIM), axis=-1
    )
    delta = delta.reshape(2, SUBS, sub, KV_HEADS, 2).transpose(3, 0, 1, 4, 2)
    grad_stack = grad_mixed.reshape(2 * SUBS, sub, KV_HEADS, 2, HEAD_DIM).transpose(2, 0, 3, 1, 4)
    grad_stack = grad_stack.reshape(KV_HEADS, 2 * count, HEAD_DIM)
    dq, dkv, (out_grad, gate_grad, up_grad, down_grad) = backward(
        sizes, meta, queries, grad_stack, kv_all, log_total, delta, parts
    )

    dwq, dwk, dwv, dx, in_part, qk_part = project_back(
        dq, dkv, pre, normed, x, grad_hidden, in_weight, query_full, kv_full, query_weight, key_weight, cosine, sine
    )

    def gain_column(values):
        if values.shape[0] == D:
            return values[:, None]
        spread = jnp.pad(values.reshape(-1, gain_rows), ((0, 0), (0, shard_rows - gain_rows)))
        return spread.reshape(D, 1)

    gain_parts = jnp.concatenate(
        [
            gain_column(in_part[0]),
            gain_column(jnp.sum(post_part, axis=0)),
            gain_column(qk_part[0]),
            gain_column(qk_part[1]),
        ],
        axis=1,
    )
    gain_parts = jnp.pad(gain_parts, ((0, 0), (0, GAIN_COLS - 4))).astype(BF16)
    (query_grad, key_grad, value_grad, gain_grad), input_grad = scatter_end(
        sizes, [dwq, dwk, dwv, gain_parts], dx.reshape(2, rows, D)
    )
    return (
        output,
        input_grad.astype(F32),
        gain_grad[:, 0],
        query_grad,
        key_grad,
        value_grad,
        gain_grad[:gain_rows, 2],
        gain_grad[:gain_rows, 3],
        out_grad.T,
        gain_grad[:, 1],
        gate_grad,
        up_grad,
        down_grad.T,
    )


def solution(mesh):
    dp, ctx = mesh.shape["dp"], mesh.shape["ctx"]
    sizes = (2, dp // 2, ctx // 2)
    return jax.shard_map(
        functools.partial(shards, sizes),
        mesh=mesh,
        in_specs=(
            P("dp", "ctx", None),
            P("dp", "ctx", None),
            P("dp", None),
            P("dp", None),
            P("dp", None),
            P(("dp", "ctx")),
            P(("dp", "ctx"), None),
            P(("dp", "ctx"), None),
            P(("dp", "ctx"), None),
            P(("dp", "ctx")),
            P(("dp", "ctx")),
            P(None, ("dp", "ctx")),
            P(("dp", "ctx")),
            P(("dp", "ctx"), None),
            P(("dp", "ctx"), None),
            P(None, ("dp", "ctx")),
        ),
        out_specs=(
            P("dp", "ctx", None),
            P("dp", "ctx", None),
            P(("dp", "ctx")),
            P(("dp", "ctx"), None),
            P(("dp", "ctx"), None),
            P(("dp", "ctx"), None),
            P(("dp", "ctx")),
            P(("dp", "ctx")),
            P(None, ("dp", "ctx")),
            P(("dp", "ctx")),
            P(("dp", "ctx"), None),
            P(("dp", "ctx"), None),
            P(None, ("dp", "ctx")),
        ),
        check_vma=False,
    )
```

```python
import functools
import math

import jax
import jax.numpy as jnp
from jax import lax
from jax.experimental import pallas as pl
from jax.experimental.pallas import tpu as pltpu
from jax.sharding import PartitionSpec as P

D = 1024
HEADS = 16
KV_HEADS = 8
HEAD_DIM = 128
FF = 3072
TRUNK = 1024
SEG = 128
TREE = 2560
QD = HEADS * HEAD_DIM
KVD = KV_HEADS * HEAD_DIM
SUBS = 5
CHUNK = 256
GAIN_COLS = 128
FF_CHUNK = 512
FF_CHUNKS = FF // FF_CHUNK
FF_EARLY = 4
LOCAL_RUNS = 3
MIB = 1024 * 1024

eps_norm = 1e-06
rope_base = 1000000.0
exp2_scale = math.log2(math.e) / math.sqrt(HEAD_DIM)
score_scale = HEAD_DIM ** (-0.5)

MESH = pl.DeviceIdType.MESH
ANY = pl.BlockSpec(memory_space=pl.ANY)
F32 = jnp.float32
BF16 = jnp.bfloat16


def matmul(left_side, right_side):
    return jnp.dot(left_side, right_side, preferred_element_type=F32)


def nt(left_side, right_side):
    return lax.dot_general(
        left_side, right_side, (((1,), (1,)), ((), ())), preferred_element_type=F32
    )


def contract_rows(left_side, right_side):
    return lax.dot_general(
        left_side, right_side, (((0,), (0,)), ((), ())), preferred_element_type=F32
    )


def norm_factor(values):
    return lax.rsqrt(jnp.mean(values * values, axis=-1, keepdims=True) + eps_norm)


def norm_backward(grad_out, weight, normed, factor):
    weighted = grad_out * weight
    grad_in = factor * (weighted - normed * jnp.mean(weighted * normed, axis=-1, keepdims=True))
    return (grad_in, grad_out * normed)


def rope_tables(positions):
    steps_half = jnp.arange(HEAD_DIM // 2, dtype=F32)
    inverse = rope_base ** (-(steps_half * 2.0 / HEAD_DIM))
    angles = positions.astype(F32)[:, None] * inverse[None, :]
    cosine, sine = jnp.cos(angles), jnp.sin(angles)
    return jnp.concatenate([cosine, cosine], axis=-1), jnp.concatenate([-sine, sine], axis=-1)


class Links:
    def __init__(self, sizes, send_sem, recv_sem):
        self.sizes = sizes
        self.send_sem = send_sem
        self.recv_sem = recv_sem
        self.index = {}

    def place(self):
        _, nx, _ = self.sizes
        dp, ctx = lax.axis_index("dp"), lax.axis_index("ctx")
        return dp // nx, lax.rem(dp, nx), ctx // 2, lax.rem(ctx, 2)

    def device(self, y, x, z, core):
        return (y * self.sizes[1] + x, z * 2 + core)

    def peers(self, axis, back=False):
        y, x, z, core = self.place()
        at = {"y": y, "x": x, "z": z}
        n = self.sizes["yxz".index(axis)]
        found = []
        for s in range(1, n):
            moved = dict(at)
            moved[axis] = lax.rem(at[axis] + (n - s if back else s), n)
            found.append((moved["y"], moved["x"], moved["z"], core))
        return found

    def sibling(self):
        y, x, z, core = self.place()
        return self.device(y, x, z, 1 - core)

    def across(self):
        y, x, z, core = self.place()
        nz = self.sizes[2]
        return self.device(y, x, lax.rem(z + nz // 2, nz), core)

    def group(self, back=False):
        y, x, z, core = self.place()
        chips = self.sizes[2] // 2
        base = (z // chips) * chips
        here = z - base
        chosen = [lax.rem(here + (chips - s if back else s), chips) for s in range(1, chips)]
        return [(chip, self.device(y, x, base + chip, core)) for chip in chosen]

    def meet(self):
        barrier = pltpu.get_barrier_semaphore()
        partners = [self.device(*p) for a in "zxy" for p in self.peers(a)] + [self.sibling()]
        for partner in partners:
            pl.semaphore_signal(barrier, inc=1, device_id=partner, device_id_type=MESH)
        pl.semaphore_wait(barrier, len(partners))

    def copy(self, key, src, dst, target):
        k = self.index.setdefault(key, len(self.index))
        return pltpu.make_async_remote_copy(
            src_ref=src,
            dst_ref=dst,
            send_sem=self.send_sem.at[k],
            recv_sem=self.recv_sem.at[k],
            device_id=target,
            device_id_type=MESH,
        )


class Exchange:
    def __init__(self, links, source, placed, local_sem):
        self.links = links
        self.source = source
        self.placed = placed
        self.local_sem = local_sem

    def copies_(self):
        _, _, z, _ = self.links.place()
        half = z // (self.links.sizes[2] // 2)
        return [
            self.links.copy("swap", self.source.at[1 - half], self.placed.at[half], self.links.across()),
            pltpu.make_async_copy(self.source.at[half], self.placed.at[half], self.local_sem),
        ]

    def start(self):
        for copy in self.copies_():
            copy.start()

    def wait(self):
        for copy in self.copies_():
            copy.wait()


class Gather:
    def __init__(self, links, tag, shard, whole, order, cols, local_sem):
        self.links = links
        self.tag = tag
        self.shard = shard
        self.whole = whole
        self.order = order
        self.cols = cols
        self.local_sem = local_sem

    def own(self):
        y, x, z, core = self.links.place()
        return self.whole.at[y, x, z, core, :, self.cols]

    def slab(self, stage, at):
        y, x, z, core = at
        if stage == 0:
            return self.whole.at[y, x, z, core, :, self.cols]
        if stage == 1:
            return self.whole.at[y, x, :, core, :, self.cols]
        if self.order[0] == "x":
            return self.whole.at[y, :, :, core, :, self.cols]
        return self.whole.at[:, x, :, core, :, self.cols]

    def axis(self, stage):
        return ("z",) + tuple(self.order)[0:2] if stage is None else ("z", self.order[0], self.order[1])[stage]

    def send(self, stage):
        me = self.links.place()
        src = self.shard.at[:, self.cols] if stage == 0 else self.slab(stage, me)
        dst = self.slab(stage, me)
        return [
            self.links.copy((self.tag, stage, i), src, dst, self.links.device(*p))
            for i, p in enumerate(self.links.peers(self.axis(stage)))
        ]

    def forward(self, stage):
        sibling = self.links.sibling()
        if stage < 0:
            return [self.links.copy((self.tag, "own"), self.shard.at[:, self.cols], self.own(), sibling)]
        return [
            self.links.copy((self.tag, "pass", stage, i), self.slab(stage, p), self.slab(stage, p), sibling)
            for i, p in enumerate(self.links.peers(self.axis(stage), back=True))
        ]

    def local(self):
        return pltpu.make_async_copy(self.shard.at[:, self.cols], self.own(), self.local_sem)

    def start(self):
        self.local().start()
        for copy in self.send(0) + self.forward(-1):
            copy.start()

    def step(self, stage):
        if stage == 1:
            self.local().wait()
        for copy in self.send(stage - 1):
            copy.wait()
        if stage < 3:
            for copy in self.send(stage):
                copy.start()
        for copy in self.forward(stage - 1):
            copy.start()

    def close(self):
        for stage in range(-1, 3):
            for copy in self.forward(stage):
                copy.wait()

    @staticmethod
    def copies(sizes):
        return 2 * sum(n - 1 for n in sizes) + 1


class Scatter:
    def __init__(self, links, tag, part, order, cols, halves, firsts, seconds, thirds, temp, temp_sem, out):
        self.links = links
        self.tag = tag
        self.part = part
        self.order = order
        self.cols = cols
        self.sums = halves
        self.got = (firsts, seconds, thirds)
        self.temp = temp
        self.temp_sem = temp_sem
        self.out = out

    def first(self):
        _, _, _, core = self.links.place()
        return self.links.copy(
            (self.tag, "core"), self.part.at[:, :, :, 1 - core, :, self.cols], self.sums, self.links.sibling()
        )

    def load(self):
        _, _, _, core = self.links.place()
        return pltpu.make_async_copy(
            self.part.at[:, :, :, core, :, self.cols], self.temp, self.temp_sem
        )

    def axis(self, stage):
        return (self.order[0], self.order[1], "z")[stage]

    def at(self, stage, place, rest=None):
        y, x, z, _ = place
        if stage == 0:
            return (y,) if self.order[0] == "y" else (slice(None), x)
        if stage == 1:
            return (y, x)
        return (y, x, z)

    def send(self, stage):
        me = self.links.place()
        found = []
        for i, p in enumerate(self.links.peers(self.axis(stage))):
            index = self.at(stage, p)
            found.append(
                self.links.copy(
                    (self.tag, stage, i), self.sums.at[index], self.got[stage].at[i], self.links.device(*p)
                )
            )
        return found

    def start(self):
        self.first().start()

    def begin(self):
        self.first().wait()
        if self.temp_sem is not None:
            self.load().wait()
        ny, nx, nz = self.links.sizes

        def add(i, carry):
            a, b, c = i // (nx * nz), lax.rem(i // nz, nx), lax.rem(i, nz)
            self.sums[a, b, c] = (
                self.sums[a, b, c].astype(F32) + self.temp[a, b, c].astype(F32)
            ).astype(BF16)
            return carry

        lax.fori_loop(0, ny * nx * nz, add, 0)
        for copy in self.send(0):
            copy.start()

    def middle(self, stage):
        for copy in self.send(stage):
            copy.wait()
        y, x, z, _ = self.links.place()
        _, _, nz = self.links.sizes
        got = self.got[stage]
        peers = got.shape[0]
        if stage == 0:
            other = got.shape[1]

            def add(i, carry):
                b, c = i // nz, lax.rem(i, nz)
                index = (y, b, c) if self.order[0] == "y" else (b, x, c)
                total = self.sums[index].astype(F32)
                for p in range(peers):
                    total = total + got[p, b, c].astype(F32)
                self.sums[index] = total.astype(BF16)
                return carry

            lax.fori_loop(0, other * nz, add, 0)
        else:

            def add(c, carry):
                total = self.sums[y, x, c].astype(F32)
                for p in range(peers):
                    total = total + got[p, c].astype(F32)
                self.sums[y, x, c] = total.astype(BF16)
                return carry

            lax.fori_loop(0, nz, add, 0)
        for copy in self.send(stage + 1):
            copy.start()

    def finish(self):
        for copy in self.send(2):
            copy.wait()
        y, x, z, _ = self.links.place()
        total = self.sums[y, x, z].astype(F32)
        for p in range(self.got[2].shape[0]):
            total = total + self.got[2][p].astype(F32)
        self.out[:, self.cols] = total

    @staticmethod
    def copies(sizes):
        return sum(n - 1 for n in sizes) + 1

    @staticmethod
    def scratch(sizes, order, rows, width):
        ny, nx, nz = sizes
        na, nb = (ny, nx) if order[0] == "y" else (nx, ny)
        return [
            pltpu.VMEM((ny, nx, nz, rows, width), BF16),
            pltpu.VMEM((na - 1, nb, nz, rows, width), BF16),
            pltpu.VMEM((nb - 1, nz, rows, width), BF16),
            pltpu.VMEM((nz - 1, rows, width), BF16),
        ]


ORDERS = ("xy", "yx")

FORWARD_START = [(0, 0), ("kv", 0), (1, 0), (0, 1), ("use", 0), (2, 0), (0, 2)]
FORWARD_BEFORE = {
    0: [("got", 0), ("kv", 1)],
    2: [("use", 1), (0, 4), ("kv", 2), (3, 1), ("got", 1)],
    4: [("use", 2), (0, 6), ("kv", 3), (2, 3), ("got", 2)],
    6: [("use", 3), (1, 6), ("swap", 0), ("got", 3)],
}
FORWARD_AFTER = {
    0: [(1, 1), (3, 0), (2, 1), (0, 3)],
    1: [(1, 2), (2, 2)],
    2: [(1, 3), (3, 2)],
    3: [(0, 5), (1, 4)],
    4: [(2, 4), (1, 5)],
    5: [(3, 3), (2, 5)],
    6: [(3, 4), (2, 6), (3, 5)],
    7: [(3, 6)],
}
FEED_MIDDLE = {
    1: [("begin", 0)],
    2: [("begin", 1), (1, 0)],
    3: [("begin", 2), (1, 1)],
    4: [("begin", 3), (1, 2)],
    5: [(1, 3)],
}
FEED_AFTER = {
    0: [("core", 0)],
    1: [("core", 1), (0, 0)],
    2: [("core", 2), (0, 1)],
    3: [("core", 3), (0, 2)],
    4: [(0, 3)],
}
FEED_LAST = []
BACKWARD_AFTER = {
    0: [(0, 0)],
    1: [(1, 0), (0, 1)],
    2: [(2, 0), (1, 1), (0, 2)],
    3: [(2, 1), (1, 2)],
    4: [(2, 2)],
}


def halves_of(width):
    return (slice(0, width // 2), slice(width // 2, width)) if width >= 512 else (slice(0, width),)


def gather_kernel(sizes, query_ref, kv_ref, moved_ref, query_whole, kv_whole, placed_ref, send_sem, recv_sem, local_sem):
    links = Links(sizes, send_sem, recv_sem)
    links.meet()
    _, _, z, _ = links.place()
    half = z // (sizes[2] // 2)
    parts = []
    for a, (shard, whole) in enumerate(((query_ref, query_whole), (kv_ref, kv_whole))):
        width = shard.shape[-1]
        for b in range(2):
            edge = width // 2 // HEAD_DIM * HEAD_DIM
            cols = slice(0, edge) if b == 0 else slice(edge, width)
            parts.append(
                Gather(links, (a, b), shard, whole, ORDERS[b], cols, local_sem.at[2 * a + b])
            )
    keep = pltpu.make_async_copy(moved_ref.at[half], placed_ref.at[half], local_sem.at[4])
    give = links.copy("moved", moved_ref.at[1 - half], placed_ref.at[half], links.across())
    for part in parts[:2]:
        part.start()
    keep.start()
    for part in parts[2:]:
        part.start()
    for part in parts[:2]:
        part.step(1)
    give.start()
    for part in parts[2:]:
        part.step(1)
    for part in parts[:2]:
        part.step(2)
    for part in parts[2:]:
        part.step(2)
    for part in parts:
        part.step(3)
    for part in parts:
        part.close()
    keep.wait()
    give.wait()


def gather_start(sizes, query, key_value, moved):
    ny, nx, nz = sizes
    rounds = 4 * Gather.copies(sizes) + 1
    query_whole, kv_whole, placed = pl.pallas_call(
        functools.partial(gather_kernel, sizes),
        out_shape=[
            jax.ShapeDtypeStruct((ny, nx, nz, 2) + query.shape, BF16),
            jax.ShapeDtypeStruct((ny, nx, nz, 2) + key_value.shape, BF16),
            jax.ShapeDtypeStruct(moved.shape, BF16),
        ],
        in_specs=[ANY] * 3,
        out_specs=[ANY] * 3,
        scratch_shapes=[
            pltpu.SemaphoreType.DMA((rounds,)),
            pltpu.SemaphoreType.DMA((rounds,)),
            pltpu.SemaphoreType.DMA((5,)),
        ],
        compiler_params=pltpu.CompilerParams(collective_id=1, has_side_effects=True),
        name="gather_start",
    )(query, key_value, moved)
    return query_whole.reshape(D, -1), kv_whole.reshape(D, -1), placed


def roll_half(values):
    return pltpu.roll(values, HEAD_DIM // 2, 1)


def project_kernel(rows, x_ref, gain_ref, wq_ref, wk_ref, wv_ref, qg_ref, kg_ref, cos_ref, sin_ref, normed_ref, q_ref, kv_ref, pre_ref):
    sub = rows // SUBS

    @pl.when(pl.program_id(0) == 0)
    def _():
        values = x_ref[...].astype(F32)
        normed_ref[...] = (values * norm_factor(values) * gain_ref[...]).astype(BF16)

    normed = normed_ref[...]
    cosine, sine = cos_ref[...], sin_ref[...]

    def turned(pre, gain):
        values = pre * norm_factor(pre) * gain
        return (values * cosine + roll_half(values) * sine).astype(BF16)

    query = matmul(normed, wq_ref[...])
    for h in range(2):
        pre = query[:, h * HEAD_DIM : (h + 1) * HEAD_DIM]
        pre_ref[0, :, h * HEAD_DIM : (h + 1) * HEAD_DIM] = pre
        low = turned(pre, qg_ref[...])
        for s in range(2 * SUBS):
            q_ref[0, (2 * s + h) * sub : (2 * s + h + 1) * sub] = low[s * sub : (s + 1) * sub]
    pre = matmul(normed, wk_ref[...])
    pre_ref[0, :, 2 * HEAD_DIM :] = pre
    kv_ref[0, 0] = turned(pre, kg_ref[...]).reshape(2, rows, HEAD_DIM)
    kv_ref[1, 0] = matmul(normed, wv_ref[...]).astype(BF16).reshape(2, rows, HEAD_DIM)


def project(x, gain, query_full, kv_full, query_gain, key_gain, cosine, sine):
    count = x.shape[0]
    rows = count // 2
    full = pl.BlockSpec((count, D), lambda h: (0, 0))
    row = lambda n: pl.BlockSpec((1, n), lambda h: (0, 0))
    table = pl.BlockSpec((count, HEAD_DIM), lambda h: (0, 0))
    return pl.pallas_call(
        functools.partial(project_kernel, rows),
        grid=(KV_HEADS,),
        out_shape=[
            jax.ShapeDtypeStruct((count, D), BF16),
            jax.ShapeDtypeStruct((KV_HEADS, 2 * count, HEAD_DIM), BF16),
            jax.ShapeDtypeStruct((2, KV_HEADS, 2, rows, HEAD_DIM), BF16),
            jax.ShapeDtypeStruct((KV_HEADS, count, 3 * HEAD_DIM), F32),
        ],
        in_specs=[
            full,
            row(D),
            pl.BlockSpec((D, 2 * HEAD_DIM), lambda h: (0, h)),
            pl.BlockSpec((D, HEAD_DIM), lambda h: (0, h)),
            pl.BlockSpec((D, HEAD_DIM), lambda h: (0, KV_HEADS + h)),
            row(HEAD_DIM),
            row(HEAD_DIM),
            table,
            table,
        ],
        out_specs=[
            full,
            pl.BlockSpec((1, 2 * count, HEAD_DIM), lambda h: (h, 0, 0)),
            pl.BlockSpec((2, 1, 2, rows, HEAD_DIM), lambda h: (0, h, 0, 0, 0)),
            pl.BlockSpec((1, count, 3 * HEAD_DIM), lambda h: (h, 0, 0)),
        ],
        compiler_params=pltpu.CompilerParams(vmem_limit_bytes=40 * MIB),
        name="project",
    )(x, gain, query_full, kv_full, kv_full, query_gain, key_gain, cosine, sine)


def project_back_kernel(
    rows, dq_ref, dkv_ref, pre_ref, normed_ref, x_ref, hid_ref, gain_ref, wq_ref, wk_ref, wv_ref, qg_ref, kg_ref, cos_ref, sin_ref,
    dwq_ref, dwk_ref, dwv_ref, dx_ref, in_ref, qk_ref, normed_t, grads,
):
    sub = rows // SUBS
    head = pl.program_id(0)

    @pl.when(head == 0)
    def _():
        normed_t[...] = normed_ref[...].astype(F32).T.astype(BF16)
        grads[...] = jnp.zeros_like(grads)
        qk_ref[...] = jnp.zeros_like(qk_ref)

    cosine, sine = cos_ref[...], sin_ref[...]

    def back(turned_grad, pre, gain):
        grad = turned_grad * cosine - roll_half(turned_grad) * sine
        factor = norm_factor(pre)
        grad_pre, part = norm_backward(grad, gain, pre * factor, factor)
        return grad_pre.astype(BF16), jnp.sum(part, axis=0, keepdims=True)

    pieces = []
    for h in range(2):
        grad = jnp.concatenate(
            [dq_ref[0, (2 * s + h) * sub : (2 * s + h + 1) * sub] for s in range(2 * SUBS)], axis=0
        )
        low, part = back(grad, pre_ref[0, :, h * HEAD_DIM : (h + 1) * HEAD_DIM], qg_ref[...])
        qk_ref[0:1] += part
        pieces.append(low)
    low, part = back(dkv_ref[0, 0].reshape(2 * rows, HEAD_DIM), pre_ref[0, :, 2 * HEAD_DIM :], kg_ref[...])
    qk_ref[1:2] += part
    pieces.append(low)
    pieces.append(dkv_ref[1, 0].reshape(2 * rows, HEAD_DIM).astype(BF16))
    low = jnp.concatenate(pieces, axis=1)
    weights = jnp.concatenate([wq_ref[...], wk_ref[...], wv_ref[...]], axis=1)
    grads[...] += nt(low, weights)
    part = matmul(normed_t[...], low).astype(BF16)
    dwq_ref[...] = part[:, : 2 * HEAD_DIM]
    dwk_ref[...] = part[:, 2 * HEAD_DIM : 3 * HEAD_DIM]
    dwv_ref[...] = part[:, 3 * HEAD_DIM :]

    @pl.when(head == KV_HEADS - 1)
    def _():
        values = x_ref[...].astype(F32)
        factor = norm_factor(values)
        grad_in, part = norm_backward(grads[...], gain_ref[...], values * factor, factor)
        dx_ref[...] = (hid_ref[...] + grad_in).astype(BF16)
        in_ref[...] = jnp.sum(part, axis=0, keepdims=True)


def project_back(dq, dkv, pre, normed, x, grad_hidden, gain, query_full, kv_full, query_gain, key_gain, cosine, sine):
    count = x.shape[0]
    rows = count // 2
    full = pl.BlockSpec((count, D), lambda h: (0, 0))
    row = lambda n: pl.BlockSpec((1, n), lambda h: (0, 0))
    table = pl.BlockSpec((count, HEAD_DIM), lambda h: (0, 0))
    wide = pl.BlockSpec((D, 2 * HEAD_DIM), lambda h: (0, h))
    thin = pl.BlockSpec((D, HEAD_DIM), lambda h: (0, h))
    return pl.pallas_call(
        functools.partial(project_back_kernel, rows),
        grid=(KV_HEADS,),
        out_shape=[
            jax.ShapeDtypeStruct((D, QD), BF16),
            jax.ShapeDtypeStruct((D, KVD), BF16),
            jax.ShapeDtypeStruct((D, KVD), BF16),
            jax.ShapeDtypeStruct((count, D), BF16),
            jax.ShapeDtypeStruct((1, D), F32),
            jax.ShapeDtypeStruct((8, HEAD_DIM), F32),
        ],
        in_specs=[
            pl.BlockSpec((1, 2 * count, HEAD_DIM), lambda h: (h, 0, 0)),
            pl.BlockSpec((2, 1, 2, rows, HEAD_DIM), lambda h: (0, h, 0, 0, 0)),
            pl.BlockSpec((1, count, 3 * HEAD_DIM), lambda h: (h, 0, 0)),
            full,
            full,
            full,
            row(D),
            wide,
            thin,
            pl.BlockSpec((D, HEAD_DIM), lambda h: (0, KV_HEADS + h)),
            row(HEAD_DIM),
            row(HEAD_DIM),
            table,
            table,
        ],
        out_specs=[wide, thin, thin, full, row(D), pl.BlockSpec((8, HEAD_DIM), lambda h: (0, 0))],
        scratch_shapes=[pltpu.VMEM((D, count), BF16), pltpu.VMEM((count, D), F32)],
        compiler_params=pltpu.CompilerParams(vmem_limit_bytes=48 * MIB),
        name="project_back",
    )(dq, dkv, pre, normed, x, grad_hidden, gain, query_full, kv_full, kv_full, query_gain, key_gain, cosine, sine)


class KeyValues:
    def __init__(self, links, rows, own, held, local_sem):
        self.links = links
        self.rows = rows
        self.own = own
        self.held = held
        self.local_sem = local_sem

    def slab(self, group, piece, member):
        members = self.links.sizes[2]
        start = pl.multiple_of(self.rows * (piece * members + member), self.rows)
        return self.held.at[:, 2 * group : 2 * group + 2, pl.ds(start, self.rows)]

    def mine(self):
        _, _, z, core = self.links.place()
        return lax.rem(z, self.links.sizes[2] // 2) * 2 + core

    def across(self, group):
        found = []
        for piece in range(2):
            src = self.own.at[:, 2 * group : 2 * group + 2, piece]
            dst = self.slab(group, piece, self.mine())
            for i, (_, target) in enumerate(self.links.group()):
                found.append(self.links.copy(("kv", group, piece, i), src, dst, target))
        return found

    def near(self, group):
        found = []
        for piece in range(2):
            src = self.own.at[:, 2 * group : 2 * group + 2, piece]
            dst = self.slab(group, piece, self.mine())
            found.append(self.links.copy(("kv own", group, piece), src, dst, self.links.sibling()))
            found.append(pltpu.make_async_copy(src, dst, self.local_sem.at[2 * group + piece]))
        return found

    def forward(self, group):
        _, _, _, core = self.links.place()
        found = []
        for piece in range(2):
            for i, (chip, _) in enumerate(self.links.group(back=True)):
                slab = self.slab(group, piece, chip * 2 + core)
                found.append(
                    self.links.copy(("kv pass", group, piece, i), slab, slab, self.links.sibling())
                )
        return found

    @staticmethod
    def copies(sizes):
        return 4 * 2 * (2 * (sizes[2] // 2 - 1) + 1)


def run_all(copies, act):
    for copy in copies:
        if act == "start":
            copy.start()
        else:
            copy.wait()


def row_places(shape, dim, sub):
    t = lax.broadcasted_iota(jnp.int32, shape, dim)
    return (t // (2 * sub)) * sub + t % sub


def gather_parents(meta, lead, slot, pairs):
    runs = (TREE - TRUNK) // SEG
    for k in range(LOCAL_RUNS):
        parent = meta[jnp.minimum(lead + k, runs - 1)]
        for read, out in pairs:
            total = None
            for b in range(runs):
                share = (1 - jnp.minimum(jnp.abs(parent - b), 1)).astype(F32).astype(BF16)
                term = read(b) * share
                total = term if total is None else total + term
            out[slot + k] = total


def forward_kernel(sizes, rows, meta, q_ref, kv_ref, cot_ref, out_shard, *refs):
    shard = (out_shard,) + refs[:FF_CHUNKS]
    mixed_ref, l_ref, kv_all, out_whole, feed_whole, cot_placed = refs[FF_CHUNKS : FF_CHUNKS + 6]
    whole = (out_whole,) + tuple(feed_whole.at[c] for c in range(FF_CHUNKS))
    kvs, acc, part, places, kp, vp, send_sem, recv_sem, local_sem = refs[FF_CHUNKS + 6 :]
    members = sizes[2]
    sub = rows // SUBS
    head = pl.program_id(0)
    links = Links(sizes, send_sem, recv_sem)
    kv = KeyValues(links, rows, kv_ref, kvs, local_sem)
    swap = Exchange(links, cot_ref, cot_placed, local_sem.at[12 + 2 * (FF_CHUNKS + 1)])
    weights_ = [
        [
            Gather(links, (a, b), shard[a], whole[a], ORDERS[b], cols, local_sem.at[12 + 2 * a + b])
            for b, cols in enumerate(halves_of(shard[a].shape[-1]))
        ]
        for a in range(FF_CHUNKS + 1)
    ]

    def kept(group):
        return pltpu.make_async_copy(
            kvs.at[:, 2 * group : 2 * group + 2],
            kv_all.at[:, 2 * group : 2 * group + 2],
            local_sem.at[8 + group],
        )

    def act(steps):
        for what, a in steps:
            if what == "swap":
                swap.start()
            elif what == "kv":
                run_all(kv.across(a), "start")
                run_all(kv.near(a), "start")
            elif what == "use":
                run_all(kv.across(a), "wait")
                run_all(kv.forward(a), "start")
            elif what == "got":
                run_all(kv.near(a), "wait")
                run_all(kv.forward(a), "wait")
                kept(a).start()
            else:
                for g in weights_[a]:
                    if what == 0:
                        g.start()
                    else:
                        g.step(what)

    @pl.when(head == 0)
    def _():
        links.meet()
        act(FORWARD_START)
        l_ref[...] = jnp.zeros_like(l_ref)
        places[...] = row_places(places.shape, 0, sub)

    for moment, steps in FORWARD_BEFORE.items():
        pl.when(head == moment)(functools.partial(act, steps))

    _, _, z, core = links.place()
    mine = lax.rem(z, members // 2) * 2 + core
    lane = lax.broadcasted_iota(jnp.int32, (2 * rows, HEAD_DIM), 1)
    for piece in range(2):
        base = rows * (piece * members + mine)
        region = slice(piece * 2 * rows, (piece + 1) * 2 * rows)
        acc[...] = jnp.zeros_like(acc)
        part[...] = jnp.zeros_like(part)

        def trunk(step, masked):
            start = pl.multiple_of(step * CHUNK, CHUNK)
            weights = jnp.exp2(nt(q_ref[0, region], kvs[0, head, pl.ds(start, CHUNK)]) * exp2_scale)
            low, high = weights[:, :HEAD_DIM], weights[:, HEAD_DIM:]
            if masked:
                room = places[...] + (base - start)
                low = jnp.where(lane <= room, low, 0.0)
                high = jnp.where(lane + HEAD_DIM <= room, high, 0.0)
                weights = jnp.concatenate([low, high], axis=1)
            part[...] += low + high
            acc[...] += matmul(weights.astype(BF16), kvs[1, head, pl.ds(start, CHUNK)])
            return masked

        if piece == 0:
            clear = jnp.minimum(base // CHUNK, TRUNK // CHUNK)
            last = jnp.minimum((base + rows + CHUNK - 1) // CHUNK, TRUNK // CHUNK)
            lax.fori_loop(0, clear, lambda i, c: (trunk(i, False), c)[1], 0)
            lax.fori_loop(clear, last, lambda i, c: (trunk(i, True), c)[1], 0)
        else:
            lax.fori_loop(0, TRUNK // CHUNK, lambda i, c: (trunk(i, False), c)[1], 0)

        lead = jnp.maximum(base - TRUNK, 0) // SEG

        def parents_():
            gather_parents(
                meta,
                lead,
                0,
                [
                    (lambda b: kvs[0, head, TRUNK + b * SEG : TRUNK + (b + 1) * SEG], kp),
                    (lambda b: kvs[1, head, TRUNK + b * SEG : TRUNK + (b + 1) * SEG], vp),
                ],
            )

        if piece == 0:
            pl.when(base + rows > TRUNK)(parents_)
        else:
            parents_()
        for s in range(SUBS):
            block = slice(2 * sub * s, 2 * sub * (s + 1))

            def runs():
                row = base + s * sub - TRUNK
                run = row // SEG
                own = pl.multiple_of(TRUNK + run * SEG, SEG)
                flag = jnp.minimum(meta[run] + 1, 1).astype(F32)
                query = q_ref[0, piece * 2 * rows + 2 * sub * s : piece * 2 * rows + 2 * sub * (s + 1)]
                room = places[block] + (lax.rem(row, SEG) - s * sub)
                weights = jnp.exp2(nt(query, kvs[0, head, pl.ds(own, SEG)]) * exp2_scale)
                weights = jnp.where(lane[block] <= room, weights, 0.0)
                above = jnp.exp2(nt(query, kp[run - lead]) * exp2_scale) * flag
                part[block] += weights + above
                acc[block] += matmul(weights.astype(BF16), kvs[1, head, pl.ds(own, SEG)]) + matmul(
                    above.astype(BF16), vp[run - lead]
                )

            if piece == 0:
                pl.when(base + s * sub >= TRUNK)(runs)
            else:
                runs()

        total = jnp.sum(part[...], axis=-1, keepdims=True)
        mixed = (acc[...] / total).astype(BF16)
        for s in range(SUBS):
            for h in range(2):
                row = piece * rows + sub * s
                mixed_ref[row : row + sub, h * HEAD_DIM : (h + 1) * HEAD_DIM] = mixed[
                    (2 * s + h) * sub : (2 * s + h + 1) * sub
                ]
        l_ref[region] = jnp.where(lane == head, total, l_ref[region])

    for moment, steps in FORWARD_AFTER.items():
        pl.when(head == moment)(functools.partial(act, steps))

    @pl.when(head == KV_HEADS - 1)
    def _():
        for pair in weights_:
            for g in pair:
                g.close()
        for group in range(4):
            kept(group).wait()
        swap.wait()


def forward(sizes, meta, queries, kv, cotangent, out_shard, feed_shards):
    ny, nx, nz = sizes
    rows = kv.shape[3]
    count = 1 + FF_CHUNKS
    rounds = KeyValues.copies(sizes) + 2 * count * Gather.copies(sizes) + 1
    results = pl.pallas_call(
        functools.partial(forward_kernel, sizes, rows),
        out_shape=[
            jax.ShapeDtypeStruct((2 * rows, QD), BF16),
            jax.ShapeDtypeStruct((4 * rows, HEAD_DIM), F32),
            jax.ShapeDtypeStruct((2, KV_HEADS, TREE, HEAD_DIM), BF16),
            jax.ShapeDtypeStruct((ny, nx, nz, 2) + out_shard.shape, BF16),
            jax.ShapeDtypeStruct((FF_CHUNKS, ny, nx, nz, 2) + feed_shards[0].shape, BF16),
            jax.ShapeDtypeStruct(cotangent.shape, BF16),
        ],
        grid_spec=pltpu.PrefetchScalarGridSpec(
            num_scalar_prefetch=1,
            grid=(KV_HEADS,),
            in_specs=[pl.BlockSpec((1, 4 * rows, HEAD_DIM), lambda h, meta: (h, 0, 0)), ANY, ANY] + [ANY] * count,
            out_specs=[
                pl.BlockSpec((2 * rows, 2 * HEAD_DIM), lambda h, meta: (0, h)),
                pl.BlockSpec((4 * rows, HEAD_DIM), lambda h, meta: (0, 0)),
                ANY,
                ANY,
                ANY,
                ANY,
            ],
            scratch_shapes=[
                pltpu.VMEM((2, KV_HEADS, TREE, HEAD_DIM), BF16),
                pltpu.VMEM((2 * rows, HEAD_DIM), F32),
                pltpu.VMEM((2 * rows, HEAD_DIM), F32),
                pltpu.VMEM((2 * rows, HEAD_DIM), jnp.int32),
                pltpu.VMEM((LOCAL_RUNS, SEG, HEAD_DIM), BF16),
                pltpu.VMEM((LOCAL_RUNS, SEG, HEAD_DIM), BF16),
                pltpu.SemaphoreType.DMA((rounds,)),
                pltpu.SemaphoreType.DMA((rounds,)),
                pltpu.SemaphoreType.DMA((13 + 2 * count,)),
            ],
        ),
        compiler_params=pltpu.CompilerParams(
            collective_id=2, has_side_effects=True, vmem_limit_bytes=48 * MIB
        ),
        name="forward",
    )(meta, queries, kv, cotangent, out_shard, *feed_shards)
    mixed, totals, kv_all, out_whole, feed_whole, cot = results
    return mixed, totals, kv_all, out_whole.reshape(D, QD), feed_whole.reshape(FF_CHUNKS, D, -1), cot


def feed_kernel(
    sizes, rows, x_ref, mixed_ref, cot_ref, out_ref, gain_ref, w_ref,
    result_ref, hid_ref, stack_ref, delta_ref, post_ref, dout_ref, late_ref, early_ref, *refs,
):
    hidden, second, second_t, cot_t, total, grads, inner, gate_up, low, stack, part = refs[:11]
    buffers = refs[11:-3]
    send_sem, recv_sem, local_sem = refs[-3:]
    ny, nx, nz = sizes
    count = 2 * rows
    sub = rows // SUBS
    shard_rows = part.shape[5]
    width = 3 * FF_CHUNK
    tile = 256
    chunk = pl.program_id(0)
    links = Links(sizes, send_sem, recv_sem)
    _, _, _, core = links.place()
    scatters = []
    for c in range(FF_EARLY):
        for b, cols in enumerate(halves_of(width)):
            k = 4 * len(scatters)
            scatters.append(
                Scatter(
                    links,
                    (c, b),
                    part.at[c % 2],
                    ORDERS[b],
                    cols,
                    *buffers[k : k + 4],
                    part.at[c % 2, :, :, :, core, :, cols],
                    None,
                    early_ref.at[c],
                )
            )

    def act(steps):
        for what, c in steps:
            for s in scatters[2 * c : 2 * c + 2]:
                if what == "core":
                    s.start()
                elif what == "begin":
                    s.begin()
                elif what == "finish":
                    s.finish()
                else:
                    s.middle(what)

    def rows_of(block):
        return (block // (2 * nz * nx), lax.rem(block // (2 * nz), nx), lax.rem(block // 2, nz), lax.rem(block, 2))

    def put(slot, first, cols, value):
        for k in range(value.shape[0] // shard_rows):
            y, x, z, c = rows_of(first // shard_rows + k)
            part[slot, y, x, z, c, :, cols] = value[k * shard_rows : (k + 1) * shard_rows].astype(BF16)

    def late(c):
        return pltpu.make_async_copy(part.at[c % 2], late_ref.at[c - FF_EARLY], local_sem.at[c % 2])

    @pl.when(chunk == 0)
    def _():
        links.meet()

        def project_out(t, carry):
            at = pl.multiple_of(t * tile, tile)
            hidden[:, pl.ds(at, tile)] = x_ref[:, pl.ds(at, tile)].astype(F32) + nt(
                mixed_ref[...], out_ref[pl.ds(at, tile), :]
            )
            return carry

        lax.fori_loop(0, D // tile, project_out, 0)
        values = hidden[...]
        values = values * norm_factor(values) * gain_ref[...]
        second[...] = values.astype(BF16)
        second_t[...] = values.T.astype(BF16)
        cot_t[...] = cot_ref[...].astype(F32).T.astype(BF16)
        total[...] = jnp.zeros_like(total)
        grads[...] = jnp.zeros_like(grads)

    slot = lax.rem(chunk, 2)

    def columns(t, carry):
        at = pl.multiple_of(t * tile, tile)
        gate = matmul(second[...], w_ref[0, :, pl.ds(at, tile)])
        up = matmul(second[...], w_ref[0, :, pl.ds(FF_CHUNK + at, tile)])
        grad = matmul(cot_ref[...], w_ref[0, :, pl.ds(2 * FF_CHUNK + at, tile)])
        sigmoid = 1.0 / (1.0 + jnp.exp(-gate))
        active = gate * sigmoid
        inner[:, pl.ds(at, tile)] = (active * up).astype(BF16)
        gate_up[:, pl.ds(at, tile)] = (grad * up * sigmoid * (1.0 + gate * (1.0 - sigmoid))).astype(BF16)
        gate_up[:, pl.ds(FF_CHUNK + at, tile)] = (grad * active).astype(BF16)
        return carry

    lax.fori_loop(0, FF_CHUNK // tile, columns, 0)
    for moment, steps in FEED_MIDDLE.items():
        pl.when(chunk == moment)(functools.partial(act, steps))
    for c in range(FF_EARLY, FF_CHUNKS - 2):
        pl.when(chunk == c + 2)(lambda: late(c).wait())

    def model(t, carry):
        at = pl.multiple_of(t * tile, tile)
        total[:, pl.ds(at, tile)] += nt(inner[...], w_ref[0, pl.ds(at, tile), 2 * FF_CHUNK :])
        grads[:, pl.ds(at, tile)] += nt(gate_up[...], w_ref[0, pl.ds(at, tile), : 2 * FF_CHUNK])
        put(slot, at, slice(0, 2 * FF_CHUNK), matmul(second_t[pl.ds(at, tile)], gate_up[...]))
        put(slot, at, slice(2 * FF_CHUNK, width), matmul(cot_t[pl.ds(at, tile)], inner[...]))
        return carry

    lax.fori_loop(0, D // tile, model, 0)
    for c in range(FF_EARLY, FF_CHUNKS):
        pl.when(chunk == c)(lambda: late(c).start())
    for moment, steps in FEED_AFTER.items():
        pl.when(chunk == moment)(functools.partial(act, steps))

    @pl.when(chunk == FF_CHUNKS - 1)
    def _():
        values = hidden[...]
        low[...] = (values + total[...]).astype(BF16)
        output = pltpu.make_async_copy(low, result_ref, local_sem.at[2])
        output.start()
        factor = norm_factor(values)
        grad_in, share = norm_backward(grads[...], gain_ref[...], values * factor, factor)
        post_ref[...] = jnp.sum(share, axis=0, keepdims=True)
        hidden[...] = cot_ref[...].astype(F32) + grad_in
        saved = pltpu.make_async_copy(hidden, hid_ref, local_sem.at[3])
        saved.start()
        second[...] = hidden[...].astype(BF16)
        second_t[...] = hidden[...].T.astype(BF16)
        lane = lax.broadcasted_iota(jnp.int32, (count, HEAD_DIM), 1)
        dots = jnp.zeros((count, HEAD_DIM), F32)
        for h in range(KV_HEADS):
            cols = slice(2 * h * HEAD_DIM, 2 * (h + 1) * HEAD_DIM)
            grad = matmul(second[...], out_ref[:, cols]).astype(BF16)
            for g in range(2):
                one = grad[:, g * HEAD_DIM : (g + 1) * HEAD_DIM]
                for s in range(2 * SUBS):
                    stack[h, (2 * s + g) * sub : (2 * s + g + 1) * sub] = one[s * sub : (s + 1) * sub]
                head = 2 * h + g
                product = one.astype(F32) * mixed_ref[:, head * HEAD_DIM : (head + 1) * HEAD_DIM].astype(F32)
                dots = jnp.where(lane == head, jnp.sum(product, axis=-1, keepdims=True), dots)
        delta_ref[...] = dots.T
        stacked_ = pltpu.make_async_copy(stack, stack_ref, local_sem.at[4])
        stacked_.start()
        act(FEED_LAST)
        for c in range(FF_CHUNKS - 2, FF_CHUNKS):
            late(c).wait()

        def model_out(t, carry):
            at = pl.multiple_of(t * tile, tile)
            for a in range(0, QD, 2 * FF_CHUNK):
                cols = slice(a, a + 2 * FF_CHUNK)
                value = matmul(second_t[pl.ds(at, tile)], mixed_ref[:, cols])
                slot = a // (2 * FF_CHUNK)
                put(slot, at, slice(0, 2 * FF_CHUNK), value)
            return carry

        lax.fori_loop(0, D // tile, model_out, 0)
        gone = [
            pltpu.make_async_copy(
                part.at[k, :, :, :, :, :, : 2 * FF_CHUNK],
                dout_ref.at[:, :, :, :, :, 2 * FF_CHUNK * k : 2 * FF_CHUNK * (k + 1)],
                local_sem.at[k],
            )
            for k in range(2)
        ]
        run_all(gone, "start")
        for c in range(FF_EARLY):
            act([("finish", c)])
        run_all(gone + [output, saved, stacked_], "wait")


def feed(sizes, x, mixed, cot, out_t, gain, feed_whole):
    ny, nx, nz = sizes
    count = x.shape[0]
    rows = count // 2
    shard_rows = D // (ny * nx * nz * 2)
    width = 3 * FF_CHUNK
    buffers = []
    for c in range(FF_EARLY):
        for b, cols in enumerate(halves_of(width)):
            buffers += Scatter.scratch(sizes, ORDERS[b], shard_rows, cols.stop - cols.start)
    rounds = 2 * FF_EARLY * Scatter.copies(sizes)

    def whole_block(shape):
        return pl.BlockSpec(shape, lambda c: (0,) * len(shape), pipeline_mode=pl.Buffered(1))

    blocks = (ny, nx, nz, 2, shard_rows)
    return pl.pallas_call(
        functools.partial(feed_kernel, sizes, rows),
        grid=(FF_CHUNKS,),
        out_shape=[
            jax.ShapeDtypeStruct((count, D), BF16),
            jax.ShapeDtypeStruct((count, D), F32),
            jax.ShapeDtypeStruct((KV_HEADS, 2 * count, HEAD_DIM), BF16),
            jax.ShapeDtypeStruct((HEAD_DIM, count), F32),
            jax.ShapeDtypeStruct((1, D), F32),
            jax.ShapeDtypeStruct(blocks + (QD,), BF16),
            jax.ShapeDtypeStruct((FF_CHUNKS - FF_EARLY,) + blocks + (width,), BF16),
            jax.ShapeDtypeStruct((FF_EARLY, shard_rows, width), F32),
        ],
        in_specs=[
            whole_block((count, D)),
            whole_block((count, QD)),
            whole_block((count, D)),
            whole_block((D, QD)),
            whole_block((1, D)),
            pl.BlockSpec((1, D, width), lambda c: (c, 0, 0)),
        ],
        out_specs=[
            ANY,
            ANY,
            ANY,
            pl.BlockSpec((HEAD_DIM, count), lambda c: (0, 0)),
            pl.BlockSpec((1, D), lambda c: (0, 0)),
            ANY,
            ANY,
            pl.BlockSpec((FF_EARLY, shard_rows, width), lambda c: (0, 0, 0)),
        ],
        scratch_shapes=[
            pltpu.VMEM((count, D), F32),
            pltpu.VMEM((count, D), BF16),
            pltpu.VMEM((D, count), BF16),
            pltpu.VMEM((D, count), BF16),
            pltpu.VMEM((count, D), F32),
            pltpu.VMEM((count, D), F32),
            pltpu.VMEM((count, FF_CHUNK), BF16),
            pltpu.VMEM((count, 2 * FF_CHUNK), BF16),
            pltpu.VMEM((count, D), BF16),
            pltpu.VMEM((KV_HEADS, 2 * count, HEAD_DIM), BF16),
            pltpu.VMEM((2,) + blocks + (width,), BF16),
        ]
        + buffers
        + [
            pltpu.SemaphoreType.DMA((rounds,)),
            pltpu.SemaphoreType.DMA((rounds,)),
            pltpu.SemaphoreType.DMA((5,)),
        ],
        compiler_params=pltpu.CompilerParams(
            collective_id=5, has_side_effects=True, vmem_limit_bytes=61 * MIB
        ),
        name="feed",
    )(x, mixed, cot, out_t, gain, feed_whole)


def backward_kernel(sizes, rows, widths, meta, q_ref, g_ref, k_ref, v_ref, lse_ref, del_ref, late_ref, dout_ref, done_ref, *refs):
    dq_ref, dkv_ref, late_out, dout_out, done_placed = refs[:5]
    dq, dk, dv, pk, pv, kp, vp, stage, near, sums, far, last = refs[5:17]
    buffers = refs[17:-3]
    send_sem, recv_sem, local_sem = refs[-3:]
    members = sizes[2]
    chips = members // 2
    sub = rows // SUBS
    head = pl.program_id(0)
    links = Links(sizes, send_sem, recv_sem)
    scatters = []
    late = FF_CHUNKS - FF_EARLY
    for a, width in enumerate(widths):
        for b, cols in enumerate(halves_of(width)):
            k = 5 * len(scatters)
            scatters.append(
                Scatter(
                    links,
                    (a, b),
                    late_ref.at[a] if a < late else dout_ref,
                    ORDERS[b],
                    cols,
                    *buffers[k : k + 5],
                    local_sem.at[2 + len(scatters)],
                    late_out.at[a] if a < late else dout_out,
                )
            )

    swap = Exchange(links, done_ref, done_placed, local_sem.at[2 + len(scatters)])

    def each(array):
        return scatters[2 * array : 2 * array + 2]

    @pl.when(head == 0)
    def _():
        for s in scatters:
            s.load().start()
        links.meet()
        for s in scatters:
            s.start()
        swap.start()

    _, _, z, core = links.place()
    here = lax.rem(z, chips)
    mine = here * 2 + core
    dk[...] = jnp.zeros_like(dk)
    dv[...] = jnp.zeros_like(dv)
    pk[...] = jnp.zeros_like(pk)
    pv[...] = jnp.zeros_like(pv)
    for piece in range(2):
        base = rows * (piece * members + mine)
        at = piece * 2 * rows
        region = slice(at, at + 2 * rows)
        dq[...] = jnp.zeros_like(dq)

        def pair(key, value, block, mask):
            spot = slice(at + block.start, at + block.stop)
            weights = jnp.exp2(nt(key, q_ref[0, spot]) * exp2_scale - lse_ref[0, :, spot])
            if mask is not None:
                weights = mask(weights)
            grads = (weights * (nt(value, g_ref[0, spot]) - del_ref[0, :, spot])).astype(BF16)
            weights = weights.astype(BF16)
            dq[block] += contract_rows(grads, key)
            return matmul(grads, q_ref[0, spot]), matmul(weights, g_ref[0, spot])

        everything = slice(0, 2 * rows)

        def trunk(step, masked):
            start = pl.multiple_of(step * CHUNK, CHUNK)

            def mask(weights):
                shape = weights.shape
                room = row_places((1, shape[1]), 1, sub) + (base - start)
                return jnp.where(lax.broadcasted_iota(jnp.int32, shape, 0) <= room, weights, 0.0)

            key_grad, value_grad = pair(
                k_ref[0, 0, pl.ds(start, CHUNK)],
                v_ref[0, 0, pl.ds(start, CHUNK)],
                everything,
                mask if masked else None,
            )
            dk[pl.ds(start, CHUNK)] += key_grad
            dv[pl.ds(start, CHUNK)] += value_grad

        if piece == 0:
            clear = jnp.minimum(base // CHUNK, TRUNK // CHUNK)
            end = jnp.minimum((base + rows + CHUNK - 1) // CHUNK, TRUNK // CHUNK)
            lax.fori_loop(0, clear, lambda i, c: (trunk(i, False), c)[1], 0)
            lax.fori_loop(clear, end, lambda i, c: (trunk(i, True), c)[1], 0)
        else:
            lax.fori_loop(0, TRUNK // CHUNK, lambda i, c: (trunk(i, False), c)[1], 0)

        lead = jnp.maximum(base - TRUNK, 0) // SEG

        def parents_():
            gather_parents(
                meta,
                lead,
                0,
                [
                    (lambda b: k_ref[0, 0, TRUNK + b * SEG : TRUNK + (b + 1) * SEG], kp),
                    (lambda b: v_ref[0, 0, TRUNK + b * SEG : TRUNK + (b + 1) * SEG], vp),
                ],
            )

        if piece == 0:
            pl.when(base + rows > TRUNK)(parents_)
        else:
            parents_()
        for s in range(SUBS):
            block = slice(2 * sub * s, 2 * sub * (s + 1))

            def runs():
                row = base + s * sub - TRUNK
                run = row // SEG
                own = pl.multiple_of(TRUNK + run * SEG, SEG)
                flag = jnp.minimum(meta[run] + 1, 1).astype(F32)

                def mask(weights):
                    shape = (SEG, 2 * sub)
                    room = lax.broadcasted_iota(jnp.int32, shape, 1) % sub + lax.rem(row, SEG)
                    seen = lax.broadcasted_iota(jnp.int32, shape, 0) <= room
                    return jnp.concatenate(
                        [jnp.where(seen, weights[:SEG], 0.0), weights[SEG:] * flag], axis=0
                    )

                key_grad, value_grad = pair(
                    jnp.concatenate([k_ref[0, 0, pl.ds(own, SEG)], kp[run - lead]], axis=0),
                    jnp.concatenate([v_ref[0, 0, pl.ds(own, SEG)], vp[run - lead]], axis=0),
                    block,
                    mask,
                )
                dk[pl.ds(own, SEG)] += key_grad[:SEG]
                dv[pl.ds(own, SEG)] += value_grad[:SEG]
                slot = LOCAL_RUNS * piece + run - lead
                pk[slot] += key_grad[SEG:]
                pv[slot] += value_grad[SEG:]

            if piece == 0:
                pl.when(base + s * sub >= TRUNK)(runs)
            else:
                runs()

        dq_ref[0, region] = dq[...] * score_scale

        def spread():
            parents = [meta[jnp.minimum(lead + k, TREE // SEG - TRUNK // SEG - 1)] for k in range(LOCAL_RUNS)]

            def place(b, carry):
                start = pl.multiple_of(TRUNK + b * SEG, SEG)
                key_grad, value_grad = dk[pl.ds(start, SEG)], dv[pl.ds(start, SEG)]
                for k in range(LOCAL_RUNS):
                    share = (1 - jnp.minimum(jnp.abs(parents[k] - b), 1)).astype(F32)
                    key_grad += pk[LOCAL_RUNS * piece + k] * share
                    value_grad += pv[LOCAL_RUNS * piece + k] * share
                dk[pl.ds(start, SEG)] = key_grad
                dv[pl.ds(start, SEG)] = value_grad
                return carry

            lax.fori_loop(0, (TREE - TRUNK) // SEG, place, 0)

        if piece == 0:
            pl.when(base + rows > TRUNK)(spread)
        else:
            spread()

    def core_copy(h):
        return links.copy(("kv core", h), stage.at[h % 2, :, 1 - core], near.at[h % 2], links.sibling())

    def far_copies(h):
        return [
            links.copy(("kv z", h, i), sums.at[h, chip], far.at[h, i], target)
            for i, (chip, target) in enumerate(links.group())
        ]

    def pass_on(h):
        core_copy(h).wait()

        def add(i, carry):
            chip, which, piece = i // 4, lax.rem(i // 2, 2), lax.rem(i, 2)
            sums[h, chip, which, piece] = (
                stage[h % 2, chip, core, which, piece].astype(F32) + near[h % 2, chip, which, piece].astype(F32)
            ).astype(BF16)
            return carry

        lax.fori_loop(0, chips * 4, add, 0)
        run_all(far_copies(h), "start")

    for h in range(1, KV_HEADS):
        pl.when(head == h)(functools.partial(pass_on, h - 1))

    for which, grad, scale in ((0, dk, score_scale), (1, dv, 1.0)):
        for piece in range(2):
            for member in range(members):
                start = rows * (piece * members + member)
                stage[lax.rem(head, 2), member // 2, member % 2, which, piece] = (
                    grad[start : start + rows] * scale
                ).astype(BF16)
    for h in range(KV_HEADS):

        @pl.when(head == h)
        def _():
            core_copy(h).start()

    for moment, steps in BACKWARD_AFTER.items():

        @pl.when(head == moment)
        def _():
            for step, array in steps:
                for s in each(array):
                    if step == 0:
                        s.begin()
                    else:
                        s.middle(step - 1)

    def result(h):
        return pltpu.make_async_copy(last.at[h % 2], dkv_ref.at[:, h], local_sem.at[h % 2])

    @pl.when(head == KV_HEADS - 1)
    def _():
        pass_on(KV_HEADS - 1)
        for s in scatters:
            s.finish()
        for h in range(KV_HEADS):
            run_all(far_copies(h), "wait")
            if h > 1:
                result(h - 2).wait()
            for which in range(2):
                for piece in range(2):
                    total = sums[h, here, which, piece].astype(F32)
                    for i in range(chips - 1):
                        total = total + far[h, i, which, piece].astype(F32)
                    last[h % 2, which, piece] = total
            result(h).start()
        for h in (KV_HEADS - 2, KV_HEADS - 1):
            result(h).wait()
        swap.wait()


def backward(sizes, meta, queries, grads, kv_all, log_total, delta, late, dout, done):
    ny, nx, nz = sizes
    chips = nz // 2
    rows = queries.shape[1] // 4
    widths = (late.shape[-1],) * late.shape[0] + (dout.shape[-1],)
    shard_rows = dout.shape[4]
    stack = pl.BlockSpec((1, 4 * rows, HEAD_DIM), lambda h, meta: (h, 0, 0))
    line = pl.BlockSpec((1, 1, 4 * rows), lambda h, meta: (h, 0, 0))
    buffers, count = [], 0
    for w in widths:
        for b, cols in enumerate(halves_of(w)):
            buffers += Scatter.scratch(sizes, ORDERS[b], shard_rows, cols.stop - cols.start)
            buffers.append(pltpu.VMEM((ny, nx, nz, shard_rows, cols.stop - cols.start), BF16))
            count += 1
    rounds = count * Scatter.copies(sizes) + KV_HEADS * chips + 1
    late_shape = (late.shape[0], shard_rows, late.shape[-1])
    dout_shape = (shard_rows, dout.shape[-1])
    return pl.pallas_call(
        functools.partial(backward_kernel, sizes, rows, widths),
        out_shape=[
            jax.ShapeDtypeStruct((KV_HEADS, 4 * rows, HEAD_DIM), F32),
            jax.ShapeDtypeStruct((2, KV_HEADS, 2, rows, HEAD_DIM), F32),
            jax.ShapeDtypeStruct(late_shape, F32),
            jax.ShapeDtypeStruct(dout_shape, F32),
            jax.ShapeDtypeStruct(done.shape, BF16),
        ],
        grid_spec=pltpu.PrefetchScalarGridSpec(
            num_scalar_prefetch=1,
            grid=(KV_HEADS,),
            in_specs=[
                stack,
                stack,
                pl.BlockSpec((1, 1, TREE, HEAD_DIM), lambda h, meta: (0, h, 0, 0)),
                pl.BlockSpec((1, 1, TREE, HEAD_DIM), lambda h, meta: (1, h, 0, 0)),
                line,
                line,
                ANY,
                ANY,
                ANY,
            ],
            out_specs=[
                stack,
                ANY,
                pl.BlockSpec(late_shape, lambda h, meta: (0, 0, 0)),
                pl.BlockSpec(dout_shape, lambda h, meta: (0, 0)),
                ANY,
            ],
            scratch_shapes=[
                pltpu.VMEM((2 * rows, HEAD_DIM), F32),
                pltpu.VMEM((TREE, HEAD_DIM), F32),
                pltpu.VMEM((TREE, HEAD_DIM), F32),
                pltpu.VMEM((2 * LOCAL_RUNS, SEG, HEAD_DIM), F32),
                pltpu.VMEM((2 * LOCAL_RUNS, SEG, HEAD_DIM), F32),
                pltpu.VMEM((LOCAL_RUNS, SEG, HEAD_DIM), BF16),
                pltpu.VMEM((LOCAL_RUNS, SEG, HEAD_DIM), BF16),
                pltpu.VMEM((2, chips, 2, 2, 2, rows, HEAD_DIM), BF16),
                pltpu.VMEM((2, chips, 2, 2, rows, HEAD_DIM), BF16),
                pltpu.VMEM((KV_HEADS, chips, 2, 2, rows, HEAD_DIM), BF16),
                pltpu.VMEM((KV_HEADS, chips - 1, 2, 2, rows, HEAD_DIM), BF16),
                pltpu.VMEM((2, 2, 2, rows, HEAD_DIM), F32),
            ]
            + buffers
            + [
                pltpu.SemaphoreType.DMA((rounds,)),
                pltpu.SemaphoreType.DMA((rounds,)),
                pltpu.SemaphoreType.DMA((3 + count,)),
            ],
        ),
        compiler_params=pltpu.CompilerParams(
            collective_id=3, has_side_effects=True, vmem_limit_bytes=60 * MIB
        ),
        name="backward",
    )(
        meta,
        queries,
        grads,
        kv_all,
        kv_all,
        log_total.reshape(KV_HEADS, 1, 4 * rows),
        delta.reshape(KV_HEADS, 1, 4 * rows),
        late,
        dout,
        done,
    )


def scatter_kernel(sizes, widths, *refs):
    count = len(widths)
    parts = refs[:count]
    moved_ref = refs[count]
    outs = refs[count + 1 : 2 * count + 1]
    placed_ref = refs[2 * count + 1]
    rest = refs[2 * count + 2 :]
    send_sem, recv_sem, local_sem = rest[-3:]
    links = Links(sizes, send_sem, recv_sem)
    scatters = []
    used = 0
    for a in range(count):
        for b, cols in enumerate(halves_of(widths[a])):
            k = 5 * used
            scatters.append(
                Scatter(
                    links,
                    (a, b),
                    parts[a],
                    ORDERS[b],
                    cols,
                    *rest[k : k + 4],
                    rest[k + 4],
                    local_sem.at[used],
                    outs[a],
                )
            )
            used += 1
    for s in scatters:
        s.load().start()
    links.meet()
    for s in scatters:
        s.start()
    _, _, z, _ = links.place()
    half = z // (sizes[2] // 2)
    keep = pltpu.make_async_copy(moved_ref.at[half], placed_ref.at[half], local_sem.at[used])
    give = links.copy("moved", moved_ref.at[1 - half], placed_ref.at[half], links.across())
    keep.start()
    give.start()
    depth = 2
    for i, s in enumerate(scatters):
        if i >= depth:
            scatters[i - depth].middle(0)
        s.begin()
    for s in scatters[-depth:]:
        s.middle(0)
    for s in scatters:
        s.middle(1)
    for s in scatters:
        s.finish()
    keep.wait()
    give.wait()


def scatter_end(sizes, parts, moved):
    ny, nx, nz = sizes
    shard_rows = D // (ny * nx * nz * 2)
    widths = tuple(p.shape[-1] for p in parts)
    pieces = [p.reshape(ny, nx, nz, 2, shard_rows, p.shape[-1]) for p in parts]
    buffers, count = [], 0
    for w in widths:
        for b, cols in enumerate(halves_of(w)):
            buffers += Scatter.scratch(sizes, ORDERS[b], shard_rows, cols.stop - cols.start)
            buffers.append(pltpu.VMEM((ny, nx, nz, shard_rows, cols.stop - cols.start), BF16))
            count += 1
    rounds = count * Scatter.copies(sizes) + 1
    results = pl.pallas_call(
        functools.partial(scatter_kernel, sizes, widths),
        out_shape=[jax.ShapeDtypeStruct((shard_rows, w), F32) for w in widths]
        + [jax.ShapeDtypeStruct(moved.shape, BF16)],
        in_specs=[ANY] * (len(widths) + 1),
        out_specs=[pl.BlockSpec(memory_space=pltpu.VMEM)] * len(widths) + [ANY],
        scratch_shapes=buffers
        + [
            pltpu.SemaphoreType.DMA((rounds,)),
            pltpu.SemaphoreType.DMA((rounds,)),
            pltpu.SemaphoreType.DMA((count + 1,)),
        ],
        compiler_params=pltpu.CompilerParams(
            collective_id=4, has_side_effects=True, vmem_limit_bytes=48 * MIB
        ),
        name="scatter_end",
    )(*pieces, moved)
    return results[:-1], results[-1]


def shards(
    sizes,
    tokens,
    cotangent,
    segment_ids,
    positions,
    parents,
    input_norm,
    query_proj,
    key_proj,
    value_proj,
    query_norm,
    key_norm,
    out_proj,
    post_norm,
    gate_proj,
    up_proj,
    down_proj,
):
    nz = sizes[2]
    rows = tokens.shape[1]
    shard_rows = query_proj.shape[0]
    gain_rows = query_norm.shape[0]
    ctx = lax.axis_index("ctx")
    half = ctx // nz
    member = ctx % nz
    count = 2 * rows
    sub = rows // SUBS

    def column(gain):
        return jnp.pad(gain, (0, shard_rows - gain.shape[0]))[:, None]

    gains = jnp.concatenate(
        [column(input_norm), column(post_norm), column(query_norm), column(key_norm)], axis=1
    )
    gains = jnp.pad(gains, ((0, 0), (0, GAIN_COLS - 4)))
    key_value = jnp.concatenate([key_proj, value_proj, gains], axis=1)
    query_full, kv_full, placed = gather_start(sizes, query_proj, key_value, tokens)
    x = placed.reshape(count, D)

    gain_block = kv_full[:, 2 * KVD :].astype(F32)
    in_weight = gain_block[:, 0][None, :]
    post_weight = gain_block[:, 1][None, :]
    by_device = gain_block.reshape(-1, shard_rows, GAIN_COLS)
    query_weight = by_device[:, :gain_rows, 2].reshape(1, HEAD_DIM)
    key_weight = by_device[:, :gain_rows, 3].reshape(1, HEAD_DIM)

    run_seg = segment_ids[half][TRUNK::SEG]
    run_parent = parents[half][run_seg]
    parent_run = jnp.argmax(run_seg[None, :] == run_parent[:, None], axis=1).astype(jnp.int32)
    meta = jnp.where(run_parent > 0, parent_run, -1)
    pos_tree = positions[half].reshape(2, nz, rows)
    pos_local = lax.dynamic_index_in_dim(pos_tree, member, 1, keepdims=False).reshape(count)
    cosine, sine = rope_tables(pos_local)

    normed, queries, kv, pre = project(
        x, in_weight, query_full, kv_full, query_weight, key_weight, cosine, sine
    )
    down_t = down_proj.T
    feed_shards = [
        jnp.concatenate(
            [w[:, c * FF_CHUNK : (c + 1) * FF_CHUNK] for w in (gate_proj, up_proj, down_t)], axis=1
        )
        for c in range(FF_CHUNKS)
    ]
    mixed, totals, kv_all, out_t, feed_whole, cot = forward(
        sizes, meta, queries, kv, cotangent, out_proj.T, feed_shards
    )
    log_total = jnp.log2(totals[:, :KV_HEADS]).T
    cot = cot.reshape(count, D)
    result, grad_hidden, grad_stack, delta, post_part, dout, late, early_grad = feed(
        sizes, x, mixed, cot, out_t, post_weight, feed_whole
    )
    delta = delta[:HEADS].reshape(KV_HEADS, 2, 2 * SUBS, sub).transpose(0, 2, 1, 3)
    dq, dkv, late_grad, out_grad, output = backward(
        sizes, meta, queries, grad_stack, kv_all, log_total, delta, late, dout, result.reshape(2, rows, D)
    )
    feed_grad = jnp.concatenate([early_grad, late_grad], axis=0)

    def feed_columns(k):
        piece = feed_grad[:, :, k * FF_CHUNK : (k + 1) * FF_CHUNK]
        return piece.transpose(1, 0, 2).reshape(shard_rows, FF)

    dwq, dwk, dwv, dx, in_part, qk_part = project_back(
        dq, dkv, pre, normed, x, grad_hidden, in_weight, query_full, kv_full, query_weight, key_weight, cosine, sine
    )

    def gain_column(values):
        if values.shape[0] == D:
            return values[:, None]
        spread = jnp.pad(values.reshape(-1, gain_rows), ((0, 0), (0, shard_rows - gain_rows)))
        return spread.reshape(D, 1)

    gain_parts = jnp.concatenate(
        [
            gain_column(in_part[0]),
            gain_column(post_part[0]),
            gain_column(qk_part[0]),
            gain_column(qk_part[1]),
        ],
        axis=1,
    )
    gain_parts = jnp.pad(gain_parts, ((0, 0), (0, GAIN_COLS - 4))).astype(BF16)
    (query_grad, key_grad, value_grad, gain_grad), input_grad = scatter_end(
        sizes, [dwq, dwk, dwv, gain_parts], dx.reshape(2, rows, D)
    )
    return (
        output,
        input_grad.astype(F32),
        gain_grad[:, 0],
        query_grad,
        key_grad,
        value_grad,
        gain_grad[:gain_rows, 2],
        gain_grad[:gain_rows, 3],
        out_grad.T,
        gain_grad[:, 1],
        feed_columns(0),
        feed_columns(1),
        feed_columns(2).T,
    )


def solution(mesh):
    dp, ctx = mesh.shape["dp"], mesh.shape["ctx"]
    sizes = (2, dp // 2, ctx // 2)
    return jax.shard_map(
        functools.partial(shards, sizes),
        mesh=mesh,
        in_specs=(
            P("dp", "ctx", None),
            P("dp", "ctx", None),
            P("dp", None),
            P("dp", None),
            P("dp", None),
            P(("dp", "ctx")),
            P(("dp", "ctx"), None),
            P(("dp", "ctx"), None),
            P(("dp", "ctx"), None),
            P(("dp", "ctx")),
            P(("dp", "ctx")),
            P(None, ("dp", "ctx")),
            P(("dp", "ctx")),
            P(("dp", "ctx"), None),
            P(("dp", "ctx"), None),
            P(None, ("dp", "ctx")),
        ),
        out_specs=(
            P("dp", "ctx", None),
            P("dp", "ctx", None),
            P(("dp", "ctx")),
            P(("dp", "ctx"), None),
            P(("dp", "ctx"), None),
            P(("dp", "ctx"), None),
            P(("dp", "ctx")),
            P(("dp", "ctx")),
            P(None, ("dp", "ctx")),
            P(("dp", "ctx")),
            P(("dp", "ctx"), None),
            P(("dp", "ctx"), None),
            P(None, ("dp", "ctx")),
        ),
        check_vma=False,
    )
```

```python
import functools
import math

import jax
import jax.numpy as jnp
from jax import lax
from jax.experimental import pallas as pl
from jax.experimental.pallas import tpu as pltpu
from jax.sharding import PartitionSpec as P

D = 1024
HEADS = 16
KV_HEADS = 8
HEAD_DIM = 128
FF = 3072
TRUNK = 1024
SEG = 128
TREE = 2560
QD = HEADS * HEAD_DIM
KVD = KV_HEADS * HEAD_DIM
SUBS = 5
CHUNK = 256
GAIN_COLS = 128
FF_CHUNK = 512
PAIRS = KV_HEADS // 2
FF_CHUNKS = FF // FF_CHUNK
FF_EARLY = 4
LOCAL_RUNS = 3
MIB = 1024 * 1024

eps_norm = 1e-06
rope_base = 1000000.0
exp2_scale = math.log2(math.e) / math.sqrt(HEAD_DIM)
score_scale = HEAD_DIM ** (-0.5)

MESH = pl.DeviceIdType.MESH
ANY = pl.BlockSpec(memory_space=pl.ANY)
F32 = jnp.float32
BF16 = jnp.bfloat16


def matmul(left_side, right_side):
    return jnp.dot(left_side, right_side, preferred_element_type=F32)


def nt(left_side, right_side):
    return lax.dot_general(
        left_side, right_side, (((1,), (1,)), ((), ())), preferred_element_type=F32
    )


def contract_rows(left_side, right_side):
    return lax.dot_general(
        left_side, right_side, (((0,), (0,)), ((), ())), preferred_element_type=F32
    )


def norm_factor(values):
    return lax.rsqrt(jnp.mean(values * values, axis=-1, keepdims=True) + eps_norm)


def norm_backward(grad_out, weight, normed, factor):
    weighted = grad_out * weight
    grad_in = factor * (weighted - normed * jnp.mean(weighted * normed, axis=-1, keepdims=True))
    return (grad_in, grad_out * normed)


def rope_tables(positions):
    steps_half = jnp.arange(HEAD_DIM // 2, dtype=F32)
    inverse = rope_base ** (-(steps_half * 2.0 / HEAD_DIM))
    angles = positions.astype(F32)[:, None] * inverse[None, :]
    cosine, sine = jnp.cos(angles), jnp.sin(angles)
    return jnp.concatenate([cosine, cosine], axis=-1), jnp.concatenate([-sine, sine], axis=-1)


class Links:
    def __init__(self, sizes, send_sem, recv_sem):
        self.sizes = sizes
        self.send_sem = send_sem
        self.recv_sem = recv_sem
        self.index = {}

    def place(self):
        _, nx, _ = self.sizes
        dp, ctx = lax.axis_index("dp"), lax.axis_index("ctx")
        return dp // nx, lax.rem(dp, nx), ctx // 2, lax.rem(ctx, 2)

    def device(self, y, x, z, core):
        return (y * self.sizes[1] + x, z * 2 + core)

    def peers(self, axis, back=False):
        y, x, z, core = self.place()
        at = {"y": y, "x": x, "z": z}
        n = self.sizes["yxz".index(axis)]
        found = []
        for s in range(1, n):
            moved = dict(at)
            moved[axis] = lax.rem(at[axis] + (n - s if back else s), n)
            found.append((moved["y"], moved["x"], moved["z"], core))
        return found

    def sibling(self):
        y, x, z, core = self.place()
        return self.device(y, x, z, 1 - core)

    def across(self):
        y, x, z, core = self.place()
        nz = self.sizes[2]
        return self.device(y, x, lax.rem(z + nz // 2, nz), core)

    def group(self, back=False):
        y, x, z, core = self.place()
        chips = self.sizes[2] // 2
        base = (z // chips) * chips
        here = z - base
        chosen = [lax.rem(here + (chips - s if back else s), chips) for s in range(1, chips)]
        return [(chip, self.device(y, x, base + chip, core)) for chip in chosen]

    def meet(self):
        barrier = pltpu.get_barrier_semaphore()
        partners = [self.device(*p) for a in "zxy" for p in self.peers(a)] + [self.sibling()]
        for partner in partners:
            pl.semaphore_signal(barrier, inc=1, device_id=partner, device_id_type=MESH)
        pl.semaphore_wait(barrier, len(partners))

    def copy(self, key, src, dst, target):
        k = self.index.setdefault(key, len(self.index))
        return pltpu.make_async_remote_copy(
            src_ref=src,
            dst_ref=dst,
            send_sem=self.send_sem.at[k],
            recv_sem=self.recv_sem.at[k],
            device_id=target,
            device_id_type=MESH,
        )


class Exchange:
    def __init__(self, links, source, placed, local_sem, tag="swap"):
        self.tag = tag
        self.links = links
        self.source = source
        self.placed = placed
        self.local_sem = local_sem

    def copies_(self):
        _, _, z, _ = self.links.place()
        half = z // (self.links.sizes[2] // 2)
        return [
            self.links.copy(self.tag, self.source.at[1 - half], self.placed.at[half], self.links.across()),
            pltpu.make_async_copy(self.source.at[half], self.placed.at[half], self.local_sem),
        ]

    def start(self):
        for copy in self.copies_():
            copy.start()

    def wait(self):
        for copy in self.copies_():
            copy.wait()


class Gather:
    def __init__(self, links, tag, shard, whole, order, cols, local_sem):
        self.links = links
        self.tag = tag
        self.shard = shard
        self.whole = whole
        self.order = order
        self.cols = cols
        self.local_sem = local_sem

    def own(self):
        y, x, z, core = self.links.place()
        return self.whole.at[y, x, z, core, :, self.cols]

    def slab(self, stage, at):
        y, x, z, core = at
        if stage == 0:
            return self.whole.at[y, x, z, core, :, self.cols]
        if stage == 1:
            return self.whole.at[y, x, :, core, :, self.cols]
        if self.order[0] == "x":
            return self.whole.at[y, :, :, core, :, self.cols]
        return self.whole.at[:, x, :, core, :, self.cols]

    def axis(self, stage):
        return ("z",) + tuple(self.order)[0:2] if stage is None else ("z", self.order[0], self.order[1])[stage]

    def send(self, stage):
        me = self.links.place()
        src = self.shard.at[:, self.cols] if stage == 0 else self.slab(stage, me)
        dst = self.slab(stage, me)
        return [
            self.links.copy((self.tag, stage, i), src, dst, self.links.device(*p))
            for i, p in enumerate(self.links.peers(self.axis(stage)))
        ]

    def forward(self, stage):
        sibling = self.links.sibling()
        if stage < 0:
            return [self.links.copy((self.tag, "own"), self.shard.at[:, self.cols], self.own(), sibling)]
        return [
            self.links.copy((self.tag, "pass", stage, i), self.slab(stage, p), self.slab(stage, p), sibling)
            for i, p in enumerate(self.links.peers(self.axis(stage), back=True))
        ]

    def local(self):
        return pltpu.make_async_copy(self.shard.at[:, self.cols], self.own(), self.local_sem)

    def start(self):
        self.local().start()
        for copy in self.send(0) + self.forward(-1):
            copy.start()

    def step(self, stage):
        if stage == 1:
            self.local().wait()
        for copy in self.send(stage - 1):
            copy.wait()
        if stage < 3:
            for copy in self.send(stage):
                copy.start()
        for copy in self.forward(stage - 1):
            copy.start()

    def close(self):
        for stage in range(-1, 3):
            for copy in self.forward(stage):
                copy.wait()

    @staticmethod
    def copies(sizes):
        return 2 * sum(n - 1 for n in sizes) + 1


class Scatter:
    def __init__(self, links, tag, part, order, cols, halves, firsts, seconds, thirds, temp, temp_sem, out):
        self.links = links
        self.tag = tag
        self.part = part
        self.order = order
        self.cols = cols
        self.sums = halves
        self.got = (firsts, seconds, thirds)
        self.temp = temp
        self.temp_sem = temp_sem
        self.out = out

    def first(self):
        _, _, _, core = self.links.place()
        return self.links.copy(
            (self.tag, "core"), self.part.at[:, :, :, 1 - core, :, self.cols], self.sums, self.links.sibling()
        )

    def load(self):
        _, _, _, core = self.links.place()
        return pltpu.make_async_copy(
            self.part.at[:, :, :, core, :, self.cols], self.temp, self.temp_sem
        )

    def axis(self, stage):
        return (self.order[0], self.order[1], "z")[stage]

    def at(self, stage, place, rest=None):
        y, x, z, _ = place
        if stage == 0:
            return (y,) if self.order[0] == "y" else (slice(None), x)
        if stage == 1:
            return (y, x)
        return (y, x, z)

    def send(self, stage):
        me = self.links.place()
        found = []
        for i, p in enumerate(self.links.peers(self.axis(stage))):
            index = self.at(stage, p)
            found.append(
                self.links.copy(
                    (self.tag, stage, i), self.sums.at[index], self.got[stage].at[i], self.links.device(*p)
                )
            )
        return found

    def start(self):
        self.first().start()

    def begin(self):
        self.first().wait()
        if self.temp_sem is not None:
            self.load().wait()
        ny, nx, nz = self.links.sizes

        def add(i, carry):
            a, b, c = i // (nx * nz), lax.rem(i // nz, nx), lax.rem(i, nz)
            self.sums[a, b, c] = (
                self.sums[a, b, c].astype(F32) + self.temp[a, b, c].astype(F32)
            ).astype(BF16)
            return carry

        lax.fori_loop(0, ny * nx * nz, add, 0)
        for copy in self.send(0):
            copy.start()

    def middle(self, stage):
        for copy in self.send(stage):
            copy.wait()
        y, x, z, _ = self.links.place()
        _, _, nz = self.links.sizes
        got = self.got[stage]
        peers = got.shape[0]
        if stage == 0:
            other = got.shape[1]

            def add(i, carry):
                b, c = i // nz, lax.rem(i, nz)
                index = (y, b, c) if self.order[0] == "y" else (b, x, c)
                total = self.sums[index].astype(F32)
                for p in range(peers):
                    total = total + got[p, b, c].astype(F32)
                self.sums[index] = total.astype(BF16)
                return carry

            lax.fori_loop(0, other * nz, add, 0)
        else:

            def add(c, carry):
                total = self.sums[y, x, c].astype(F32)
                for p in range(peers):
                    total = total + got[p, c].astype(F32)
                self.sums[y, x, c] = total.astype(BF16)
                return carry

            lax.fori_loop(0, nz, add, 0)
        for copy in self.send(stage + 1):
            copy.start()

    def finish(self):
        for copy in self.send(2):
            copy.wait()
        y, x, z, _ = self.links.place()
        total = self.sums[y, x, z].astype(F32)
        for p in range(self.got[2].shape[0]):
            total = total + self.got[2][p].astype(F32)
        self.out[:, self.cols] = total

    @staticmethod
    def copies(sizes):
        return sum(n - 1 for n in sizes) + 1

    @staticmethod
    def scratch(sizes, order, rows, width):
        ny, nx, nz = sizes
        na, nb = (ny, nx) if order[0] == "y" else (nx, ny)
        return [
            pltpu.VMEM((ny, nx, nz, rows, width), BF16),
            pltpu.VMEM((na - 1, nb, nz, rows, width), BF16),
            pltpu.VMEM((nb - 1, nz, rows, width), BF16),
            pltpu.VMEM((nz - 1, rows, width), BF16),
        ]


ORDERS = ("xy", "yx")

FORWARD_START = [("swap", "tokens"), (0, 2), (0, 0), (1, 0), (0, 1), (1, 1), (1, 2), (0, 11), (2, 1), (1, 11), (2, 11), (0, 10), (2, 0), (0, 3), (3, 11), (0, 5), (3, 1), (0, 6), (3, 0), (2, 2), ("swapped", "tokens"), (4, 11), (0, 8)]
FORWARD_AFTER = {
    0: [(1, 3), (3, 2), ("kv", 0), (2, 3), (1, 10)],
    1: [(1, 5), (1, 8), (2, 10), (1, 6), ("kv", 1), ("use", 0), (3, 3), (0, 7)],
    3: [(0, 4), (1, 7), (2, 6), ("got", 0)],
    4: [("use", 1), (2, 8), ("kv", 2)],
    5: [("got", 1), (1, 4)],
    6: [("kv", 3), (3, 6), (2, 5), (0, 9), (2, 7), ("use", 2), (3, 10)],
    7: [("got", 2)],
    8: [(3, 8), (1, 9), (2, 4), ("swap", "cot")],
    9: [("use", 3), (3, 7), ("got", 3)],
    10: [(2, 9), (3, 5)],
    11: [(3, 4), (3, 9), ("swapped", "cot")],
}
FEED_MIDDLE = {
    1: [("begin", 0)],
    2: [("begin", 1), (1, 0)],
    3: [("begin", 2), (1, 1)],
    4: [("begin", 3), (1, 2)],
    5: [(1, 3)],
}
FEED_AFTER = {
    0: [("core", 0)],
    1: [("core", 1), (0, 0)],
    2: [("core", 2), (0, 1)],
    3: [("core", 3), (0, 2)],
    4: [(0, 3)],
}
FEED_LAST = []
BACKWARD_AFTER = {
    0: [(0, 0)],
    1: [(1, 0), (0, 1)],
    2: [(2, 0), (1, 1), (0, 2)],
    3: [(2, 1), (1, 2)],
    4: [(2, 2)],
}


def halves_of(width):
    return (slice(0, width // 2), slice(width // 2, width)) if width >= 512 else (slice(0, width),)


def roll_half(values):
    return pltpu.roll(values, HEAD_DIM // 2, 1)


def project_back_kernel(
    rows, dq_ref, dkv_ref, pre_ref, normed_ref, x_ref, hid_ref, gain_ref, wq_ref, wk_ref, wv_ref, qg_ref, kg_ref, cos_ref, sin_ref,
    dwq_ref, dwk_ref, dwv_ref, dx_ref, in_ref, qk_ref, normed_t, grads,
):
    sub = rows // SUBS
    head = pl.program_id(0)

    @pl.when(head == 0)
    def _():
        normed_t[...] = normed_ref[...].astype(F32).T.astype(BF16)
        grads[...] = jnp.zeros_like(grads)
        qk_ref[...] = jnp.zeros_like(qk_ref)

    cosine, sine = cos_ref[...], sin_ref[...]

    def back(turned_grad, pre, gain):
        grad = turned_grad * cosine - roll_half(turned_grad) * sine
        factor = norm_factor(pre)
        grad_pre, part = norm_backward(grad, gain, pre * factor, factor)
        return grad_pre.astype(BF16), jnp.sum(part, axis=0, keepdims=True)

    pieces = []
    for h in range(2):
        grad = jnp.concatenate(
            [dq_ref[0, (2 * s + h) * sub : (2 * s + h + 1) * sub] for s in range(2 * SUBS)], axis=0
        )
        low, part = back(grad, pre_ref[0, :, h * HEAD_DIM : (h + 1) * HEAD_DIM], qg_ref[...])
        qk_ref[0:1] += part
        pieces.append(low)
    low, part = back(dkv_ref[0, 0].reshape(2 * rows, HEAD_DIM), pre_ref[0, :, 2 * HEAD_DIM :], kg_ref[...])
    qk_ref[1:2] += part
    pieces.append(low)
    pieces.append(dkv_ref[1, 0].reshape(2 * rows, HEAD_DIM).astype(BF16))
    low = jnp.concatenate(pieces, axis=1)
    weights = jnp.concatenate([wq_ref[0], wk_ref[0], wv_ref[0]], axis=1)
    grads[...] += nt(low, weights)
    part = matmul(normed_t[...], low).astype(BF16)
    dwq_ref[...] = part[:, : 2 * HEAD_DIM]
    dwk_ref[...] = part[:, 2 * HEAD_DIM : 3 * HEAD_DIM]
    dwv_ref[...] = part[:, 3 * HEAD_DIM :]

    @pl.when(head == KV_HEADS - 1)
    def _():
        values = x_ref[...].astype(F32)
        factor = norm_factor(values)
        grad_in, part = norm_backward(grads[...], gain_ref[...], values * factor, factor)
        dx_ref[...] = (hid_ref[...] + grad_in).astype(BF16)
        in_ref[...] = jnp.sum(part, axis=0, keepdims=True)


def project_back(dq, dkv, pre, normed, x, grad_hidden, gain, qkv_full, query_gain, key_gain, cosine, sine):
    count = x.shape[0]
    rows = count // 2
    full = pl.BlockSpec((count, D), lambda h: (0, 0))
    row = lambda n: pl.BlockSpec((1, n), lambda h: (0, 0))
    table = pl.BlockSpec((count, HEAD_DIM), lambda h: (0, 0))
    wide = pl.BlockSpec((D, 2 * HEAD_DIM), lambda h: (0, h))
    thin = pl.BlockSpec((D, HEAD_DIM), lambda h: (0, h))
    return pl.pallas_call(
        functools.partial(project_back_kernel, rows),
        grid=(KV_HEADS,),
        out_shape=[
            jax.ShapeDtypeStruct((D, QD), BF16),
            jax.ShapeDtypeStruct((D, KVD), BF16),
            jax.ShapeDtypeStruct((D, KVD), BF16),
            jax.ShapeDtypeStruct((count, D), BF16),
            jax.ShapeDtypeStruct((1, D), F32),
            jax.ShapeDtypeStruct((8, HEAD_DIM), F32),
        ],
        in_specs=[
            pl.BlockSpec((1, 2 * count, HEAD_DIM), lambda h: (h, 0, 0)),
            pl.BlockSpec((2, 1, 2, rows, HEAD_DIM), lambda h: (0, h, 0, 0, 0)),
            pl.BlockSpec((1, count, 3 * HEAD_DIM), lambda h: (h, 0, 0)),
            full,
            full,
            full,
            row(D),
            pl.BlockSpec((1, D, 2 * HEAD_DIM), lambda h: (h // 2, 0, h % 2)),
            pl.BlockSpec((1, D, HEAD_DIM), lambda h: (h // 2, 0, 4 + h % 2)),
            pl.BlockSpec((1, D, HEAD_DIM), lambda h: (h // 2, 0, 6 + h % 2)),
            row(HEAD_DIM),
            row(HEAD_DIM),
            table,
            table,
        ],
        out_specs=[wide, thin, thin, full, row(D), pl.BlockSpec((8, HEAD_DIM), lambda h: (0, 0))],
        scratch_shapes=[pltpu.VMEM((D, count), BF16), pltpu.VMEM((count, D), F32)],
        compiler_params=pltpu.CompilerParams(vmem_limit_bytes=48 * MIB),
        name="project_back",
    )(dq, dkv, pre, normed, x, grad_hidden, gain, qkv_full, qkv_full, qkv_full, query_gain, key_gain, cosine, sine)


class KeyValues:
    def __init__(self, links, rows, held):
        self.links = links
        self.rows = rows
        self.held = held

    def slab(self, group, piece, member):
        members = self.links.sizes[2]
        start = pl.multiple_of(self.rows * (piece * members + member), self.rows)
        return self.held.at[:, 2 * group : 2 * group + 2, pl.ds(start, self.rows)]

    def mine(self):
        _, _, z, core = self.links.place()
        return lax.rem(z, self.links.sizes[2] // 2) * 2 + core

    def across(self, group):
        found = []
        for piece in range(2):
            slab = self.slab(group, piece, self.mine())
            for i, (_, target) in enumerate(self.links.group()):
                found.append(self.links.copy(("kv", group, piece, i), slab, slab, target))
        return found

    def near(self, group):
        found = []
        for piece in range(2):
            slab = self.slab(group, piece, self.mine())
            found.append(self.links.copy(("kv own", group, piece), slab, slab, self.links.sibling()))
        return found

    def forward(self, group):
        _, _, _, core = self.links.place()
        found = []
        for piece in range(2):
            for i, (chip, _) in enumerate(self.links.group(back=True)):
                slab = self.slab(group, piece, chip * 2 + core)
                found.append(
                    self.links.copy(("kv pass", group, piece, i), slab, slab, self.links.sibling())
                )
        return found

    @staticmethod
    def copies(sizes):
        return 4 * 2 * (2 * (sizes[2] // 2 - 1) + 1)


def run_all(copies, act):
    for copy in copies:
        if act == "start":
            copy.start()
        else:
            copy.wait()


def row_places(shape, dim, sub):
    t = lax.broadcasted_iota(jnp.int32, shape, dim)
    return (t // (2 * sub)) * sub + t % sub


def gather_parents(meta, lead, slot, pairs):
    runs = (TREE - TRUNK) // SEG
    for k in range(LOCAL_RUNS):
        parent = meta[jnp.minimum(lead + k, runs - 1)]
        for read, out in pairs:
            total = None
            for b in range(runs):
                share = (1 - jnp.minimum(jnp.abs(parent - b), 1)).astype(F32).astype(BF16)
                term = read(b) * share
                total = term if total is None else total + term
            out[slot + k] = total


def forward_kernel(sizes, rows, meta, cos_ref, sin_ref, tok_ref, cot_ref, *refs):
    arrays = PAIRS + 2 + FF_CHUNKS
    shard = refs[:arrays]
    (mixed_ref, l_ref, pre_ref, normed_ref, gains_ref, qk_ref,
     placed, cot_placed, q_all, kv_all, qkv_whole, gain_whole, out_whole, feed_whole) = refs[arrays : arrays + 14]
    whole = (
        tuple(qkv_whole.at[c] for c in range(PAIRS))
        + (out_whole,)
        + tuple(feed_whole.at[c] for c in range(FF_CHUNKS))
        + (gain_whole,)
    )
    (qs, kvs, xs, ws, gs, acc, part, places, kp, vp, send_sem, recv_sem, local_sem) = refs[arrays + 14 :]
    members = sizes[2]
    sub = rows // SUBS
    count = 2 * rows
    step = pl.program_id(0)
    head = jnp.maximum(step - PAIRS, 0)
    links = Links(sizes, send_sem, recv_sem)
    kv = KeyValues(links, rows, kvs)
    swaps = {
        "tokens": Exchange(links, tok_ref, placed, local_sem.at[0], "tokens"),
        "cot": Exchange(links, cot_ref, cot_placed, local_sem.at[1], "cot"),
    }
    weights_ = [
        [
            Gather(links, (a, b), shard[a], whole[a], ORDERS[b], cols, local_sem.at[12 + 2 * a + b])
            for b, cols in enumerate(halves_of(shard[a].shape[-1]))
        ]
        for a in range(arrays)
    ]
    _, _, z, core = links.place()
    mine = lax.rem(z, members // 2) * 2 + core

    def kept(group):
        pair = slice(2 * group, 2 * group + 2)
        return [
            pltpu.make_async_copy(kvs.at[:, pair], kv_all.at[:, pair], local_sem.at[2 + group]),
            pltpu.make_async_copy(qs.at[pair], q_all.at[pair], local_sem.at[6 + group]),
        ]

    def fetch(src, dst):
        ny, nx, nz = sizes
        shard_rows = src.shape[4]
        copies = []
        for i in range(ny * nx * nz * 2):
            block = src.at[i // (nx * nz * 2), i // (nz * 2) % nx, i // 2 % nz, i % 2]
            copies.append(
                pltpu.make_async_copy(block, dst.at[i * shard_rows : (i + 1) * shard_rows], local_sem.at[10])
            )
        run_all(copies, "start")
        pltpu.make_async_copy(dst, dst, local_sem.at[10]).wait()

    def act(steps):
        for what, a in steps:
            if what == "swap":
                swaps[a].start()
            elif what == "swapped":
                swaps[a].wait()
            elif what == "kv":
                run_all(kv.across(a), "start")
                run_all(kv.near(a), "start")
            elif what == "use":
                run_all(kv.across(a), "wait")
                run_all(kv.forward(a), "start")
            elif what == "got":
                run_all(kv.near(a), "wait")
                run_all(kv.forward(a), "wait")
                run_all(kept(a), "start")
            else:
                for g in weights_[a]:
                    if what == 0:
                        g.start()
                    elif what == 4:
                        g.close()
                    else:
                        g.step(what)

    @pl.when(step == 0)
    def _():
        links.meet()
        act(FORWARD_START)
        l_ref[...] = jnp.zeros_like(l_ref)
        places[...] = row_places(places.shape, 0, sub)
        fetch(gain_whole, gs)
        loaded = pltpu.make_async_copy(placed, xs, local_sem.at[11])
        loaded.start()
        gains_ref[...] = gs[:, :GAIN_COLS].astype(F32).T[:8]
        qk_ref[0:1] = jnp.sum(gs[:, GAIN_COLS : 2 * GAIN_COLS].astype(F32), axis=0, keepdims=True)
        qk_ref[1:2] = jnp.sum(gs[:, 2 * GAIN_COLS :].astype(F32), axis=0, keepdims=True)
        loaded.wait()
        values = xs[...].reshape(count, D).astype(F32)
        normed_ref[...] = (values * norm_factor(values) * gains_ref[0:1]).astype(BF16)

    for c in range(PAIRS):

        @pl.when(step == c)
        def _():
            act([(4, c)])
            fetch(qkv_whole.at[c], ws)

    @pl.when(step < PAIRS)
    def _():
        normed = normed_ref[...]
        cosine, sine = cos_ref[...], sin_ref[...]

        def turned(pre, gain):
            values = pre * norm_factor(pre) * gain
            return (values * cosine + roll_half(values) * sine).astype(BF16)

        for hh in range(2):
            at = 2 * step + hh
            query = matmul(normed, ws[:, 2 * hh * HEAD_DIM : 2 * (hh + 1) * HEAD_DIM])
            for h in range(2):
                pre = query[:, h * HEAD_DIM : (h + 1) * HEAD_DIM]
                pre_ref[hh, :, h * HEAD_DIM : (h + 1) * HEAD_DIM] = pre
                low = turned(pre, qk_ref[0:1])
                for s in range(2 * SUBS):
                    qs[at, (2 * s + h) * sub : (2 * s + h + 1) * sub] = low[s * sub : (s + 1) * sub]
            pre = matmul(normed, ws[:, (4 + hh) * HEAD_DIM : (5 + hh) * HEAD_DIM])
            pre_ref[hh, :, 2 * HEAD_DIM :] = pre
            low = turned(pre, qk_ref[1:2])
            value = matmul(normed, ws[:, (6 + hh) * HEAD_DIM : (7 + hh) * HEAD_DIM]).astype(BF16)
            for piece in range(2):
                start = pl.multiple_of(rows * (piece * members + mine), rows)
                kvs[0, at, pl.ds(start, rows)] = low[piece * rows : (piece + 1) * rows]
                kvs[1, at, pl.ds(start, rows)] = value[piece * rows : (piece + 1) * rows]

    def attend():
        lane = lax.broadcasted_iota(jnp.int32, (2 * rows, HEAD_DIM), 1)
        for piece in range(2):
            base = rows * (piece * members + mine)
            region = slice(piece * 2 * rows, (piece + 1) * 2 * rows)
            acc[...] = jnp.zeros_like(acc)
            part[...] = jnp.zeros_like(part)

            def trunk(step, masked):
                start = pl.multiple_of(step * CHUNK, CHUNK)
                weights = jnp.exp2(nt(qs[head, region], kvs[0, head, pl.ds(start, CHUNK)]) * exp2_scale)
                low, high = weights[:, :HEAD_DIM], weights[:, HEAD_DIM:]
                if masked:
                    room = places[...] + (base - start)
                    low = jnp.where(lane <= room, low, 0.0)
                    high = jnp.where(lane + HEAD_DIM <= room, high, 0.0)
                    weights = jnp.concatenate([low, high], axis=1)
                part[...] += low + high
                acc[...] += matmul(weights.astype(BF16), kvs[1, head, pl.ds(start, CHUNK)])
                return masked

            if piece == 0:
                clear = jnp.minimum(base // CHUNK, TRUNK // CHUNK)
                last = jnp.minimum((base + rows + CHUNK - 1) // CHUNK, TRUNK // CHUNK)
                lax.fori_loop(0, clear, lambda i, c: (trunk(i, False), c)[1], 0)
                lax.fori_loop(clear, last, lambda i, c: (trunk(i, True), c)[1], 0)
            else:
                lax.fori_loop(0, TRUNK // CHUNK, lambda i, c: (trunk(i, False), c)[1], 0)

            lead = jnp.maximum(base - TRUNK, 0) // SEG

            def parents_():
                gather_parents(
                    meta,
                    lead,
                    0,
                    [
                        (lambda b: kvs[0, head, TRUNK + b * SEG : TRUNK + (b + 1) * SEG], kp),
                        (lambda b: kvs[1, head, TRUNK + b * SEG : TRUNK + (b + 1) * SEG], vp),
                    ],
                )

            if piece == 0:
                pl.when(base + rows > TRUNK)(parents_)
            else:
                parents_()
            for s in range(SUBS):
                block = slice(2 * sub * s, 2 * sub * (s + 1))

                def runs():
                    row = base + s * sub - TRUNK
                    run = row // SEG
                    own = pl.multiple_of(TRUNK + run * SEG, SEG)
                    flag = jnp.minimum(meta[run] + 1, 1).astype(F32)
                    query = qs[head, piece * 2 * rows + 2 * sub * s : piece * 2 * rows + 2 * sub * (s + 1)]
                    room = places[block] + (lax.rem(row, SEG) - s * sub)
                    weights = jnp.exp2(nt(query, kvs[0, head, pl.ds(own, SEG)]) * exp2_scale)
                    weights = jnp.where(lane[block] <= room, weights, 0.0)
                    above = jnp.exp2(nt(query, kp[run - lead]) * exp2_scale) * flag
                    part[block] += weights + above
                    acc[block] += matmul(weights.astype(BF16), kvs[1, head, pl.ds(own, SEG)]) + matmul(
                        above.astype(BF16), vp[run - lead]
                    )

                if piece == 0:
                    pl.when(base + s * sub >= TRUNK)(runs)
                else:
                    runs()

            total = jnp.sum(part[...], axis=-1, keepdims=True)
            mixed = (acc[...] / total).astype(BF16)
            for s in range(SUBS):
                for h in range(2):
                    row = piece * rows + sub * s
                    mixed_ref[row : row + sub, h * HEAD_DIM : (h + 1) * HEAD_DIM] = mixed[
                        (2 * s + h) * sub : (2 * s + h + 1) * sub
                    ]
            l_ref[region] = jnp.where(lane == head, total, l_ref[region])


    pl.when(step >= PAIRS)(attend)
    for moment, steps in FORWARD_AFTER.items():
        pl.when(step == moment)(functools.partial(act, steps))

    @pl.when(step == PAIRS + KV_HEADS - 1)
    def _():
        for array in weights_[PAIRS : PAIRS + 1 + FF_CHUNKS]:
            for g in array:
                g.close()
        for group in range(4):
            run_all(kept(group), "wait")


def forward(sizes, meta, cosine, sine, tokens, cotangent, shards_):
    ny, nx, nz = sizes
    rows = tokens.shape[1]
    count = 2 * rows
    arrays = PAIRS + 2 + FF_CHUNKS
    shard_rows = shards_[0].shape[0]
    blocks = (ny, nx, nz, 2, shard_rows)
    widths = [w.shape[-1] for w in shards_]
    rounds = KeyValues.copies(sizes) + 2 * arrays * Gather.copies(sizes) + 2

    def at_head(s):
        return jnp.maximum(s - PAIRS, 0)

    results = pl.pallas_call(
        functools.partial(forward_kernel, sizes, rows),
        out_shape=[
            jax.ShapeDtypeStruct((count, QD), BF16),
            jax.ShapeDtypeStruct((2 * count, HEAD_DIM), F32),
            jax.ShapeDtypeStruct((KV_HEADS, count, 3 * HEAD_DIM), F32),
            jax.ShapeDtypeStruct((count, D), BF16),
            jax.ShapeDtypeStruct((8, D), F32),
            jax.ShapeDtypeStruct((8, HEAD_DIM), F32),
            jax.ShapeDtypeStruct(tokens.shape, BF16),
            jax.ShapeDtypeStruct(tokens.shape, BF16),
            jax.ShapeDtypeStruct((KV_HEADS, 2 * count, HEAD_DIM), BF16),
            jax.ShapeDtypeStruct((2, KV_HEADS, TREE, HEAD_DIM), BF16),
            jax.ShapeDtypeStruct((PAIRS,) + blocks + (widths[0],), BF16),
            jax.ShapeDtypeStruct(blocks + (widths[-1],), BF16),
            jax.ShapeDtypeStruct(blocks + (widths[PAIRS],), BF16),
            jax.ShapeDtypeStruct((FF_CHUNKS,) + blocks + (widths[PAIRS + 1],), BF16),
        ],
        grid_spec=pltpu.PrefetchScalarGridSpec(
            num_scalar_prefetch=1,
            grid=(PAIRS + KV_HEADS,),
            in_specs=[pl.BlockSpec((count, HEAD_DIM), lambda s, meta: (0, 0))] * 2 + [ANY] * (2 + arrays),
            out_specs=[
                pl.BlockSpec((count, 2 * HEAD_DIM), lambda s, meta: (0, at_head(s))),
                pl.BlockSpec((2 * count, HEAD_DIM), lambda s, meta: (0, 0)),
                pl.BlockSpec((2, count, 3 * HEAD_DIM), lambda s, meta: (jnp.minimum(s, PAIRS - 1), 0, 0)),
                pl.BlockSpec((count, D), lambda s, meta: (0, 0)),
                pl.BlockSpec((8, D), lambda s, meta: (0, 0)),
                pl.BlockSpec((8, HEAD_DIM), lambda s, meta: (0, 0)),
            ]
            + [ANY] * 8,
            scratch_shapes=[
                pltpu.VMEM((KV_HEADS, 2 * count, HEAD_DIM), BF16),
                pltpu.VMEM((2, KV_HEADS, TREE, HEAD_DIM), BF16),
                pltpu.VMEM(tokens.shape, BF16),
                pltpu.VMEM((D, widths[0]), BF16),
                pltpu.VMEM((D, widths[-1]), BF16),
                pltpu.VMEM((count, HEAD_DIM), F32),
                pltpu.VMEM((count, HEAD_DIM), F32),
                pltpu.VMEM((count, HEAD_DIM), jnp.int32),
                pltpu.VMEM((LOCAL_RUNS, SEG, HEAD_DIM), BF16),
                pltpu.VMEM((LOCAL_RUNS, SEG, HEAD_DIM), BF16),
                pltpu.SemaphoreType.DMA((rounds,)),
                pltpu.SemaphoreType.DMA((rounds,)),
                pltpu.SemaphoreType.DMA((12 + 2 * arrays,)),
            ],
        ),
        compiler_params=pltpu.CompilerParams(
            collective_id=2, has_side_effects=True, vmem_limit_bytes=56 * MIB
        ),
        name="forward",
    )(meta, cosine, sine, tokens, cotangent, *shards_)
    return results


def feed_kernel(
    sizes, rows, x_ref, mixed_ref, cot_ref, out_ref, gain_ref, w_ref,
    result_ref, hid_ref, stack_ref, delta_ref, post_ref, dout_ref, late_ref, early_ref, *refs,
):
    hidden, second, second_t, cot_t, total, grads, inner, gate_up, low, stack, part = refs[:11]
    buffers = refs[11:-3]
    send_sem, recv_sem, local_sem = refs[-3:]
    ny, nx, nz = sizes
    count = 2 * rows
    sub = rows // SUBS
    shard_rows = part.shape[5]
    width = 3 * FF_CHUNK
    tile = 256
    chunk = pl.program_id(0)
    links = Links(sizes, send_sem, recv_sem)
    _, _, _, core = links.place()
    scatters = []
    for c in range(FF_EARLY):
        for b, cols in enumerate(halves_of(width)):
            k = 4 * len(scatters)
            scatters.append(
                Scatter(
                    links,
                    (c, b),
                    part.at[c % 2],
                    ORDERS[b],
                    cols,
                    *buffers[k : k + 4],
                    part.at[c % 2, :, :, :, core, :, cols],
                    None,
                    early_ref.at[c],
                )
            )

    def act(steps):
        for what, c in steps:
            for s in scatters[2 * c : 2 * c + 2]:
                if what == "core":
                    s.start()
                elif what == "begin":
                    s.begin()
                elif what == "finish":
                    s.finish()
                else:
                    s.middle(what)

    def rows_of(block):
        return (block // (2 * nz * nx), lax.rem(block // (2 * nz), nx), lax.rem(block // 2, nz), lax.rem(block, 2))

    def put(slot, first, cols, value):
        for k in range(value.shape[0] // shard_rows):
            y, x, z, c = rows_of(first // shard_rows + k)
            part[slot, y, x, z, c, :, cols] = value[k * shard_rows : (k + 1) * shard_rows].astype(BF16)

    def late(c):
        return pltpu.make_async_copy(part.at[c % 2], late_ref.at[c - FF_EARLY], local_sem.at[c % 2])

    @pl.when(chunk == 0)
    def _():
        links.meet()

        def project_out(t, carry):
            at = pl.multiple_of(t * tile, tile)
            hidden[:, pl.ds(at, tile)] = x_ref[:, pl.ds(at, tile)].astype(F32) + nt(
                mixed_ref[...], out_ref[pl.ds(at, tile), :]
            )
            return carry

        lax.fori_loop(0, D // tile, project_out, 0)
        values = hidden[...]
        values = values * norm_factor(values) * gain_ref[...]
        second[...] = values.astype(BF16)
        second_t[...] = values.T.astype(BF16)
        cot_t[...] = cot_ref[...].astype(F32).T.astype(BF16)
        total[...] = jnp.zeros_like(total)
        grads[...] = jnp.zeros_like(grads)

    slot = lax.rem(chunk, 2)

    def columns(t, carry):
        at = pl.multiple_of(t * tile, tile)
        gate = matmul(second[...], w_ref[0, :, pl.ds(at, tile)])
        up = matmul(second[...], w_ref[0, :, pl.ds(FF_CHUNK + at, tile)])
        grad = matmul(cot_ref[...], w_ref[0, :, pl.ds(2 * FF_CHUNK + at, tile)])
        sigmoid = 1.0 / (1.0 + jnp.exp(-gate))
        active = gate * sigmoid
        inner[:, pl.ds(at, tile)] = (active * up).astype(BF16)
        gate_up[:, pl.ds(at, tile)] = (grad * up * sigmoid * (1.0 + gate * (1.0 - sigmoid))).astype(BF16)
        gate_up[:, pl.ds(FF_CHUNK + at, tile)] = (grad * active).astype(BF16)
        return carry

    lax.fori_loop(0, FF_CHUNK // tile, columns, 0)
    for moment, steps in FEED_MIDDLE.items():
        pl.when(chunk == moment)(functools.partial(act, steps))
    for c in range(FF_EARLY, FF_CHUNKS - 2):
        pl.when(chunk == c + 2)(lambda: late(c).wait())

    def model(t, carry):
        at = pl.multiple_of(t * tile, tile)
        total[:, pl.ds(at, tile)] += nt(inner[...], w_ref[0, pl.ds(at, tile), 2 * FF_CHUNK :])
        grads[:, pl.ds(at, tile)] += nt(gate_up[...], w_ref[0, pl.ds(at, tile), : 2 * FF_CHUNK])
        put(slot, at, slice(0, 2 * FF_CHUNK), matmul(second_t[pl.ds(at, tile)], gate_up[...]))
        put(slot, at, slice(2 * FF_CHUNK, width), matmul(cot_t[pl.ds(at, tile)], inner[...]))
        return carry

    lax.fori_loop(0, D // tile, model, 0)
    for c in range(FF_EARLY, FF_CHUNKS):
        pl.when(chunk == c)(lambda: late(c).start())
    for moment, steps in FEED_AFTER.items():
        pl.when(chunk == moment)(functools.partial(act, steps))

    @pl.when(chunk == FF_CHUNKS - 1)
    def _():
        values = hidden[...]
        low[...] = (values + total[...]).astype(BF16)
        output = pltpu.make_async_copy(low, result_ref, local_sem.at[2])
        output.start()
        factor = norm_factor(values)
        grad_in, share = norm_backward(grads[...], gain_ref[...], values * factor, factor)
        post_ref[...] = jnp.sum(share, axis=0, keepdims=True)
        hidden[...] = cot_ref[...].astype(F32) + grad_in
        saved = pltpu.make_async_copy(hidden, hid_ref, local_sem.at[3])
        saved.start()
        second[...] = hidden[...].astype(BF16)
        second_t[...] = hidden[...].T.astype(BF16)
        lane = lax.broadcasted_iota(jnp.int32, (count, HEAD_DIM), 1)
        dots = jnp.zeros((count, HEAD_DIM), F32)
        for h in range(KV_HEADS):
            cols = slice(2 * h * HEAD_DIM, 2 * (h + 1) * HEAD_DIM)
            grad = matmul(second[...], out_ref[:, cols]).astype(BF16)
            for g in range(2):
                one = grad[:, g * HEAD_DIM : (g + 1) * HEAD_DIM]
                for s in range(2 * SUBS):
                    stack[h, (2 * s + g) * sub : (2 * s + g + 1) * sub] = one[s * sub : (s + 1) * sub]
                head = 2 * h + g
                product = one.astype(F32) * mixed_ref[:, head * HEAD_DIM : (head + 1) * HEAD_DIM].astype(F32)
                dots = jnp.where(lane == head, jnp.sum(product, axis=-1, keepdims=True), dots)
        delta_ref[...] = dots.T
        stacked_ = pltpu.make_async_copy(stack, stack_ref, local_sem.at[4])
        stacked_.start()
        act(FEED_LAST)
        for c in range(FF_CHUNKS - 2, FF_CHUNKS):
            late(c).wait()

        def model_out(t, carry):
            at = pl.multiple_of(t * tile, tile)
            for a in range(0, QD, 2 * FF_CHUNK):
                cols = slice(a, a + 2 * FF_CHUNK)
                value = matmul(second_t[pl.ds(at, tile)], mixed_ref[:, cols])
                slot = a // (2 * FF_CHUNK)
                put(slot, at, slice(0, 2 * FF_CHUNK), value)
            return carry

        lax.fori_loop(0, D // tile, model_out, 0)
        gone = [
            pltpu.make_async_copy(
                part.at[k, :, :, :, :, :, : 2 * FF_CHUNK],
                dout_ref.at[:, :, :, :, :, 2 * FF_CHUNK * k : 2 * FF_CHUNK * (k + 1)],
                local_sem.at[k],
            )
            for k in range(2)
        ]
        run_all(gone, "start")
        for c in range(FF_EARLY):
            act([("finish", c)])
        run_all(gone + [output, saved, stacked_], "wait")


def feed(sizes, x, mixed, cot, out_t, gain, feed_whole):
    ny, nx, nz = sizes
    count = x.shape[0]
    rows = count // 2
    shard_rows = D // (ny * nx * nz * 2)
    width = 3 * FF_CHUNK
    buffers = []
    for c in range(FF_EARLY):
        for b, cols in enumerate(halves_of(width)):
            buffers += Scatter.scratch(sizes, ORDERS[b], shard_rows, cols.stop - cols.start)
    rounds = 2 * FF_EARLY * Scatter.copies(sizes)

    def whole_block(shape):
        return pl.BlockSpec(shape, lambda c: (0,) * len(shape), pipeline_mode=pl.Buffered(1))

    blocks = (ny, nx, nz, 2, shard_rows)
    return pl.pallas_call(
        functools.partial(feed_kernel, sizes, rows),
        grid=(FF_CHUNKS,),
        out_shape=[
            jax.ShapeDtypeStruct((count, D), BF16),
            jax.ShapeDtypeStruct((count, D), F32),
            jax.ShapeDtypeStruct((KV_HEADS, 2 * count, HEAD_DIM), BF16),
            jax.ShapeDtypeStruct((HEAD_DIM, count), F32),
            jax.ShapeDtypeStruct((1, D), F32),
            jax.ShapeDtypeStruct(blocks + (QD,), BF16),
            jax.ShapeDtypeStruct((FF_CHUNKS - FF_EARLY,) + blocks + (width,), BF16),
            jax.ShapeDtypeStruct((FF_EARLY, shard_rows, width), F32),
        ],
        in_specs=[
            whole_block((count, D)),
            whole_block((count, QD)),
            whole_block((count, D)),
            whole_block((D, QD)),
            whole_block((1, D)),
            pl.BlockSpec((1, D, width), lambda c: (c, 0, 0)),
        ],
        out_specs=[
            ANY,
            ANY,
            ANY,
            pl.BlockSpec((HEAD_DIM, count), lambda c: (0, 0)),
            pl.BlockSpec((1, D), lambda c: (0, 0)),
            ANY,
            ANY,
            pl.BlockSpec((FF_EARLY, shard_rows, width), lambda c: (0, 0, 0)),
        ],
        scratch_shapes=[
            pltpu.VMEM((count, D), F32),
            pltpu.VMEM((count, D), BF16),
            pltpu.VMEM((D, count), BF16),
            pltpu.VMEM((D, count), BF16),
            pltpu.VMEM((count, D), F32),
            pltpu.VMEM((count, D), F32),
            pltpu.VMEM((count, FF_CHUNK), BF16),
            pltpu.VMEM((count, 2 * FF_CHUNK), BF16),
            pltpu.VMEM((count, D), BF16),
            pltpu.VMEM((KV_HEADS, 2 * count, HEAD_DIM), BF16),
            pltpu.VMEM((2,) + blocks + (width,), BF16),
        ]
        + buffers
        + [
            pltpu.SemaphoreType.DMA((rounds,)),
            pltpu.SemaphoreType.DMA((rounds,)),
            pltpu.SemaphoreType.DMA((5,)),
        ],
        compiler_params=pltpu.CompilerParams(
            collective_id=5, has_side_effects=True, vmem_limit_bytes=61 * MIB
        ),
        name="feed",
    )(x, mixed, cot, out_t, gain, feed_whole)


def backward_kernel(sizes, rows, widths, meta, q_ref, g_ref, k_ref, v_ref, lse_ref, del_ref, late_ref, dout_ref, done_ref, *refs):
    dq_ref, dkv_ref, late_out, dout_out, done_placed = refs[:5]
    dq, dk, dv, pk, pv, kp, vp, stage, near, sums, far, last = refs[5:17]
    buffers = refs[17:-3]
    send_sem, recv_sem, local_sem = refs[-3:]
    members = sizes[2]
    chips = members // 2
    sub = rows // SUBS
    head = pl.program_id(0)
    links = Links(sizes, send_sem, recv_sem)
    scatters = []
    late = FF_CHUNKS - FF_EARLY
    for a, width in enumerate(widths):
        for b, cols in enumerate(halves_of(width)):
            k = 5 * len(scatters)
            scatters.append(
                Scatter(
                    links,
                    (a, b),
                    late_ref.at[a] if a < late else dout_ref,
                    ORDERS[b],
                    cols,
                    *buffers[k : k + 5],
                    local_sem.at[2 + len(scatters)],
                    late_out.at[a] if a < late else dout_out,
                )
            )

    swap = Exchange(links, done_ref, done_placed, local_sem.at[2 + len(scatters)])

    def each(array):
        return scatters[2 * array : 2 * array + 2]

    @pl.when(head == 0)
    def _():
        for s in scatters:
            s.load().start()
        links.meet()
        for s in scatters:
            s.start()
        swap.start()

    _, _, z, core = links.place()
    here = lax.rem(z, chips)
    mine = here * 2 + core
    dk[...] = jnp.zeros_like(dk)
    dv[...] = jnp.zeros_like(dv)
    pk[...] = jnp.zeros_like(pk)
    pv[...] = jnp.zeros_like(pv)
    for piece in range(2):
        base = rows * (piece * members + mine)
        at = piece * 2 * rows
        region = slice(at, at + 2 * rows)
        dq[...] = jnp.zeros_like(dq)

        def pair(key, value, block, mask):
            spot = slice(at + block.start, at + block.stop)
            weights = jnp.exp2(nt(key, q_ref[0, spot]) * exp2_scale - lse_ref[0, :, spot])
            if mask is not None:
                weights = mask(weights)
            grads = (weights * (nt(value, g_ref[0, spot]) - del_ref[0, :, spot])).astype(BF16)
            weights = weights.astype(BF16)
            dq[block] += contract_rows(grads, key)
            return matmul(grads, q_ref[0, spot]), matmul(weights, g_ref[0, spot])

        everything = slice(0, 2 * rows)

        def trunk(step, masked):
            start = pl.multiple_of(step * CHUNK, CHUNK)

            def mask(weights):
                shape = weights.shape
                room = row_places((1, shape[1]), 1, sub) + (base - start)
                return jnp.where(lax.broadcasted_iota(jnp.int32, shape, 0) <= room, weights, 0.0)

            key_grad, value_grad = pair(
                k_ref[0, 0, pl.ds(start, CHUNK)],
                v_ref[0, 0, pl.ds(start, CHUNK)],
                everything,
                mask if masked else None,
            )
            dk[pl.ds(start, CHUNK)] += key_grad
            dv[pl.ds(start, CHUNK)] += value_grad

        if piece == 0:
            clear = jnp.minimum(base // CHUNK, TRUNK // CHUNK)
            end = jnp.minimum((base + rows + CHUNK - 1) // CHUNK, TRUNK // CHUNK)
            lax.fori_loop(0, clear, lambda i, c: (trunk(i, False), c)[1], 0)
            lax.fori_loop(clear, end, lambda i, c: (trunk(i, True), c)[1], 0)
        else:
            lax.fori_loop(0, TRUNK // CHUNK, lambda i, c: (trunk(i, False), c)[1], 0)

        lead = jnp.maximum(base - TRUNK, 0) // SEG

        def parents_():
            gather_parents(
                meta,
                lead,
                0,
                [
                    (lambda b: k_ref[0, 0, TRUNK + b * SEG : TRUNK + (b + 1) * SEG], kp),
                    (lambda b: v_ref[0, 0, TRUNK + b * SEG : TRUNK + (b + 1) * SEG], vp),
                ],
            )

        if piece == 0:
            pl.when(base + rows > TRUNK)(parents_)
        else:
            parents_()
        for s in range(SUBS):
            block = slice(2 * sub * s, 2 * sub * (s + 1))

            def runs():
                row = base + s * sub - TRUNK
                run = row // SEG
                own = pl.multiple_of(TRUNK + run * SEG, SEG)
                flag = jnp.minimum(meta[run] + 1, 1).astype(F32)

                def mask(weights):
                    shape = (SEG, 2 * sub)
                    room = lax.broadcasted_iota(jnp.int32, shape, 1) % sub + lax.rem(row, SEG)
                    seen = lax.broadcasted_iota(jnp.int32, shape, 0) <= room
                    return jnp.concatenate(
                        [jnp.where(seen, weights[:SEG], 0.0), weights[SEG:] * flag], axis=0
                    )

                key_grad, value_grad = pair(
                    jnp.concatenate([k_ref[0, 0, pl.ds(own, SEG)], kp[run - lead]], axis=0),
                    jnp.concatenate([v_ref[0, 0, pl.ds(own, SEG)], vp[run - lead]], axis=0),
                    block,
                    mask,
                )
                dk[pl.ds(own, SEG)] += key_grad[:SEG]
                dv[pl.ds(own, SEG)] += value_grad[:SEG]
                slot = LOCAL_RUNS * piece + run - lead
                pk[slot] += key_grad[SEG:]
                pv[slot] += value_grad[SEG:]

            if piece == 0:
                pl.when(base + s * sub >= TRUNK)(runs)
            else:
                runs()

        dq_ref[0, region] = dq[...] * score_scale

        def spread():
            parents = [meta[jnp.minimum(lead + k, TREE // SEG - TRUNK // SEG - 1)] for k in range(LOCAL_RUNS)]

            def place(b, carry):
                start = pl.multiple_of(TRUNK + b * SEG, SEG)
                key_grad, value_grad = dk[pl.ds(start, SEG)], dv[pl.ds(start, SEG)]
                for k in range(LOCAL_RUNS):
                    share = (1 - jnp.minimum(jnp.abs(parents[k] - b), 1)).astype(F32)
                    key_grad += pk[LOCAL_RUNS * piece + k] * share
                    value_grad += pv[LOCAL_RUNS * piece + k] * share
                dk[pl.ds(start, SEG)] = key_grad
                dv[pl.ds(start, SEG)] = value_grad
                return carry

            lax.fori_loop(0, (TREE - TRUNK) // SEG, place, 0)

        if piece == 0:
            pl.when(base + rows > TRUNK)(spread)
        else:
            spread()

    def core_copy(h):
        return links.copy(("kv core", h), stage.at[h % 2, :, 1 - core], near.at[h % 2], links.sibling())

    def far_copies(h):
        return [
            links.copy(("kv z", h, i), sums.at[h, chip], far.at[h, i], target)
            for i, (chip, target) in enumerate(links.group())
        ]

    def pass_on(h):
        core_copy(h).wait()

        def add(i, carry):
            chip, which, piece = i // 4, lax.rem(i // 2, 2), lax.rem(i, 2)
            sums[h, chip, which, piece] = (
                stage[h % 2, chip, core, which, piece].astype(F32) + near[h % 2, chip, which, piece].astype(F32)
            ).astype(BF16)
            return carry

        lax.fori_loop(0, chips * 4, add, 0)
        run_all(far_copies(h), "start")

    for h in range(1, KV_HEADS):
        pl.when(head == h)(functools.partial(pass_on, h - 1))

    for which, grad, scale in ((0, dk, score_scale), (1, dv, 1.0)):
        for piece in range(2):
            for member in range(members):
                start = rows * (piece * members + member)
                stage[lax.rem(head, 2), member // 2, member % 2, which, piece] = (
                    grad[start : start + rows] * scale
                ).astype(BF16)
    for h in range(KV_HEADS):

        @pl.when(head == h)
        def _():
            core_copy(h).start()

    for moment, steps in BACKWARD_AFTER.items():

        @pl.when(head == moment)
        def _():
            for step, array in steps:
                for s in each(array):
                    if step == 0:
                        s.begin()
                    else:
                        s.middle(step - 1)

    def result(h):
        return pltpu.make_async_copy(last.at[h % 2], dkv_ref.at[:, h], local_sem.at[h % 2])

    @pl.when(head == KV_HEADS - 1)
    def _():
        pass_on(KV_HEADS - 1)
        for s in scatters:
            s.finish()
        for h in range(KV_HEADS):
            run_all(far_copies(h), "wait")
            if h > 1:
                result(h - 2).wait()
            for which in range(2):
                for piece in range(2):
                    total = sums[h, here, which, piece].astype(F32)
                    for i in range(chips - 1):
                        total = total + far[h, i, which, piece].astype(F32)
                    last[h % 2, which, piece] = total
            result(h).start()
        for h in (KV_HEADS - 2, KV_HEADS - 1):
            result(h).wait()
        swap.wait()


def backward(sizes, meta, queries, grads, kv_all, log_total, delta, late, dout, done):
    ny, nx, nz = sizes
    chips = nz // 2
    rows = queries.shape[1] // 4
    widths = (late.shape[-1],) * late.shape[0] + (dout.shape[-1],)
    shard_rows = dout.shape[4]
    stack = pl.BlockSpec((1, 4 * rows, HEAD_DIM), lambda h, meta: (h, 0, 0))
    line = pl.BlockSpec((1, 1, 4 * rows), lambda h, meta: (h, 0, 0))
    buffers, count = [], 0
    for w in widths:
        for b, cols in enumerate(halves_of(w)):
            buffers += Scatter.scratch(sizes, ORDERS[b], shard_rows, cols.stop - cols.start)
            buffers.append(pltpu.VMEM((ny, nx, nz, shard_rows, cols.stop - cols.start), BF16))
            count += 1
    rounds = count * Scatter.copies(sizes) + KV_HEADS * chips + 1
    late_shape = (late.shape[0], shard_rows, late.shape[-1])
    dout_shape = (shard_rows, dout.shape[-1])
    return pl.pallas_call(
        functools.partial(backward_kernel, sizes, rows, widths),
        out_shape=[
            jax.ShapeDtypeStruct((KV_HEADS, 4 * rows, HEAD_DIM), F32),
            jax.ShapeDtypeStruct((2, KV_HEADS, 2, rows, HEAD_DIM), F32),
            jax.ShapeDtypeStruct(late_shape, F32),
            jax.ShapeDtypeStruct(dout_shape, F32),
            jax.ShapeDtypeStruct(done.shape, BF16),
        ],
        grid_spec=pltpu.PrefetchScalarGridSpec(
            num_scalar_prefetch=1,
            grid=(KV_HEADS,),
            in_specs=[
                stack,
                stack,
                pl.BlockSpec((1, 1, TREE, HEAD_DIM), lambda h, meta: (0, h, 0, 0)),
                pl.BlockSpec((1, 1, TREE, HEAD_DIM), lambda h, meta: (1, h, 0, 0)),
                line,
                line,
                ANY,
                ANY,
                ANY,
            ],
            out_specs=[
                stack,
                ANY,
                pl.BlockSpec(late_shape, lambda h, meta: (0, 0, 0)),
                pl.BlockSpec(dout_shape, lambda h, meta: (0, 0)),
                ANY,
            ],
            scratch_shapes=[
                pltpu.VMEM((2 * rows, HEAD_DIM), F32),
                pltpu.VMEM((TREE, HEAD_DIM), F32),
                pltpu.VMEM((TREE, HEAD_DIM), F32),
                pltpu.VMEM((2 * LOCAL_RUNS, SEG, HEAD_DIM), F32),
                pltpu.VMEM((2 * LOCAL_RUNS, SEG, HEAD_DIM), F32),
                pltpu.VMEM((LOCAL_RUNS, SEG, HEAD_DIM), BF16),
                pltpu.VMEM((LOCAL_RUNS, SEG, HEAD_DIM), BF16),
                pltpu.VMEM((2, chips, 2, 2, 2, rows, HEAD_DIM), BF16),
                pltpu.VMEM((2, chips, 2, 2, rows, HEAD_DIM), BF16),
                pltpu.VMEM((KV_HEADS, chips, 2, 2, rows, HEAD_DIM), BF16),
                pltpu.VMEM((KV_HEADS, chips - 1, 2, 2, rows, HEAD_DIM), BF16),
                pltpu.VMEM((2, 2, 2, rows, HEAD_DIM), F32),
            ]
            + buffers
            + [
                pltpu.SemaphoreType.DMA((rounds,)),
                pltpu.SemaphoreType.DMA((rounds,)),
                pltpu.SemaphoreType.DMA((3 + count,)),
            ],
        ),
        compiler_params=pltpu.CompilerParams(
            collective_id=3, has_side_effects=True, vmem_limit_bytes=60 * MIB
        ),
        name="backward",
    )(
        meta,
        queries,
        grads,
        kv_all,
        kv_all,
        log_total.reshape(KV_HEADS, 1, 4 * rows),
        delta.reshape(KV_HEADS, 1, 4 * rows),
        late,
        dout,
        done,
    )


def scatter_kernel(sizes, widths, *refs):
    count = len(widths)
    parts = refs[:count]
    moved_ref = refs[count]
    outs = refs[count + 1 : 2 * count + 1]
    placed_ref = refs[2 * count + 1]
    rest = refs[2 * count + 2 :]
    send_sem, recv_sem, local_sem = rest[-3:]
    links = Links(sizes, send_sem, recv_sem)
    scatters = []
    used = 0
    for a in range(count):
        for b, cols in enumerate(halves_of(widths[a])):
            k = 5 * used
            scatters.append(
                Scatter(
                    links,
                    (a, b),
                    parts[a],
                    ORDERS[b],
                    cols,
                    *rest[k : k + 4],
                    rest[k + 4],
                    local_sem.at[used],
                    outs[a],
                )
            )
            used += 1
    for s in scatters:
        s.load().start()
    links.meet()
    for s in scatters:
        s.start()
    _, _, z, _ = links.place()
    half = z // (sizes[2] // 2)
    keep = pltpu.make_async_copy(moved_ref.at[half], placed_ref.at[half], local_sem.at[used])
    give = links.copy("moved", moved_ref.at[1 - half], placed_ref.at[half], links.across())
    keep.start()
    give.start()
    depth = 2
    for i, s in enumerate(scatters):
        if i >= depth:
            scatters[i - depth].middle(0)
        s.begin()
    for s in scatters[-depth:]:
        s.middle(0)
    for s in scatters:
        s.middle(1)
    for s in scatters:
        s.finish()
    keep.wait()
    give.wait()


def scatter_end(sizes, parts, moved):
    ny, nx, nz = sizes
    shard_rows = D // (ny * nx * nz * 2)
    widths = tuple(p.shape[-1] for p in parts)
    pieces = [p.reshape(ny, nx, nz, 2, shard_rows, p.shape[-1]) for p in parts]
    buffers, count = [], 0
    for w in widths:
        for b, cols in enumerate(halves_of(w)):
            buffers += Scatter.scratch(sizes, ORDERS[b], shard_rows, cols.stop - cols.start)
            buffers.append(pltpu.VMEM((ny, nx, nz, shard_rows, cols.stop - cols.start), BF16))
            count += 1
    rounds = count * Scatter.copies(sizes) + 1
    results = pl.pallas_call(
        functools.partial(scatter_kernel, sizes, widths),
        out_shape=[jax.ShapeDtypeStruct((shard_rows, w), F32) for w in widths]
        + [jax.ShapeDtypeStruct(moved.shape, BF16)],
        in_specs=[ANY] * (len(widths) + 1),
        out_specs=[pl.BlockSpec(memory_space=pltpu.VMEM)] * len(widths) + [ANY],
        scratch_shapes=buffers
        + [
            pltpu.SemaphoreType.DMA((rounds,)),
            pltpu.SemaphoreType.DMA((rounds,)),
            pltpu.SemaphoreType.DMA((count + 1,)),
        ],
        compiler_params=pltpu.CompilerParams(
            collective_id=4, has_side_effects=True, vmem_limit_bytes=48 * MIB
        ),
        name="scatter_end",
    )(*pieces, moved)
    return results[:-1], results[-1]


def shards(
    sizes,
    tokens,
    cotangent,
    segment_ids,
    positions,
    parents,
    input_norm,
    query_proj,
    key_proj,
    value_proj,
    query_norm,
    key_norm,
    out_proj,
    post_norm,
    gate_proj,
    up_proj,
    down_proj,
):
    nz = sizes[2]
    rows = tokens.shape[1]
    shard_rows = query_proj.shape[0]
    gain_rows = query_norm.shape[0]
    ctx = lax.axis_index("ctx")
    half = ctx // nz
    member = ctx % nz
    count = 2 * rows
    sub = rows // SUBS

    device = lax.axis_index("dp") * 2 * nz + ctx

    def spread(gain):
        line = jnp.zeros((1, HEAD_DIM), BF16)
        line = lax.dynamic_update_slice(line, gain[None, :], (0, device * gain_rows))
        return jnp.pad(line, ((0, shard_rows - 1), (0, 0)))

    gains = jnp.pad(
        jnp.stack([input_norm, post_norm], axis=1), ((0, 0), (0, GAIN_COLS - 2))
    )
    gains = jnp.concatenate([gains, spread(query_norm), spread(key_norm)], axis=1)
    qkv_shards = [
        jnp.concatenate(
            [
                query_proj[:, 4 * HEAD_DIM * c : 4 * HEAD_DIM * (c + 1)],
                key_proj[:, 2 * HEAD_DIM * c : 2 * HEAD_DIM * (c + 1)],
                value_proj[:, 2 * HEAD_DIM * c : 2 * HEAD_DIM * (c + 1)],
            ],
            axis=1,
        )
        for c in range(PAIRS)
    ]
    down_t = down_proj.T
    feed_shards = [
        jnp.concatenate(
            [w[:, c * FF_CHUNK : (c + 1) * FF_CHUNK] for w in (gate_proj, up_proj, down_t)], axis=1
        )
        for c in range(FF_CHUNKS)
    ]

    run_seg = segment_ids[half][TRUNK::SEG]
    run_parent = parents[half][run_seg]
    parent_run = jnp.argmax(run_seg[None, :] == run_parent[:, None], axis=1).astype(jnp.int32)
    meta = jnp.where(run_parent > 0, parent_run, -1)
    pos_tree = positions[half].reshape(2, nz, rows)
    pos_local = lax.dynamic_index_in_dim(pos_tree, member, 1, keepdims=False).reshape(count)
    cosine, sine = rope_tables(pos_local)

    (mixed, totals, pre, normed, gain_rows_, qk_gains, placed, cot, queries, kv_all,
     qkv_full, _, out_t, feed_whole) = forward(
        sizes, meta, cosine, sine, tokens, cotangent, qkv_shards + [out_proj.T] + feed_shards + [gains]
    )
    x = placed.reshape(count, D)
    cot = cot.reshape(count, D)
    in_weight, post_weight = gain_rows_[0:1], gain_rows_[1:2]
    query_weight, key_weight = qk_gains[0:1], qk_gains[1:2]
    qkv_full = qkv_full.reshape(PAIRS, D, -1)
    out_t = out_t.reshape(D, QD)
    feed_whole = feed_whole.reshape(FF_CHUNKS, D, -1)
    log_total = jnp.log2(totals[:, :KV_HEADS]).T
    result, grad_hidden, grad_stack, delta, post_part, dout, late, early_grad = feed(
        sizes, x, mixed, cot, out_t, post_weight, feed_whole
    )
    delta = delta[:HEADS].reshape(KV_HEADS, 2, 2 * SUBS, sub).transpose(0, 2, 1, 3)
    dq, dkv, late_grad, out_grad, output = backward(
        sizes, meta, queries, grad_stack, kv_all, log_total, delta, late, dout, result.reshape(2, rows, D)
    )
    feed_grad = jnp.concatenate([early_grad, late_grad], axis=0)

    def feed_columns(k):
        piece = feed_grad[:, :, k * FF_CHUNK : (k + 1) * FF_CHUNK]
        return piece.transpose(1, 0, 2).reshape(shard_rows, FF)

    dwq, dwk, dwv, dx, in_part, qk_part = project_back(
        dq, dkv, pre, normed, x, grad_hidden, in_weight, qkv_full, query_weight, key_weight, cosine, sine
    )

    def gain_column(values):
        if values.shape[0] == D:
            return values[:, None]
        spread = jnp.pad(values.reshape(-1, gain_rows), ((0, 0), (0, shard_rows - gain_rows)))
        return spread.reshape(D, 1)

    gain_parts = jnp.concatenate(
        [
            gain_column(in_part[0]),
            gain_column(post_part[0]),
            gain_column(qk_part[0]),
            gain_column(qk_part[1]),
        ],
        axis=1,
    )
    gain_parts = jnp.pad(gain_parts, ((0, 0), (0, GAIN_COLS - 4))).astype(BF16)
    (query_grad, key_grad, value_grad, gain_grad), input_grad = scatter_end(
        sizes, [dwq, dwk, dwv, gain_parts], dx.reshape(2, rows, D)
    )
    return (
        output,
        input_grad.astype(F32),
        gain_grad[:, 0],
        query_grad,
        key_grad,
        value_grad,
        gain_grad[:gain_rows, 2],
        gain_grad[:gain_rows, 3],
        out_grad.T,
        gain_grad[:, 1],
        feed_columns(0),
        feed_columns(1),
        feed_columns(2).T,
    )


def solution(mesh):
    dp, ctx = mesh.shape["dp"], mesh.shape["ctx"]
    sizes = (2, dp // 2, ctx // 2)
    return jax.shard_map(
        functools.partial(shards, sizes),
        mesh=mesh,
        in_specs=(
            P("dp", "ctx", None),
            P("dp", "ctx", None),
            P("dp", None),
            P("dp", None),
            P("dp", None),
            P(("dp", "ctx")),
            P(("dp", "ctx"), None),
            P(("dp", "ctx"), None),
            P(("dp", "ctx"), None),
            P(("dp", "ctx")),
            P(("dp", "ctx")),
            P(None, ("dp", "ctx")),
            P(("dp", "ctx")),
            P(("dp", "ctx"), None),
            P(("dp", "ctx"), None),
            P(None, ("dp", "ctx")),
        ),
        out_specs=(
            P("dp", "ctx", None),
            P("dp", "ctx", None),
            P(("dp", "ctx")),
            P(("dp", "ctx"), None),
            P(("dp", "ctx"), None),
            P(("dp", "ctx"), None),
            P(("dp", "ctx")),
            P(("dp", "ctx")),
            P(None, ("dp", "ctx")),
            P(("dp", "ctx")),
            P(("dp", "ctx"), None),
            P(("dp", "ctx"), None),
            P(None, ("dp", "ctx")),
        ),
        check_vma=False,
    )
```

```python
import functools
import math

import jax
import jax.numpy as jnp
from jax import lax
from jax.experimental import pallas as pl
from jax.experimental.pallas import tpu as pltpu
from jax.sharding import PartitionSpec as P

D = 1024
HEADS = 16
KV_HEADS = 8
HEAD_DIM = 128
FF = 3072
TRUNK = 1024
SEG = 128
TREE = 2560
QD = HEADS * HEAD_DIM
KVD = KV_HEADS * HEAD_DIM
SUBS = 5
CHUNK = 256
GAIN_COLS = 128
FF_CHUNK = 512
PAIRS = KV_HEADS // 2
FF_CHUNKS = FF // FF_CHUNK
FF_EARLY = 3
FF_FIRST = 4
LOCAL_RUNS = 3
MIB = 1024 * 1024

eps_norm = 1e-06
rope_base = 1000000.0
exp2_scale = math.log2(math.e) / math.sqrt(HEAD_DIM)
score_scale = HEAD_DIM ** (-0.5)

MESH = pl.DeviceIdType.MESH
ANY = pl.BlockSpec(memory_space=pl.ANY)
F32 = jnp.float32
BF16 = jnp.bfloat16


def matmul(left_side, right_side):
    return jnp.dot(left_side, right_side, preferred_element_type=F32)


def nt(left_side, right_side):
    return lax.dot_general(
        left_side, right_side, (((1,), (1,)), ((), ())), preferred_element_type=F32
    )


def contract_rows(left_side, right_side):
    return lax.dot_general(
        left_side, right_side, (((0,), (0,)), ((), ())), preferred_element_type=F32
    )


def norm_factor(values):
    return lax.rsqrt(jnp.mean(values * values, axis=-1, keepdims=True) + eps_norm)


def norm_backward(grad_out, weight, normed, factor):
    weighted = grad_out * weight
    grad_in = factor * (weighted - normed * jnp.mean(weighted * normed, axis=-1, keepdims=True))
    return (grad_in, grad_out * normed)


def rope_tables(positions):
    steps_half = jnp.arange(HEAD_DIM // 2, dtype=F32)
    inverse = rope_base ** (-(steps_half * 2.0 / HEAD_DIM))
    angles = positions.astype(F32)[:, None] * inverse[None, :]
    cosine, sine = jnp.cos(angles), jnp.sin(angles)
    return jnp.concatenate([cosine, cosine], axis=-1), jnp.concatenate([-sine, sine], axis=-1)


class Links:
    def __init__(self, sizes, send_sem, recv_sem):
        self.sizes = sizes
        self.send_sem = send_sem
        self.recv_sem = recv_sem
        self.index = {}

    def place(self):
        _, nx, _ = self.sizes
        dp, ctx = lax.axis_index("dp"), lax.axis_index("ctx")
        return dp // nx, lax.rem(dp, nx), ctx // 2, lax.rem(ctx, 2)

    def device(self, y, x, z, core):
        return (y * self.sizes[1] + x, z * 2 + core)

    def peers(self, axis, back=False):
        y, x, z, core = self.place()
        at = {"y": y, "x": x, "z": z}
        n = self.sizes["yxz".index(axis)]
        found = []
        for s in range(1, n):
            moved = dict(at)
            moved[axis] = lax.rem(at[axis] + (n - s if back else s), n)
            found.append((moved["y"], moved["x"], moved["z"], core))
        return found

    def sibling(self):
        y, x, z, core = self.place()
        return self.device(y, x, z, 1 - core)

    def across(self):
        y, x, z, core = self.place()
        nz = self.sizes[2]
        return self.device(y, x, lax.rem(z + nz // 2, nz), core)

    def group(self, back=False):
        y, x, z, core = self.place()
        chips = self.sizes[2] // 2
        base = (z // chips) * chips
        here = z - base
        chosen = [lax.rem(here + (chips - s if back else s), chips) for s in range(1, chips)]
        return [(chip, self.device(y, x, base + chip, core)) for chip in chosen]

    def meet(self):
        barrier = pltpu.get_barrier_semaphore()
        partners = [self.device(*p) for a in "zxy" for p in self.peers(a)] + [self.sibling()]
        for partner in partners:
            pl.semaphore_signal(barrier, inc=1, device_id=partner, device_id_type=MESH)
        pl.semaphore_wait(barrier, len(partners))

    def copy(self, key, src, dst, target):
        k = self.index.setdefault(key, len(self.index))
        return pltpu.make_async_remote_copy(
            src_ref=src,
            dst_ref=dst,
            send_sem=self.send_sem.at[k],
            recv_sem=self.recv_sem.at[k],
            device_id=target,
            device_id_type=MESH,
        )


class Exchange:
    def __init__(self, links, source, placed, local_sem, tag="swap"):
        self.tag = tag
        self.links = links
        self.source = source
        self.placed = placed
        self.local_sem = local_sem

    def copies_(self):
        _, _, z, _ = self.links.place()
        half = z // (self.links.sizes[2] // 2)
        return [
            self.links.copy(self.tag, self.source.at[1 - half], self.placed.at[half], self.links.across()),
            pltpu.make_async_copy(self.source.at[half], self.placed.at[half], self.local_sem),
        ]

    def start(self):
        for copy in self.copies_():
            copy.start()

    def wait(self):
        for copy in self.copies_():
            copy.wait()


class Gather:
    def __init__(self, links, tag, shard, whole, order, cols, local_sem):
        self.links = links
        self.tag = tag
        self.shard = shard
        self.whole = whole
        self.order = order
        self.cols = cols
        self.local_sem = local_sem

    def own(self):
        y, x, z, core = self.links.place()
        return self.whole.at[y, x, z, core, :, self.cols]

    def slab(self, stage, at):
        y, x, z, core = at
        if stage == 0:
            return self.whole.at[y, x, z, core, :, self.cols]
        if stage == 1:
            return self.whole.at[y, x, :, core, :, self.cols]
        if self.order[0] == "x":
            return self.whole.at[y, :, :, core, :, self.cols]
        return self.whole.at[:, x, :, core, :, self.cols]

    def axis(self, stage):
        return ("z",) + tuple(self.order)[0:2] if stage is None else ("z", self.order[0], self.order[1])[stage]

    def send(self, stage):
        me = self.links.place()
        src = self.shard.at[:, self.cols] if stage == 0 else self.slab(stage, me)
        dst = self.slab(stage, me)
        return [
            self.links.copy((self.tag, stage, i), src, dst, self.links.device(*p))
            for i, p in enumerate(self.links.peers(self.axis(stage)))
        ]

    def forward(self, stage):
        sibling = self.links.sibling()
        if stage < 0:
            return [self.links.copy((self.tag, "own"), self.shard.at[:, self.cols], self.own(), sibling)]
        return [
            self.links.copy((self.tag, "pass", stage, i), self.slab(stage, p), self.slab(stage, p), sibling)
            for i, p in enumerate(self.links.peers(self.axis(stage), back=True))
        ]

    def local(self):
        return pltpu.make_async_copy(self.shard.at[:, self.cols], self.own(), self.local_sem)

    def start(self):
        self.local().start()
        for copy in self.send(0) + self.forward(-1):
            copy.start()

    def step(self, stage):
        if stage == 1:
            self.local().wait()
        for copy in self.send(stage - 1):
            copy.wait()
        if stage < 3:
            for copy in self.send(stage):
                copy.start()
        for copy in self.forward(stage - 1):
            copy.start()

    def close(self):
        for stage in range(-1, 3):
            for copy in self.forward(stage):
                copy.wait()

    @staticmethod
    def copies(sizes):
        return 2 * sum(n - 1 for n in sizes) + 1


class Scatter:
    def __init__(self, links, tag, part, order, cols, halves, firsts, seconds, thirds, temp, temp_sem, out):
        self.links = links
        self.tag = tag
        self.part = part
        self.order = order
        self.cols = cols
        self.sums = halves
        self.got = (firsts, seconds, thirds)
        self.temp = temp
        self.temp_sem = temp_sem
        self.out = out

    def first(self):
        _, _, _, core = self.links.place()
        return self.links.copy(
            (self.tag, "core"), self.part.at[:, :, :, 1 - core, :, self.cols], self.sums, self.links.sibling()
        )

    def load(self):
        _, _, _, core = self.links.place()
        return pltpu.make_async_copy(
            self.part.at[:, :, :, core, :, self.cols], self.temp, self.temp_sem
        )

    def axis(self, stage):
        return (self.order[0], self.order[1], "z")[stage]

    def at(self, stage, place, rest=None):
        y, x, z, _ = place
        if stage == 0:
            return (y,) if self.order[0] == "y" else (slice(None), x)
        if stage == 1:
            return (y, x)
        return (y, x, z)

    def send(self, stage):
        me = self.links.place()
        found = []
        for i, p in enumerate(self.links.peers(self.axis(stage))):
            index = self.at(stage, p)
            found.append(
                self.links.copy(
                    (self.tag, stage, i), self.sums.at[index], self.got[stage].at[i], self.links.device(*p)
                )
            )
        return found

    def start(self):
        self.first().start()

    def begin(self):
        self.first().wait()
        if self.temp_sem is not None:
            self.load().wait()
        ny, nx, nz = self.links.sizes

        def add(i, carry):
            a, b, c = i // (nx * nz), lax.rem(i // nz, nx), lax.rem(i, nz)
            self.sums[a, b, c] = (
                self.sums[a, b, c].astype(F32) + self.temp[a, b, c].astype(F32)
            ).astype(BF16)
            return carry

        lax.fori_loop(0, ny * nx * nz, add, 0)
        for copy in self.send(0):
            copy.start()

    def middle(self, stage):
        for copy in self.send(stage):
            copy.wait()
        y, x, z, _ = self.links.place()
        _, _, nz = self.links.sizes
        got = self.got[stage]
        peers = got.shape[0]
        if stage == 0:
            other = got.shape[1]

            def add(i, carry):
                b, c = i // nz, lax.rem(i, nz)
                index = (y, b, c) if self.order[0] == "y" else (b, x, c)
                total = self.sums[index].astype(F32)
                for p in range(peers):
                    total = total + got[p, b, c].astype(F32)
                self.sums[index] = total.astype(BF16)
                return carry

            lax.fori_loop(0, other * nz, add, 0)
        else:

            def add(c, carry):
                total = self.sums[y, x, c].astype(F32)
                for p in range(peers):
                    total = total + got[p, c].astype(F32)
                self.sums[y, x, c] = total.astype(BF16)
                return carry

            lax.fori_loop(0, nz, add, 0)
        for copy in self.send(stage + 1):
            copy.start()

    def finish(self):
        for copy in self.send(2):
            copy.wait()
        y, x, z, _ = self.links.place()
        total = self.sums[y, x, z].astype(F32)
        for p in range(self.got[2].shape[0]):
            total = total + self.got[2][p].astype(F32)
        if callable(self.out):
            self.out(total)
        else:
            self.out[:, self.cols] = total

    @staticmethod
    def copies(sizes):
        return sum(n - 1 for n in sizes) + 1

    @staticmethod
    def scratch(sizes, order, rows, width):
        ny, nx, nz = sizes
        na, nb = (ny, nx) if order[0] == "y" else (nx, ny)
        return [
            pltpu.VMEM((ny, nx, nz, rows, width), BF16),
            pltpu.VMEM((na - 1, nb, nz, rows, width), BF16),
            pltpu.VMEM((nb - 1, nz, rows, width), BF16),
            pltpu.VMEM((nz - 1, rows, width), BF16),
        ]


ORDERS = ("xy", "yx")

FORWARD_START = [
    (0, 9), (0, 0), (0, 1), (1, 9), (1, 0), ("swap", "tokens"), (2, 9), (2, 0), (1, 1), (3, 9), (4, 9), (3, 0),
    (2, 1), (0, 2), ("swapped", "tokens"), (1, 2),
]
FORWARD_AFTER = {
    0: [("kv", 0), (3, 1), (2, 2), (0, 3), (0, 4)],
    1: [("kv", 1), (3, 2), (1, 3), (1, 4), (0, 5)],
    2: [("use", 0), (2, 3), (2, 4), (1, 5), (0, 6), (3, 3)],
    3: [("got", 0), ("kv", 2), (3, 4), (2, 5), (1, 6)],
    4: [("use", 1), ("got", 1), ("kv", 3), (3, 5), (2, 6), (0, 7)],
    5: [(1, 7)],
    6: [("use", 2), (3, 6), (2, 7), (0, 8)],
    7: [("got", 2), (1, 8), ("swap", "cot")],
    8: [("use", 3), (3, 7), (2, 8)],
    9: [("got", 3)],
    10: [(3, 8)],
    11: [("swapped", "cot")],
}
FEED_START = [("fetch", 0), ("send", (0, 4)), ("fetch", 1)]
FEED_NEXT = [("send", (1, 4)), ("send", (0, 5))]
FEED_MIDDLE = {
    0: [("send", (2, 4))],
    1: [("send", (3, 4)), ("send", (2, 5)), ("fetch", 2)],
    2: [("send", (3, 5)), ("fetch", 3)],
    3: [(1, 0), ("fetch", 4)],
    4: [(1, 1), ("fetch", 5)],
    5: [(1, 2)],
}
FEED_AFTER = {
    0: [("send", (1, 5)), ("core", 0)],
    1: [("begin", 0), ("core", 1)],
    2: [(0, 0), ("begin", 1), ("core", 2)],
    3: [(0, 1), ("begin", 2)],
    4: [(0, 2)],
}
FEED_LAST = []
FINISH_MIDDLE = {
    1: [("begin", 0)],
    2: [("begin", 1), (1, 0)],
    3: [("begin", 2), (1, 1)],
}
FINISH_AFTER = {
    0: [("core", 0)],
    1: [("core", 1), (0, 0)],
    2: [("core", 2), (0, 1)],
    3: [("core", 3)],
}
BACKWARD_AFTER = {
    0: [(0, 0)],
    1: [(1, 0), (0, 1)],
    2: [(2, 0), (1, 1)],
    3: [(2, 1), (0, 2)],
    4: [(1, 2), (0, 3)],
    5: [(2, 2), (1, 3)],
    6: [(2, 3)],
}


def halves_of(width):
    return (slice(0, width // 2), slice(width // 2, width)) if width >= 512 else (slice(0, width),)


def roll_half(values):
    return pltpu.roll(values, HEAD_DIM // 2, 1)


class KeyValues:
    def __init__(self, links, rows, held):
        self.links = links
        self.rows = rows
        self.held = held

    def slab(self, group, piece, member):
        members = self.links.sizes[2]
        start = pl.multiple_of(self.rows * (piece * members + member), self.rows)
        return self.held.at[:, 2 * group : 2 * group + 2, pl.ds(start, self.rows)]

    def mine(self):
        _, _, z, core = self.links.place()
        return lax.rem(z, self.links.sizes[2] // 2) * 2 + core

    def across(self, group):
        found = []
        for piece in range(2):
            slab = self.slab(group, piece, self.mine())
            for i, (_, target) in enumerate(self.links.group()):
                found.append(self.links.copy(("kv", group, piece, i), slab, slab, target))
        return found

    def near(self, group):
        found = []
        for piece in range(2):
            slab = self.slab(group, piece, self.mine())
            found.append(self.links.copy(("kv own", group, piece), slab, slab, self.links.sibling()))
        return found

    def forward(self, group):
        _, _, _, core = self.links.place()
        found = []
        for piece in range(2):
            for i, (chip, _) in enumerate(self.links.group(back=True)):
                slab = self.slab(group, piece, chip * 2 + core)
                found.append(
                    self.links.copy(("kv pass", group, piece, i), slab, slab, self.links.sibling())
                )
        return found

    @staticmethod
    def copies(sizes):
        return 4 * 2 * (2 * (sizes[2] // 2 - 1) + 1)


def run_all(copies, act):
    for copy in copies:
        if act == "start":
            copy.start()
        else:
            copy.wait()


def row_places(shape, dim, sub):
    t = lax.broadcasted_iota(jnp.int32, shape, dim)
    return (t // (2 * sub)) * sub + t % sub


def block_copies(sizes, src, dst, sem):
    ny, nx, nz = sizes
    shard_rows = src.shape[-2]
    found = []
    for i in range(ny * nx * nz * 2):
        block = src.at[i // (nx * nz * 2), i // (nz * 2) % nx, i // 2 % nz, i % 2]
        found.append(pltpu.make_async_copy(block, dst.at[i * shard_rows : (i + 1) * shard_rows], sem))
    return found


def gather_parents(meta, lead, slot, pairs):
    runs = (TREE - TRUNK) // SEG
    for k in range(LOCAL_RUNS):
        parent = meta[jnp.minimum(lead + k, runs - 1)]
        for read, out in pairs:
            total = None
            for b in range(runs):
                share = (1 - jnp.minimum(jnp.abs(parent - b), 1)).astype(F32).astype(BF16)
                term = read(b) * share
                total = term if total is None else total + term
            out[slot + k] = total


def forward_kernel(sizes, rows, meta, cos_ref, sin_ref, tok_ref, cot_ref, *refs):
    arrays = PAIRS + 2 + FF_FIRST
    shard = refs[:arrays]
    (mixed_ref, l_ref, pre_ref, normed_ref, gains_ref, qk_ref,
     placed, cot_placed, q_all, kv_all, qkv_whole, gain_whole, out_whole, feed_whole) = refs[arrays : arrays + 14]
    whole = (
        tuple(qkv_whole.at[c] for c in range(PAIRS))
        + (out_whole,)
        + tuple(feed_whole.at[c] for c in range(FF_FIRST))
        + (gain_whole,)
    )
    (qs, kvs, xs, ws, gs, acc, part, places, kp, vp, send_sem, recv_sem, local_sem) = refs[arrays + 14 :]
    members = sizes[2]
    sub = rows // SUBS
    count = 2 * rows
    step = pl.program_id(0)
    head = jnp.maximum(step - PAIRS, 0)
    links = Links(sizes, send_sem, recv_sem)
    kv = KeyValues(links, rows, kvs)
    swaps = {
        "tokens": Exchange(links, tok_ref, placed, local_sem.at[0], "tokens"),
        "cot": Exchange(links, cot_ref, cot_placed, local_sem.at[1], "cot"),
    }
    weights_ = [
        [
            Gather(links, (a, b), shard[a], whole[a], ORDERS[b], cols, local_sem.at[12 + 2 * a + b])
            for b, cols in enumerate(halves_of(shard[a].shape[-1]))
        ]
        for a in range(arrays)
    ]
    _, _, z, core = links.place()
    mine = lax.rem(z, members // 2) * 2 + core

    def kept(group):
        pair = slice(2 * group, 2 * group + 2)
        return [
            pltpu.make_async_copy(kvs.at[:, pair], kv_all.at[:, pair], local_sem.at[2 + group]),
            pltpu.make_async_copy(qs.at[pair], q_all.at[pair], local_sem.at[6 + group]),
        ]

    def act(steps):
        for what, a in steps:
            if what == "swap":
                swaps[a].start()
            elif what == "swapped":
                swaps[a].wait()
            elif what == "kv":
                run_all(kv.across(a), "start")
                run_all(kv.near(a), "start")
            elif what == "use":
                run_all(kv.across(a), "wait")
                run_all(kv.forward(a), "start")
            elif what == "got":
                run_all(kv.near(a), "wait")
                run_all(kv.forward(a), "wait")
                run_all(kept(a), "start")
            else:
                for g in weights_[a]:
                    if what == 0:
                        g.start()
                    elif what == 4:
                        g.close()
                    else:
                        g.step(what)

    @pl.when(step == 0)
    def _():
        links.meet()
        act(FORWARD_START)
        l_ref[...] = jnp.zeros_like(l_ref)
        places[...] = row_places(places.shape, 0, sub)
        run_all(block_copies(sizes, gain_whole, gs, local_sem.at[10]), "start")
        pltpu.make_async_copy(gs, gs, local_sem.at[10]).wait()
        loaded = pltpu.make_async_copy(placed, xs, local_sem.at[11])
        loaded.start()
        gains_ref[...] = gs[:, :GAIN_COLS].astype(F32).T[:8]
        qk_ref[0:1] = jnp.sum(gs[:, GAIN_COLS : 2 * GAIN_COLS].astype(F32), axis=0, keepdims=True)
        qk_ref[1:2] = jnp.sum(gs[:, 2 * GAIN_COLS :].astype(F32), axis=0, keepdims=True)
        loaded.wait()
        values = xs[...].reshape(count, D).astype(F32)
        normed_ref[...] = (values * norm_factor(values) * gains_ref[0:1]).astype(BF16)

    for c in range(PAIRS):

        @pl.when(step == c)
        def _():
            act([(4, c)])
            run_all(block_copies(sizes, qkv_whole.at[c], ws, local_sem.at[10]), "start")
            pltpu.make_async_copy(ws, ws, local_sem.at[10]).wait()

    @pl.when(step < PAIRS)
    def _():
        normed = normed_ref[...]
        cosine, sine = cos_ref[...], sin_ref[...]

        def turned(pre, gain):
            values = pre * norm_factor(pre) * gain
            return (values * cosine + roll_half(values) * sine).astype(BF16)

        for hh in range(2):
            at = 2 * step + hh
            query = matmul(normed, ws[:, 2 * hh * HEAD_DIM : 2 * (hh + 1) * HEAD_DIM])
            for h in range(2):
                pre = query[:, h * HEAD_DIM : (h + 1) * HEAD_DIM]
                pre_ref[hh, :, h * HEAD_DIM : (h + 1) * HEAD_DIM] = pre
                low = turned(pre, qk_ref[0:1])
                for s in range(2 * SUBS):
                    qs[at, (2 * s + h) * sub : (2 * s + h + 1) * sub] = low[s * sub : (s + 1) * sub]
            pre = matmul(normed, ws[:, (4 + hh) * HEAD_DIM : (5 + hh) * HEAD_DIM])
            pre_ref[hh, :, 2 * HEAD_DIM :] = pre
            low = turned(pre, qk_ref[1:2])
            value = matmul(normed, ws[:, (6 + hh) * HEAD_DIM : (7 + hh) * HEAD_DIM]).astype(BF16)
            for piece in range(2):
                start = pl.multiple_of(rows * (piece * members + mine), rows)
                kvs[0, at, pl.ds(start, rows)] = low[piece * rows : (piece + 1) * rows]
                kvs[1, at, pl.ds(start, rows)] = value[piece * rows : (piece + 1) * rows]

    def attend():
        lane = lax.broadcasted_iota(jnp.int32, (2 * rows, HEAD_DIM), 1)
        for piece in range(2):
            base = rows * (piece * members + mine)
            region = slice(piece * 2 * rows, (piece + 1) * 2 * rows)
            acc[...] = jnp.zeros_like(acc)
            part[...] = jnp.zeros_like(part)

            def trunk(step, masked):
                start = pl.multiple_of(step * CHUNK, CHUNK)
                weights = jnp.exp2(nt(qs[head, region], kvs[0, head, pl.ds(start, CHUNK)]) * exp2_scale)
                low, high = weights[:, :HEAD_DIM], weights[:, HEAD_DIM:]
                if masked:
                    room = places[...] + (base - start)
                    low = jnp.where(lane <= room, low, 0.0)
                    high = jnp.where(lane + HEAD_DIM <= room, high, 0.0)
                    weights = jnp.concatenate([low, high], axis=1)
                part[...] += low + high
                acc[...] += matmul(weights.astype(BF16), kvs[1, head, pl.ds(start, CHUNK)])
                return masked

            if piece == 0:
                clear = jnp.minimum(base // CHUNK, TRUNK // CHUNK)
                last = jnp.minimum((base + rows + CHUNK - 1) // CHUNK, TRUNK // CHUNK)
                lax.fori_loop(0, clear, lambda i, c: (trunk(i, False), c)[1], 0)
                lax.fori_loop(clear, last, lambda i, c: (trunk(i, True), c)[1], 0)
            else:
                lax.fori_loop(0, TRUNK // CHUNK, lambda i, c: (trunk(i, False), c)[1], 0)

            lead = jnp.maximum(base - TRUNK, 0) // SEG

            def parents_():
                gather_parents(
                    meta,
                    lead,
                    0,
                    [
                        (lambda b: kvs[0, head, TRUNK + b * SEG : TRUNK + (b + 1) * SEG], kp),
                        (lambda b: kvs[1, head, TRUNK + b * SEG : TRUNK + (b + 1) * SEG], vp),
                    ],
                )

            if piece == 0:
                pl.when(base + rows > TRUNK)(parents_)
            else:
                parents_()
            for s in range(SUBS):
                block = slice(2 * sub * s, 2 * sub * (s + 1))

                def runs():
                    row = base + s * sub - TRUNK
                    run = row // SEG
                    own = pl.multiple_of(TRUNK + run * SEG, SEG)
                    flag = jnp.minimum(meta[run] + 1, 1).astype(F32)
                    query = qs[head, piece * 2 * rows + 2 * sub * s : piece * 2 * rows + 2 * sub * (s + 1)]
                    room = places[block] + (lax.rem(row, SEG) - s * sub)
                    weights = jnp.exp2(nt(query, kvs[0, head, pl.ds(own, SEG)]) * exp2_scale)
                    weights = jnp.where(lane[block] <= room, weights, 0.0)
                    above = jnp.exp2(nt(query, kp[run - lead]) * exp2_scale) * flag
                    part[block] += weights + above
                    acc[block] += matmul(weights.astype(BF16), kvs[1, head, pl.ds(own, SEG)]) + matmul(
                        above.astype(BF16), vp[run - lead]
                    )

                if piece == 0:
                    pl.when(base + s * sub >= TRUNK)(runs)
                else:
                    runs()

            total = jnp.sum(part[...], axis=-1, keepdims=True)
            mixed = (acc[...] / total).astype(BF16)
            for s in range(SUBS):
                for h in range(2):
                    row = piece * rows + sub * s
                    mixed_ref[row : row + sub, h * HEAD_DIM : (h + 1) * HEAD_DIM] = mixed[
                        (2 * s + h) * sub : (2 * s + h + 1) * sub
                    ]
            l_ref[region] = jnp.where(lane == head, total, l_ref[region])


    pl.when(step >= PAIRS)(attend)
    for moment, steps in FORWARD_AFTER.items():
        pl.when(step == moment)(functools.partial(act, steps))

    @pl.when(step == PAIRS + KV_HEADS - 1)
    def _():
        for array in weights_[PAIRS : PAIRS + 1 + FF_FIRST]:
            for g in array:
                g.close()
        for group in range(4):
            run_all(kept(group), "wait")


def forward(sizes, meta, cosine, sine, tokens, cotangent, shards_):
    ny, nx, nz = sizes
    rows = tokens.shape[1]
    count = 2 * rows
    arrays = PAIRS + 2 + FF_FIRST
    shard_rows = shards_[0].shape[0]
    blocks = (ny, nx, nz, 2, shard_rows)
    widths = [w.shape[-1] for w in shards_]
    rounds = KeyValues.copies(sizes) + 2 * arrays * Gather.copies(sizes) + 2

    def at_head(s):
        return jnp.maximum(s - PAIRS, 0)

    results = pl.pallas_call(
        functools.partial(forward_kernel, sizes, rows),
        out_shape=[
            jax.ShapeDtypeStruct((count, QD), BF16),
            jax.ShapeDtypeStruct((2 * count, HEAD_DIM), F32),
            jax.ShapeDtypeStruct((KV_HEADS, count, 3 * HEAD_DIM), F32),
            jax.ShapeDtypeStruct((count, D), BF16),
            jax.ShapeDtypeStruct((8, D), F32),
            jax.ShapeDtypeStruct((8, HEAD_DIM), F32),
            jax.ShapeDtypeStruct(tokens.shape, BF16),
            jax.ShapeDtypeStruct(tokens.shape, BF16),
            jax.ShapeDtypeStruct((KV_HEADS, 2 * count, HEAD_DIM), BF16),
            jax.ShapeDtypeStruct((2, KV_HEADS, TREE, HEAD_DIM), BF16),
            jax.ShapeDtypeStruct((PAIRS,) + blocks + (widths[0],), BF16),
            jax.ShapeDtypeStruct(blocks + (widths[-1],), BF16),
            jax.ShapeDtypeStruct(blocks + (widths[PAIRS],), BF16),
            jax.ShapeDtypeStruct((FF_FIRST,) + blocks + (widths[PAIRS + 1],), BF16),
        ],
        grid_spec=pltpu.PrefetchScalarGridSpec(
            num_scalar_prefetch=1,
            grid=(PAIRS + KV_HEADS,),
            in_specs=[pl.BlockSpec((count, HEAD_DIM), lambda s, meta: (0, 0))] * 2 + [ANY] * (2 + arrays),
            out_specs=[
                pl.BlockSpec((count, 2 * HEAD_DIM), lambda s, meta: (0, at_head(s))),
                pl.BlockSpec((2 * count, HEAD_DIM), lambda s, meta: (0, 0)),
                pl.BlockSpec((2, count, 3 * HEAD_DIM), lambda s, meta: (jnp.minimum(s, PAIRS - 1), 0, 0)),
                pl.BlockSpec((count, D), lambda s, meta: (0, 0)),
                pl.BlockSpec((8, D), lambda s, meta: (0, 0)),
                pl.BlockSpec((8, HEAD_DIM), lambda s, meta: (0, 0)),
            ]
            + [ANY] * 8,
            scratch_shapes=[
                pltpu.VMEM((KV_HEADS, 2 * count, HEAD_DIM), BF16),
                pltpu.VMEM((2, KV_HEADS, TREE, HEAD_DIM), BF16),
                pltpu.VMEM(tokens.shape, BF16),
                pltpu.VMEM((D, widths[0]), BF16),
                pltpu.VMEM((D, widths[-1]), BF16),
                pltpu.VMEM((count, HEAD_DIM), F32),
                pltpu.VMEM((count, HEAD_DIM), F32),
                pltpu.VMEM((count, HEAD_DIM), jnp.int32),
                pltpu.VMEM((LOCAL_RUNS, SEG, HEAD_DIM), BF16),
                pltpu.VMEM((LOCAL_RUNS, SEG, HEAD_DIM), BF16),
                pltpu.SemaphoreType.DMA((rounds,)),
                pltpu.SemaphoreType.DMA((rounds,)),
                pltpu.SemaphoreType.DMA((12 + 2 * arrays,)),
            ],
        ),
        compiler_params=pltpu.CompilerParams(
            collective_id=2, has_side_effects=True, vmem_limit_bytes=56 * MIB
        ),
        name="forward",
    )(meta, cosine, sine, tokens, cotangent, *shards_)
    return results


def feed_kernel(
    sizes, rows, x_ref, mixed_ref, cot_ref, out_ref, gain_ref, first_ref, *refs,
):
    shard = refs[: FF_CHUNKS - FF_FIRST]
    refs = refs[FF_CHUNKS - FF_FIRST :]
    result_ref, hid_ref, stack_ref, delta_ref, post_ref, dout_ref, late_ref, rest_ref, early_ref = refs[:9]
    hidden, second, second_t, cot_t, total, grads, inner, gate_up, low, stack, part, wbuf = refs[9:21]
    buffers = refs[21:-3]
    send_sem, recv_sem, local_sem = refs[-3:]
    ny, nx, nz = sizes
    count = 2 * rows
    sub = rows // SUBS
    shard_rows = part.shape[5]
    width = 3 * FF_CHUNK
    tile = 256
    chunk = pl.program_id(0)
    links = Links(sizes, send_sem, recv_sem)
    _, _, _, core = links.place()
    scatters = []
    for c in range(FF_EARLY):
        for b, cols in enumerate(halves_of(width)):
            k = 4 * len(scatters)
            scatters.append(
                Scatter(
                    links,
                    (c, b),
                    part.at[c % 2],
                    ORDERS[b],
                    cols,
                    *buffers[k : k + 4],
                    part.at[c % 2, :, :, :, core, :, cols],
                    None,
                    early_ref.at[c],
                )
            )

    gathers = [
        [
            Gather(links, ("w", c, b), shard[c], rest_ref.at[c], ORDERS[b], cols, local_sem.at[8 + 2 * c + b])
            for b, cols in enumerate(halves_of(width))
        ]
        for c in range(FF_CHUNKS - FF_FIRST)
    ]

    def fetch(c):
        if c < FF_FIRST:
            pltpu.make_async_copy(first_ref.at[c], wbuf.at[c % 2], local_sem.at[6 + c % 2]).start()
        else:
            for g in gathers[c - FF_FIRST]:
                g.close()
            run_all(
                block_copies(sizes, rest_ref.at[c - FF_FIRST], wbuf.at[c % 2], local_sem.at[6 + c % 2]), "start"
            )

    def act(steps):
        for what, c in steps:
            if what == "fetch":
                fetch(c)
                continue
            if what == "send":
                for g in gathers[c[1] - FF_FIRST]:
                    if c[0] == 0:
                        g.start()
                    else:
                        g.step(c[0])
                continue
            for s in scatters[2 * c : 2 * c + 2]:
                if what == "core":
                    s.start()
                elif what == "begin":
                    s.begin()
                elif what == "finish":
                    s.finish()
                else:
                    s.middle(what)

    def rows_of(block):
        return (block // (2 * nz * nx), lax.rem(block // (2 * nz), nx), lax.rem(block // 2, nz), lax.rem(block, 2))

    def put(slot, first, cols, value):
        for k in range(value.shape[0] // shard_rows):
            y, x, z, c = rows_of(first // shard_rows + k)
            part[slot, y, x, z, c, :, cols] = value[k * shard_rows : (k + 1) * shard_rows].astype(BF16)

    def late(c):
        return pltpu.make_async_copy(part.at[c % 2], late_ref.at[c - FF_EARLY], local_sem.at[c % 2])

    @pl.when(chunk == 0)
    def _():
        links.meet()
        act(FEED_START)

        def project_out(t, carry):
            at = pl.multiple_of(t * tile, tile)
            hidden[:, pl.ds(at, tile)] = x_ref[:, pl.ds(at, tile)].astype(F32) + nt(
                mixed_ref[...], out_ref[pl.ds(at, tile), :]
            )
            return carry

        lax.fori_loop(0, D // tile, project_out, 0)
        act(FEED_NEXT)
        values = hidden[...]
        values = values * norm_factor(values) * gain_ref[...]
        second[...] = values.astype(BF16)
        second_t[...] = values.T.astype(BF16)
        cot_t[...] = cot_ref[...].astype(F32).T.astype(BF16)
        total[...] = jnp.zeros_like(total)
        grads[...] = jnp.zeros_like(grads)

    slot = lax.rem(chunk, 2)
    pltpu.make_async_copy(wbuf.at[slot], wbuf.at[slot], local_sem.at[6 + slot]).wait()

    def columns(t, carry):
        at = pl.multiple_of(t * tile, tile)
        gate = matmul(second[...], wbuf[slot, :, pl.ds(at, tile)])
        up = matmul(second[...], wbuf[slot, :, pl.ds(FF_CHUNK + at, tile)])
        grad = matmul(cot_ref[...], wbuf[slot, :, pl.ds(2 * FF_CHUNK + at, tile)])
        sigmoid = 1.0 / (1.0 + jnp.exp(-gate))
        active = gate * sigmoid
        inner[:, pl.ds(at, tile)] = (active * up).astype(BF16)
        gate_up[:, pl.ds(at, tile)] = (grad * up * sigmoid * (1.0 + gate * (1.0 - sigmoid))).astype(BF16)
        gate_up[:, pl.ds(FF_CHUNK + at, tile)] = (grad * active).astype(BF16)
        return carry

    lax.fori_loop(0, FF_CHUNK // tile, columns, 0)
    for moment, steps in FEED_MIDDLE.items():
        pl.when(chunk == moment)(functools.partial(act, steps))
    for c in range(FF_EARLY, FF_CHUNKS - 2):
        pl.when(chunk == c + 2)(lambda: late(c).wait())

    def model(t, carry):
        at = pl.multiple_of(t * tile, tile)
        total[:, pl.ds(at, tile)] += nt(inner[...], wbuf[slot, pl.ds(at, tile), 2 * FF_CHUNK :])
        grads[:, pl.ds(at, tile)] += nt(gate_up[...], wbuf[slot, pl.ds(at, tile), : 2 * FF_CHUNK])
        put(slot, at, slice(0, 2 * FF_CHUNK), matmul(second_t[pl.ds(at, tile)], gate_up[...]))
        put(slot, at, slice(2 * FF_CHUNK, width), matmul(cot_t[pl.ds(at, tile)], inner[...]))
        return carry

    lax.fori_loop(0, D // tile, model, 0)
    for c in range(FF_EARLY, FF_CHUNKS):
        pl.when(chunk == c)(lambda: late(c).start())
    for moment, steps in FEED_AFTER.items():
        pl.when(chunk == moment)(functools.partial(act, steps))

    @pl.when(chunk == FF_CHUNKS - 1)
    def _():
        values = hidden[...]
        low[...] = (values + total[...]).astype(BF16)
        output = pltpu.make_async_copy(low, result_ref, local_sem.at[2])
        output.start()
        factor = norm_factor(values)
        grad_in, share = norm_backward(grads[...], gain_ref[...], values * factor, factor)
        post_ref[...] = jnp.sum(share, axis=0, keepdims=True)
        hidden[...] = cot_ref[...].astype(F32) + grad_in
        saved = pltpu.make_async_copy(hidden, hid_ref, local_sem.at[3])
        saved.start()
        second[...] = hidden[...].astype(BF16)
        second_t[...] = hidden[...].T.astype(BF16)
        lane = lax.broadcasted_iota(jnp.int32, (count, HEAD_DIM), 1)
        dots = jnp.zeros((count, HEAD_DIM), F32)
        for h in range(KV_HEADS):
            cols = slice(2 * h * HEAD_DIM, 2 * (h + 1) * HEAD_DIM)
            grad = matmul(second[...], out_ref[:, cols]).astype(BF16)
            for g in range(2):
                one = grad[:, g * HEAD_DIM : (g + 1) * HEAD_DIM]
                for s in range(2 * SUBS):
                    stack[h, (2 * s + g) * sub : (2 * s + g + 1) * sub] = one[s * sub : (s + 1) * sub]
                head = 2 * h + g
                product = one.astype(F32) * mixed_ref[:, head * HEAD_DIM : (head + 1) * HEAD_DIM].astype(F32)
                dots = jnp.where(lane == head, jnp.sum(product, axis=-1, keepdims=True), dots)
        delta_ref[...] = dots.T
        stacked_ = pltpu.make_async_copy(stack, stack_ref, local_sem.at[4])
        stacked_.start()
        act(FEED_LAST)
        for c in range(FF_CHUNKS - 2, FF_CHUNKS):
            late(c).wait()

        def model_out(t, carry):
            at = pl.multiple_of(t * tile, tile)
            for a in range(0, QD, 2 * FF_CHUNK):
                cols = slice(a, a + 2 * FF_CHUNK)
                value = matmul(second_t[pl.ds(at, tile)], mixed_ref[:, cols])
                slot = a // (2 * FF_CHUNK)
                put(slot, at, slice(0, 2 * FF_CHUNK), value)
            return carry

        lax.fori_loop(0, D // tile, model_out, 0)
        gone = [
            pltpu.make_async_copy(
                part.at[k, :, :, :, :, :, : 2 * FF_CHUNK],
                dout_ref.at[:, :, :, :, :, 2 * FF_CHUNK * k : 2 * FF_CHUNK * (k + 1)],
                local_sem.at[k],
            )
            for k in range(2)
        ]
        run_all(gone, "start")
        for c in range(FF_EARLY):
            act([("finish", c)])
        run_all(gone + [output, saved, stacked_], "wait")


def feed(sizes, x, mixed, cot, out_t, gain, first, shards_):
    ny, nx, nz = sizes
    count = x.shape[0]
    rows = count // 2
    shard_rows = D // (ny * nx * nz * 2)
    width = 3 * FF_CHUNK
    buffers = []
    for c in range(FF_EARLY):
        for b, cols in enumerate(halves_of(width)):
            buffers += Scatter.scratch(sizes, ORDERS[b], shard_rows, cols.stop - cols.start)
    late = FF_CHUNKS - FF_FIRST
    rounds = 2 * FF_EARLY * Scatter.copies(sizes) + 2 * late * Gather.copies(sizes)

    def whole_block(shape):
        return pl.BlockSpec(shape, lambda c: (0,) * len(shape), pipeline_mode=pl.Buffered(1))

    blocks = (ny, nx, nz, 2, shard_rows)
    return pl.pallas_call(
        functools.partial(feed_kernel, sizes, rows),
        grid=(FF_CHUNKS,),
        out_shape=[
            jax.ShapeDtypeStruct((count, D), BF16),
            jax.ShapeDtypeStruct((count, D), F32),
            jax.ShapeDtypeStruct((KV_HEADS, 2 * count, HEAD_DIM), BF16),
            jax.ShapeDtypeStruct((HEAD_DIM, count), F32),
            jax.ShapeDtypeStruct((1, D), F32),
            jax.ShapeDtypeStruct(blocks + (QD,), BF16),
            jax.ShapeDtypeStruct((FF_CHUNKS - FF_EARLY,) + blocks + (width,), BF16),
            jax.ShapeDtypeStruct((late,) + blocks + (width,), BF16),
            jax.ShapeDtypeStruct((FF_EARLY, shard_rows, width), F32),
        ],
        in_specs=[
            whole_block((count, D)),
            whole_block((count, QD)),
            whole_block((count, D)),
            whole_block((D, QD)),
            whole_block((1, D)),
            ANY,
        ]
        + [ANY] * late,
        out_specs=[
            ANY,
            ANY,
            ANY,
            pl.BlockSpec((HEAD_DIM, count), lambda c: (0, 0)),
            pl.BlockSpec((1, D), lambda c: (0, 0)),
            ANY,
            ANY,
            ANY,
            pl.BlockSpec((FF_EARLY, shard_rows, width), lambda c: (0, 0, 0)),
        ],
        scratch_shapes=[
            pltpu.VMEM((count, D), F32),
            pltpu.VMEM((count, D), BF16),
            pltpu.VMEM((D, count), BF16),
            pltpu.VMEM((D, count), BF16),
            pltpu.VMEM((count, D), F32),
            pltpu.VMEM((count, D), F32),
            pltpu.VMEM((count, FF_CHUNK), BF16),
            pltpu.VMEM((count, 2 * FF_CHUNK), BF16),
            pltpu.VMEM((count, D), BF16),
            pltpu.VMEM((KV_HEADS, 2 * count, HEAD_DIM), BF16),
            pltpu.VMEM((2,) + blocks + (width,), BF16),
            pltpu.VMEM((2, D, width), BF16),
        ]
        + buffers
        + [
            pltpu.SemaphoreType.DMA((rounds,)),
            pltpu.SemaphoreType.DMA((rounds,)),
            pltpu.SemaphoreType.DMA((8 + 2 * late,)),
        ],
        compiler_params=pltpu.CompilerParams(
            collective_id=5, has_side_effects=True, vmem_limit_bytes=61 * MIB
        ),
        name="feed",
    )(x, mixed, cot, out_t, gain, first, *shards_)


def backward_kernel(sizes, rows, widths, meta, q_ref, g_ref, k_ref, v_ref, lse_ref, del_ref, late_ref, dout_ref, done_ref, *refs):
    dq_ref, dkv_ref, late_out, dout_out, done_placed = refs[:5]
    dq, dk, dv, pk, pv, kp, vp, stage, near, sums, far, last = refs[5:17]
    buffers = refs[17:-3]
    send_sem, recv_sem, local_sem = refs[-3:]
    members = sizes[2]
    chips = members // 2
    sub = rows // SUBS
    head = pl.program_id(0)
    links = Links(sizes, send_sem, recv_sem)
    scatters = []
    late = FF_CHUNKS - FF_EARLY
    for a, width in enumerate(widths):
        for b, cols in enumerate(halves_of(width)):
            k = 5 * len(scatters)
            scatters.append(
                Scatter(
                    links,
                    (a, b),
                    late_ref.at[a] if a < late else dout_ref,
                    ORDERS[b],
                    cols,
                    *buffers[k : k + 5],
                    local_sem.at[2 + len(scatters)],
                    late_out.at[a] if a < late else dout_out,
                )
            )

    swap = Exchange(links, done_ref, done_placed, local_sem.at[2 + len(scatters)])

    def each(array):
        return scatters[2 * array : 2 * array + 2]

    @pl.when(head == 0)
    def _():
        for s in scatters:
            s.load().start()
        links.meet()
        for s in scatters:
            s.start()
        swap.start()

    _, _, z, core = links.place()
    here = lax.rem(z, chips)
    mine = here * 2 + core
    dk[...] = jnp.zeros_like(dk)
    dv[...] = jnp.zeros_like(dv)
    pk[...] = jnp.zeros_like(pk)
    pv[...] = jnp.zeros_like(pv)
    for piece in range(2):
        base = rows * (piece * members + mine)
        at = piece * 2 * rows
        region = slice(at, at + 2 * rows)
        dq[...] = jnp.zeros_like(dq)

        def pair(key, value, block, mask):
            spot = slice(at + block.start, at + block.stop)
            weights = jnp.exp2(nt(key, q_ref[0, spot]) * exp2_scale - lse_ref[0, :, spot])
            if mask is not None:
                weights = mask(weights)
            grads = (weights * (nt(value, g_ref[0, spot]) - del_ref[0, :, spot])).astype(BF16)
            weights = weights.astype(BF16)
            dq[block] += contract_rows(grads, key)
            return matmul(grads, q_ref[0, spot]), matmul(weights, g_ref[0, spot])

        everything = slice(0, 2 * rows)

        def trunk(step, masked):
            start = pl.multiple_of(step * CHUNK, CHUNK)

            def mask(weights):
                shape = weights.shape
                room = row_places((1, shape[1]), 1, sub) + (base - start)
                return jnp.where(lax.broadcasted_iota(jnp.int32, shape, 0) <= room, weights, 0.0)

            key_grad, value_grad = pair(
                k_ref[0, 0, pl.ds(start, CHUNK)],
                v_ref[0, 0, pl.ds(start, CHUNK)],
                everything,
                mask if masked else None,
            )
            dk[pl.ds(start, CHUNK)] += key_grad
            dv[pl.ds(start, CHUNK)] += value_grad

        if piece == 0:
            clear = jnp.minimum(base // CHUNK, TRUNK // CHUNK)
            end = jnp.minimum((base + rows + CHUNK - 1) // CHUNK, TRUNK // CHUNK)
            lax.fori_loop(0, clear, lambda i, c: (trunk(i, False), c)[1], 0)
            lax.fori_loop(clear, end, lambda i, c: (trunk(i, True), c)[1], 0)
        else:
            lax.fori_loop(0, TRUNK // CHUNK, lambda i, c: (trunk(i, False), c)[1], 0)

        lead = jnp.maximum(base - TRUNK, 0) // SEG

        def parents_():
            gather_parents(
                meta,
                lead,
                0,
                [
                    (lambda b: k_ref[0, 0, TRUNK + b * SEG : TRUNK + (b + 1) * SEG], kp),
                    (lambda b: v_ref[0, 0, TRUNK + b * SEG : TRUNK + (b + 1) * SEG], vp),
                ],
            )

        if piece == 0:
            pl.when(base + rows > TRUNK)(parents_)
        else:
            parents_()
        for s in range(SUBS):
            block = slice(2 * sub * s, 2 * sub * (s + 1))

            def runs():
                row = base + s * sub - TRUNK
                run = row // SEG
                own = pl.multiple_of(TRUNK + run * SEG, SEG)
                flag = jnp.minimum(meta[run] + 1, 1).astype(F32)

                def mask(weights):
                    shape = (SEG, 2 * sub)
                    room = lax.broadcasted_iota(jnp.int32, shape, 1) % sub + lax.rem(row, SEG)
                    seen = lax.broadcasted_iota(jnp.int32, shape, 0) <= room
                    return jnp.concatenate(
                        [jnp.where(seen, weights[:SEG], 0.0), weights[SEG:] * flag], axis=0
                    )

                key_grad, value_grad = pair(
                    jnp.concatenate([k_ref[0, 0, pl.ds(own, SEG)], kp[run - lead]], axis=0),
                    jnp.concatenate([v_ref[0, 0, pl.ds(own, SEG)], vp[run - lead]], axis=0),
                    block,
                    mask,
                )
                dk[pl.ds(own, SEG)] += key_grad[:SEG]
                dv[pl.ds(own, SEG)] += value_grad[:SEG]
                slot = LOCAL_RUNS * piece + run - lead
                pk[slot] += key_grad[SEG:]
                pv[slot] += value_grad[SEG:]

            if piece == 0:
                pl.when(base + s * sub >= TRUNK)(runs)
            else:
                runs()

        dq_ref[0, region] = dq[...] * score_scale

        def spread():
            parents = [meta[jnp.minimum(lead + k, TREE // SEG - TRUNK // SEG - 1)] for k in range(LOCAL_RUNS)]

            def place(b, carry):
                start = pl.multiple_of(TRUNK + b * SEG, SEG)
                key_grad, value_grad = dk[pl.ds(start, SEG)], dv[pl.ds(start, SEG)]
                for k in range(LOCAL_RUNS):
                    share = (1 - jnp.minimum(jnp.abs(parents[k] - b), 1)).astype(F32)
                    key_grad += pk[LOCAL_RUNS * piece + k] * share
                    value_grad += pv[LOCAL_RUNS * piece + k] * share
                dk[pl.ds(start, SEG)] = key_grad
                dv[pl.ds(start, SEG)] = value_grad
                return carry

            lax.fori_loop(0, (TREE - TRUNK) // SEG, place, 0)

        if piece == 0:
            pl.when(base + rows > TRUNK)(spread)
        else:
            spread()

    def core_copy(h):
        return links.copy(("kv core", h), stage.at[h % 2, :, 1 - core], near.at[h % 2], links.sibling())

    def far_copies(h):
        return [
            links.copy(("kv z", h, i), sums.at[h, chip], far.at[h, i], target)
            for i, (chip, target) in enumerate(links.group())
        ]

    def pass_on(h):
        core_copy(h).wait()

        def add(i, carry):
            chip, which, piece = i // 4, lax.rem(i // 2, 2), lax.rem(i, 2)
            sums[h, chip, which, piece] = (
                stage[h % 2, chip, core, which, piece].astype(F32) + near[h % 2, chip, which, piece].astype(F32)
            ).astype(BF16)
            return carry

        lax.fori_loop(0, chips * 4, add, 0)
        run_all(far_copies(h), "start")

    for h in range(1, KV_HEADS):
        pl.when(head == h)(functools.partial(pass_on, h - 1))

    for which, grad, scale in ((0, dk, score_scale), (1, dv, 1.0)):
        for piece in range(2):
            for member in range(members):
                start = rows * (piece * members + member)
                stage[lax.rem(head, 2), member // 2, member % 2, which, piece] = (
                    grad[start : start + rows] * scale
                ).astype(BF16)
    for h in range(KV_HEADS):

        @pl.when(head == h)
        def _():
            core_copy(h).start()

    for moment, steps in BACKWARD_AFTER.items():

        @pl.when(head == moment)
        def _():
            for step, array in steps:
                for s in each(array):
                    if step == 0:
                        s.begin()
                    else:
                        s.middle(step - 1)

    def result(h):
        return pltpu.make_async_copy(last.at[h % 2], dkv_ref.at[:, h], local_sem.at[h % 2])

    @pl.when(head == KV_HEADS - 1)
    def _():
        pass_on(KV_HEADS - 1)
        for s in scatters:
            s.finish()
        for h in range(KV_HEADS):
            run_all(far_copies(h), "wait")
            if h > 1:
                result(h - 2).wait()
            for which in range(2):
                for piece in range(2):
                    total = sums[h, here, which, piece].astype(F32)
                    for i in range(chips - 1):
                        total = total + far[h, i, which, piece].astype(F32)
                    last[h % 2, which, piece] = total
            result(h).start()
        for h in (KV_HEADS - 2, KV_HEADS - 1):
            result(h).wait()
        swap.wait()


def backward(sizes, meta, queries, grads, kv_all, log_total, delta, late, dout, done):
    ny, nx, nz = sizes
    chips = nz // 2
    rows = queries.shape[1] // 4
    widths = (late.shape[-1],) * late.shape[0] + (dout.shape[-1],)
    shard_rows = dout.shape[4]
    stack = pl.BlockSpec((1, 4 * rows, HEAD_DIM), lambda h, meta: (h, 0, 0))
    line = pl.BlockSpec((1, 1, 4 * rows), lambda h, meta: (h, 0, 0))
    buffers, count = [], 0
    for w in widths:
        for b, cols in enumerate(halves_of(w)):
            buffers += Scatter.scratch(sizes, ORDERS[b], shard_rows, cols.stop - cols.start)
            buffers.append(pltpu.VMEM((ny, nx, nz, shard_rows, cols.stop - cols.start), BF16))
            count += 1
    rounds = count * Scatter.copies(sizes) + KV_HEADS * chips + 1
    late_shape = (late.shape[0], shard_rows, late.shape[-1])
    dout_shape = (shard_rows, dout.shape[-1])
    return pl.pallas_call(
        functools.partial(backward_kernel, sizes, rows, widths),
        out_shape=[
            jax.ShapeDtypeStruct((KV_HEADS, 4 * rows, HEAD_DIM), F32),
            jax.ShapeDtypeStruct((2, KV_HEADS, 2, rows, HEAD_DIM), F32),
            jax.ShapeDtypeStruct(late_shape, F32),
            jax.ShapeDtypeStruct(dout_shape, F32),
            jax.ShapeDtypeStruct(done.shape, BF16),
        ],
        grid_spec=pltpu.PrefetchScalarGridSpec(
            num_scalar_prefetch=1,
            grid=(KV_HEADS,),
            in_specs=[
                stack,
                stack,
                pl.BlockSpec((1, 1, TREE, HEAD_DIM), lambda h, meta: (0, h, 0, 0)),
                pl.BlockSpec((1, 1, TREE, HEAD_DIM), lambda h, meta: (1, h, 0, 0)),
                line,
                line,
                ANY,
                ANY,
                ANY,
            ],
            out_specs=[
                stack,
                ANY,
                pl.BlockSpec(late_shape, lambda h, meta: (0, 0, 0)),
                pl.BlockSpec(dout_shape, lambda h, meta: (0, 0)),
                ANY,
            ],
            scratch_shapes=[
                pltpu.VMEM((2 * rows, HEAD_DIM), F32),
                pltpu.VMEM((TREE, HEAD_DIM), F32),
                pltpu.VMEM((TREE, HEAD_DIM), F32),
                pltpu.VMEM((2 * LOCAL_RUNS, SEG, HEAD_DIM), F32),
                pltpu.VMEM((2 * LOCAL_RUNS, SEG, HEAD_DIM), F32),
                pltpu.VMEM((LOCAL_RUNS, SEG, HEAD_DIM), BF16),
                pltpu.VMEM((LOCAL_RUNS, SEG, HEAD_DIM), BF16),
                pltpu.VMEM((2, chips, 2, 2, 2, rows, HEAD_DIM), BF16),
                pltpu.VMEM((2, chips, 2, 2, rows, HEAD_DIM), BF16),
                pltpu.VMEM((KV_HEADS, chips, 2, 2, rows, HEAD_DIM), BF16),
                pltpu.VMEM((KV_HEADS, chips - 1, 2, 2, rows, HEAD_DIM), BF16),
                pltpu.VMEM((2, 2, 2, rows, HEAD_DIM), F32),
            ]
            + buffers
            + [
                pltpu.SemaphoreType.DMA((rounds,)),
                pltpu.SemaphoreType.DMA((rounds,)),
                pltpu.SemaphoreType.DMA((3 + count,)),
            ],
        ),
        compiler_params=pltpu.CompilerParams(
            collective_id=3, has_side_effects=True, vmem_limit_bytes=60 * MIB
        ),
        name="backward",
    )(
        meta,
        queries,
        grads,
        kv_all,
        kv_all,
        log_total.reshape(KV_HEADS, 1, 4 * rows),
        delta.reshape(KV_HEADS, 1, 4 * rows),
        late,
        dout,
        done,
    )


def finish_kernel(
    sizes, rows, dq_ref, dkv_ref, pre_ref, w_ref, normed_ref, x_ref, hid_ref, gain_ref, post_ref, qg_ref, kg_ref, cos_ref, sin_ref,
    q_out, k_out, v_out, g_out, dx_placed, *refs,
):
    normed_t, low, grads, qk, dx, part, part_g = refs[:7]
    buffers = refs[7:-3]
    send_sem, recv_sem, local_sem = refs[-3:]
    ny, nx, nz = sizes
    count = 2 * rows
    sub = rows // SUBS
    shard_rows = part.shape[5]
    tile = 256
    pair = pl.program_id(0)
    links = Links(sizes, send_sem, recv_sem)
    _, _, _, core = links.place()
    swap = Exchange(links, dx, dx_placed, local_sem.at[0])

    def to_query(c):
        def store(total):
            q_out[:, 4 * HEAD_DIM * c : 4 * HEAD_DIM * (c + 1)] = total

        return store

    def to_key_value(c):
        def store(total):
            k_out[:, 2 * HEAD_DIM * c : 2 * HEAD_DIM * (c + 1)] = total[:, : 2 * HEAD_DIM]
            v_out[:, 2 * HEAD_DIM * c : 2 * HEAD_DIM * (c + 1)] = total[:, 2 * HEAD_DIM :]

        return store

    scatters = []
    for c in range(PAIRS):
        for b, cols in enumerate(halves_of(8 * HEAD_DIM)):
            k = 4 * len(scatters)
            scatters.append(
                Scatter(
                    links,
                    (c, b),
                    part.at[c % 2],
                    ORDERS[b],
                    cols,
                    *buffers[k : k + 4],
                    part.at[c % 2, :, :, :, core, :, cols],
                    None,
                    to_key_value(c) if b else to_query(c),
                )
            )
    k = 4 * len(scatters)
    whole = slice(0, 3 * GAIN_COLS)
    scatters.append(
        Scatter(
            links, "gains", part_g, ORDERS[0], whole, *buffers[k : k + 4], part_g.at[:, :, :, core], None, g_out
        )
    )

    def act(steps):
        for what, c in steps:
            for s in scatters[2 * c : 2 * c + 2]:
                if what == "core":
                    s.start()
                elif what == "begin":
                    s.begin()
                elif what == "finish":
                    s.finish()
                else:
                    s.middle(what)

    def rows_of(block):
        return (block // (2 * nz * nx), lax.rem(block // (2 * nz), nx), lax.rem(block // 2, nz), lax.rem(block, 2))

    @pl.when(pair == 0)
    def _():
        links.meet()
        normed_t[...] = normed_ref[...].astype(F32).T.astype(BF16)
        grads[...] = jnp.zeros_like(grads)
        qk[...] = jnp.zeros_like(qk)

    cosine, sine = cos_ref[...], sin_ref[...]

    def back(turned_grad, pre, gain):
        grad = turned_grad * cosine - roll_half(turned_grad) * sine
        factor = norm_factor(pre)
        grad_pre, share = norm_backward(grad, gain, pre * factor, factor)
        return grad_pre.astype(BF16), jnp.sum(share, axis=0, keepdims=True)

    for hh in range(2):
        for h in range(2):
            grad = jnp.concatenate(
                [dq_ref[hh, (2 * s + h) * sub : (2 * s + h + 1) * sub] for s in range(2 * SUBS)], axis=0
            )
            value, share = back(grad, pre_ref[hh, :, h * HEAD_DIM : (h + 1) * HEAD_DIM], qg_ref[...])
            qk[0:1] += share
            at = 2 * hh + h
            low[:, at * HEAD_DIM : (at + 1) * HEAD_DIM] = value
        value, share = back(dkv_ref[0, hh].reshape(count, HEAD_DIM), pre_ref[hh, :, 2 * HEAD_DIM :], kg_ref[...])
        qk[1:2] += share
        low[:, (4 + hh) * HEAD_DIM : (5 + hh) * HEAD_DIM] = value
        low[:, (6 + hh) * HEAD_DIM : (7 + hh) * HEAD_DIM] = dkv_ref[1, hh].reshape(count, HEAD_DIM).astype(BF16)
    for moment, steps in FINISH_MIDDLE.items():
        pl.when(pair == moment)(functools.partial(act, steps))
    slot = lax.rem(pair, 2)

    def model(t, carry):
        at = pl.multiple_of(t * tile, tile)
        grads[:, pl.ds(at, tile)] += nt(low[...], w_ref[0, pl.ds(at, tile), :])
        value = matmul(normed_t[pl.ds(at, tile)], low[...])
        for k in range(tile // shard_rows):
            y, x, z, c = rows_of(at // shard_rows + k)
            part[slot, y, x, z, c] = value[k * shard_rows : (k + 1) * shard_rows].astype(BF16)
        return carry

    lax.fori_loop(0, D // tile, model, 0)
    for moment, steps in FINISH_AFTER.items():
        pl.when(pair == moment)(functools.partial(act, steps))

    @pl.when(pair == PAIRS - 1)
    def _():
        values = x_ref[...].astype(F32)
        factor = norm_factor(values)
        grad_in, share = norm_backward(grads[...], gain_ref[...], values * factor, factor)
        dx[...] = (hid_ref[...] + grad_in).astype(BF16).reshape(2, rows, D)
        swap.start()
        act([(0, PAIRS - 2), ("begin", PAIRS - 1)])
        lines = jnp.concatenate(
            [jnp.sum(share, axis=0, keepdims=True), post_ref[...], jnp.zeros((GAIN_COLS - 2, D), F32)], axis=0
        )
        columns = lines.T.astype(BF16)
        first = lax.broadcasted_iota(jnp.int32, (shard_rows, GAIN_COLS), 0) == 0
        query_line = jnp.where(first, qk[0:1], 0.0).astype(BF16)
        key_line = jnp.where(first, qk[1:2], 0.0).astype(BF16)
        for k in range(D // shard_rows):
            y, x, z, c = k // (2 * nz * nx), k // (2 * nz) % nx, k // 2 % nz, k % 2
            part_g[y, x, z, c, :, :GAIN_COLS] = columns[k * shard_rows : (k + 1) * shard_rows]
            part_g[y, x, z, c, :, GAIN_COLS : 2 * GAIN_COLS] = query_line
            part_g[y, x, z, c, :, 2 * GAIN_COLS :] = key_line
        act([("core", PAIRS), (1, PAIRS - 2), ("begin", PAIRS), (0, PAIRS - 1), (0, PAIRS), (1, PAIRS - 1), (1, PAIRS)])
        for c in range(PAIRS + 1):
            act([("finish", c)])
        swap.wait()


def finish(sizes, dq, dkv, pre, normed, x, grad_hidden, gain, post_part, qkv_full, query_gain, key_gain, cosine, sine):
    ny, nx, nz = sizes
    count = x.shape[0]
    rows = count // 2
    shard_rows = D // (ny * nx * nz * 2)
    blocks = (ny, nx, nz, 2, shard_rows)
    width = 8 * HEAD_DIM

    def whole_block(shape):
        return pl.BlockSpec(shape, lambda c: (0,) * len(shape), pipeline_mode=pl.Buffered(1))

    buffers = []
    for c in range(PAIRS):
        for b, cols in enumerate(halves_of(width)):
            buffers += Scatter.scratch(sizes, ORDERS[b], shard_rows, cols.stop - cols.start)
    buffers += Scatter.scratch(sizes, ORDERS[0], shard_rows, 3 * GAIN_COLS)
    rounds = (2 * PAIRS + 1) * Scatter.copies(sizes) + 1

    def out_block(n):
        return pl.BlockSpec((shard_rows, n), lambda c: (0, 0))

    return pl.pallas_call(
        functools.partial(finish_kernel, sizes, rows),
        grid=(PAIRS,),
        out_shape=[
            jax.ShapeDtypeStruct((shard_rows, QD), F32),
            jax.ShapeDtypeStruct((shard_rows, KVD), F32),
            jax.ShapeDtypeStruct((shard_rows, KVD), F32),
            jax.ShapeDtypeStruct((shard_rows, 3 * GAIN_COLS), F32),
            jax.ShapeDtypeStruct((2, rows, D), BF16),
        ],
        in_specs=[
            pl.BlockSpec((2, 2 * count, HEAD_DIM), lambda c: (c, 0, 0)),
            pl.BlockSpec((2, 2, 2, rows, HEAD_DIM), lambda c: (0, c, 0, 0, 0)),
            pl.BlockSpec((2, count, 3 * HEAD_DIM), lambda c: (c, 0, 0)),
            pl.BlockSpec((1, D, width), lambda c: (c, 0, 0)),
            whole_block((count, D)),
            whole_block((count, D)),
            whole_block((count, D)),
            whole_block((1, D)),
            whole_block((1, D)),
            whole_block((1, HEAD_DIM)),
            whole_block((1, HEAD_DIM)),
            whole_block((count, HEAD_DIM)),
            whole_block((count, HEAD_DIM)),
        ],
        out_specs=[out_block(QD), out_block(KVD), out_block(KVD), out_block(3 * GAIN_COLS), ANY],
        scratch_shapes=[
            pltpu.VMEM((D, count), BF16),
            pltpu.VMEM((count, width), BF16),
            pltpu.VMEM((count, D), F32),
            pltpu.VMEM((8, HEAD_DIM), F32),
            pltpu.VMEM((2, rows, D), BF16),
            pltpu.VMEM((2,) + blocks + (width,), BF16),
            pltpu.VMEM(blocks + (3 * GAIN_COLS,), BF16),
        ]
        + buffers
        + [
            pltpu.SemaphoreType.DMA((rounds,)),
            pltpu.SemaphoreType.DMA((rounds,)),
            pltpu.SemaphoreType.DMA((1,)),
        ],
        compiler_params=pltpu.CompilerParams(
            collective_id=4, has_side_effects=True, vmem_limit_bytes=58 * MIB
        ),
        name="finish",
    )(dq, dkv, pre, qkv_full, normed, x, grad_hidden, gain, post_part, query_gain, key_gain, cosine, sine)


def shards(
    sizes,
    tokens,
    cotangent,
    segment_ids,
    positions,
    parents,
    input_norm,
    query_proj,
    key_proj,
    value_proj,
    query_norm,
    key_norm,
    out_proj,
    post_norm,
    gate_proj,
    up_proj,
    down_proj,
):
    nz = sizes[2]
    rows = tokens.shape[1]
    shard_rows = query_proj.shape[0]
    gain_rows = query_norm.shape[0]
    ctx = lax.axis_index("ctx")
    half = ctx // nz
    member = ctx % nz
    count = 2 * rows
    sub = rows // SUBS

    device = lax.axis_index("dp") * 2 * nz + ctx

    def spread(gain):
        line = jnp.zeros((1, HEAD_DIM), BF16)
        line = lax.dynamic_update_slice(line, gain[None, :], (0, device * gain_rows))
        return jnp.pad(line, ((0, shard_rows - 1), (0, 0)))

    gains = jnp.pad(
        jnp.stack([input_norm, post_norm], axis=1), ((0, 0), (0, GAIN_COLS - 2))
    )
    gains = jnp.concatenate([gains, spread(query_norm), spread(key_norm)], axis=1)
    qkv_shards = [
        jnp.concatenate(
            [
                query_proj[:, 4 * HEAD_DIM * c : 4 * HEAD_DIM * (c + 1)],
                key_proj[:, 2 * HEAD_DIM * c : 2 * HEAD_DIM * (c + 1)],
                value_proj[:, 2 * HEAD_DIM * c : 2 * HEAD_DIM * (c + 1)],
            ],
            axis=1,
        )
        for c in range(PAIRS)
    ]
    down_t = down_proj.T
    feed_shards = [
        jnp.concatenate(
            [w[:, c * FF_CHUNK : (c + 1) * FF_CHUNK] for w in (gate_proj, up_proj, down_t)], axis=1
        )
        for c in range(FF_CHUNKS)
    ]

    run_seg = segment_ids[half][TRUNK::SEG]
    run_parent = parents[half][run_seg]
    parent_run = jnp.argmax(run_seg[None, :] == run_parent[:, None], axis=1).astype(jnp.int32)
    meta = jnp.where(run_parent > 0, parent_run, -1)
    pos_tree = positions[half].reshape(2, nz, rows)
    pos_local = lax.dynamic_index_in_dim(pos_tree, member, 1, keepdims=False).reshape(count)
    cosine, sine = rope_tables(pos_local)

    (mixed, totals, pre, normed, gain_rows_, qk_gains, placed, cot, queries, kv_all,
     qkv_full, _, out_t, feed_whole) = forward(
        sizes, meta, cosine, sine, tokens, cotangent, qkv_shards + [out_proj.T] + feed_shards[:FF_FIRST] + [gains]
    )
    x = placed.reshape(count, D)
    cot = cot.reshape(count, D)
    in_weight, post_weight = gain_rows_[0:1], gain_rows_[1:2]
    query_weight, key_weight = qk_gains[0:1], qk_gains[1:2]
    qkv_full = qkv_full.reshape(PAIRS, D, -1)
    out_t = out_t.reshape(D, QD)
    feed_whole = feed_whole.reshape(FF_FIRST, D, -1)
    log_total = jnp.log2(totals[:, :KV_HEADS]).T
    result, grad_hidden, grad_stack, delta, post_part, dout, late, _, early_grad = feed(
        sizes, x, mixed, cot, out_t, post_weight, feed_whole, feed_shards[FF_FIRST:]
    )
    delta = delta[:HEADS].reshape(KV_HEADS, 2, 2 * SUBS, sub).transpose(0, 2, 1, 3)
    dq, dkv, late_grad, out_grad, output = backward(
        sizes, meta, queries, grad_stack, kv_all, log_total, delta, late, dout, result.reshape(2, rows, D)
    )
    feed_grad = jnp.concatenate([early_grad, late_grad], axis=0)

    def feed_columns(k):
        piece = feed_grad[:, :, k * FF_CHUNK : (k + 1) * FF_CHUNK]
        return piece.transpose(1, 0, 2).reshape(shard_rows, FF)

    query_grad, key_grad, value_grad, gain_grad, input_grad = finish(
        sizes, dq, dkv, pre, normed, x, grad_hidden, in_weight, post_part, qkv_full, query_weight, key_weight, cosine, sine
    )

    def own(line):
        return lax.dynamic_slice_in_dim(line, device * gain_rows, gain_rows)

    return (
        output,
        input_grad.astype(F32),
        gain_grad[:, 0],
        query_grad,
        key_grad,
        value_grad,
        own(gain_grad[0, GAIN_COLS : 2 * GAIN_COLS]),
        own(gain_grad[0, 2 * GAIN_COLS :]),
        out_grad.T,
        gain_grad[:, 1],
        feed_columns(0),
        feed_columns(1),
        feed_columns(2).T,
    )


def solution(mesh):
    dp, ctx = mesh.shape["dp"], mesh.shape["ctx"]
    sizes = (2, dp // 2, ctx // 2)
    return jax.shard_map(
        functools.partial(shards, sizes),
        mesh=mesh,
        in_specs=(
            P("dp", "ctx", None),
            P("dp", "ctx", None),
            P("dp", None),
            P("dp", None),
            P("dp", None),
            P(("dp", "ctx")),
            P(("dp", "ctx"), None),
            P(("dp", "ctx"), None),
            P(("dp", "ctx"), None),
            P(("dp", "ctx")),
            P(("dp", "ctx")),
            P(None, ("dp", "ctx")),
            P(("dp", "ctx")),
            P(("dp", "ctx"), None),
            P(("dp", "ctx"), None),
            P(None, ("dp", "ctx")),
        ),
        out_specs=(
            P("dp", "ctx", None),
            P("dp", "ctx", None),
            P(("dp", "ctx")),
            P(("dp", "ctx"), None),
            P(("dp", "ctx"), None),
            P(("dp", "ctx"), None),
            P(("dp", "ctx")),
            P(("dp", "ctx")),
            P(None, ("dp", "ctx")),
            P(("dp", "ctx")),
            P(("dp", "ctx"), None),
            P(("dp", "ctx"), None),
            P(None, ("dp", "ctx")),
        ),
        check_vma=False,
    )
```

```python
import functools
import math

import jax
import jax.numpy as jnp
from jax import lax
from jax.experimental import pallas as pl
from jax.experimental.pallas import tpu as pltpu
from jax.sharding import PartitionSpec as P

D = 1024
HEADS = 16
KV_HEADS = 8
HEAD_DIM = 128
FF = 3072
TRUNK = 1024
SEG = 128
TREE = 2560
QD = HEADS * HEAD_DIM
KVD = KV_HEADS * HEAD_DIM
SUBS = 5
CHUNK = 256
GAIN_COLS = 128
FF_CHUNK = 512
PAIRS = KV_HEADS // 2
FF_CHUNKS = FF // FF_CHUNK
FF_EARLY = 2
FF_FIRST = 4
LOCAL_RUNS = 3
MIB = 1024 * 1024

eps_norm = 1e-06
rope_base = 1000000.0
exp2_scale = math.log2(math.e) / math.sqrt(HEAD_DIM)
score_scale = HEAD_DIM ** (-0.5)

MESH = pl.DeviceIdType.MESH
ANY = pl.BlockSpec(memory_space=pl.ANY)
F32 = jnp.float32
BF16 = jnp.bfloat16


def matmul(left_side, right_side):
    return jnp.dot(left_side, right_side, preferred_element_type=F32)


def nt(left_side, right_side):
    return lax.dot_general(
        left_side, right_side, (((1,), (1,)), ((), ())), preferred_element_type=F32
    )


def contract_rows(left_side, right_side):
    return lax.dot_general(
        left_side, right_side, (((0,), (0,)), ((), ())), preferred_element_type=F32
    )


def norm_factor(values):
    return lax.rsqrt(jnp.mean(values * values, axis=-1, keepdims=True) + eps_norm)


def norm_backward(grad_out, weight, normed, factor):
    weighted = grad_out * weight
    grad_in = factor * (weighted - normed * jnp.mean(weighted * normed, axis=-1, keepdims=True))
    return (grad_in, grad_out * normed)


def rope_tables(positions):
    steps_half = jnp.arange(HEAD_DIM // 2, dtype=F32)
    inverse = rope_base ** (-(steps_half * 2.0 / HEAD_DIM))
    angles = positions.astype(F32)[:, None] * inverse[None, :]
    cosine, sine = jnp.cos(angles), jnp.sin(angles)
    return jnp.concatenate([cosine, cosine], axis=-1), jnp.concatenate([-sine, sine], axis=-1)


class Links:
    def __init__(self, sizes, send_sem, recv_sem):
        self.sizes = sizes
        self.send_sem = send_sem
        self.recv_sem = recv_sem
        self.index = {}

    def place(self):
        _, nx, _ = self.sizes
        dp, ctx = lax.axis_index("dp"), lax.axis_index("ctx")
        return dp // nx, lax.rem(dp, nx), ctx // 2, lax.rem(ctx, 2)

    def device(self, y, x, z, core):
        return (y * self.sizes[1] + x, z * 2 + core)

    def peers(self, axis, back=False):
        y, x, z, core = self.place()
        at = {"y": y, "x": x, "z": z}
        n = self.sizes["yxz".index(axis)]
        found = []
        for s in range(1, n):
            moved = dict(at)
            moved[axis] = lax.rem(at[axis] + (n - s if back else s), n)
            found.append((moved["y"], moved["x"], moved["z"], core))
        return found

    def sibling(self):
        y, x, z, core = self.place()
        return self.device(y, x, z, 1 - core)

    def across(self):
        y, x, z, core = self.place()
        nz = self.sizes[2]
        return self.device(y, x, lax.rem(z + nz // 2, nz), core)

    def group(self, back=False):
        y, x, z, core = self.place()
        chips = self.sizes[2] // 2
        base = (z // chips) * chips
        here = z - base
        chosen = [lax.rem(here + (chips - s if back else s), chips) for s in range(1, chips)]
        return [(chip, self.device(y, x, base + chip, core)) for chip in chosen]

    def meet(self):
        barrier = pltpu.get_barrier_semaphore()
        partners = [self.device(*p) for a in "zxy" for p in self.peers(a)] + [self.sibling()]
        for partner in partners:
            pl.semaphore_signal(barrier, inc=1, device_id=partner, device_id_type=MESH)
        pl.semaphore_wait(barrier, len(partners))

    def copy(self, key, src, dst, target):
        k = self.index.setdefault(key, len(self.index))
        return pltpu.make_async_remote_copy(
            src_ref=src,
            dst_ref=dst,
            send_sem=self.send_sem.at[k],
            recv_sem=self.recv_sem.at[k],
            device_id=target,
            device_id_type=MESH,
        )


class Exchange:
    def __init__(self, links, source, placed, local_sem, tag="swap"):
        self.tag = tag
        self.links = links
        self.source = source
        self.placed = placed
        self.local_sem = local_sem

    def copies_(self):
        _, _, z, _ = self.links.place()
        half = z // (self.links.sizes[2] // 2)
        return [
            self.links.copy(self.tag, self.source.at[1 - half], self.placed.at[half], self.links.across()),
            pltpu.make_async_copy(self.source.at[half], self.placed.at[half], self.local_sem),
        ]

    def start(self):
        for copy in self.copies_():
            copy.start()

    def wait(self):
        for copy in self.copies_():
            copy.wait()


class Gather:
    def __init__(self, links, tag, shard, whole, order, cols, local_sem):
        self.links = links
        self.tag = tag
        self.shard = shard
        self.whole = whole
        self.order = order
        self.cols = cols
        self.local_sem = local_sem

    def own(self):
        y, x, z, core = self.links.place()
        return self.whole.at[y, x, z, core, :, self.cols]

    def slab(self, stage, at):
        y, x, z, core = at
        if stage == 0:
            return self.whole.at[y, x, z, core, :, self.cols]
        if stage == 1:
            return self.whole.at[y, x, :, core, :, self.cols]
        if self.order[0] == "x":
            return self.whole.at[y, :, :, core, :, self.cols]
        return self.whole.at[:, x, :, core, :, self.cols]

    def axis(self, stage):
        return ("z",) + tuple(self.order)[0:2] if stage is None else ("z", self.order[0], self.order[1])[stage]

    def send(self, stage):
        me = self.links.place()
        src = self.shard.at[:, self.cols] if stage == 0 else self.slab(stage, me)
        dst = self.slab(stage, me)
        return [
            self.links.copy((self.tag, stage, i), src, dst, self.links.device(*p))
            for i, p in enumerate(self.links.peers(self.axis(stage)))
        ]

    def forward(self, stage):
        sibling = self.links.sibling()
        if stage < 0:
            return [self.links.copy((self.tag, "own"), self.shard.at[:, self.cols], self.own(), sibling)]
        return [
            self.links.copy((self.tag, "pass", stage, i), self.slab(stage, p), self.slab(stage, p), sibling)
            for i, p in enumerate(self.links.peers(self.axis(stage), back=True))
        ]

    def local(self):
        return pltpu.make_async_copy(self.shard.at[:, self.cols], self.own(), self.local_sem)

    def start(self):
        self.local().start()
        for copy in self.send(0) + self.forward(-1):
            copy.start()

    def step(self, stage):
        if stage == 1:
            self.local().wait()
        for copy in self.send(stage - 1):
            copy.wait()
        if stage < 3:
            for copy in self.send(stage):
                copy.start()
        for copy in self.forward(stage - 1):
            copy.start()

    def close(self):
        for stage in range(-1, 3):
            for copy in self.forward(stage):
                copy.wait()

    @staticmethod
    def copies(sizes):
        return 2 * sum(n - 1 for n in sizes) + 1


class Scatter:
    def __init__(self, links, tag, part, order, cols, halves, firsts, seconds, thirds, temp, temp_sem, out):
        self.links = links
        self.tag = tag
        self.part = part
        self.order = order
        self.cols = cols
        self.sums = halves
        self.got = (firsts, seconds, thirds)
        self.temp = temp
        self.temp_sem = temp_sem
        self.out = out

    def first(self):
        _, _, _, core = self.links.place()
        return self.links.copy(
            (self.tag, "core"), self.part.at[:, :, :, 1 - core, :, self.cols], self.sums, self.links.sibling()
        )

    def load(self):
        _, _, _, core = self.links.place()
        return pltpu.make_async_copy(
            self.part.at[:, :, :, core, :, self.cols], self.temp, self.temp_sem
        )

    def axis(self, stage):
        return (self.order[0], self.order[1], "z")[stage]

    def at(self, stage, place, rest=None):
        y, x, z, _ = place
        if stage == 0:
            return (y,) if self.order[0] == "y" else (slice(None), x)
        if stage == 1:
            return (y, x)
        return (y, x, z)

    def send(self, stage):
        me = self.links.place()
        found = []
        for i, p in enumerate(self.links.peers(self.axis(stage))):
            index = self.at(stage, p)
            found.append(
                self.links.copy(
                    (self.tag, stage, i), self.sums.at[index], self.got[stage].at[i], self.links.device(*p)
                )
            )
        return found

    def start(self):
        self.first().start()

    def begin(self):
        self.first().wait()
        if self.temp_sem is not None:
            self.load().wait()
        ny, nx, nz = self.links.sizes

        def add(i, carry):
            a, b, c = i // (nx * nz), lax.rem(i // nz, nx), lax.rem(i, nz)
            self.sums[a, b, c] = (
                self.sums[a, b, c].astype(F32) + self.temp[a, b, c].astype(F32)
            ).astype(BF16)
            return carry

        lax.fori_loop(0, ny * nx * nz, add, 0)
        for copy in self.send(0):
            copy.start()

    def middle(self, stage):
        for copy in self.send(stage):
            copy.wait()
        y, x, z, _ = self.links.place()
        _, _, nz = self.links.sizes
        got = self.got[stage]
        peers = got.shape[0]
        if stage == 0:
            other = got.shape[1]

            def add(i, carry):
                b, c = i // nz, lax.rem(i, nz)
                index = (y, b, c) if self.order[0] == "y" else (b, x, c)
                total = self.sums[index].astype(F32)
                for p in range(peers):
                    total = total + got[p, b, c].astype(F32)
                self.sums[index] = total.astype(BF16)
                return carry

            lax.fori_loop(0, other * nz, add, 0)
        else:

            def add(c, carry):
                total = self.sums[y, x, c].astype(F32)
                for p in range(peers):
                    total = total + got[p, c].astype(F32)
                self.sums[y, x, c] = total.astype(BF16)
                return carry

            lax.fori_loop(0, nz, add, 0)
        for copy in self.send(stage + 1):
            copy.start()

    def finish(self):
        for copy in self.send(2):
            copy.wait()
        y, x, z, _ = self.links.place()
        total = self.sums[y, x, z].astype(F32)
        for p in range(self.got[2].shape[0]):
            total = total + self.got[2][p].astype(F32)
        if callable(self.out):
            self.out(total)
        else:
            self.out[:, self.cols] = total

    @staticmethod
    def copies(sizes):
        return sum(n - 1 for n in sizes) + 1

    @staticmethod
    def scratch(sizes, order, rows, width):
        ny, nx, nz = sizes
        na, nb = (ny, nx) if order[0] == "y" else (nx, ny)
        return [
            pltpu.VMEM((ny, nx, nz, rows, width), BF16),
            pltpu.VMEM((na - 1, nb, nz, rows, width), BF16),
            pltpu.VMEM((nb - 1, nz, rows, width), BF16),
            pltpu.VMEM((nz - 1, rows, width), BF16),
        ]


ORDERS = ("xy", "yx")

FORWARD_START = [
    ("swap", "tokens"), (0, 9), (0, 0), (1, 9), (1, 0), (2, 9), (2, 0), (0, 1), (0, 2), (3, 9), (4, 9), (3, 0),
    (1, 1), (1, 2), (0, 3), (2, 1), (0, 4), ("swapped", "tokens"),
]
FORWARD_AFTER = {
    0: [("kv", 0), (2, 2), (1, 3), (3, 1), (1, 4), (0, 5)],
    1: [("kv", 1), (3, 2), (2, 3), (2, 4), (1, 5), (0, 6)],
    2: [("use", 0), (3, 3), (3, 4), (2, 5), (1, 6), ("swap", "cot")],
    3: [("got", 0), ("kv", 2), (0, 7), (3, 5), (2, 6)],
    4: [("use", 1), ("got", 1), ("kv", 3), (1, 7), (0, 8)],
    5: [(3, 6), (2, 7)],
    6: [("use", 2), (1, 8)],
    7: [("got", 2), (3, 7), (2, 8)],
    8: [("use", 3)],
    9: [("got", 3), (3, 8)],
    11: [("swapped", "cot")],
}
FEED_START = [("fetch", 0), ("send", (0, 4)), ("fetch", 1)]
FEED_NEXT = [("send", (1, 4)), ("send", (0, 5))]
FEED_MIDDLE = {
    0: [("send", (2, 4))],
    1: [("send", (3, 4)), ("send", (2, 5)), ("fetch", 2)],
    2: [("send", (3, 5)), ("fetch", 3)],
    3: [("fetch", 4)],
    4: [("fetch", 5)],
    5: [(1, 1)],
}
FEED_AFTER = {
    0: [("send", (1, 5)), ("core", 0)],
    1: [("begin", 0), ("core", 1)],
    2: [("begin", 1)],
    3: [(0, 0), (0, 1)],
    4: [(1, 0)],
}
FEED_LAST = []
FINISH_MIDDLE = {
    1: [("begin", 0)],
    2: [("begin", 1), (1, 0)],
    3: [("begin", 2), (1, 1)],
}
FINISH_AFTER = {
    0: [("core", 0)],
    1: [("core", 1), (0, 0)],
    2: [("core", 2), (0, 1)],
    3: [("core", 3)],
}
BACKWARD_AFTER = {
    0: [(0, 0)],
    1: [(1, 0), (0, 1)],
    2: [(2, 0), (1, 1), (0, 2)],
    3: [(2, 1), (1, 2), (0, 3)],
    4: [(2, 2), (1, 3), (0, 4)],
    5: [(2, 3), (1, 4)],
    6: [(2, 4)],
}


def halves_of(width):
    return (slice(0, width // 2), slice(width // 2, width)) if width >= 512 else (slice(0, width),)


def roll_half(values):
    return pltpu.roll(values, HEAD_DIM // 2, 1)


class KeyValues:
    def __init__(self, links, rows, held):
        self.links = links
        self.rows = rows
        self.held = held

    def slab(self, group, piece, member):
        members = self.links.sizes[2]
        start = pl.multiple_of(self.rows * (piece * members + member), self.rows)
        return self.held.at[:, 2 * group : 2 * group + 2, pl.ds(start, self.rows)]

    def mine(self):
        _, _, z, core = self.links.place()
        return lax.rem(z, self.links.sizes[2] // 2) * 2 + core

    def across(self, group):
        found = []
        for piece in range(2):
            slab = self.slab(group, piece, self.mine())
            for i, (_, target) in enumerate(self.links.group()):
                found.append(self.links.copy(("kv", group, piece, i), slab, slab, target))
        return found

    def near(self, group):
        found = []
        for piece in range(2):
            slab = self.slab(group, piece, self.mine())
            found.append(self.links.copy(("kv own", group, piece), slab, slab, self.links.sibling()))
        return found

    def forward(self, group):
        _, _, _, core = self.links.place()
        found = []
        for piece in range(2):
            for i, (chip, _) in enumerate(self.links.group(back=True)):
                slab = self.slab(group, piece, chip * 2 + core)
                found.append(
                    self.links.copy(("kv pass", group, piece, i), slab, slab, self.links.sibling())
                )
        return found

    @staticmethod
    def copies(sizes):
        return 4 * 2 * (2 * (sizes[2] // 2 - 1) + 1)


def run_all(copies, act):
    for copy in copies:
        if act == "start":
            copy.start()
        else:
            copy.wait()


def row_places(shape, dim, sub):
    t = lax.broadcasted_iota(jnp.int32, shape, dim)
    return (t // (2 * sub)) * sub + t % sub


def block_copies(sizes, src, dst, sem):
    ny, nx, nz = sizes
    shard_rows = src.shape[-2]
    found = []
    for i in range(ny * nx * nz * 2):
        block = src.at[i // (nx * nz * 2), i // (nz * 2) % nx, i // 2 % nz, i % 2]
        found.append(pltpu.make_async_copy(block, dst.at[i * shard_rows : (i + 1) * shard_rows], sem))
    return found


def gather_parents(meta, lead, slot, pairs):
    runs = (TREE - TRUNK) // SEG
    for k in range(LOCAL_RUNS):
        parent = meta[jnp.minimum(lead + k, runs - 1)]
        for read, out in pairs:
            total = None
            for b in range(runs):
                share = (1 - jnp.minimum(jnp.abs(parent - b), 1)).astype(F32).astype(BF16)
                term = read(b) * share
                total = term if total is None else total + term
            out[slot + k] = total


def forward_kernel(sizes, rows, meta, cos_ref, sin_ref, tok_ref, cot_ref, *refs):
    arrays = PAIRS + 2 + FF_FIRST
    shard = refs[:arrays]
    (mixed_ref, l_ref, pre_ref, normed_ref, gains_ref, qk_ref,
     placed, cot_placed, q_all, kv_all, qkv_whole, gain_whole, out_whole, feed_whole) = refs[arrays : arrays + 14]
    whole = (
        tuple(qkv_whole.at[c] for c in range(PAIRS))
        + (out_whole,)
        + tuple(feed_whole.at[c] for c in range(FF_FIRST))
        + (gain_whole,)
    )
    (qs, kvs, xs, ws, gs, acc, part, places, kp, vp, send_sem, recv_sem, local_sem) = refs[arrays + 14 :]
    members = sizes[2]
    sub = rows // SUBS
    count = 2 * rows
    step = pl.program_id(0)
    head = jnp.maximum(step - PAIRS, 0)
    links = Links(sizes, send_sem, recv_sem)
    kv = KeyValues(links, rows, kvs)
    swaps = {
        "tokens": Exchange(links, tok_ref, placed, local_sem.at[0], "tokens"),
        "cot": Exchange(links, cot_ref, cot_placed, local_sem.at[1], "cot"),
    }
    weights_ = [
        [
            Gather(links, (a, b), shard[a], whole[a], ORDERS[b], cols, local_sem.at[12 + 2 * a + b])
            for b, cols in enumerate(halves_of(shard[a].shape[-1]))
        ]
        for a in range(arrays)
    ]
    _, _, z, core = links.place()
    mine = lax.rem(z, members // 2) * 2 + core

    def kept(group):
        pair = slice(2 * group, 2 * group + 2)
        return [
            pltpu.make_async_copy(kvs.at[:, pair], kv_all.at[:, pair], local_sem.at[2 + group]),
            pltpu.make_async_copy(qs.at[pair], q_all.at[pair], local_sem.at[6 + group]),
        ]

    def act(steps):
        for what, a in steps:
            if what == "swap":
                swaps[a].start()
            elif what == "swapped":
                swaps[a].wait()
            elif what == "kv":
                run_all(kv.across(a), "start")
                run_all(kv.near(a), "start")
            elif what == "use":
                run_all(kv.across(a), "wait")
                run_all(kv.forward(a), "start")
            elif what == "got":
                run_all(kv.near(a), "wait")
                run_all(kv.forward(a), "wait")
                run_all(kept(a), "start")
            else:
                for g in weights_[a]:
                    if what == 0:
                        g.start()
                    elif what == 4:
                        g.close()
                    else:
                        g.step(what)

    @pl.when(step == 0)
    def _():
        links.meet()
        act(FORWARD_START)
        l_ref[...] = jnp.zeros_like(l_ref)
        places[...] = row_places(places.shape, 0, sub)
        run_all(block_copies(sizes, gain_whole, gs, local_sem.at[10]), "start")
        pltpu.make_async_copy(gs, gs, local_sem.at[10]).wait()
        loaded = pltpu.make_async_copy(placed, xs, local_sem.at[11])
        loaded.start()
        gains_ref[...] = gs[:, :GAIN_COLS].astype(F32).T[:8]
        qk_ref[0:1] = jnp.sum(gs[:, GAIN_COLS : 2 * GAIN_COLS].astype(F32), axis=0, keepdims=True)
        qk_ref[1:2] = jnp.sum(gs[:, 2 * GAIN_COLS :].astype(F32), axis=0, keepdims=True)
        loaded.wait()
        values = xs[...].reshape(count, D).astype(F32)
        normed_ref[...] = (values * norm_factor(values) * gains_ref[0:1]).astype(BF16)

    for c in range(PAIRS):

        @pl.when(step == c)
        def _():
            act([(4, c)])
            run_all(block_copies(sizes, qkv_whole.at[c], ws, local_sem.at[10]), "start")
            pltpu.make_async_copy(ws, ws, local_sem.at[10]).wait()

    @pl.when(step < PAIRS)
    def _():
        normed = normed_ref[...]
        cosine, sine = cos_ref[...], sin_ref[...]

        def turned(pre, gain):
            values = pre * norm_factor(pre) * gain
            return (values * cosine + roll_half(values) * sine).astype(BF16)

        for hh in range(2):
            at = 2 * step + hh
            query = matmul(normed, ws[:, 2 * hh * HEAD_DIM : 2 * (hh + 1) * HEAD_DIM])
            for h in range(2):
                pre = query[:, h * HEAD_DIM : (h + 1) * HEAD_DIM]
                pre_ref[hh, :, h * HEAD_DIM : (h + 1) * HEAD_DIM] = pre
                low = turned(pre, qk_ref[0:1])
                for s in range(2 * SUBS):
                    qs[at, (2 * s + h) * sub : (2 * s + h + 1) * sub] = low[s * sub : (s + 1) * sub]
            pre = matmul(normed, ws[:, (4 + hh) * HEAD_DIM : (5 + hh) * HEAD_DIM])
            pre_ref[hh, :, 2 * HEAD_DIM :] = pre
            low = turned(pre, qk_ref[1:2])
            value = matmul(normed, ws[:, (6 + hh) * HEAD_DIM : (7 + hh) * HEAD_DIM]).astype(BF16)
            for piece in range(2):
                start = pl.multiple_of(rows * (piece * members + mine), rows)
                kvs[0, at, pl.ds(start, rows)] = low[piece * rows : (piece + 1) * rows]
                kvs[1, at, pl.ds(start, rows)] = value[piece * rows : (piece + 1) * rows]

    def attend():
        lane = lax.broadcasted_iota(jnp.int32, (2 * rows, HEAD_DIM), 1)
        for piece in range(2):
            base = rows * (piece * members + mine)
            region = slice(piece * 2 * rows, (piece + 1) * 2 * rows)
            acc[...] = jnp.zeros_like(acc)
            part[...] = jnp.zeros_like(part)

            def trunk(step, masked):
                start = pl.multiple_of(step * CHUNK, CHUNK)
                weights = jnp.exp2(nt(qs[head, region], kvs[0, head, pl.ds(start, CHUNK)]) * exp2_scale)
                low, high = weights[:, :HEAD_DIM], weights[:, HEAD_DIM:]
                if masked:
                    room = places[...] + (base - start)
                    low = jnp.where(lane <= room, low, 0.0)
                    high = jnp.where(lane + HEAD_DIM <= room, high, 0.0)
                    weights = jnp.concatenate([low, high], axis=1)
                part[...] += low + high
                acc[...] += matmul(weights.astype(BF16), kvs[1, head, pl.ds(start, CHUNK)])
                return masked

            if piece == 0:
                clear = jnp.minimum(base // CHUNK, TRUNK // CHUNK)
                last = jnp.minimum((base + rows + CHUNK - 1) // CHUNK, TRUNK // CHUNK)
                lax.fori_loop(0, clear, lambda i, c: (trunk(i, False), c)[1], 0)
                lax.fori_loop(clear, last, lambda i, c: (trunk(i, True), c)[1], 0)
            else:
                lax.fori_loop(0, TRUNK // CHUNK, lambda i, c: (trunk(i, False), c)[1], 0)

            lead = jnp.maximum(base - TRUNK, 0) // SEG

            def parents_():
                gather_parents(
                    meta,
                    lead,
                    0,
                    [
                        (lambda b: kvs[0, head, TRUNK + b * SEG : TRUNK + (b + 1) * SEG], kp),
                        (lambda b: kvs[1, head, TRUNK + b * SEG : TRUNK + (b + 1) * SEG], vp),
                    ],
                )

            if piece == 0:
                pl.when(base + rows > TRUNK)(parents_)
            else:
                parents_()
            for s in range(SUBS):
                block = slice(2 * sub * s, 2 * sub * (s + 1))

                def runs():
                    row = base + s * sub - TRUNK
                    run = row // SEG
                    own = pl.multiple_of(TRUNK + run * SEG, SEG)
                    flag = jnp.minimum(meta[run] + 1, 1).astype(F32)
                    query = qs[head, piece * 2 * rows + 2 * sub * s : piece * 2 * rows + 2 * sub * (s + 1)]
                    room = places[block] + (lax.rem(row, SEG) - s * sub)
                    weights = jnp.exp2(nt(query, kvs[0, head, pl.ds(own, SEG)]) * exp2_scale)
                    weights = jnp.where(lane[block] <= room, weights, 0.0)
                    above = jnp.exp2(nt(query, kp[run - lead]) * exp2_scale) * flag
                    part[block] += weights + above
                    acc[block] += matmul(weights.astype(BF16), kvs[1, head, pl.ds(own, SEG)]) + matmul(
                        above.astype(BF16), vp[run - lead]
                    )

                if piece == 0:
                    pl.when(base + s * sub >= TRUNK)(runs)
                else:
                    runs()

            total = jnp.sum(part[...], axis=-1, keepdims=True)
            mixed = (acc[...] / total).astype(BF16)
            for s in range(SUBS):
                for h in range(2):
                    row = piece * rows + sub * s
                    mixed_ref[row : row + sub, h * HEAD_DIM : (h + 1) * HEAD_DIM] = mixed[
                        (2 * s + h) * sub : (2 * s + h + 1) * sub
                    ]
            l_ref[region] = jnp.where(lane == head, total, l_ref[region])


    pl.when(step >= PAIRS)(attend)
    for moment, steps in FORWARD_AFTER.items():
        pl.when(step == moment)(functools.partial(act, steps))

    @pl.when(step == PAIRS + KV_HEADS - 1)
    def _():
        for array in weights_[PAIRS : PAIRS + 1 + FF_FIRST]:
            for g in array:
                g.close()
        for group in range(4):
            run_all(kept(group), "wait")


def forward(sizes, meta, cosine, sine, tokens, cotangent, shards_):
    ny, nx, nz = sizes
    rows = tokens.shape[1]
    count = 2 * rows
    arrays = PAIRS + 2 + FF_FIRST
    shard_rows = shards_[0].shape[0]
    blocks = (ny, nx, nz, 2, shard_rows)
    widths = [w.shape[-1] for w in shards_]
    rounds = KeyValues.copies(sizes) + 2 * arrays * Gather.copies(sizes) + 2

    def at_head(s):
        return jnp.maximum(s - PAIRS, 0)

    results = pl.pallas_call(
        functools.partial(forward_kernel, sizes, rows),
        out_shape=[
            jax.ShapeDtypeStruct((count, QD), BF16),
            jax.ShapeDtypeStruct((2 * count, HEAD_DIM), F32),
            jax.ShapeDtypeStruct((KV_HEADS, count, 3 * HEAD_DIM), F32),
            jax.ShapeDtypeStruct((count, D), BF16),
            jax.ShapeDtypeStruct((8, D), F32),
            jax.ShapeDtypeStruct((8, HEAD_DIM), F32),
            jax.ShapeDtypeStruct(tokens.shape, BF16),
            jax.ShapeDtypeStruct(tokens.shape, BF16),
            jax.ShapeDtypeStruct((KV_HEADS, 2 * count, HEAD_DIM), BF16),
            jax.ShapeDtypeStruct((2, KV_HEADS, TREE, HEAD_DIM), BF16),
            jax.ShapeDtypeStruct((PAIRS,) + blocks + (widths[0],), BF16),
            jax.ShapeDtypeStruct(blocks + (widths[-1],), BF16),
            jax.ShapeDtypeStruct(blocks + (widths[PAIRS],), BF16),
            jax.ShapeDtypeStruct((FF_FIRST,) + blocks + (widths[PAIRS + 1],), BF16),
        ],
        grid_spec=pltpu.PrefetchScalarGridSpec(
            num_scalar_prefetch=1,
            grid=(PAIRS + KV_HEADS,),
            in_specs=[pl.BlockSpec((count, HEAD_DIM), lambda s, meta: (0, 0))] * 2 + [ANY] * (2 + arrays),
            out_specs=[
                pl.BlockSpec((count, 2 * HEAD_DIM), lambda s, meta: (0, at_head(s))),
                pl.BlockSpec((2 * count, HEAD_DIM), lambda s, meta: (0, 0)),
                pl.BlockSpec((2, count, 3 * HEAD_DIM), lambda s, meta: (jnp.minimum(s, PAIRS - 1), 0, 0)),
                pl.BlockSpec((count, D), lambda s, meta: (0, 0)),
                pl.BlockSpec((8, D), lambda s, meta: (0, 0)),
                pl.BlockSpec((8, HEAD_DIM), lambda s, meta: (0, 0)),
            ]
            + [ANY] * 8,
            scratch_shapes=[
                pltpu.VMEM((KV_HEADS, 2 * count, HEAD_DIM), BF16),
                pltpu.VMEM((2, KV_HEADS, TREE, HEAD_DIM), BF16),
                pltpu.VMEM(tokens.shape, BF16),
                pltpu.VMEM((D, widths[0]), BF16),
                pltpu.VMEM((D, widths[-1]), BF16),
                pltpu.VMEM((count, HEAD_DIM), F32),
                pltpu.VMEM((count, HEAD_DIM), F32),
                pltpu.VMEM((count, HEAD_DIM), jnp.int32),
                pltpu.VMEM((LOCAL_RUNS, SEG, HEAD_DIM), BF16),
                pltpu.VMEM((LOCAL_RUNS, SEG, HEAD_DIM), BF16),
                pltpu.SemaphoreType.DMA((rounds,)),
                pltpu.SemaphoreType.DMA((rounds,)),
                pltpu.SemaphoreType.DMA((12 + 2 * arrays,)),
            ],
        ),
        compiler_params=pltpu.CompilerParams(
            collective_id=2, has_side_effects=True, vmem_limit_bytes=56 * MIB
        ),
        name="forward",
    )(meta, cosine, sine, tokens, cotangent, *shards_)
    return results


def feed_kernel(
    sizes, rows, x_ref, mixed_ref, cot_ref, out_ref, gain_ref, first_ref, *refs,
):
    shard = refs[: FF_CHUNKS - FF_FIRST]
    refs = refs[FF_CHUNKS - FF_FIRST :]
    result_ref, hid_ref, stack_ref, delta_ref, post_ref, dout_ref, late_ref, rest_ref, early_ref = refs[:9]
    hidden, second, second_t, cot_t, total, grads, inner, gate_up, low, stack, part, wbuf = refs[9:21]
    buffers = refs[21:-3]
    send_sem, recv_sem, local_sem = refs[-3:]
    ny, nx, nz = sizes
    count = 2 * rows
    sub = rows // SUBS
    shard_rows = part.shape[5]
    width = 3 * FF_CHUNK
    tile = 256
    chunk = pl.program_id(0)
    links = Links(sizes, send_sem, recv_sem)
    _, _, _, core = links.place()
    scatters = []
    for c in range(FF_EARLY):
        for b, cols in enumerate(halves_of(width)):
            k = 4 * len(scatters)
            scatters.append(
                Scatter(
                    links,
                    (c, b),
                    part.at[c % 2],
                    ORDERS[b],
                    cols,
                    *buffers[k : k + 4],
                    part.at[c % 2, :, :, :, core, :, cols],
                    None,
                    early_ref.at[c],
                )
            )

    gathers = [
        [
            Gather(links, ("w", c, b), shard[c], rest_ref.at[c], ORDERS[b], cols, local_sem.at[8 + 2 * c + b])
            for b, cols in enumerate(halves_of(width))
        ]
        for c in range(FF_CHUNKS - FF_FIRST)
    ]

    def fetch(c):
        if c < FF_FIRST:
            pltpu.make_async_copy(first_ref.at[c], wbuf.at[c % 2], local_sem.at[6 + c % 2]).start()
        else:
            for g in gathers[c - FF_FIRST]:
                g.close()
            run_all(
                block_copies(sizes, rest_ref.at[c - FF_FIRST], wbuf.at[c % 2], local_sem.at[6 + c % 2]), "start"
            )

    def act(steps):
        for what, c in steps:
            if what == "fetch":
                fetch(c)
                continue
            if what == "send":
                for g in gathers[c[1] - FF_FIRST]:
                    if c[0] == 0:
                        g.start()
                    else:
                        g.step(c[0])
                continue
            for s in scatters[2 * c : 2 * c + 2]:
                if what == "core":
                    s.start()
                elif what == "begin":
                    s.begin()
                elif what == "finish":
                    s.finish()
                else:
                    s.middle(what)

    def rows_of(block):
        return (block // (2 * nz * nx), lax.rem(block // (2 * nz), nx), lax.rem(block // 2, nz), lax.rem(block, 2))

    def put(slot, first, cols, value):
        for k in range(value.shape[0] // shard_rows):
            y, x, z, c = rows_of(first // shard_rows + k)
            part[slot, y, x, z, c, :, cols] = value[k * shard_rows : (k + 1) * shard_rows].astype(BF16)

    def late(c):
        return pltpu.make_async_copy(part.at[c % 2], late_ref.at[c - FF_EARLY], local_sem.at[c % 2])

    @pl.when(chunk == 0)
    def _():
        links.meet()
        act(FEED_START)

        def project_out(t, carry):
            at = pl.multiple_of(t * tile, tile)
            hidden[:, pl.ds(at, tile)] = x_ref[:, pl.ds(at, tile)].astype(F32) + nt(
                mixed_ref[...], out_ref[pl.ds(at, tile), :]
            )
            return carry

        lax.fori_loop(0, D // tile, project_out, 0)
        act(FEED_NEXT)
        values = hidden[...]
        values = values * norm_factor(values) * gain_ref[1:2]
        second[...] = values.astype(BF16)
        second_t[...] = values.T.astype(BF16)
        cot_t[...] = cot_ref[...].astype(F32).T.astype(BF16)
        total[...] = jnp.zeros_like(total)
        grads[...] = jnp.zeros_like(grads)

    slot = lax.rem(chunk, 2)
    pltpu.make_async_copy(wbuf.at[slot], wbuf.at[slot], local_sem.at[6 + slot]).wait()

    def columns(t, carry):
        at = pl.multiple_of(t * tile, tile)
        gate = matmul(second[...], wbuf[slot, :, pl.ds(at, tile)])
        up = matmul(second[...], wbuf[slot, :, pl.ds(FF_CHUNK + at, tile)])
        grad = matmul(cot_ref[...], wbuf[slot, :, pl.ds(2 * FF_CHUNK + at, tile)])
        sigmoid = 1.0 / (1.0 + jnp.exp(-gate))
        active = gate * sigmoid
        inner[:, pl.ds(at, tile)] = (active * up).astype(BF16)
        gate_up[:, pl.ds(at, tile)] = (grad * up * sigmoid * (1.0 + gate * (1.0 - sigmoid))).astype(BF16)
        gate_up[:, pl.ds(FF_CHUNK + at, tile)] = (grad * active).astype(BF16)
        return carry

    lax.fori_loop(0, FF_CHUNK // tile, columns, 0)
    for moment, steps in FEED_MIDDLE.items():
        pl.when(chunk == moment)(functools.partial(act, steps))
    for c in range(FF_EARLY, FF_CHUNKS - 2):
        pl.when(chunk == c + 2)(lambda: late(c).wait())

    def model(t, carry):
        at = pl.multiple_of(t * tile, tile)
        total[:, pl.ds(at, tile)] += nt(inner[...], wbuf[slot, pl.ds(at, tile), 2 * FF_CHUNK :])
        grads[:, pl.ds(at, tile)] += nt(gate_up[...], wbuf[slot, pl.ds(at, tile), : 2 * FF_CHUNK])
        put(slot, at, slice(0, 2 * FF_CHUNK), matmul(second_t[pl.ds(at, tile)], gate_up[...]))
        put(slot, at, slice(2 * FF_CHUNK, width), matmul(cot_t[pl.ds(at, tile)], inner[...]))
        return carry

    lax.fori_loop(0, D // tile, model, 0)
    for c in range(FF_EARLY, FF_CHUNKS):
        pl.when(chunk == c)(lambda: late(c).start())
    for moment, steps in FEED_AFTER.items():
        pl.when(chunk == moment)(functools.partial(act, steps))

    @pl.when(chunk == FF_CHUNKS - 1)
    def _():
        values = hidden[...]
        low[...] = (values + total[...]).astype(BF16)
        output = pltpu.make_async_copy(low, result_ref, local_sem.at[2])
        output.start()
        factor = norm_factor(values)
        grad_in, share = norm_backward(grads[...], gain_ref[1:2], values * factor, factor)
        post_ref[...] = jnp.sum(share, axis=0, keepdims=True)
        hidden[...] = cot_ref[...].astype(F32) + grad_in
        saved = pltpu.make_async_copy(hidden, hid_ref, local_sem.at[3])
        saved.start()
        second[...] = hidden[...].astype(BF16)
        second_t[...] = hidden[...].T.astype(BF16)
        lane = lax.broadcasted_iota(jnp.int32, (count, HEAD_DIM), 1)
        dots = jnp.zeros((count, HEAD_DIM), F32)
        for h in range(KV_HEADS):
            cols = slice(2 * h * HEAD_DIM, 2 * (h + 1) * HEAD_DIM)
            grad = matmul(second[...], out_ref[:, cols]).astype(BF16)
            for g in range(2):
                one = grad[:, g * HEAD_DIM : (g + 1) * HEAD_DIM]
                for s in range(2 * SUBS):
                    stack[h, (2 * s + g) * sub : (2 * s + g + 1) * sub] = one[s * sub : (s + 1) * sub]
                head = 2 * h + g
                product = one.astype(F32) * mixed_ref[:, head * HEAD_DIM : (head + 1) * HEAD_DIM].astype(F32)
                dots = jnp.where(lane == head, jnp.sum(product, axis=-1, keepdims=True), dots)
        delta_ref[...] = dots.T
        stacked_ = pltpu.make_async_copy(stack, stack_ref, local_sem.at[4])
        stacked_.start()
        act(FEED_LAST)
        for c in range(FF_CHUNKS - 2, FF_CHUNKS):
            late(c).wait()

        def model_out(t, carry):
            at = pl.multiple_of(t * tile, tile)
            for a in range(0, QD, 2 * FF_CHUNK):
                cols = slice(a, a + 2 * FF_CHUNK)
                value = matmul(second_t[pl.ds(at, tile)], mixed_ref[:, cols])
                slot = a // (2 * FF_CHUNK)
                put(slot, at, slice(0, 2 * FF_CHUNK), value)
            return carry

        lax.fori_loop(0, D // tile, model_out, 0)
        gone = [
            pltpu.make_async_copy(
                part.at[k, :, :, :, :, :, : 2 * FF_CHUNK],
                dout_ref.at[:, :, :, :, :, 2 * FF_CHUNK * k : 2 * FF_CHUNK * (k + 1)],
                local_sem.at[k],
            )
            for k in range(2)
        ]
        run_all(gone, "start")
        for c in range(FF_EARLY):
            act([("finish", c)])
        run_all(gone + [output, saved, stacked_], "wait")


def feed(sizes, x, mixed, cot, out_t, gain, first, shards_):
    ny, nx, nz = sizes
    count = x.shape[0]
    rows = count // 2
    shard_rows = D // (ny * nx * nz * 2)
    width = 3 * FF_CHUNK
    buffers = []
    for c in range(FF_EARLY):
        for b, cols in enumerate(halves_of(width)):
            buffers += Scatter.scratch(sizes, ORDERS[b], shard_rows, cols.stop - cols.start)
    late = FF_CHUNKS - FF_FIRST
    rounds = 2 * FF_EARLY * Scatter.copies(sizes) + 2 * late * Gather.copies(sizes)

    def whole_block(shape):
        return pl.BlockSpec(shape, lambda c: (0,) * len(shape), pipeline_mode=pl.Buffered(1))

    blocks = (ny, nx, nz, 2, shard_rows)
    return pl.pallas_call(
        functools.partial(feed_kernel, sizes, rows),
        grid=(FF_CHUNKS,),
        out_shape=[
            jax.ShapeDtypeStruct((count, D), BF16),
            jax.ShapeDtypeStruct((count, D), F32),
            jax.ShapeDtypeStruct((KV_HEADS, 2 * count, HEAD_DIM), BF16),
            jax.ShapeDtypeStruct((HEAD_DIM, count), F32),
            jax.ShapeDtypeStruct((1, D), F32),
            jax.ShapeDtypeStruct(blocks + (QD,), BF16),
            jax.ShapeDtypeStruct((FF_CHUNKS - FF_EARLY,) + blocks + (width,), BF16),
            jax.ShapeDtypeStruct((late,) + blocks + (width,), BF16),
            jax.ShapeDtypeStruct((FF_EARLY, shard_rows, width), F32),
        ],
        in_specs=[
            whole_block((count, D)),
            whole_block((count, QD)),
            whole_block((count, D)),
            whole_block((D, QD)),
            whole_block((8, D)),
            ANY,
        ]
        + [ANY] * late,
        out_specs=[
            ANY,
            ANY,
            ANY,
            pl.BlockSpec((HEAD_DIM, count), lambda c: (0, 0)),
            pl.BlockSpec((1, D), lambda c: (0, 0)),
            ANY,
            ANY,
            ANY,
            pl.BlockSpec((FF_EARLY, shard_rows, width), lambda c: (0, 0, 0)),
        ],
        scratch_shapes=[
            pltpu.VMEM((count, D), F32),
            pltpu.VMEM((count, D), BF16),
            pltpu.VMEM((D, count), BF16),
            pltpu.VMEM((D, count), BF16),
            pltpu.VMEM((count, D), F32),
            pltpu.VMEM((count, D), F32),
            pltpu.VMEM((count, FF_CHUNK), BF16),
            pltpu.VMEM((count, 2 * FF_CHUNK), BF16),
            pltpu.VMEM((count, D), BF16),
            pltpu.VMEM((KV_HEADS, 2 * count, HEAD_DIM), BF16),
            pltpu.VMEM((2,) + blocks + (width,), BF16),
            pltpu.VMEM((2, D, width), BF16),
        ]
        + buffers
        + [
            pltpu.SemaphoreType.DMA((rounds,)),
            pltpu.SemaphoreType.DMA((rounds,)),
            pltpu.SemaphoreType.DMA((8 + 2 * late,)),
        ],
        compiler_params=pltpu.CompilerParams(
            collective_id=5, has_side_effects=True, vmem_limit_bytes=61 * MIB
        ),
        name="feed",
    )(x, mixed, cot, out_t, gain, first, *shards_)


def backward_kernel(sizes, rows, widths, meta, q_ref, g_ref, k_ref, v_ref, lse_ref, del_ref, late_ref, dout_ref, done_ref, *refs):
    dq_ref, dkv_ref, late_out, dout_out, done_placed = refs[:5]
    dq, dk, dv, pk, pv, kp, vp, stage, near, sums, far, last = refs[5:17]
    buffers = refs[17:-3]
    send_sem, recv_sem, local_sem = refs[-3:]
    members = sizes[2]
    chips = members // 2
    sub = rows // SUBS
    head = pl.program_id(0)
    links = Links(sizes, send_sem, recv_sem)
    scatters = []
    late = FF_CHUNKS - FF_EARLY
    for a, width in enumerate(widths):
        for b, cols in enumerate(halves_of(width)):
            k = 5 * len(scatters)
            scatters.append(
                Scatter(
                    links,
                    (a, b),
                    late_ref.at[a] if a < late else dout_ref,
                    ORDERS[b],
                    cols,
                    *buffers[k : k + 5],
                    local_sem.at[2 + len(scatters)],
                    late_out.at[a] if a < late else dout_out,
                )
            )

    swap = Exchange(links, done_ref, done_placed, local_sem.at[2 + len(scatters)])

    def each(array):
        return scatters[2 * array : 2 * array + 2]

    @pl.when(head == 0)
    def _():
        for s in scatters:
            s.load().start()
        links.meet()
        for s in scatters:
            s.start()
        swap.start()

    _, _, z, core = links.place()
    here = lax.rem(z, chips)
    mine = here * 2 + core
    dk[...] = jnp.zeros_like(dk)
    dv[...] = jnp.zeros_like(dv)
    pk[...] = jnp.zeros_like(pk)
    pv[...] = jnp.zeros_like(pv)
    for piece in range(2):
        base = rows * (piece * members + mine)
        at = piece * 2 * rows
        region = slice(at, at + 2 * rows)
        dq[...] = jnp.zeros_like(dq)

        def pair(key, value, block, mask):
            spot = slice(at + block.start, at + block.stop)
            weights = jnp.exp2(nt(key, q_ref[0, spot]) * exp2_scale - lse_ref[0, :, spot])
            if mask is not None:
                weights = mask(weights)
            grads = (weights * (nt(value, g_ref[0, spot]) - del_ref[0, :, spot])).astype(BF16)
            weights = weights.astype(BF16)
            dq[block] += contract_rows(grads, key)
            return matmul(grads, q_ref[0, spot]), matmul(weights, g_ref[0, spot])

        everything = slice(0, 2 * rows)

        def trunk(step, masked):
            start = pl.multiple_of(step * CHUNK, CHUNK)

            def mask(weights):
                shape = weights.shape
                room = row_places((1, shape[1]), 1, sub) + (base - start)
                return jnp.where(lax.broadcasted_iota(jnp.int32, shape, 0) <= room, weights, 0.0)

            key_grad, value_grad = pair(
                k_ref[0, 0, pl.ds(start, CHUNK)],
                v_ref[0, 0, pl.ds(start, CHUNK)],
                everything,
                mask if masked else None,
            )
            dk[pl.ds(start, CHUNK)] += key_grad
            dv[pl.ds(start, CHUNK)] += value_grad

        if piece == 0:
            clear = jnp.minimum(base // CHUNK, TRUNK // CHUNK)
            end = jnp.minimum((base + rows + CHUNK - 1) // CHUNK, TRUNK // CHUNK)
            lax.fori_loop(0, clear, lambda i, c: (trunk(i, False), c)[1], 0)
            lax.fori_loop(clear, end, lambda i, c: (trunk(i, True), c)[1], 0)
        else:
            lax.fori_loop(0, TRUNK // CHUNK, lambda i, c: (trunk(i, False), c)[1], 0)

        lead = jnp.maximum(base - TRUNK, 0) // SEG

        def parents_():
            gather_parents(
                meta,
                lead,
                0,
                [
                    (lambda b: k_ref[0, 0, TRUNK + b * SEG : TRUNK + (b + 1) * SEG], kp),
                    (lambda b: v_ref[0, 0, TRUNK + b * SEG : TRUNK + (b + 1) * SEG], vp),
                ],
            )

        if piece == 0:
            pl.when(base + rows > TRUNK)(parents_)
        else:
            parents_()
        for s in range(SUBS):
            block = slice(2 * sub * s, 2 * sub * (s + 1))

            def runs():
                row = base + s * sub - TRUNK
                run = row // SEG
                own = pl.multiple_of(TRUNK + run * SEG, SEG)
                flag = jnp.minimum(meta[run] + 1, 1).astype(F32)

                def mask(weights):
                    shape = (SEG, 2 * sub)
                    room = lax.broadcasted_iota(jnp.int32, shape, 1) % sub + lax.rem(row, SEG)
                    seen = lax.broadcasted_iota(jnp.int32, shape, 0) <= room
                    return jnp.concatenate(
                        [jnp.where(seen, weights[:SEG], 0.0), weights[SEG:] * flag], axis=0
                    )

                key_grad, value_grad = pair(
                    jnp.concatenate([k_ref[0, 0, pl.ds(own, SEG)], kp[run - lead]], axis=0),
                    jnp.concatenate([v_ref[0, 0, pl.ds(own, SEG)], vp[run - lead]], axis=0),
                    block,
                    mask,
                )
                dk[pl.ds(own, SEG)] += key_grad[:SEG]
                dv[pl.ds(own, SEG)] += value_grad[:SEG]
                slot = LOCAL_RUNS * piece + run - lead
                pk[slot] += key_grad[SEG:]
                pv[slot] += value_grad[SEG:]

            if piece == 0:
                pl.when(base + s * sub >= TRUNK)(runs)
            else:
                runs()

        dq_ref[0, region] = dq[...] * score_scale

        def spread():
            parents = [meta[jnp.minimum(lead + k, TREE // SEG - TRUNK // SEG - 1)] for k in range(LOCAL_RUNS)]

            def place(b, carry):
                start = pl.multiple_of(TRUNK + b * SEG, SEG)
                key_grad, value_grad = dk[pl.ds(start, SEG)], dv[pl.ds(start, SEG)]
                for k in range(LOCAL_RUNS):
                    share = (1 - jnp.minimum(jnp.abs(parents[k] - b), 1)).astype(F32)
                    key_grad += pk[LOCAL_RUNS * piece + k] * share
                    value_grad += pv[LOCAL_RUNS * piece + k] * share
                dk[pl.ds(start, SEG)] = key_grad
                dv[pl.ds(start, SEG)] = value_grad
                return carry

            lax.fori_loop(0, (TREE - TRUNK) // SEG, place, 0)

        if piece == 0:
            pl.when(base + rows > TRUNK)(spread)
        else:
            spread()

    def core_copy(h):
        return links.copy(("kv core", h), stage.at[h % 2, :, 1 - core], near.at[h % 2], links.sibling())

    def far_copies(h):
        return [
            links.copy(("kv z", h, i), sums.at[h, chip], far.at[h, i], target)
            for i, (chip, target) in enumerate(links.group())
        ]

    def pass_on(h):
        core_copy(h).wait()

        def add(i, carry):
            chip, which, piece = i // 4, lax.rem(i // 2, 2), lax.rem(i, 2)
            sums[h, chip, which, piece] = (
                stage[h % 2, chip, core, which, piece].astype(F32) + near[h % 2, chip, which, piece].astype(F32)
            ).astype(BF16)
            return carry

        lax.fori_loop(0, chips * 4, add, 0)
        run_all(far_copies(h), "start")

    for h in range(1, KV_HEADS):
        pl.when(head == h)(functools.partial(pass_on, h - 1))

    for which, grad, scale in ((0, dk, score_scale), (1, dv, 1.0)):
        for piece in range(2):
            for member in range(members):
                start = rows * (piece * members + member)
                stage[lax.rem(head, 2), member // 2, member % 2, which, piece] = (
                    grad[start : start + rows] * scale
                ).astype(BF16)
    for h in range(KV_HEADS):

        @pl.when(head == h)
        def _():
            core_copy(h).start()

    for moment, steps in BACKWARD_AFTER.items():

        @pl.when(head == moment)
        def _():
            for step, array in steps:
                for s in each(array):
                    if step == 0:
                        s.begin()
                    else:
                        s.middle(step - 1)

    def result(h):
        return pltpu.make_async_copy(last.at[h % 2], dkv_ref.at[:, h], local_sem.at[h % 2])

    @pl.when(head == KV_HEADS - 1)
    def _():
        pass_on(KV_HEADS - 1)
        for s in scatters:
            s.finish()
        for h in range(KV_HEADS):
            run_all(far_copies(h), "wait")
            if h > 1:
                result(h - 2).wait()
            for which in range(2):
                for piece in range(2):
                    total = sums[h, here, which, piece].astype(F32)
                    for i in range(chips - 1):
                        total = total + far[h, i, which, piece].astype(F32)
                    last[h % 2, which, piece] = total
            result(h).start()
        for h in (KV_HEADS - 2, KV_HEADS - 1):
            result(h).wait()
        swap.wait()


def backward(sizes, meta, queries, grads, kv_all, log_total, delta, late, dout, done):
    ny, nx, nz = sizes
    chips = nz // 2
    rows = queries.shape[1] // 4
    widths = (late.shape[-1],) * late.shape[0] + (dout.shape[-1],)
    shard_rows = dout.shape[4]
    stack = pl.BlockSpec((1, 4 * rows, HEAD_DIM), lambda h, meta: (h, 0, 0))
    line = pl.BlockSpec((1, 1, 4 * rows), lambda h, meta: (h, 0, 0))
    buffers, count = [], 0
    for w in widths:
        for b, cols in enumerate(halves_of(w)):
            buffers += Scatter.scratch(sizes, ORDERS[b], shard_rows, cols.stop - cols.start)
            buffers.append(pltpu.VMEM((ny, nx, nz, shard_rows, cols.stop - cols.start), BF16))
            count += 1
    rounds = count * Scatter.copies(sizes) + KV_HEADS * chips + 1
    late_shape = (late.shape[0], shard_rows, late.shape[-1])
    dout_shape = (shard_rows, dout.shape[-1])
    return pl.pallas_call(
        functools.partial(backward_kernel, sizes, rows, widths),
        out_shape=[
            jax.ShapeDtypeStruct((KV_HEADS, 4 * rows, HEAD_DIM), F32),
            jax.ShapeDtypeStruct((2, KV_HEADS, 2, rows, HEAD_DIM), F32),
            jax.ShapeDtypeStruct(late_shape, F32),
            jax.ShapeDtypeStruct(dout_shape, F32),
            jax.ShapeDtypeStruct(done.shape, BF16),
        ],
        grid_spec=pltpu.PrefetchScalarGridSpec(
            num_scalar_prefetch=1,
            grid=(KV_HEADS,),
            in_specs=[
                stack,
                stack,
                pl.BlockSpec((1, 1, TREE, HEAD_DIM), lambda h, meta: (0, h, 0, 0)),
                pl.BlockSpec((1, 1, TREE, HEAD_DIM), lambda h, meta: (1, h, 0, 0)),
                line,
                line,
                ANY,
                ANY,
                ANY,
            ],
            out_specs=[
                stack,
                ANY,
                pl.BlockSpec(late_shape, lambda h, meta: (0, 0, 0)),
                pl.BlockSpec(dout_shape, lambda h, meta: (0, 0)),
                ANY,
            ],
            scratch_shapes=[
                pltpu.VMEM((2 * rows, HEAD_DIM), F32),
                pltpu.VMEM((TREE, HEAD_DIM), F32),
                pltpu.VMEM((TREE, HEAD_DIM), F32),
                pltpu.VMEM((2 * LOCAL_RUNS, SEG, HEAD_DIM), F32),
                pltpu.VMEM((2 * LOCAL_RUNS, SEG, HEAD_DIM), F32),
                pltpu.VMEM((LOCAL_RUNS, SEG, HEAD_DIM), BF16),
                pltpu.VMEM((LOCAL_RUNS, SEG, HEAD_DIM), BF16),
                pltpu.VMEM((2, chips, 2, 2, 2, rows, HEAD_DIM), BF16),
                pltpu.VMEM((2, chips, 2, 2, rows, HEAD_DIM), BF16),
                pltpu.VMEM((KV_HEADS, chips, 2, 2, rows, HEAD_DIM), BF16),
                pltpu.VMEM((KV_HEADS, chips - 1, 2, 2, rows, HEAD_DIM), BF16),
                pltpu.VMEM((2, 2, 2, rows, HEAD_DIM), F32),
            ]
            + buffers
            + [
                pltpu.SemaphoreType.DMA((rounds,)),
                pltpu.SemaphoreType.DMA((rounds,)),
                pltpu.SemaphoreType.DMA((3 + count,)),
            ],
        ),
        compiler_params=pltpu.CompilerParams(
            collective_id=3, has_side_effects=True, vmem_limit_bytes=60 * MIB
        ),
        name="backward",
    )(
        meta,
        queries,
        grads,
        kv_all,
        kv_all,
        log_total.reshape(KV_HEADS, 1, 4 * rows),
        delta.reshape(KV_HEADS, 1, 4 * rows),
        late,
        dout,
        done,
    )


def finish_kernel(
    sizes, rows, dq_ref, dkv_ref, pre_ref, w_ref, normed_ref, x_ref, hid_ref, gain_ref, post_ref, qk_ref, cos_ref, sin_ref,
    q_out, k_out, v_out, g_out, dx_placed, *refs,
):
    normed_t, low, grads, qk, dx, part, part_g = refs[:7]
    buffers = refs[7:-3]
    send_sem, recv_sem, local_sem = refs[-3:]
    ny, nx, nz = sizes
    count = 2 * rows
    sub = rows // SUBS
    shard_rows = part.shape[5]
    tile = 256
    pair = pl.program_id(0)
    links = Links(sizes, send_sem, recv_sem)
    _, _, _, core = links.place()
    swap = Exchange(links, dx, dx_placed, local_sem.at[0])

    def to_query(c):
        def store(total):
            q_out[:, 4 * HEAD_DIM * c : 4 * HEAD_DIM * (c + 1)] = total

        return store

    def to_key_value(c):
        def store(total):
            k_out[:, 2 * HEAD_DIM * c : 2 * HEAD_DIM * (c + 1)] = total[:, : 2 * HEAD_DIM]
            v_out[:, 2 * HEAD_DIM * c : 2 * HEAD_DIM * (c + 1)] = total[:, 2 * HEAD_DIM :]

        return store

    scatters = []
    for c in range(PAIRS):
        for b, cols in enumerate(halves_of(8 * HEAD_DIM)):
            k = 4 * len(scatters)
            scatters.append(
                Scatter(
                    links,
                    (c, b),
                    part.at[c % 2],
                    ORDERS[b],
                    cols,
                    *buffers[k : k + 4],
                    part.at[c % 2, :, :, :, core, :, cols],
                    None,
                    to_key_value(c) if b else to_query(c),
                )
            )
    k = 4 * len(scatters)
    whole = slice(0, 3 * GAIN_COLS)
    scatters.append(
        Scatter(
            links, "gains", part_g, ORDERS[0], whole, *buffers[k : k + 4], part_g.at[:, :, :, core], None, g_out
        )
    )

    def act(steps):
        for what, c in steps:
            for s in scatters[2 * c : 2 * c + 2]:
                if what == "core":
                    s.start()
                elif what == "begin":
                    s.begin()
                elif what == "finish":
                    s.finish()
                else:
                    s.middle(what)

    def rows_of(block):
        return (block // (2 * nz * nx), lax.rem(block // (2 * nz), nx), lax.rem(block // 2, nz), lax.rem(block, 2))

    @pl.when(pair == 0)
    def _():
        links.meet()
        normed_t[...] = normed_ref[...].astype(F32).T.astype(BF16)
        grads[...] = jnp.zeros_like(grads)
        qk[...] = jnp.zeros_like(qk)

    cosine, sine = cos_ref[...], sin_ref[...]

    def back(turned_grad, pre, gain):
        grad = turned_grad * cosine - roll_half(turned_grad) * sine
        factor = norm_factor(pre)
        grad_pre, share = norm_backward(grad, gain, pre * factor, factor)
        return grad_pre.astype(BF16), jnp.sum(share, axis=0, keepdims=True)

    for hh in range(2):
        for h in range(2):
            grad = jnp.concatenate(
                [dq_ref[hh, (2 * s + h) * sub : (2 * s + h + 1) * sub] for s in range(2 * SUBS)], axis=0
            )
            value, share = back(grad, pre_ref[hh, :, h * HEAD_DIM : (h + 1) * HEAD_DIM], qk_ref[0:1])
            qk[0:1] += share
            at = 2 * hh + h
            low[:, at * HEAD_DIM : (at + 1) * HEAD_DIM] = value
        value, share = back(dkv_ref[0, hh].reshape(count, HEAD_DIM), pre_ref[hh, :, 2 * HEAD_DIM :], qk_ref[1:2])
        qk[1:2] += share
        low[:, (4 + hh) * HEAD_DIM : (5 + hh) * HEAD_DIM] = value
        low[:, (6 + hh) * HEAD_DIM : (7 + hh) * HEAD_DIM] = dkv_ref[1, hh].reshape(count, HEAD_DIM).astype(BF16)
    for moment, steps in FINISH_MIDDLE.items():
        pl.when(pair == moment)(functools.partial(act, steps))
    slot = lax.rem(pair, 2)

    def model(t, carry):
        at = pl.multiple_of(t * tile, tile)
        grads[:, pl.ds(at, tile)] += nt(low[...], w_ref[0, pl.ds(at, tile), :])
        value = matmul(normed_t[pl.ds(at, tile)], low[...])
        for k in range(tile // shard_rows):
            y, x, z, c = rows_of(at // shard_rows + k)
            part[slot, y, x, z, c] = value[k * shard_rows : (k + 1) * shard_rows].astype(BF16)
        return carry

    lax.fori_loop(0, D // tile, model, 0)
    for moment, steps in FINISH_AFTER.items():
        pl.when(pair == moment)(functools.partial(act, steps))

    @pl.when(pair == PAIRS - 1)
    def _():
        values = x_ref[...].astype(F32)
        factor = norm_factor(values)
        grad_in, share = norm_backward(grads[...], gain_ref[0:1], values * factor, factor)
        dx[...] = (hid_ref[...] + grad_in).astype(BF16).reshape(2, rows, D)
        swap.start()
        act([(0, PAIRS - 2), ("begin", PAIRS - 1)])
        lines = jnp.concatenate(
            [jnp.sum(share, axis=0, keepdims=True), post_ref[...], jnp.zeros((GAIN_COLS - 2, D), F32)], axis=0
        )
        columns = lines.T.astype(BF16)
        first = lax.broadcasted_iota(jnp.int32, (shard_rows, GAIN_COLS), 0) == 0
        query_line = jnp.where(first, qk[0:1], 0.0).astype(BF16)
        key_line = jnp.where(first, qk[1:2], 0.0).astype(BF16)
        for k in range(D // shard_rows):
            y, x, z, c = k // (2 * nz * nx), k // (2 * nz) % nx, k // 2 % nz, k % 2
            part_g[y, x, z, c, :, :GAIN_COLS] = columns[k * shard_rows : (k + 1) * shard_rows]
            part_g[y, x, z, c, :, GAIN_COLS : 2 * GAIN_COLS] = query_line
            part_g[y, x, z, c, :, 2 * GAIN_COLS :] = key_line
        act([("core", PAIRS), (1, PAIRS - 2), ("begin", PAIRS), (0, PAIRS - 1), (0, PAIRS), (1, PAIRS - 1), (1, PAIRS)])
        for c in range(PAIRS + 1):
            act([("finish", c)])
        swap.wait()


def finish(sizes, dq, dkv, pre, normed, x, grad_hidden, gain, post_part, qkv_full, qk_gain, cosine, sine):
    ny, nx, nz = sizes
    count = x.shape[0]
    rows = count // 2
    shard_rows = D // (ny * nx * nz * 2)
    blocks = (ny, nx, nz, 2, shard_rows)
    width = 8 * HEAD_DIM

    def whole_block(shape):
        return pl.BlockSpec(shape, lambda c: (0,) * len(shape), pipeline_mode=pl.Buffered(1))

    buffers = []
    for c in range(PAIRS):
        for b, cols in enumerate(halves_of(width)):
            buffers += Scatter.scratch(sizes, ORDERS[b], shard_rows, cols.stop - cols.start)
    buffers += Scatter.scratch(sizes, ORDERS[0], shard_rows, 3 * GAIN_COLS)
    rounds = (2 * PAIRS + 1) * Scatter.copies(sizes) + 1

    def out_block(n):
        return pl.BlockSpec((shard_rows, n), lambda c: (0, 0))

    return pl.pallas_call(
        functools.partial(finish_kernel, sizes, rows),
        grid=(PAIRS,),
        out_shape=[
            jax.ShapeDtypeStruct((shard_rows, QD), F32),
            jax.ShapeDtypeStruct((shard_rows, KVD), F32),
            jax.ShapeDtypeStruct((shard_rows, KVD), F32),
            jax.ShapeDtypeStruct((shard_rows, 3 * GAIN_COLS), F32),
            jax.ShapeDtypeStruct((2, rows, D), BF16),
        ],
        in_specs=[
            pl.BlockSpec((2, 2 * count, HEAD_DIM), lambda c: (c, 0, 0)),
            pl.BlockSpec((2, 2, 2, rows, HEAD_DIM), lambda c: (0, c, 0, 0, 0)),
            pl.BlockSpec((2, count, 3 * HEAD_DIM), lambda c: (c, 0, 0)),
            pl.BlockSpec((1, D, width), lambda c: (c, 0, 0)),
            whole_block((count, D)),
            whole_block((count, D)),
            whole_block((count, D)),
            whole_block((8, D)),
            whole_block((1, D)),
            whole_block((8, HEAD_DIM)),
            whole_block((count, HEAD_DIM)),
            whole_block((count, HEAD_DIM)),
        ],
        out_specs=[out_block(QD), out_block(KVD), out_block(KVD), out_block(3 * GAIN_COLS), ANY],
        scratch_shapes=[
            pltpu.VMEM((D, count), BF16),
            pltpu.VMEM((count, width), BF16),
            pltpu.VMEM((count, D), F32),
            pltpu.VMEM((8, HEAD_DIM), F32),
            pltpu.VMEM((2, rows, D), BF16),
            pltpu.VMEM((2,) + blocks + (width,), BF16),
            pltpu.VMEM(blocks + (3 * GAIN_COLS,), BF16),
        ]
        + buffers
        + [
            pltpu.SemaphoreType.DMA((rounds,)),
            pltpu.SemaphoreType.DMA((rounds,)),
            pltpu.SemaphoreType.DMA((1,)),
        ],
        compiler_params=pltpu.CompilerParams(
            collective_id=4, has_side_effects=True, vmem_limit_bytes=58 * MIB
        ),
        name="finish",
    )(dq, dkv, pre, qkv_full, normed, x, grad_hidden, gain, post_part, qk_gain, cosine, sine)


def shards(
    sizes,
    tokens,
    cotangent,
    segment_ids,
    positions,
    parents,
    input_norm,
    query_proj,
    key_proj,
    value_proj,
    query_norm,
    key_norm,
    out_proj,
    post_norm,
    gate_proj,
    up_proj,
    down_proj,
):
    nz = sizes[2]
    rows = tokens.shape[1]
    shard_rows = query_proj.shape[0]
    gain_rows = query_norm.shape[0]
    ctx = lax.axis_index("ctx")
    half = ctx // nz
    member = ctx % nz
    count = 2 * rows
    sub = rows // SUBS

    device = lax.axis_index("dp") * 2 * nz + ctx

    def spread(gain):
        line = jnp.zeros((1, HEAD_DIM), BF16)
        line = lax.dynamic_update_slice(line, gain[None, :], (0, device * gain_rows))
        return jnp.pad(line, ((0, shard_rows - 1), (0, 0)))

    gains = jnp.pad(
        jnp.stack([input_norm, post_norm], axis=1), ((0, 0), (0, GAIN_COLS - 2))
    )
    gains = jnp.concatenate([gains, spread(query_norm), spread(key_norm)], axis=1)
    qkv_shards = [
        jnp.concatenate(
            [
                query_proj[:, 4 * HEAD_DIM * c : 4 * HEAD_DIM * (c + 1)],
                key_proj[:, 2 * HEAD_DIM * c : 2 * HEAD_DIM * (c + 1)],
                value_proj[:, 2 * HEAD_DIM * c : 2 * HEAD_DIM * (c + 1)],
            ],
            axis=1,
        )
        for c in range(PAIRS)
    ]
    down_t = down_proj.T
    feed_shards = [
        jnp.concatenate(
            [w[:, c * FF_CHUNK : (c + 1) * FF_CHUNK] for w in (gate_proj, up_proj, down_t)], axis=1
        )
        for c in range(FF_CHUNKS)
    ]

    run_seg = segment_ids[half][TRUNK::SEG]
    run_parent = parents[half][run_seg]
    parent_run = jnp.argmax(run_seg[None, :] == run_parent[:, None], axis=1).astype(jnp.int32)
    meta = jnp.where(run_parent > 0, parent_run, -1)
    pos_tree = positions[half].reshape(2, nz, rows)
    pos_local = lax.dynamic_index_in_dim(pos_tree, member, 1, keepdims=False).reshape(count)
    cosine, sine = rope_tables(pos_local)

    (mixed, totals, pre, normed, gain_rows_, qk_gains, placed, cot, queries, kv_all,
     qkv_full, _, out_t, feed_whole) = forward(
        sizes, meta, cosine, sine, tokens, cotangent, qkv_shards + [out_proj.T] + feed_shards[:FF_FIRST] + [gains]
    )
    x = placed.reshape(count, D)
    cot = cot.reshape(count, D)
    qkv_full = qkv_full.reshape(PAIRS, D, -1)
    out_t = out_t.reshape(D, QD)
    feed_whole = feed_whole.reshape(FF_FIRST, D, -1)
    log_total = jnp.log2(totals[:, :KV_HEADS]).T
    result, grad_hidden, grad_stack, delta, post_part, dout, late, _, early_grad = feed(
        sizes, x, mixed, cot, out_t, gain_rows_, feed_whole, feed_shards[FF_FIRST:]
    )
    delta = delta[:HEADS].reshape(KV_HEADS, 2, 2 * SUBS, sub).transpose(0, 2, 1, 3)
    dq, dkv, late_grad, out_grad, output = backward(
        sizes, meta, queries, grad_stack, kv_all, log_total, delta, late, dout, result.reshape(2, rows, D)
    )
    feed_grad = jnp.concatenate([early_grad, late_grad], axis=0)

    def feed_columns(k):
        piece = feed_grad[:, :, k * FF_CHUNK : (k + 1) * FF_CHUNK]
        return piece.transpose(1, 0, 2).reshape(shard_rows, FF)

    query_grad, key_grad, value_grad, gain_grad, input_grad = finish(
        sizes, dq, dkv, pre, normed, x, grad_hidden, gain_rows_, post_part, qkv_full, qk_gains, cosine, sine
    )

    def own(line):
        return lax.dynamic_slice_in_dim(line, device * gain_rows, gain_rows)

    return (
        output,
        input_grad.astype(F32),
        gain_grad[:, 0],
        query_grad,
        key_grad,
        value_grad,
        own(gain_grad[0, GAIN_COLS : 2 * GAIN_COLS]),
        own(gain_grad[0, 2 * GAIN_COLS :]),
        out_grad.T,
        gain_grad[:, 1],
        feed_columns(0),
        feed_columns(1),
        feed_columns(2).T,
    )


def solution(mesh):
    dp, ctx = mesh.shape["dp"], mesh.shape["ctx"]
    sizes = (2, dp // 2, ctx // 2)
    return jax.shard_map(
        functools.partial(shards, sizes),
        mesh=mesh,
        in_specs=(
            P("dp", "ctx", None),
            P("dp", "ctx", None),
            P("dp", None),
            P("dp", None),
            P("dp", None),
            P(("dp", "ctx")),
            P(("dp", "ctx"), None),
            P(("dp", "ctx"), None),
            P(("dp", "ctx"), None),
            P(("dp", "ctx")),
            P(("dp", "ctx")),
            P(None, ("dp", "ctx")),
            P(("dp", "ctx")),
            P(("dp", "ctx"), None),
            P(("dp", "ctx"), None),
            P(None, ("dp", "ctx")),
        ),
        out_specs=(
            P("dp", "ctx", None),
            P("dp", "ctx", None),
            P(("dp", "ctx")),
            P(("dp", "ctx"), None),
            P(("dp", "ctx"), None),
            P(("dp", "ctx"), None),
            P(("dp", "ctx")),
            P(("dp", "ctx")),
            P(None, ("dp", "ctx")),
            P(("dp", "ctx")),
            P(("dp", "ctx"), None),
            P(("dp", "ctx"), None),
            P(None, ("dp", "ctx")),
        ),
        check_vma=False,
    )
```

```python
import functools
import math

import jax
import jax.numpy as jnp
from jax import lax
from jax.experimental import pallas as pl
from jax.experimental.pallas import tpu as pltpu
from jax.sharding import PartitionSpec as P

D = 1024
HEADS = 16
KV_HEADS = 8
HEAD_DIM = 128
FF = 3072
TRUNK = 1024
SEG = 128
TREE = 2560
QD = HEADS * HEAD_DIM
KVD = KV_HEADS * HEAD_DIM
SUBS = 5
CHUNK = 256
GAIN_COLS = 128
FF_CHUNK = 512
PAIRS = KV_HEADS // 2
FF_CHUNKS = FF // FF_CHUNK
FF_EARLY = 2
FF_FIRST = 4
LOCAL_RUNS = 3
MIB = 1024 * 1024

eps_norm = 1e-06
rope_base = 1000000.0
exp2_scale = math.log2(math.e) / math.sqrt(HEAD_DIM)
score_scale = HEAD_DIM ** (-0.5)

MESH = pl.DeviceIdType.MESH
ANY = pl.BlockSpec(memory_space=pl.ANY)
F32 = jnp.float32
BF16 = jnp.bfloat16


def matmul(left_side, right_side):
    return jnp.dot(left_side, right_side, preferred_element_type=F32)


def nt(left_side, right_side):
    return lax.dot_general(
        left_side, right_side, (((1,), (1,)), ((), ())), preferred_element_type=F32
    )


def contract_rows(left_side, right_side):
    return lax.dot_general(
        left_side, right_side, (((0,), (0,)), ((), ())), preferred_element_type=F32
    )


def norm_factor(values):
    return lax.rsqrt(jnp.mean(values * values, axis=-1, keepdims=True) + eps_norm)


def norm_backward(grad_out, weight, normed, factor):
    weighted = grad_out * weight
    grad_in = factor * (weighted - normed * jnp.mean(weighted * normed, axis=-1, keepdims=True))
    return (grad_in, grad_out * normed)


def rope_tables(positions):
    steps_half = jnp.arange(HEAD_DIM // 2, dtype=F32)
    inverse = rope_base ** (-(steps_half * 2.0 / HEAD_DIM))
    angles = positions.astype(F32)[:, None] * inverse[None, :]
    cosine, sine = jnp.cos(angles), jnp.sin(angles)
    return jnp.concatenate([cosine, cosine], axis=-1), jnp.concatenate([-sine, sine], axis=-1)


class Links:
    def __init__(self, sizes, send_sem, recv_sem):
        self.sizes = sizes
        self.send_sem = send_sem
        self.recv_sem = recv_sem
        self.index = {}

    def place(self):
        _, nx, _ = self.sizes
        dp, ctx = lax.axis_index("dp"), lax.axis_index("ctx")
        return dp // nx, lax.rem(dp, nx), ctx // 2, lax.rem(ctx, 2)

    def device(self, y, x, z, core):
        return (y * self.sizes[1] + x, z * 2 + core)

    def peers(self, axis, back=False):
        y, x, z, core = self.place()
        at = {"y": y, "x": x, "z": z}
        n = self.sizes["yxz".index(axis)]
        found = []
        for s in range(1, n):
            moved = dict(at)
            moved[axis] = lax.rem(at[axis] + (n - s if back else s), n)
            found.append((moved["y"], moved["x"], moved["z"], core))
        return found

    def sibling(self):
        y, x, z, core = self.place()
        return self.device(y, x, z, 1 - core)

    def across(self):
        y, x, z, core = self.place()
        nz = self.sizes[2]
        return self.device(y, x, lax.rem(z + nz // 2, nz), core)

    def group(self, back=False):
        y, x, z, core = self.place()
        chips = self.sizes[2] // 2
        base = (z // chips) * chips
        here = z - base
        chosen = [lax.rem(here + (chips - s if back else s), chips) for s in range(1, chips)]
        return [(chip, self.device(y, x, base + chip, core)) for chip in chosen]

    def meet(self):
        barrier = pltpu.get_barrier_semaphore()
        partners = [self.device(*p) for a in "zxy" for p in self.peers(a)] + [self.sibling()]
        for partner in partners:
            pl.semaphore_signal(barrier, inc=1, device_id=partner, device_id_type=MESH)
        pl.semaphore_wait(barrier, len(partners))

    def copy(self, key, src, dst, target):
        k = self.index.setdefault(key, len(self.index))
        return pltpu.make_async_remote_copy(
            src_ref=src,
            dst_ref=dst,
            send_sem=self.send_sem.at[k],
            recv_sem=self.recv_sem.at[k],
            device_id=target,
            device_id_type=MESH,
        )


class Exchange:
    def __init__(self, links, source, placed, local_sem, tag="swap"):
        self.tag = tag
        self.links = links
        self.source = source
        self.placed = placed
        self.local_sem = local_sem

    def copies_(self):
        _, _, z, _ = self.links.place()
        half = z // (self.links.sizes[2] // 2)
        return [
            self.links.copy(self.tag, self.source.at[1 - half], self.placed.at[half], self.links.across()),
            pltpu.make_async_copy(self.source.at[half], self.placed.at[half], self.local_sem),
        ]

    def start(self):
        for copy in self.copies_():
            copy.start()

    def wait(self):
        for copy in self.copies_():
            copy.wait()


class Gather:
    def __init__(self, links, tag, shard, whole, order, cols, local_sem):
        self.links = links
        self.tag = tag
        self.shard = shard
        self.whole = whole
        self.order = order
        self.cols = cols
        self.local_sem = local_sem

    def own(self):
        y, x, z, core = self.links.place()
        return self.whole.at[y, x, z, core, :, self.cols]

    def slab(self, stage, at):
        y, x, z, core = at
        if stage == 0:
            return self.whole.at[y, x, z, core, :, self.cols]
        if stage == 1:
            return self.whole.at[y, x, :, core, :, self.cols]
        if self.order[0] == "x":
            return self.whole.at[y, :, :, core, :, self.cols]
        return self.whole.at[:, x, :, core, :, self.cols]

    def axis(self, stage):
        return ("z",) + tuple(self.order)[0:2] if stage is None else ("z", self.order[0], self.order[1])[stage]

    def send(self, stage):
        me = self.links.place()
        src = self.shard.at[:, self.cols] if stage == 0 else self.slab(stage, me)
        dst = self.slab(stage, me)
        return [
            self.links.copy((self.tag, stage, i), src, dst, self.links.device(*p))
            for i, p in enumerate(self.links.peers(self.axis(stage)))
        ]

    def forward(self, stage):
        sibling = self.links.sibling()
        if stage < 0:
            return [self.links.copy((self.tag, "own"), self.shard.at[:, self.cols], self.own(), sibling)]
        return [
            self.links.copy((self.tag, "pass", stage, i), self.slab(stage, p), self.slab(stage, p), sibling)
            for i, p in enumerate(self.links.peers(self.axis(stage), back=True))
        ]

    def local(self):
        return pltpu.make_async_copy(self.shard.at[:, self.cols], self.own(), self.local_sem)

    def start(self):
        self.local().start()
        for copy in self.send(0) + self.forward(-1):
            copy.start()

    def step(self, stage):
        if stage == 1:
            self.local().wait()
        for copy in self.send(stage - 1):
            copy.wait()
        if stage < 3:
            for copy in self.send(stage):
                copy.start()
        for copy in self.forward(stage - 1):
            copy.start()

    def close(self):
        for stage in range(-1, 3):
            for copy in self.forward(stage):
                copy.wait()

    @staticmethod
    def copies(sizes):
        return 2 * sum(n - 1 for n in sizes) + 1


class Scatter:
    def __init__(self, links, tag, part, order, cols, halves, firsts, seconds, thirds, temp, temp_sem, out):
        self.links = links
        self.tag = tag
        self.part = part
        self.order = order
        self.cols = cols
        self.sums = halves
        self.got = (firsts, seconds, thirds)
        self.temp = temp
        self.temp_sem = temp_sem
        self.out = out

    def first(self):
        _, _, _, core = self.links.place()
        return self.links.copy(
            (self.tag, "core"), self.part.at[:, :, :, 1 - core, :, self.cols], self.sums, self.links.sibling()
        )

    def load(self):
        _, _, _, core = self.links.place()
        return pltpu.make_async_copy(
            self.part.at[:, :, :, core, :, self.cols], self.temp, self.temp_sem
        )

    def axis(self, stage):
        return (self.order[0], self.order[1], "z")[stage]

    def at(self, stage, place, rest=None):
        y, x, z, _ = place
        if stage == 0:
            return (y,) if self.order[0] == "y" else (slice(None), x)
        if stage == 1:
            return (y, x)
        return (y, x, z)

    def send(self, stage):
        me = self.links.place()
        found = []
        for i, p in enumerate(self.links.peers(self.axis(stage))):
            index = self.at(stage, p)
            found.append(
                self.links.copy(
                    (self.tag, stage, i), self.sums.at[index], self.got[stage].at[i], self.links.device(*p)
                )
            )
        return found

    def start(self):
        self.first().start()

    def begin(self):
        self.first().wait()
        if self.temp_sem is not None:
            self.load().wait()
        ny, nx, nz = self.links.sizes

        def add(i, carry):
            a, b, c = i // (nx * nz), lax.rem(i // nz, nx), lax.rem(i, nz)
            self.sums[a, b, c] = (
                self.sums[a, b, c].astype(F32) + self.temp[a, b, c].astype(F32)
            ).astype(BF16)
            return carry

        lax.fori_loop(0, ny * nx * nz, add, 0)
        for copy in self.send(0):
            copy.start()

    def middle(self, stage):
        for copy in self.send(stage):
            copy.wait()
        y, x, z, _ = self.links.place()
        _, _, nz = self.links.sizes
        got = self.got[stage]
        peers = got.shape[0]
        if stage == 0:
            other = got.shape[1]

            def add(i, carry):
                b, c = i // nz, lax.rem(i, nz)
                index = (y, b, c) if self.order[0] == "y" else (b, x, c)
                total = self.sums[index].astype(F32)
                for p in range(peers):
                    total = total + got[p, b, c].astype(F32)
                self.sums[index] = total.astype(BF16)
                return carry

            lax.fori_loop(0, other * nz, add, 0)
        else:

            def add(c, carry):
                total = self.sums[y, x, c].astype(F32)
                for p in range(peers):
                    total = total + got[p, c].astype(F32)
                self.sums[y, x, c] = total.astype(BF16)
                return carry

            lax.fori_loop(0, nz, add, 0)
        for copy in self.send(stage + 1):
            copy.start()

    def finish(self):
        for copy in self.send(2):
            copy.wait()
        y, x, z, _ = self.links.place()
        total = self.sums[y, x, z].astype(F32)
        for p in range(self.got[2].shape[0]):
            total = total + self.got[2][p].astype(F32)
        if callable(self.out):
            self.out(total)
        else:
            self.out[:, self.cols] = total

    @staticmethod
    def copies(sizes):
        return sum(n - 1 for n in sizes) + 1

    @staticmethod
    def scratch(sizes, order, rows, width):
        ny, nx, nz = sizes
        na, nb = (ny, nx) if order[0] == "y" else (nx, ny)
        return [
            pltpu.VMEM((ny, nx, nz, rows, width), BF16),
            pltpu.VMEM((na - 1, nb, nz, rows, width), BF16),
            pltpu.VMEM((nb - 1, nz, rows, width), BF16),
            pltpu.VMEM((nz - 1, rows, width), BF16),
        ]


ORDERS = ("xy", "yx")

FORWARD_START = [
    ("swap", "tokens"), (0, 9), (0, 0), (1, 9), (1, 0), (2, 9), (2, 0), (0, 1), (0, 2), (3, 9), (4, 9), (3, 0),
    (1, 1), (1, 2), (0, 3), (2, 1), (0, 4), ("swapped", "tokens"),
]
FORWARD_AFTER = {
    0: [("kv", 0), (2, 2), (1, 3), (3, 1), (1, 4), (0, 5)],
    1: [("kv", 1), (3, 2), (2, 3), (2, 4), (1, 5)],
    2: [("use", 0), (3, 3), (3, 4), (2, 5), (0, 6), ("kv", 2)],
    3: [("got", 0), (1, 6), (0, 7), (3, 5)],
    4: [("use", 1), ("got", 1), ("kv", 3), (2, 6), (1, 7)],
    5: [(3, 6), (2, 7), (0, 8)],
    6: [("use", 2), ("swap", "cot"), (1, 8)],
    7: [("got", 2), (3, 7), (2, 8)],
    8: [("use", 3)],
    9: [("got", 3), (3, 8)],
    11: [("swapped", "cot")],
}
FEED_START = [("fetch", 0), ("send", (0, 4)), ("fetch", 1)]
FEED_NEXT = [("send", (1, 4)), ("send", (0, 5))]
FEED_MIDDLE = {
    0: [("send", (2, 4))],
    1: [("send", (3, 4)), ("send", (2, 5)), ("fetch", 2)],
    2: [("send", (3, 5)), ("fetch", 3)],
    3: [("fetch", 4)],
    4: [("fetch", 5)],
    5: [(1, 1)],
}
FEED_AFTER = {
    0: [("send", (1, 5)), ("core", 0)],
    1: [("begin", 0), ("core", 1)],
    2: [("begin", 1)],
    3: [(0, 0), (0, 1)],
    4: [(1, 0)],
}
FEED_LAST = []
FINISH_MIDDLE = {
    1: [("begin", 0)],
    2: [("begin", 1), (1, 0)],
    3: [("begin", 2), (1, 1)],
}
FINISH_AFTER = {
    0: [("core", 0)],
    1: [("core", 1), (0, 0)],
    2: [("core", 2), (0, 1)],
    3: [("core", 3)],
}
BACKWARD_AFTER = {
    0: [(0, 0)],
    1: [(1, 0), (0, 1)],
    2: [(2, 0), (1, 1), (0, 2)],
    3: [(2, 1), (1, 2), (0, 3)],
    4: [(2, 2), (1, 3), (0, 4)],
    5: [(2, 3), (1, 4)],
    6: [(2, 4)],
}


def halves_of(width):
    return (slice(0, width // 2), slice(width // 2, width)) if width >= 512 else (slice(0, width),)


def roll_half(values):
    return pltpu.roll(values, HEAD_DIM // 2, 1)


class KeyValues:
    def __init__(self, links, rows, held):
        self.links = links
        self.rows = rows
        self.held = held

    def slab(self, group, piece, member):
        members = self.links.sizes[2]
        start = pl.multiple_of(self.rows * (piece * members + member), self.rows)
        return self.held.at[:, 2 * group : 2 * group + 2, pl.ds(start, self.rows)]

    def mine(self):
        _, _, z, core = self.links.place()
        return lax.rem(z, self.links.sizes[2] // 2) * 2 + core

    def across(self, group):
        found = []
        for piece in range(2):
            slab = self.slab(group, piece, self.mine())
            for i, (_, target) in enumerate(self.links.group()):
                found.append(self.links.copy(("kv", group, piece, i), slab, slab, target))
        return found

    def near(self, group):
        found = []
        for piece in range(2):
            slab = self.slab(group, piece, self.mine())
            found.append(self.links.copy(("kv own", group, piece), slab, slab, self.links.sibling()))
        return found

    def forward(self, group):
        _, _, _, core = self.links.place()
        found = []
        for piece in range(2):
            for i, (chip, _) in enumerate(self.links.group(back=True)):
                slab = self.slab(group, piece, chip * 2 + core)
                found.append(
                    self.links.copy(("kv pass", group, piece, i), slab, slab, self.links.sibling())
                )
        return found

    @staticmethod
    def copies(sizes):
        return 4 * 2 * (2 * (sizes[2] // 2 - 1) + 1)


def run_all(copies, act):
    for copy in copies:
        if act == "start":
            copy.start()
        else:
            copy.wait()


def row_places(shape, dim, sub):
    t = lax.broadcasted_iota(jnp.int32, shape, dim)
    return (t // (2 * sub)) * sub + t % sub


def block_copies(sizes, src, dst, sem):
    ny, nx, nz = sizes
    shard_rows = src.shape[-2]
    found = []
    for i in range(ny * nx * nz * 2):
        block = src.at[i // (nx * nz * 2), i // (nz * 2) % nx, i // 2 % nz, i % 2]
        found.append(pltpu.make_async_copy(block, dst.at[i * shard_rows : (i + 1) * shard_rows], sem))
    return found


def gather_parents(meta, lead, slot, pairs):
    runs = (TREE - TRUNK) // SEG
    for k in range(LOCAL_RUNS):
        parent = meta[jnp.minimum(lead + k, runs - 1)]
        for read, out in pairs:
            total = None
            for b in range(runs):
                share = (1 - jnp.minimum(jnp.abs(parent - b), 1)).astype(F32).astype(BF16)
                term = read(b) * share
                total = term if total is None else total + term
            out[slot + k] = total


def forward_kernel(sizes, rows, meta, cos_ref, sin_ref, tok_ref, cot_ref, *refs):
    arrays = PAIRS + 2 + FF_FIRST
    shard = refs[:arrays]
    (mixed_ref, l_ref, pre_ref, normed_ref, gains_ref, qk_ref,
     placed, cot_placed, q_all, kv_all, qkv_whole, gain_whole, out_whole, feed_whole) = refs[arrays : arrays + 14]
    whole = (
        tuple(qkv_whole.at[c] for c in range(PAIRS))
        + (out_whole,)
        + tuple(feed_whole.at[c] for c in range(FF_FIRST))
        + (gain_whole,)
    )
    (qs, kvs, xs, ws, gs, acc, part, places, kp, vp, send_sem, recv_sem, local_sem) = refs[arrays + 14 :]
    members = sizes[2]
    sub = rows // SUBS
    count = 2 * rows
    step = pl.program_id(0)
    head = jnp.maximum(step - PAIRS, 0)
    links = Links(sizes, send_sem, recv_sem)
    kv = KeyValues(links, rows, kvs)
    swaps = {
        "tokens": Exchange(links, tok_ref, placed, local_sem.at[0], "tokens"),
        "cot": Exchange(links, cot_ref, cot_placed, local_sem.at[1], "cot"),
    }
    weights_ = [
        [
            Gather(links, (a, b), shard[a], whole[a], ORDERS[b], cols, local_sem.at[12 + 2 * a + b])
            for b, cols in enumerate(halves_of(shard[a].shape[-1]))
        ]
        for a in range(arrays)
    ]
    _, _, z, core = links.place()
    mine = lax.rem(z, members // 2) * 2 + core

    def kept(group):
        pair = slice(2 * group, 2 * group + 2)
        return [
            pltpu.make_async_copy(kvs.at[:, pair], kv_all.at[:, pair], local_sem.at[2 + group]),
            pltpu.make_async_copy(qs.at[pair], q_all.at[pair], local_sem.at[6 + group]),
        ]

    def act(steps):
        for what, a in steps:
            if what == "swap":
                swaps[a].start()
            elif what == "swapped":
                swaps[a].wait()
            elif what == "kv":
                run_all(kv.across(a), "start")
                run_all(kv.near(a), "start")
            elif what == "use":
                run_all(kv.across(a), "wait")
                run_all(kv.forward(a), "start")
            elif what == "got":
                run_all(kv.near(a), "wait")
                run_all(kv.forward(a), "wait")
                run_all(kept(a), "start")
            else:
                for g in weights_[a]:
                    if what == 0:
                        g.start()
                    elif what == 4:
                        g.close()
                    else:
                        g.step(what)

    @pl.when(step == 0)
    def _():
        links.meet()
        act(FORWARD_START)
        l_ref[...] = jnp.zeros_like(l_ref)
        places[...] = row_places(places.shape, 0, sub)
        run_all(block_copies(sizes, gain_whole, gs, local_sem.at[10]), "start")
        pltpu.make_async_copy(gs, gs, local_sem.at[10]).wait()
        loaded = pltpu.make_async_copy(placed, xs, local_sem.at[11])
        loaded.start()
        gains_ref[...] = gs[:, :GAIN_COLS].astype(F32).T[:8]
        qk_ref[0:1] = jnp.sum(gs[:, GAIN_COLS : 2 * GAIN_COLS].astype(F32), axis=0, keepdims=True)
        qk_ref[1:2] = jnp.sum(gs[:, 2 * GAIN_COLS :].astype(F32), axis=0, keepdims=True)
        loaded.wait()
        values = xs[...].reshape(count, D).astype(F32)
        normed_ref[...] = (values * norm_factor(values) * gains_ref[0:1]).astype(BF16)

    for c in range(PAIRS):

        @pl.when(step == c)
        def _():
            act([(4, c)])
            run_all(block_copies(sizes, qkv_whole.at[c], ws, local_sem.at[10]), "start")
            pltpu.make_async_copy(ws, ws, local_sem.at[10]).wait()

    @pl.when(step < PAIRS)
    def _():
        normed = normed_ref[...]
        cosine, sine = cos_ref[...], sin_ref[...]

        def turned(pre, gain):
            values = pre * norm_factor(pre) * gain
            return (values * cosine + roll_half(values) * sine).astype(BF16)

        for hh in range(2):
            at = 2 * step + hh
            query = matmul(normed, ws[:, 2 * hh * HEAD_DIM : 2 * (hh + 1) * HEAD_DIM])
            for h in range(2):
                pre = query[:, h * HEAD_DIM : (h + 1) * HEAD_DIM]
                pre_ref[hh, :, h * HEAD_DIM : (h + 1) * HEAD_DIM] = pre
                low = turned(pre, qk_ref[0:1])
                for s in range(2 * SUBS):
                    qs[at, (2 * s + h) * sub : (2 * s + h + 1) * sub] = low[s * sub : (s + 1) * sub]
            pre = matmul(normed, ws[:, (4 + hh) * HEAD_DIM : (5 + hh) * HEAD_DIM])
            pre_ref[hh, :, 2 * HEAD_DIM :] = pre
            low = turned(pre, qk_ref[1:2])
            value = matmul(normed, ws[:, (6 + hh) * HEAD_DIM : (7 + hh) * HEAD_DIM]).astype(BF16)
            for piece in range(2):
                start = pl.multiple_of(rows * (piece * members + mine), rows)
                kvs[0, at, pl.ds(start, rows)] = low[piece * rows : (piece + 1) * rows]
                kvs[1, at, pl.ds(start, rows)] = value[piece * rows : (piece + 1) * rows]

    def attend():
        lane = lax.broadcasted_iota(jnp.int32, (2 * rows, HEAD_DIM), 1)
        for piece in range(2):
            base = rows * (piece * members + mine)
            region = slice(piece * 2 * rows, (piece + 1) * 2 * rows)
            acc[...] = jnp.zeros_like(acc)
            part[...] = jnp.zeros_like(part)

            def trunk(step, masked):
                start = pl.multiple_of(step * CHUNK, CHUNK)
                weights = jnp.exp2(nt(qs[head, region], kvs[0, head, pl.ds(start, CHUNK)]) * exp2_scale)
                low, high = weights[:, :HEAD_DIM], weights[:, HEAD_DIM:]
                if masked:
                    room = places[...] + (base - start)
                    low = jnp.where(lane <= room, low, 0.0)
                    high = jnp.where(lane + HEAD_DIM <= room, high, 0.0)
                    weights = jnp.concatenate([low, high], axis=1)
                part[...] += low + high
                acc[...] += matmul(weights.astype(BF16), kvs[1, head, pl.ds(start, CHUNK)])
                return masked

            if piece == 0:
                clear = jnp.minimum(base // CHUNK, TRUNK // CHUNK)
                last = jnp.minimum((base + rows + CHUNK - 1) // CHUNK, TRUNK // CHUNK)
                lax.fori_loop(0, clear, lambda i, c: (trunk(i, False), c)[1], 0)
                lax.fori_loop(clear, last, lambda i, c: (trunk(i, True), c)[1], 0)
            else:
                lax.fori_loop(0, TRUNK // CHUNK, lambda i, c: (trunk(i, False), c)[1], 0)

            lead = jnp.maximum(base - TRUNK, 0) // SEG

            def parents_():
                gather_parents(
                    meta,
                    lead,
                    0,
                    [
                        (lambda b: kvs[0, head, TRUNK + b * SEG : TRUNK + (b + 1) * SEG], kp),
                        (lambda b: kvs[1, head, TRUNK + b * SEG : TRUNK + (b + 1) * SEG], vp),
                    ],
                )

            if piece == 0:
                pl.when(base + rows > TRUNK)(parents_)
            else:
                parents_()
            for s in range(SUBS):
                block = slice(2 * sub * s, 2 * sub * (s + 1))

                def runs():
                    row = base + s * sub - TRUNK
                    run = row // SEG
                    own = pl.multiple_of(TRUNK + run * SEG, SEG)
                    flag = jnp.minimum(meta[run] + 1, 1).astype(F32)
                    query = qs[head, piece * 2 * rows + 2 * sub * s : piece * 2 * rows + 2 * sub * (s + 1)]
                    room = places[block] + (lax.rem(row, SEG) - s * sub)
                    weights = jnp.exp2(nt(query, kvs[0, head, pl.ds(own, SEG)]) * exp2_scale)
                    weights = jnp.where(lane[block] <= room, weights, 0.0)
                    above = jnp.exp2(nt(query, kp[run - lead]) * exp2_scale) * flag
                    part[block] += weights + above
                    acc[block] += matmul(weights.astype(BF16), kvs[1, head, pl.ds(own, SEG)]) + matmul(
                        above.astype(BF16), vp[run - lead]
                    )

                if piece == 0:
                    pl.when(base + s * sub >= TRUNK)(runs)
                else:
                    runs()

            total = jnp.sum(part[...], axis=-1, keepdims=True)
            mixed = (acc[...] / total).astype(BF16)
            for s in range(SUBS):
                for h in range(2):
                    row = piece * rows + sub * s
                    mixed_ref[row : row + sub, h * HEAD_DIM : (h + 1) * HEAD_DIM] = mixed[
                        (2 * s + h) * sub : (2 * s + h + 1) * sub
                    ]
            l_ref[region] = jnp.where(lane == head, total, l_ref[region])


    pl.when(step >= PAIRS)(attend)
    for moment, steps in FORWARD_AFTER.items():
        pl.when(step == moment)(functools.partial(act, steps))

    @pl.when(step == PAIRS + KV_HEADS - 1)
    def _():
        for array in weights_[PAIRS : PAIRS + 1 + FF_FIRST]:
            for g in array:
                g.close()
        for group in range(4):
            run_all(kept(group), "wait")


def forward(sizes, meta, cosine, sine, tokens, cotangent, shards_):
    ny, nx, nz = sizes
    rows = tokens.shape[1]
    count = 2 * rows
    arrays = PAIRS + 2 + FF_FIRST
    shard_rows = shards_[0].shape[0]
    blocks = (ny, nx, nz, 2, shard_rows)
    widths = [w.shape[-1] for w in shards_]
    rounds = KeyValues.copies(sizes) + 2 * arrays * Gather.copies(sizes) + 2

    def at_head(s):
        return jnp.maximum(s - PAIRS, 0)

    results = pl.pallas_call(
        functools.partial(forward_kernel, sizes, rows),
        out_shape=[
            jax.ShapeDtypeStruct((count, QD), BF16),
            jax.ShapeDtypeStruct((2 * count, HEAD_DIM), F32),
            jax.ShapeDtypeStruct((KV_HEADS, count, 3 * HEAD_DIM), F32),
            jax.ShapeDtypeStruct((count, D), BF16),
            jax.ShapeDtypeStruct((8, D), F32),
            jax.ShapeDtypeStruct((8, HEAD_DIM), F32),
            jax.ShapeDtypeStruct(tokens.shape, BF16),
            jax.ShapeDtypeStruct(tokens.shape, BF16),
            jax.ShapeDtypeStruct((KV_HEADS, 2 * count, HEAD_DIM), BF16),
            jax.ShapeDtypeStruct((2, KV_HEADS, TREE, HEAD_DIM), BF16),
            jax.ShapeDtypeStruct((PAIRS,) + blocks + (widths[0],), BF16),
            jax.ShapeDtypeStruct(blocks + (widths[-1],), BF16),
            jax.ShapeDtypeStruct(blocks + (widths[PAIRS],), BF16),
            jax.ShapeDtypeStruct((FF_FIRST,) + blocks + (widths[PAIRS + 1],), BF16),
        ],
        grid_spec=pltpu.PrefetchScalarGridSpec(
            num_scalar_prefetch=1,
            grid=(PAIRS + KV_HEADS,),
            in_specs=[pl.BlockSpec((count, HEAD_DIM), lambda s, meta: (0, 0))] * 2 + [ANY] * (2 + arrays),
            out_specs=[
                pl.BlockSpec((count, 2 * HEAD_DIM), lambda s, meta: (0, at_head(s))),
                pl.BlockSpec((2 * count, HEAD_DIM), lambda s, meta: (0, 0)),
                pl.BlockSpec((2, count, 3 * HEAD_DIM), lambda s, meta: (jnp.minimum(s, PAIRS - 1), 0, 0)),
                pl.BlockSpec((count, D), lambda s, meta: (0, 0)),
                pl.BlockSpec((8, D), lambda s, meta: (0, 0)),
                pl.BlockSpec((8, HEAD_DIM), lambda s, meta: (0, 0)),
            ]
            + [ANY] * 8,
            scratch_shapes=[
                pltpu.VMEM((KV_HEADS, 2 * count, HEAD_DIM), BF16),
                pltpu.VMEM((2, KV_HEADS, TREE, HEAD_DIM), BF16),
                pltpu.VMEM(tokens.shape, BF16),
                pltpu.VMEM((D, widths[0]), BF16),
                pltpu.VMEM((D, widths[-1]), BF16),
                pltpu.VMEM((count, HEAD_DIM), F32),
                pltpu.VMEM((count, HEAD_DIM), F32),
                pltpu.VMEM((count, HEAD_DIM), jnp.int32),
                pltpu.VMEM((LOCAL_RUNS, SEG, HEAD_DIM), BF16),
                pltpu.VMEM((LOCAL_RUNS, SEG, HEAD_DIM), BF16),
                pltpu.SemaphoreType.DMA((rounds,)),
                pltpu.SemaphoreType.DMA((rounds,)),
                pltpu.SemaphoreType.DMA((12 + 2 * arrays,)),
            ],
        ),
        compiler_params=pltpu.CompilerParams(
            collective_id=2, has_side_effects=True, vmem_limit_bytes=56 * MIB
        ),
        name="forward",
    )(meta, cosine, sine, tokens, cotangent, *shards_)
    return results


def feed_kernel(
    sizes, rows, x_ref, mixed_ref, cot_ref, out_ref, gain_ref, first_ref, *refs,
):
    shard = refs[: FF_CHUNKS - FF_FIRST]
    refs = refs[FF_CHUNKS - FF_FIRST :]
    result_ref, hid_ref, stack_ref, delta_ref, post_ref, dout_ref, late_ref, rest_ref, early_ref = refs[:9]
    hidden, second, second_t, cot_t, total, grads, inner, gate_up, low, stack, part, wbuf = refs[9:21]
    buffers = refs[21:-3]
    send_sem, recv_sem, local_sem = refs[-3:]
    ny, nx, nz = sizes
    count = 2 * rows
    sub = rows // SUBS
    shard_rows = part.shape[5]
    width = 3 * FF_CHUNK
    tile = 256
    chunk = pl.program_id(0)
    links = Links(sizes, send_sem, recv_sem)
    _, _, _, core = links.place()
    scatters = []
    for c in range(FF_EARLY):
        for b, cols in enumerate(halves_of(width)):
            k = 4 * len(scatters)
            scatters.append(
                Scatter(
                    links,
                    (c, b),
                    part.at[c % 2],
                    ORDERS[b],
                    cols,
                    *buffers[k : k + 4],
                    part.at[c % 2, :, :, :, core, :, cols],
                    None,
                    early_ref.at[c],
                )
            )

    gathers = [
        [
            Gather(links, ("w", c, b), shard[c], rest_ref.at[c], ORDERS[b], cols, local_sem.at[8 + 2 * c + b])
            for b, cols in enumerate(halves_of(width))
        ]
        for c in range(FF_CHUNKS - FF_FIRST)
    ]

    def fetch(c):
        if c < FF_FIRST:
            pltpu.make_async_copy(first_ref.at[c], wbuf.at[c % 2], local_sem.at[6 + c % 2]).start()
        else:
            for g in gathers[c - FF_FIRST]:
                g.close()
            run_all(
                block_copies(sizes, rest_ref.at[c - FF_FIRST], wbuf.at[c % 2], local_sem.at[6 + c % 2]), "start"
            )

    def act(steps):
        for what, c in steps:
            if what == "fetch":
                fetch(c)
                continue
            if what == "send":
                for g in gathers[c[1] - FF_FIRST]:
                    if c[0] == 0:
                        g.start()
                    else:
                        g.step(c[0])
                continue
            for s in scatters[2 * c : 2 * c + 2]:
                if what == "core":
                    s.start()
                elif what == "begin":
                    s.begin()
                elif what == "finish":
                    s.finish()
                else:
                    s.middle(what)

    def rows_of(block):
        return (block // (2 * nz * nx), lax.rem(block // (2 * nz), nx), lax.rem(block // 2, nz), lax.rem(block, 2))

    def put(slot, first, cols, value):
        for k in range(value.shape[0] // shard_rows):
            y, x, z, c = rows_of(first // shard_rows + k)
            part[slot, y, x, z, c, :, cols] = value[k * shard_rows : (k + 1) * shard_rows].astype(BF16)

    def late(c):
        return pltpu.make_async_copy(part.at[c % 2], late_ref.at[c - FF_EARLY], local_sem.at[c % 2])

    @pl.when(chunk == 0)
    def _():
        links.meet()
        act(FEED_START)

        def project_out(t, carry):
            at = pl.multiple_of(t * tile, tile)
            hidden[:, pl.ds(at, tile)] = x_ref[:, pl.ds(at, tile)].astype(F32) + nt(
                mixed_ref[...], out_ref[pl.ds(at, tile), :]
            )
            return carry

        lax.fori_loop(0, D // tile, project_out, 0)
        act(FEED_NEXT)
        values = hidden[...]
        values = values * norm_factor(values) * gain_ref[1:2]
        second[...] = values.astype(BF16)
        second_t[...] = values.T.astype(BF16)
        cot_t[...] = cot_ref[...].astype(F32).T.astype(BF16)
        total[...] = jnp.zeros_like(total)
        grads[...] = jnp.zeros_like(grads)

    slot = lax.rem(chunk, 2)
    pltpu.make_async_copy(wbuf.at[slot], wbuf.at[slot], local_sem.at[6 + slot]).wait()

    def columns(t, carry):
        at = pl.multiple_of(t * tile, tile)
        gate = matmul(second[...], wbuf[slot, :, pl.ds(at, tile)])
        up = matmul(second[...], wbuf[slot, :, pl.ds(FF_CHUNK + at, tile)])
        grad = matmul(cot_ref[...], wbuf[slot, :, pl.ds(2 * FF_CHUNK + at, tile)])
        sigmoid = 1.0 / (1.0 + jnp.exp(-gate))
        active = gate * sigmoid
        inner[:, pl.ds(at, tile)] = (active * up).astype(BF16)
        gate_up[:, pl.ds(at, tile)] = (grad * up * sigmoid * (1.0 + gate * (1.0 - sigmoid))).astype(BF16)
        gate_up[:, pl.ds(FF_CHUNK + at, tile)] = (grad * active).astype(BF16)
        return carry

    lax.fori_loop(0, FF_CHUNK // tile, columns, 0)
    for moment, steps in FEED_MIDDLE.items():
        pl.when(chunk == moment)(functools.partial(act, steps))
    for c in range(FF_EARLY, FF_CHUNKS - 2):
        pl.when(chunk == c + 2)(lambda: late(c).wait())

    def model(t, carry):
        at = pl.multiple_of(t * tile, tile)
        total[:, pl.ds(at, tile)] += nt(inner[...], wbuf[slot, pl.ds(at, tile), 2 * FF_CHUNK :])
        grads[:, pl.ds(at, tile)] += nt(gate_up[...], wbuf[slot, pl.ds(at, tile), : 2 * FF_CHUNK])
        put(slot, at, slice(0, 2 * FF_CHUNK), matmul(second_t[pl.ds(at, tile)], gate_up[...]))
        put(slot, at, slice(2 * FF_CHUNK, width), matmul(cot_t[pl.ds(at, tile)], inner[...]))
        return carry

    lax.fori_loop(0, D // tile, model, 0)
    for c in range(FF_EARLY, FF_CHUNKS):
        pl.when(chunk == c)(lambda: late(c).start())
    for moment, steps in FEED_AFTER.items():
        pl.when(chunk == moment)(functools.partial(act, steps))

    @pl.when(chunk == FF_CHUNKS - 1)
    def _():
        values = hidden[...]
        low[...] = (values + total[...]).astype(BF16)
        output = pltpu.make_async_copy(low, result_ref, local_sem.at[2])
        output.start()
        factor = norm_factor(values)
        grad_in, share = norm_backward(grads[...], gain_ref[1:2], values * factor, factor)
        post_ref[...] = jnp.sum(share, axis=0, keepdims=True)
        hidden[...] = cot_ref[...].astype(F32) + grad_in
        saved = pltpu.make_async_copy(hidden, hid_ref, local_sem.at[3])
        saved.start()
        second[...] = hidden[...].astype(BF16)
        second_t[...] = hidden[...].T.astype(BF16)
        lane = lax.broadcasted_iota(jnp.int32, (count, HEAD_DIM), 1)
        dots = jnp.zeros((count, HEAD_DIM), F32)
        for h in range(KV_HEADS):
            cols = slice(2 * h * HEAD_DIM, 2 * (h + 1) * HEAD_DIM)
            grad = matmul(second[...], out_ref[:, cols]).astype(BF16)
            for g in range(2):
                one = grad[:, g * HEAD_DIM : (g + 1) * HEAD_DIM]
                for s in range(2 * SUBS):
                    stack[h, (2 * s + g) * sub : (2 * s + g + 1) * sub] = one[s * sub : (s + 1) * sub]
                head = 2 * h + g
                product = one.astype(F32) * mixed_ref[:, head * HEAD_DIM : (head + 1) * HEAD_DIM].astype(F32)
                dots = jnp.where(lane == head, jnp.sum(product, axis=-1, keepdims=True), dots)
        delta_ref[...] = dots.T
        stacked_ = pltpu.make_async_copy(stack, stack_ref, local_sem.at[4])
        stacked_.start()
        act(FEED_LAST)
        for c in range(FF_CHUNKS - 2, FF_CHUNKS):
            late(c).wait()

        def model_out(t, carry):
            at = pl.multiple_of(t * tile, tile)
            for a in range(0, QD, 2 * FF_CHUNK):
                cols = slice(a, a + 2 * FF_CHUNK)
                value = matmul(second_t[pl.ds(at, tile)], mixed_ref[:, cols])
                slot = a // (2 * FF_CHUNK)
                put(slot, at, slice(0, 2 * FF_CHUNK), value)
            return carry

        lax.fori_loop(0, D // tile, model_out, 0)
        gone = [
            pltpu.make_async_copy(
                part.at[k, :, :, :, :, :, : 2 * FF_CHUNK],
                dout_ref.at[:, :, :, :, :, 2 * FF_CHUNK * k : 2 * FF_CHUNK * (k + 1)],
                local_sem.at[k],
            )
            for k in range(2)
        ]
        run_all(gone, "start")
        for c in range(FF_EARLY):
            act([("finish", c)])
        run_all(gone + [output, saved, stacked_], "wait")


def feed(sizes, x, mixed, cot, out_t, gain, first, shards_):
    ny, nx, nz = sizes
    count = x.shape[0]
    rows = count // 2
    shard_rows = D // (ny * nx * nz * 2)
    width = 3 * FF_CHUNK
    buffers = []
    for c in range(FF_EARLY):
        for b, cols in enumerate(halves_of(width)):
            buffers += Scatter.scratch(sizes, ORDERS[b], shard_rows, cols.stop - cols.start)
    late = FF_CHUNKS - FF_FIRST
    rounds = 2 * FF_EARLY * Scatter.copies(sizes) + 2 * late * Gather.copies(sizes)

    def whole_block(shape):
        return pl.BlockSpec(shape, lambda c: (0,) * len(shape), pipeline_mode=pl.Buffered(1))

    blocks = (ny, nx, nz, 2, shard_rows)
    return pl.pallas_call(
        functools.partial(feed_kernel, sizes, rows),
        grid=(FF_CHUNKS,),
        out_shape=[
            jax.ShapeDtypeStruct((count, D), BF16),
            jax.ShapeDtypeStruct((count, D), F32),
            jax.ShapeDtypeStruct((KV_HEADS, 2 * count, HEAD_DIM), BF16),
            jax.ShapeDtypeStruct((HEAD_DIM, count), F32),
            jax.ShapeDtypeStruct((1, D), F32),
            jax.ShapeDtypeStruct(blocks + (QD,), BF16),
            jax.ShapeDtypeStruct((FF_CHUNKS - FF_EARLY,) + blocks + (width,), BF16),
            jax.ShapeDtypeStruct((late,) + blocks + (width,), BF16),
            jax.ShapeDtypeStruct((FF_EARLY, shard_rows, width), F32),
        ],
        in_specs=[
            whole_block((count, D)),
            whole_block((count, QD)),
            whole_block((count, D)),
            whole_block((D, QD)),
            whole_block((8, D)),
            ANY,
        ]
        + [ANY] * late,
        out_specs=[
            ANY,
            ANY,
            ANY,
            pl.BlockSpec((HEAD_DIM, count), lambda c: (0, 0)),
            pl.BlockSpec((1, D), lambda c: (0, 0)),
            ANY,
            ANY,
            ANY,
            pl.BlockSpec((FF_EARLY, shard_rows, width), lambda c: (0, 0, 0)),
        ],
        scratch_shapes=[
            pltpu.VMEM((count, D), F32),
            pltpu.VMEM((count, D), BF16),
            pltpu.VMEM((D, count), BF16),
            pltpu.VMEM((D, count), BF16),
            pltpu.VMEM((count, D), F32),
            pltpu.VMEM((count, D), F32),
            pltpu.VMEM((count, FF_CHUNK), BF16),
            pltpu.VMEM((count, 2 * FF_CHUNK), BF16),
            pltpu.VMEM((count, D), BF16),
            pltpu.VMEM((KV_HEADS, 2 * count, HEAD_DIM), BF16),
            pltpu.VMEM((2,) + blocks + (width,), BF16),
            pltpu.VMEM((2, D, width), BF16),
        ]
        + buffers
        + [
            pltpu.SemaphoreType.DMA((rounds,)),
            pltpu.SemaphoreType.DMA((rounds,)),
            pltpu.SemaphoreType.DMA((8 + 2 * late,)),
        ],
        compiler_params=pltpu.CompilerParams(
            collective_id=5, has_side_effects=True, vmem_limit_bytes=61 * MIB
        ),
        name="feed",
    )(x, mixed, cot, out_t, gain, first, *shards_)


def backward_kernel(sizes, rows, widths, meta, q_ref, g_ref, k_ref, v_ref, lse_ref, del_ref, late_ref, dout_ref, done_ref, *refs):
    dq_ref, dkv_ref, late_out, dout_out, done_placed = refs[:5]
    dq, dk, dv, pk, pv, kp, vp, stage, near, sums, far, last = refs[5:17]
    buffers = refs[17:-3]
    send_sem, recv_sem, local_sem = refs[-3:]
    members = sizes[2]
    chips = members // 2
    sub = rows // SUBS
    head = pl.program_id(0)
    links = Links(sizes, send_sem, recv_sem)
    scatters = []
    late = FF_CHUNKS - FF_EARLY
    for a, width in enumerate(widths):
        for b, cols in enumerate(halves_of(width)):
            k = 5 * len(scatters)
            scatters.append(
                Scatter(
                    links,
                    (a, b),
                    late_ref.at[a] if a < late else dout_ref,
                    ORDERS[b],
                    cols,
                    *buffers[k : k + 5],
                    local_sem.at[2 + len(scatters)],
                    late_out.at[a] if a < late else dout_out,
                )
            )

    swap = Exchange(links, done_ref, done_placed, local_sem.at[2 + len(scatters)])

    def each(array):
        return scatters[2 * array : 2 * array + 2]

    @pl.when(head == 0)
    def _():
        for s in scatters:
            s.load().start()
        links.meet()
        for s in scatters:
            s.start()
        swap.start()

    _, _, z, core = links.place()
    here = lax.rem(z, chips)
    mine = here * 2 + core
    dk[...] = jnp.zeros_like(dk)
    dv[...] = jnp.zeros_like(dv)
    pk[...] = jnp.zeros_like(pk)
    pv[...] = jnp.zeros_like(pv)
    for piece in range(2):
        base = rows * (piece * members + mine)
        at = piece * 2 * rows
        region = slice(at, at + 2 * rows)
        dq[...] = jnp.zeros_like(dq)

        def pair(key, value, block, mask):
            spot = slice(at + block.start, at + block.stop)
            weights = jnp.exp2(nt(key, q_ref[0, spot]) * exp2_scale - lse_ref[0, :, spot])
            if mask is not None:
                weights = mask(weights)
            grads = (weights * (nt(value, g_ref[0, spot]) - del_ref[0, :, spot])).astype(BF16)
            weights = weights.astype(BF16)
            dq[block] += contract_rows(grads, key)
            return matmul(grads, q_ref[0, spot]), matmul(weights, g_ref[0, spot])

        everything = slice(0, 2 * rows)

        def trunk(step, masked):
            start = pl.multiple_of(step * CHUNK, CHUNK)

            def mask(weights):
                shape = weights.shape
                room = row_places((1, shape[1]), 1, sub) + (base - start)
                return jnp.where(lax.broadcasted_iota(jnp.int32, shape, 0) <= room, weights, 0.0)

            key_grad, value_grad = pair(
                k_ref[0, 0, pl.ds(start, CHUNK)],
                v_ref[0, 0, pl.ds(start, CHUNK)],
                everything,
                mask if masked else None,
            )
            dk[pl.ds(start, CHUNK)] += key_grad
            dv[pl.ds(start, CHUNK)] += value_grad

        if piece == 0:
            clear = jnp.minimum(base // CHUNK, TRUNK // CHUNK)
            end = jnp.minimum((base + rows + CHUNK - 1) // CHUNK, TRUNK // CHUNK)
            lax.fori_loop(0, clear, lambda i, c: (trunk(i, False), c)[1], 0)
            lax.fori_loop(clear, end, lambda i, c: (trunk(i, True), c)[1], 0)
        else:
            lax.fori_loop(0, TRUNK // CHUNK, lambda i, c: (trunk(i, False), c)[1], 0)

        lead = jnp.maximum(base - TRUNK, 0) // SEG

        def parents_():
            gather_parents(
                meta,
                lead,
                0,
                [
                    (lambda b: k_ref[0, 0, TRUNK + b * SEG : TRUNK + (b + 1) * SEG], kp),
                    (lambda b: v_ref[0, 0, TRUNK + b * SEG : TRUNK + (b + 1) * SEG], vp),
                ],
            )

        if piece == 0:
            pl.when(base + rows > TRUNK)(parents_)
        else:
            parents_()
        for s in range(SUBS):
            block = slice(2 * sub * s, 2 * sub * (s + 1))

            def runs():
                row = base + s * sub - TRUNK
                run = row // SEG
                own = pl.multiple_of(TRUNK + run * SEG, SEG)
                flag = jnp.minimum(meta[run] + 1, 1).astype(F32)

                def mask(weights):
                    shape = (SEG, 2 * sub)
                    room = lax.broadcasted_iota(jnp.int32, shape, 1) % sub + lax.rem(row, SEG)
                    seen = lax.broadcasted_iota(jnp.int32, shape, 0) <= room
                    return jnp.concatenate(
                        [jnp.where(seen, weights[:SEG], 0.0), weights[SEG:] * flag], axis=0
                    )

                key_grad, value_grad = pair(
                    jnp.concatenate([k_ref[0, 0, pl.ds(own, SEG)], kp[run - lead]], axis=0),
                    jnp.concatenate([v_ref[0, 0, pl.ds(own, SEG)], vp[run - lead]], axis=0),
                    block,
                    mask,
                )
                dk[pl.ds(own, SEG)] += key_grad[:SEG]
                dv[pl.ds(own, SEG)] += value_grad[:SEG]
                slot = LOCAL_RUNS * piece + run - lead
                pk[slot] += key_grad[SEG:]
                pv[slot] += value_grad[SEG:]

            if piece == 0:
                pl.when(base + s * sub >= TRUNK)(runs)
            else:
                runs()

        dq_ref[0, region] = dq[...] * score_scale

        def spread():
            parents = [meta[jnp.minimum(lead + k, TREE // SEG - TRUNK // SEG - 1)] for k in range(LOCAL_RUNS)]

            def place(b, carry):
                start = pl.multiple_of(TRUNK + b * SEG, SEG)
                key_grad, value_grad = dk[pl.ds(start, SEG)], dv[pl.ds(start, SEG)]
                for k in range(LOCAL_RUNS):
                    share = (1 - jnp.minimum(jnp.abs(parents[k] - b), 1)).astype(F32)
                    key_grad += pk[LOCAL_RUNS * piece + k] * share
                    value_grad += pv[LOCAL_RUNS * piece + k] * share
                dk[pl.ds(start, SEG)] = key_grad
                dv[pl.ds(start, SEG)] = value_grad
                return carry

            lax.fori_loop(0, (TREE - TRUNK) // SEG, place, 0)

        if piece == 0:
            pl.when(base + rows > TRUNK)(spread)
        else:
            spread()

    def core_copy(h):
        return links.copy(("kv core", h), stage.at[h % 2, :, 1 - core], near.at[h % 2], links.sibling())

    def far_copies(h):
        return [
            links.copy(("kv z", h, i), sums.at[h, chip], far.at[h, i], target)
            for i, (chip, target) in enumerate(links.group())
        ]

    def pass_on(h):
        core_copy(h).wait()

        def add(i, carry):
            chip, which, piece = i // 4, lax.rem(i // 2, 2), lax.rem(i, 2)
            sums[h, chip, which, piece] = (
                stage[h % 2, chip, core, which, piece].astype(F32) + near[h % 2, chip, which, piece].astype(F32)
            ).astype(BF16)
            return carry

        lax.fori_loop(0, chips * 4, add, 0)
        run_all(far_copies(h), "start")

    for h in range(1, KV_HEADS):
        pl.when(head == h)(functools.partial(pass_on, h - 1))

    for which, grad, scale in ((0, dk, score_scale), (1, dv, 1.0)):
        for piece in range(2):
            for member in range(members):
                start = rows * (piece * members + member)
                stage[lax.rem(head, 2), member // 2, member % 2, which, piece] = (
                    grad[start : start + rows] * scale
                ).astype(BF16)
    for h in range(KV_HEADS):

        @pl.when(head == h)
        def _():
            core_copy(h).start()

    for moment, steps in BACKWARD_AFTER.items():

        @pl.when(head == moment)
        def _():
            for step, array in steps:
                for s in each(array):
                    if step == 0:
                        s.begin()
                    else:
                        s.middle(step - 1)

    def result(h):
        return pltpu.make_async_copy(last.at[h % 2], dkv_ref.at[:, h], local_sem.at[h % 2])

    @pl.when(head == KV_HEADS - 1)
    def _():
        pass_on(KV_HEADS - 1)
        for s in scatters:
            s.finish()
        for h in range(KV_HEADS):
            run_all(far_copies(h), "wait")
            if h > 1:
                result(h - 2).wait()
            for which in range(2):
                for piece in range(2):
                    total = sums[h, here, which, piece].astype(F32)
                    for i in range(chips - 1):
                        total = total + far[h, i, which, piece].astype(F32)
                    last[h % 2, which, piece] = total
            result(h).start()
        for h in (KV_HEADS - 2, KV_HEADS - 1):
            result(h).wait()
        swap.wait()


def backward(sizes, meta, queries, grads, kv_all, log_total, delta, late, dout, done):
    ny, nx, nz = sizes
    chips = nz // 2
    rows = queries.shape[1] // 4
    widths = (late.shape[-1],) * late.shape[0] + (dout.shape[-1],)
    shard_rows = dout.shape[4]
    stack = pl.BlockSpec((1, 4 * rows, HEAD_DIM), lambda h, meta: (h, 0, 0))
    line = pl.BlockSpec((1, 1, 4 * rows), lambda h, meta: (h, 0, 0))
    buffers, count = [], 0
    for w in widths:
        for b, cols in enumerate(halves_of(w)):
            buffers += Scatter.scratch(sizes, ORDERS[b], shard_rows, cols.stop - cols.start)
            buffers.append(pltpu.VMEM((ny, nx, nz, shard_rows, cols.stop - cols.start), BF16))
            count += 1
    rounds = count * Scatter.copies(sizes) + KV_HEADS * chips + 1
    late_shape = (late.shape[0], shard_rows, late.shape[-1])
    dout_shape = (shard_rows, dout.shape[-1])
    return pl.pallas_call(
        functools.partial(backward_kernel, sizes, rows, widths),
        out_shape=[
            jax.ShapeDtypeStruct((KV_HEADS, 4 * rows, HEAD_DIM), F32),
            jax.ShapeDtypeStruct((2, KV_HEADS, 2, rows, HEAD_DIM), F32),
            jax.ShapeDtypeStruct(late_shape, F32),
            jax.ShapeDtypeStruct(dout_shape, F32),
            jax.ShapeDtypeStruct(done.shape, BF16),
        ],
        grid_spec=pltpu.PrefetchScalarGridSpec(
            num_scalar_prefetch=1,
            grid=(KV_HEADS,),
            in_specs=[
                stack,
                stack,
                pl.BlockSpec((1, 1, TREE, HEAD_DIM), lambda h, meta: (0, h, 0, 0)),
                pl.BlockSpec((1, 1, TREE, HEAD_DIM), lambda h, meta: (1, h, 0, 0)),
                line,
                line,
                ANY,
                ANY,
                ANY,
            ],
            out_specs=[
                stack,
                ANY,
                pl.BlockSpec(late_shape, lambda h, meta: (0, 0, 0)),
                pl.BlockSpec(dout_shape, lambda h, meta: (0, 0)),
                ANY,
            ],
            scratch_shapes=[
                pltpu.VMEM((2 * rows, HEAD_DIM), F32),
                pltpu.VMEM((TREE, HEAD_DIM), F32),
                pltpu.VMEM((TREE, HEAD_DIM), F32),
                pltpu.VMEM((2 * LOCAL_RUNS, SEG, HEAD_DIM), F32),
                pltpu.VMEM((2 * LOCAL_RUNS, SEG, HEAD_DIM), F32),
                pltpu.VMEM((LOCAL_RUNS, SEG, HEAD_DIM), BF16),
                pltpu.VMEM((LOCAL_RUNS, SEG, HEAD_DIM), BF16),
                pltpu.VMEM((2, chips, 2, 2, 2, rows, HEAD_DIM), BF16),
                pltpu.VMEM((2, chips, 2, 2, rows, HEAD_DIM), BF16),
                pltpu.VMEM((KV_HEADS, chips, 2, 2, rows, HEAD_DIM), BF16),
                pltpu.VMEM((KV_HEADS, chips - 1, 2, 2, rows, HEAD_DIM), BF16),
                pltpu.VMEM((2, 2, 2, rows, HEAD_DIM), F32),
            ]
            + buffers
            + [
                pltpu.SemaphoreType.DMA((rounds,)),
                pltpu.SemaphoreType.DMA((rounds,)),
                pltpu.SemaphoreType.DMA((3 + count,)),
            ],
        ),
        compiler_params=pltpu.CompilerParams(
            collective_id=3, has_side_effects=True, vmem_limit_bytes=60 * MIB
        ),
        name="backward",
    )(
        meta,
        queries,
        grads,
        kv_all,
        kv_all,
        log_total.reshape(KV_HEADS, 1, 4 * rows),
        delta.reshape(KV_HEADS, 1, 4 * rows),
        late,
        dout,
        done,
    )


def finish_kernel(
    sizes, rows, dq_ref, dkv_ref, pre_ref, w_ref, normed_ref, x_ref, hid_ref, gain_ref, post_ref, qk_ref, cos_ref, sin_ref,
    q_out, k_out, v_out, g_out, dx_placed, *refs,
):
    normed_t, low, grads, qk, sums, dx, part, part_g = refs[:8]
    buffers = refs[8:-3]
    send_sem, recv_sem, local_sem = refs[-3:]
    ny, nx, nz = sizes
    count = 2 * rows
    sub = rows // SUBS
    shard_rows = part.shape[5]
    tile = 256
    pair = pl.program_id(0)
    links = Links(sizes, send_sem, recv_sem)
    _, _, _, core = links.place()
    swap = Exchange(links, dx, dx_placed, local_sem.at[0])

    def to_query(c):
        def store(total):
            q_out[:, 4 * HEAD_DIM * c : 4 * HEAD_DIM * (c + 1)] = total

        return store

    def to_key_value(c):
        def store(total):
            k_out[:, 2 * HEAD_DIM * c : 2 * HEAD_DIM * (c + 1)] = total[:, : 2 * HEAD_DIM]
            v_out[:, 2 * HEAD_DIM * c : 2 * HEAD_DIM * (c + 1)] = total[:, 2 * HEAD_DIM :]

        return store

    scatters = []
    for c in range(PAIRS):
        for b, cols in enumerate(halves_of(8 * HEAD_DIM)):
            k = 4 * len(scatters)
            scatters.append(
                Scatter(
                    links,
                    (c, b),
                    part.at[c % 2],
                    ORDERS[b],
                    cols,
                    *buffers[k : k + 4],
                    part.at[c % 2, :, :, :, core, :, cols],
                    None,
                    to_key_value(c) if b else to_query(c),
                )
            )
    k = 4 * len(scatters)
    whole = slice(0, 3 * GAIN_COLS)
    scatters.append(
        Scatter(
            links, "gains", part_g, ORDERS[0], whole, *buffers[k : k + 4], part_g.at[:, :, :, core], None, g_out
        )
    )

    def act(steps):
        for what, c in steps:
            for s in scatters[2 * c : 2 * c + 2]:
                if what == "core":
                    s.start()
                elif what == "begin":
                    s.begin()
                elif what == "finish":
                    s.finish()
                else:
                    s.middle(what)

    def rows_of(block):
        return (block // (2 * nz * nx), lax.rem(block // (2 * nz), nx), lax.rem(block // 2, nz), lax.rem(block, 2))

    @pl.when(pair == 0)
    def _():
        links.meet()
        normed_t[...] = normed_ref[...].astype(F32).T.astype(BF16)
        grads[...] = jnp.zeros_like(grads)
        qk[...] = jnp.zeros_like(qk)

    cosine, sine = cos_ref[...], sin_ref[...]

    def back(turned_grad, pre, gain):
        grad = turned_grad * cosine - roll_half(turned_grad) * sine
        factor = norm_factor(pre)
        grad_pre, share = norm_backward(grad, gain, pre * factor, factor)
        return grad_pre.astype(BF16), jnp.sum(share, axis=0, keepdims=True)

    for hh in range(2):
        for h in range(2):
            grad = jnp.concatenate(
                [dq_ref[hh, (2 * s + h) * sub : (2 * s + h + 1) * sub] for s in range(2 * SUBS)], axis=0
            )
            value, share = back(grad, pre_ref[hh, :, h * HEAD_DIM : (h + 1) * HEAD_DIM], qk_ref[0:1])
            qk[0:1] += share
            at = 2 * hh + h
            low[:, at * HEAD_DIM : (at + 1) * HEAD_DIM] = value
        value, share = back(dkv_ref[0, hh].reshape(count, HEAD_DIM), pre_ref[hh, :, 2 * HEAD_DIM :], qk_ref[1:2])
        qk[1:2] += share
        low[:, (4 + hh) * HEAD_DIM : (5 + hh) * HEAD_DIM] = value
        low[:, (6 + hh) * HEAD_DIM : (7 + hh) * HEAD_DIM] = dkv_ref[1, hh].reshape(count, HEAD_DIM).astype(BF16)
    def inward(t, carry):
        at = pl.multiple_of(t * tile, tile)
        grads[:, pl.ds(at, tile)] += nt(low[...], w_ref[0, pl.ds(at, tile), :])
        return carry

    lax.fori_loop(0, D // tile, inward, 0)

    @pl.when(pair == PAIRS - 1)
    def _():
        values = x_ref[...].astype(F32)
        factor = norm_factor(values)
        grad_in, share = norm_backward(grads[...], gain_ref[0:1], values * factor, factor)
        dx[...] = (hid_ref[...] + grad_in).astype(BF16).reshape(2, rows, D)
        swap.start()
        sums[...] = jnp.sum(share, axis=0, keepdims=True)

    for moment, steps in FINISH_MIDDLE.items():
        pl.when(pair == moment)(functools.partial(act, steps))
    slot = lax.rem(pair, 2)

    def model(t, carry):
        at = pl.multiple_of(t * tile, tile)
        value = matmul(normed_t[pl.ds(at, tile)], low[...])
        for k in range(tile // shard_rows):
            y, x, z, c = rows_of(at // shard_rows + k)
            part[slot, y, x, z, c] = value[k * shard_rows : (k + 1) * shard_rows].astype(BF16)
        return carry

    lax.fori_loop(0, D // tile, model, 0)
    for moment, steps in FINISH_AFTER.items():
        pl.when(pair == moment)(functools.partial(act, steps))

    @pl.when(pair == PAIRS - 1)
    def _():
        lines = jnp.concatenate(
            [sums[...], post_ref[...], jnp.zeros((GAIN_COLS - 2, D), F32)], axis=0
        )
        columns = lines.T.astype(BF16)
        first = lax.broadcasted_iota(jnp.int32, (shard_rows, GAIN_COLS), 0) == 0
        query_line = jnp.where(first, qk[0:1], 0.0).astype(BF16)
        key_line = jnp.where(first, qk[1:2], 0.0).astype(BF16)
        for k in range(D // shard_rows):
            y, x, z, c = k // (2 * nz * nx), k // (2 * nz) % nx, k // 2 % nz, k % 2
            part_g[y, x, z, c, :, :GAIN_COLS] = columns[k * shard_rows : (k + 1) * shard_rows]
            part_g[y, x, z, c, :, GAIN_COLS : 2 * GAIN_COLS] = query_line
            part_g[y, x, z, c, :, 2 * GAIN_COLS :] = key_line
        act([("core", PAIRS), (0, PAIRS - 2), ("begin", PAIRS - 1), ("begin", PAIRS), (1, PAIRS - 2)])
        act([(0, PAIRS - 1), (0, PAIRS), (1, PAIRS - 1), (1, PAIRS)])
        for c in range(PAIRS + 1):
            act([("finish", c)])
        swap.wait()


def finish(sizes, dq, dkv, pre, normed, x, grad_hidden, gain, post_part, qkv_full, qk_gain, cosine, sine):
    ny, nx, nz = sizes
    count = x.shape[0]
    rows = count // 2
    shard_rows = D // (ny * nx * nz * 2)
    blocks = (ny, nx, nz, 2, shard_rows)
    width = 8 * HEAD_DIM

    def whole_block(shape):
        return pl.BlockSpec(shape, lambda c: (0,) * len(shape), pipeline_mode=pl.Buffered(1))

    buffers = []
    for c in range(PAIRS):
        for b, cols in enumerate(halves_of(width)):
            buffers += Scatter.scratch(sizes, ORDERS[b], shard_rows, cols.stop - cols.start)
    buffers += Scatter.scratch(sizes, ORDERS[0], shard_rows, 3 * GAIN_COLS)
    rounds = (2 * PAIRS + 1) * Scatter.copies(sizes) + 1

    def out_block(n):
        return pl.BlockSpec((shard_rows, n), lambda c: (0, 0))

    return pl.pallas_call(
        functools.partial(finish_kernel, sizes, rows),
        grid=(PAIRS,),
        out_shape=[
            jax.ShapeDtypeStruct((shard_rows, QD), F32),
            jax.ShapeDtypeStruct((shard_rows, KVD), F32),
            jax.ShapeDtypeStruct((shard_rows, KVD), F32),
            jax.ShapeDtypeStruct((shard_rows, 3 * GAIN_COLS), F32),
            jax.ShapeDtypeStruct((2, rows, D), BF16),
        ],
        in_specs=[
            pl.BlockSpec((2, 2 * count, HEAD_DIM), lambda c: (c, 0, 0)),
            pl.BlockSpec((2, 2, 2, rows, HEAD_DIM), lambda c: (0, c, 0, 0, 0)),
            pl.BlockSpec((2, count, 3 * HEAD_DIM), lambda c: (c, 0, 0)),
            pl.BlockSpec((1, D, width), lambda c: (c, 0, 0)),
            whole_block((count, D)),
            whole_block((count, D)),
            whole_block((count, D)),
            whole_block((8, D)),
            whole_block((1, D)),
            whole_block((8, HEAD_DIM)),
            whole_block((count, HEAD_DIM)),
            whole_block((count, HEAD_DIM)),
        ],
        out_specs=[out_block(QD), out_block(KVD), out_block(KVD), out_block(3 * GAIN_COLS), ANY],
        scratch_shapes=[
            pltpu.VMEM((D, count), BF16),
            pltpu.VMEM((count, width), BF16),
            pltpu.VMEM((count, D), F32),
            pltpu.VMEM((8, HEAD_DIM), F32),
            pltpu.VMEM((1, D), F32),
            pltpu.VMEM((2, rows, D), BF16),
            pltpu.VMEM((2,) + blocks + (width,), BF16),
            pltpu.VMEM(blocks + (3 * GAIN_COLS,), BF16),
        ]
        + buffers
        + [
            pltpu.SemaphoreType.DMA((rounds,)),
            pltpu.SemaphoreType.DMA((rounds,)),
            pltpu.SemaphoreType.DMA((1,)),
        ],
        compiler_params=pltpu.CompilerParams(
            collective_id=4, has_side_effects=True, vmem_limit_bytes=58 * MIB
        ),
        name="finish",
    )(dq, dkv, pre, qkv_full, normed, x, grad_hidden, gain, post_part, qk_gain, cosine, sine)


def shards(
    sizes,
    tokens,
    cotangent,
    segment_ids,
    positions,
    parents,
    input_norm,
    query_proj,
    key_proj,
    value_proj,
    query_norm,
    key_norm,
    out_proj,
    post_norm,
    gate_proj,
    up_proj,
    down_proj,
):
    nz = sizes[2]
    rows = tokens.shape[1]
    shard_rows = query_proj.shape[0]
    gain_rows = query_norm.shape[0]
    ctx = lax.axis_index("ctx")
    half = ctx // nz
    member = ctx % nz
    count = 2 * rows
    sub = rows // SUBS

    device = lax.axis_index("dp") * 2 * nz + ctx

    def spread(gain):
        line = jnp.zeros((1, HEAD_DIM), BF16)
        line = lax.dynamic_update_slice(line, gain[None, :], (0, device * gain_rows))
        return jnp.pad(line, ((0, shard_rows - 1), (0, 0)))

    gains = jnp.pad(
        jnp.stack([input_norm, post_norm], axis=1), ((0, 0), (0, GAIN_COLS - 2))
    )
    gains = jnp.concatenate([gains, spread(query_norm), spread(key_norm)], axis=1)
    qkv_shards = [
        jnp.concatenate(
            [
                query_proj[:, 4 * HEAD_DIM * c : 4 * HEAD_DIM * (c + 1)],
                key_proj[:, 2 * HEAD_DIM * c : 2 * HEAD_DIM * (c + 1)],
                value_proj[:, 2 * HEAD_DIM * c : 2 * HEAD_DIM * (c + 1)],
            ],
            axis=1,
        )
        for c in range(PAIRS)
    ]
    down_t = down_proj.T
    feed_shards = [
        jnp.concatenate(
            [w[:, c * FF_CHUNK : (c + 1) * FF_CHUNK] for w in (gate_proj, up_proj, down_t)], axis=1
        )
        for c in range(FF_CHUNKS)
    ]

    run_seg = segment_ids[half][TRUNK::SEG]
    run_parent = parents[half][run_seg]
    parent_run = jnp.argmax(run_seg[None, :] == run_parent[:, None], axis=1).astype(jnp.int32)
    meta = jnp.where(run_parent > 0, parent_run, -1)
    pos_tree = positions[half].reshape(2, nz, rows)
    pos_local = lax.dynamic_index_in_dim(pos_tree, member, 1, keepdims=False).reshape(count)
    cosine, sine = rope_tables(pos_local)

    (mixed, totals, pre, normed, gain_rows_, qk_gains, placed, cot, queries, kv_all,
     qkv_full, _, out_t, feed_whole) = forward(
        sizes, meta, cosine, sine, tokens, cotangent, qkv_shards + [out_proj.T] + feed_shards[:FF_FIRST] + [gains]
    )
    x = placed.reshape(count, D)
    cot = cot.reshape(count, D)
    qkv_full = qkv_full.reshape(PAIRS, D, -1)
    out_t = out_t.reshape(D, QD)
    feed_whole = feed_whole.reshape(FF_FIRST, D, -1)
    log_total = jnp.log2(totals[:, :KV_HEADS]).T
    result, grad_hidden, grad_stack, delta, post_part, dout, late, _, early_grad = feed(
        sizes, x, mixed, cot, out_t, gain_rows_, feed_whole, feed_shards[FF_FIRST:]
    )
    delta = delta[:HEADS].reshape(KV_HEADS, 2, 2 * SUBS, sub).transpose(0, 2, 1, 3)
    dq, dkv, late_grad, out_grad, output = backward(
        sizes, meta, queries, grad_stack, kv_all, log_total, delta, late, dout, result.reshape(2, rows, D)
    )
    feed_grad = jnp.concatenate([early_grad, late_grad], axis=0)

    def feed_columns(k):
        piece = feed_grad[:, :, k * FF_CHUNK : (k + 1) * FF_CHUNK]
        return piece.transpose(1, 0, 2).reshape(shard_rows, FF)

    query_grad, key_grad, value_grad, gain_grad, input_grad = finish(
        sizes, dq, dkv, pre, normed, x, grad_hidden, gain_rows_, post_part, qkv_full, qk_gains, cosine, sine
    )

    def own(line):
        return lax.dynamic_slice_in_dim(line, device * gain_rows, gain_rows)

    return (
        output,
        input_grad.astype(F32),
        gain_grad[:, 0],
        query_grad,
        key_grad,
        value_grad,
        own(gain_grad[0, GAIN_COLS : 2 * GAIN_COLS]),
        own(gain_grad[0, 2 * GAIN_COLS :]),
        out_grad.T,
        gain_grad[:, 1],
        feed_columns(0),
        feed_columns(1),
        feed_columns(2).T,
    )


def solution(mesh):
    dp, ctx = mesh.shape["dp"], mesh.shape["ctx"]
    sizes = (2, dp // 2, ctx // 2)
    return jax.shard_map(
        functools.partial(shards, sizes),
        mesh=mesh,
        in_specs=(
            P("dp", "ctx", None),
            P("dp", "ctx", None),
            P("dp", None),
            P("dp", None),
            P("dp", None),
            P(("dp", "ctx")),
            P(("dp", "ctx"), None),
            P(("dp", "ctx"), None),
            P(("dp", "ctx"), None),
            P(("dp", "ctx")),
            P(("dp", "ctx")),
            P(None, ("dp", "ctx")),
            P(("dp", "ctx")),
            P(("dp", "ctx"), None),
            P(("dp", "ctx"), None),
            P(None, ("dp", "ctx")),
        ),
        out_specs=(
            P("dp", "ctx", None),
            P("dp", "ctx", None),
            P(("dp", "ctx")),
            P(("dp", "ctx"), None),
            P(("dp", "ctx"), None),
            P(("dp", "ctx"), None),
            P(("dp", "ctx")),
            P(("dp", "ctx")),
            P(None, ("dp", "ctx")),
            P(("dp", "ctx")),
            P(("dp", "ctx"), None),
            P(("dp", "ctx"), None),
            P(None, ("dp", "ctx")),
        ),
        check_vma=False,
    )
```

```python
import functools
import math

import jax
import jax.numpy as jnp
from jax import lax
from jax.experimental import pallas as pl
from jax.experimental.pallas import tpu as pltpu
from jax.sharding import PartitionSpec as P

D = 1024
HEADS = 16
KV_HEADS = 8
HEAD_DIM = 128
FF = 3072
TRUNK = 1024
SEG = 128
TREE = 2560
QD = HEADS * HEAD_DIM
KVD = KV_HEADS * HEAD_DIM
SUBS = 5
CHUNK = 256
GAIN_COLS = 128
FF_CHUNK = 512
PAIRS = KV_HEADS // 2
FF_CHUNKS = FF // FF_CHUNK
FF_EARLY = 2
FF_FIRST = 4
LOCAL_RUNS = 3
MIB = 1024 * 1024

eps_norm = 1e-06
rope_base = 1000000.0
exp2_scale = math.log2(math.e) / math.sqrt(HEAD_DIM)
score_scale = HEAD_DIM ** (-0.5)

MESH = pl.DeviceIdType.MESH
ANY = pl.BlockSpec(memory_space=pl.ANY)
F32 = jnp.float32
BF16 = jnp.bfloat16


def matmul(left_side, right_side):
    return jnp.dot(left_side, right_side, preferred_element_type=F32)


def nt(left_side, right_side):
    return lax.dot_general(
        left_side, right_side, (((1,), (1,)), ((), ())), preferred_element_type=F32
    )


def contract_rows(left_side, right_side):
    return lax.dot_general(
        left_side, right_side, (((0,), (0,)), ((), ())), preferred_element_type=F32
    )


def norm_factor(values):
    return lax.rsqrt(jnp.mean(values * values, axis=-1, keepdims=True) + eps_norm)


def norm_backward(grad_out, weight, normed, factor):
    weighted = grad_out * weight
    grad_in = factor * (weighted - normed * jnp.mean(weighted * normed, axis=-1, keepdims=True))
    return (grad_in, grad_out * normed)


def rope_tables(positions):
    steps_half = jnp.arange(HEAD_DIM // 2, dtype=F32)
    inverse = rope_base ** (-(steps_half * 2.0 / HEAD_DIM))
    angles = positions.astype(F32)[:, None] * inverse[None, :]
    cosine, sine = jnp.cos(angles), jnp.sin(angles)
    return jnp.concatenate([cosine, cosine], axis=-1), jnp.concatenate([-sine, sine], axis=-1)


class Links:
    def __init__(self, sizes, send_sem, recv_sem):
        self.sizes = sizes
        self.send_sem = send_sem
        self.recv_sem = recv_sem
        self.index = {}

    def place(self):
        _, nx, _ = self.sizes
        dp, ctx = lax.axis_index("dp"), lax.axis_index("ctx")
        return dp // nx, lax.rem(dp, nx), ctx // 2, lax.rem(ctx, 2)

    def device(self, y, x, z, core):
        return (y * self.sizes[1] + x, z * 2 + core)

    def peers(self, axis, back=False):
        y, x, z, core = self.place()
        at = {"y": y, "x": x, "z": z}
        n = self.sizes["yxz".index(axis)]
        found = []
        for s in range(1, n):
            moved = dict(at)
            moved[axis] = lax.rem(at[axis] + (n - s if back else s), n)
            found.append((moved["y"], moved["x"], moved["z"], core))
        return found

    def sibling(self):
        y, x, z, core = self.place()
        return self.device(y, x, z, 1 - core)

    def across(self):
        y, x, z, core = self.place()
        nz = self.sizes[2]
        return self.device(y, x, lax.rem(z + nz // 2, nz), core)

    def group(self, back=False):
        y, x, z, core = self.place()
        chips = self.sizes[2] // 2
        base = (z // chips) * chips
        here = z - base
        chosen = [lax.rem(here + (chips - s if back else s), chips) for s in range(1, chips)]
        return [(chip, self.device(y, x, base + chip, core)) for chip in chosen]

    def meet(self):
        barrier = pltpu.get_barrier_semaphore()
        partners = [self.device(*p) for a in "zxy" for p in self.peers(a)] + [self.sibling()]
        for partner in partners:
            pl.semaphore_signal(barrier, inc=1, device_id=partner, device_id_type=MESH)
        pl.semaphore_wait(barrier, len(partners))

    def copy(self, key, src, dst, target):
        k = self.index.setdefault(key, len(self.index))
        return pltpu.make_async_remote_copy(
            src_ref=src,
            dst_ref=dst,
            send_sem=self.send_sem.at[k],
            recv_sem=self.recv_sem.at[k],
            device_id=target,
            device_id_type=MESH,
        )


class Exchange:
    def __init__(self, links, source, placed, local_sem, tag="swap"):
        self.tag = tag
        self.links = links
        self.source = source
        self.placed = placed
        self.local_sem = local_sem

    def copies_(self):
        _, _, z, _ = self.links.place()
        half = z // (self.links.sizes[2] // 2)
        return [
            self.links.copy(self.tag, self.source.at[1 - half], self.placed.at[half], self.links.across()),
            pltpu.make_async_copy(self.source.at[half], self.placed.at[half], self.local_sem),
        ]

    def start(self):
        for copy in self.copies_():
            copy.start()

    def wait(self):
        for copy in self.copies_():
            copy.wait()


class Gather:
    def __init__(self, links, tag, shard, whole, order, cols, local_sem):
        self.links = links
        self.tag = tag
        self.shard = shard
        self.whole = whole
        self.order = order
        self.cols = cols
        self.local_sem = local_sem

    def own(self):
        y, x, z, core = self.links.place()
        return self.whole.at[y, x, z, core, :, self.cols]

    def slab(self, stage, at):
        y, x, z, core = at
        if stage == 0:
            return self.whole.at[y, x, z, core, :, self.cols]
        if stage == 1:
            return self.whole.at[y, x, :, core, :, self.cols]
        if self.order[0] == "x":
            return self.whole.at[y, :, :, core, :, self.cols]
        return self.whole.at[:, x, :, core, :, self.cols]

    def axis(self, stage):
        return ("z",) + tuple(self.order)[0:2] if stage is None else ("z", self.order[0], self.order[1])[stage]

    def send(self, stage):
        me = self.links.place()
        src = self.shard.at[:, self.cols] if stage == 0 else self.slab(stage, me)
        dst = self.slab(stage, me)
        return [
            self.links.copy((self.tag, stage, i), src, dst, self.links.device(*p))
            for i, p in enumerate(self.links.peers(self.axis(stage)))
        ]

    def forward(self, stage):
        sibling = self.links.sibling()
        if stage < 0:
            return [self.links.copy((self.tag, "own"), self.shard.at[:, self.cols], self.own(), sibling)]
        return [
            self.links.copy((self.tag, "pass", stage, i), self.slab(stage, p), self.slab(stage, p), sibling)
            for i, p in enumerate(self.links.peers(self.axis(stage), back=True))
        ]

    def local(self):
        return pltpu.make_async_copy(self.shard.at[:, self.cols], self.own(), self.local_sem)

    def start(self):
        self.local().start()
        for copy in self.send(0) + self.forward(-1):
            copy.start()

    def step(self, stage):
        if stage == 1:
            self.local().wait()
        for copy in self.send(stage - 1):
            copy.wait()
        if stage < 3:
            for copy in self.send(stage):
                copy.start()
        for copy in self.forward(stage - 1):
            copy.start()

    def close(self):
        for stage in range(-1, 3):
            for copy in self.forward(stage):
                copy.wait()

    @staticmethod
    def copies(sizes):
        return 2 * sum(n - 1 for n in sizes) + 1


class Scatter:
    def __init__(self, links, tag, part, order, cols, halves, firsts, seconds, thirds, temp, temp_sem, out):
        self.links = links
        self.tag = tag
        self.part = part
        self.order = order
        self.cols = cols
        self.sums = halves
        self.got = (firsts, seconds, thirds)
        self.temp = temp
        self.temp_sem = temp_sem
        self.out = out

    def first(self):
        _, _, _, core = self.links.place()
        return self.links.copy(
            (self.tag, "core"), self.part.at[:, :, :, 1 - core, :, self.cols], self.sums, self.links.sibling()
        )

    def load(self):
        _, _, _, core = self.links.place()
        return pltpu.make_async_copy(
            self.part.at[:, :, :, core, :, self.cols], self.temp, self.temp_sem
        )

    def axis(self, stage):
        return (self.order[0], self.order[1], "z")[stage]

    def at(self, stage, place, rest=None):
        y, x, z, _ = place
        if stage == 0:
            return (y,) if self.order[0] == "y" else (slice(None), x)
        if stage == 1:
            return (y, x)
        return (y, x, z)

    def send(self, stage):
        me = self.links.place()
        found = []
        for i, p in enumerate(self.links.peers(self.axis(stage))):
            index = self.at(stage, p)
            found.append(
                self.links.copy(
                    (self.tag, stage, i), self.sums.at[index], self.got[stage].at[i], self.links.device(*p)
                )
            )
        return found

    def start(self):
        self.first().start()

    def begin(self):
        self.first().wait()
        if self.temp_sem is not None:
            self.load().wait()
        ny, nx, nz = self.links.sizes

        def add(i, carry):
            a, b, c = i // (nx * nz), lax.rem(i // nz, nx), lax.rem(i, nz)
            self.sums[a, b, c] = (
                self.sums[a, b, c].astype(F32) + self.temp[a, b, c].astype(F32)
            ).astype(BF16)
            return carry

        lax.fori_loop(0, ny * nx * nz, add, 0)
        for copy in self.send(0):
            copy.start()

    def middle(self, stage):
        for copy in self.send(stage):
            copy.wait()
        y, x, z, _ = self.links.place()
        _, _, nz = self.links.sizes
        got = self.got[stage]
        peers = got.shape[0]
        if stage == 0:
            other = got.shape[1]

            def add(i, carry):
                b, c = i // nz, lax.rem(i, nz)
                index = (y, b, c) if self.order[0] == "y" else (b, x, c)
                total = self.sums[index].astype(F32)
                for p in range(peers):
                    total = total + got[p, b, c].astype(F32)
                self.sums[index] = total.astype(BF16)
                return carry

            lax.fori_loop(0, other * nz, add, 0)
        else:

            def add(c, carry):
                total = self.sums[y, x, c].astype(F32)
                for p in range(peers):
                    total = total + got[p, c].astype(F32)
                self.sums[y, x, c] = total.astype(BF16)
                return carry

            lax.fori_loop(0, nz, add, 0)
        for copy in self.send(stage + 1):
            copy.start()

    def finish(self):
        for copy in self.send(2):
            copy.wait()
        y, x, z, _ = self.links.place()
        total = self.sums[y, x, z].astype(F32)
        for p in range(self.got[2].shape[0]):
            total = total + self.got[2][p].astype(F32)
        if callable(self.out):
            self.out(total)
        else:
            self.out[:, self.cols] = total

    @staticmethod
    def copies(sizes):
        return sum(n - 1 for n in sizes) + 1

    @staticmethod
    def scratch(sizes, order, rows, width):
        ny, nx, nz = sizes
        na, nb = (ny, nx) if order[0] == "y" else (nx, ny)
        return [
            pltpu.VMEM((ny, nx, nz, rows, width), BF16),
            pltpu.VMEM((na - 1, nb, nz, rows, width), BF16),
            pltpu.VMEM((nb - 1, nz, rows, width), BF16),
            pltpu.VMEM((nz - 1, rows, width), BF16),
        ]


ORDERS = ("xy", "yx")

FORWARD_START = [
    ("swap", "tokens"), (0, 9), (0, 0), (1, 9), (1, 0), (2, 9), (2, 0), (0, 1), (0, 2), (3, 9), (4, 9), (3, 0),
    (1, 1), (1, 2), (0, 3), (2, 1), (0, 4), ("swapped", "tokens"),
]
FORWARD_AFTER = {
    0: [("kv", 0), (2, 2), (1, 3), (3, 1), (1, 4), (0, 5)],
    1: [("kv", 1), (3, 2), (2, 3), (2, 4), (1, 5)],
    2: [("use", 0), (3, 3), (3, 4), (2, 5), (0, 6), ("kv", 2)],
    3: [("got", 0), (1, 6), (0, 7), (3, 5)],
    4: [("use", 1), ("got", 1), ("kv", 3), (2, 6), (1, 7)],
    5: [(3, 6), (2, 7), (0, 8)],
    6: [("use", 2), ("swap", "cot"), (1, 8)],
    7: [("got", 2), (3, 7), (2, 8)],
    8: [("use", 3)],
    9: [("got", 3), (3, 8)],
    11: [("swapped", "cot")],
}
FEED_START = [("fetch", 0), ("send", (0, 4)), ("fetch", 1)]
FEED_NEXT = [("send", (1, 4)), ("send", (0, 5))]
FEED_MIDDLE = {
    0: [("send", (2, 4))],
    1: [("send", (3, 4)), ("send", (2, 5)), ("fetch", 2)],
    2: [("send", (3, 5)), ("fetch", 3)],
    3: [("fetch", 4)],
    4: [("fetch", 5)],
    5: [(1, 1)],
}
FEED_AFTER = {
    0: [("send", (1, 5)), ("core", 0)],
    1: [("begin", 0), ("core", 1)],
    2: [("begin", 1)],
    3: [(0, 0), (0, 1)],
    4: [(1, 0)],
}
FEED_LAST = []
FINISH_MIDDLE = {
    1: [("begin", 0)],
    2: [("begin", 1), (1, 0)],
    3: [("begin", 2), (1, 1)],
}
FINISH_AFTER = {
    0: [("core", 0)],
    1: [("core", 1), (0, 0)],
    2: [("core", 2), (0, 1)],
    3: [("core", 3)],
}
BACKWARD_AFTER = {
    0: [(0, 0)],
    1: [(1, 0), (0, 1)],
    2: [(2, 0), (1, 1), (0, 2)],
    3: [(2, 1), (1, 2), (0, 3)],
    4: [(2, 2), (1, 3), (0, 4)],
    5: [(2, 3), (1, 4)],
    6: [(2, 4)],
}


def halves_of(width):
    return (slice(0, width // 2), slice(width // 2, width)) if width >= 512 else (slice(0, width),)


def roll_half(values):
    return pltpu.roll(values, HEAD_DIM // 2, 1)


class KeyValues:
    def __init__(self, links, rows, held):
        self.links = links
        self.rows = rows
        self.held = held

    def slab(self, group, piece, member):
        members = self.links.sizes[2]
        start = pl.multiple_of(self.rows * (piece * members + member), self.rows)
        return self.held.at[:, 2 * group : 2 * group + 2, pl.ds(start, self.rows)]

    def mine(self):
        _, _, z, core = self.links.place()
        return lax.rem(z, self.links.sizes[2] // 2) * 2 + core

    def across(self, group):
        found = []
        for piece in range(2):
            slab = self.slab(group, piece, self.mine())
            for i, (_, target) in enumerate(self.links.group()):
                found.append(self.links.copy(("kv", group, piece, i), slab, slab, target))
        return found

    def near(self, group):
        found = []
        for piece in range(2):
            slab = self.slab(group, piece, self.mine())
            found.append(self.links.copy(("kv own", group, piece), slab, slab, self.links.sibling()))
        return found

    def forward(self, group):
        _, _, _, core = self.links.place()
        found = []
        for piece in range(2):
            for i, (chip, _) in enumerate(self.links.group(back=True)):
                slab = self.slab(group, piece, chip * 2 + core)
                found.append(
                    self.links.copy(("kv pass", group, piece, i), slab, slab, self.links.sibling())
                )
        return found

    @staticmethod
    def copies(sizes):
        return 4 * 2 * (2 * (sizes[2] // 2 - 1) + 1)


def run_all(copies, act):
    for copy in copies:
        if act == "start":
            copy.start()
        else:
            copy.wait()


def row_places(shape, dim, sub):
    t = lax.broadcasted_iota(jnp.int32, shape, dim)
    return (t // (2 * sub)) * sub + t % sub


def block_copies(sizes, src, dst, sem):
    ny, nx, nz = sizes
    shard_rows = src.shape[-2]
    found = []
    for i in range(ny * nx * nz * 2):
        block = src.at[i // (nx * nz * 2), i // (nz * 2) % nx, i // 2 % nz, i % 2]
        found.append(pltpu.make_async_copy(block, dst.at[i * shard_rows : (i + 1) * shard_rows], sem))
    return found


def gather_parents(meta, lead, slot, pairs):
    runs = (TREE - TRUNK) // SEG
    for k in range(LOCAL_RUNS):
        parent = meta[jnp.minimum(lead + k, runs - 1)]
        for read, out in pairs:
            total = None
            for b in range(runs):
                share = (1 - jnp.minimum(jnp.abs(parent - b), 1)).astype(F32).astype(BF16)
                term = read(b) * share
                total = term if total is None else total + term
            out[slot + k] = total


def forward_kernel(sizes, rows, meta, cos_ref, sin_ref, tok_ref, cot_ref, *refs):
    arrays = PAIRS + 2 + FF_FIRST
    shard = refs[:arrays]
    (mixed_ref, l_ref, pre_ref, normed_ref, gains_ref, qk_ref,
     placed, cot_placed, q_all, kv_all, qkv_whole, gain_whole, out_whole, feed_whole) = refs[arrays : arrays + 14]
    whole = (
        tuple(qkv_whole.at[c] for c in range(PAIRS))
        + (out_whole,)
        + tuple(feed_whole.at[c] for c in range(FF_FIRST))
        + (gain_whole,)
    )
    (qs, kvs, xs, ws, gs, acc, part, places, kp, vp, send_sem, recv_sem, local_sem) = refs[arrays + 14 :]
    members = sizes[2]
    sub = rows // SUBS
    count = 2 * rows
    step = pl.program_id(0)
    head = jnp.maximum(step - PAIRS, 0)
    links = Links(sizes, send_sem, recv_sem)
    kv = KeyValues(links, rows, kvs)
    swaps = {
        "tokens": Exchange(links, tok_ref, placed, local_sem.at[0], "tokens"),
        "cot": Exchange(links, cot_ref, cot_placed, local_sem.at[1], "cot"),
    }
    weights_ = [
        [
            Gather(links, (a, b), shard[a], whole[a], ORDERS[b], cols, local_sem.at[12 + 2 * a + b])
            for b, cols in enumerate(halves_of(shard[a].shape[-1]))
        ]
        for a in range(arrays)
    ]
    _, _, z, core = links.place()
    mine = lax.rem(z, members // 2) * 2 + core

    def kept(group):
        pair = slice(2 * group, 2 * group + 2)
        return [
            pltpu.make_async_copy(kvs.at[:, pair], kv_all.at[:, pair], local_sem.at[2 + group]),
            pltpu.make_async_copy(qs.at[pair], q_all.at[pair], local_sem.at[6 + group]),
        ]

    def act(steps):
        for what, a in steps:
            if what == "swap":
                swaps[a].start()
            elif what == "swapped":
                swaps[a].wait()
            elif what == "kv":
                run_all(kv.across(a), "start")
                run_all(kv.near(a), "start")
            elif what == "use":
                run_all(kv.across(a), "wait")
                run_all(kv.forward(a), "start")
            elif what == "got":
                run_all(kv.near(a), "wait")
                run_all(kv.forward(a), "wait")
                run_all(kept(a), "start")
            else:
                for g in weights_[a]:
                    if what == 0:
                        g.start()
                    elif what == 4:
                        g.close()
                    else:
                        g.step(what)

    @pl.when(step == 0)
    def _():
        links.meet()
        act(FORWARD_START)
        l_ref[...] = jnp.zeros_like(l_ref)
        places[...] = row_places(places.shape, 0, sub)
        run_all(block_copies(sizes, gain_whole, gs, local_sem.at[10]), "start")
        pltpu.make_async_copy(gs, gs, local_sem.at[10]).wait()
        loaded = pltpu.make_async_copy(placed, xs, local_sem.at[11])
        loaded.start()
        gains_ref[...] = gs[:, :GAIN_COLS].astype(F32).T[:8]
        qk_ref[0:1] = jnp.sum(gs[:, GAIN_COLS : 2 * GAIN_COLS].astype(F32), axis=0, keepdims=True)
        qk_ref[1:2] = jnp.sum(gs[:, 2 * GAIN_COLS :].astype(F32), axis=0, keepdims=True)
        loaded.wait()
        values = xs[...].reshape(count, D).astype(F32)
        normed_ref[...] = (values * norm_factor(values) * gains_ref[0:1]).astype(BF16)

    for c in range(PAIRS):

        @pl.when(step == c)
        def _():
            act([(4, c)])
            run_all(block_copies(sizes, qkv_whole.at[c], ws, local_sem.at[10]), "start")
            pltpu.make_async_copy(ws, ws, local_sem.at[10]).wait()

    @pl.when(step < PAIRS)
    def _():
        normed = normed_ref[...]
        cosine, sine = cos_ref[...], sin_ref[...]

        def turned(pre, gain):
            values = pre * norm_factor(pre) * gain
            return (values * cosine + roll_half(values) * sine).astype(BF16)

        for hh in range(2):
            at = 2 * step + hh
            query = matmul(normed, ws[:, 2 * hh * HEAD_DIM : 2 * (hh + 1) * HEAD_DIM])
            for h in range(2):
                pre = query[:, h * HEAD_DIM : (h + 1) * HEAD_DIM]
                pre_ref[hh, :, h * HEAD_DIM : (h + 1) * HEAD_DIM] = pre
                low = turned(pre, qk_ref[0:1])
                for s in range(2 * SUBS):
                    qs[at, (2 * s + h) * sub : (2 * s + h + 1) * sub] = low[s * sub : (s + 1) * sub]
            pre = matmul(normed, ws[:, (4 + hh) * HEAD_DIM : (5 + hh) * HEAD_DIM])
            pre_ref[hh, :, 2 * HEAD_DIM :] = pre
            low = turned(pre, qk_ref[1:2])
            value = matmul(normed, ws[:, (6 + hh) * HEAD_DIM : (7 + hh) * HEAD_DIM]).astype(BF16)
            for piece in range(2):
                start = pl.multiple_of(rows * (piece * members + mine), rows)
                kvs[0, at, pl.ds(start, rows)] = low[piece * rows : (piece + 1) * rows]
                kvs[1, at, pl.ds(start, rows)] = value[piece * rows : (piece + 1) * rows]

    def attend():
        lane = lax.broadcasted_iota(jnp.int32, (2 * rows, HEAD_DIM), 1)
        for piece in range(2):
            base = rows * (piece * members + mine)
            region = slice(piece * 2 * rows, (piece + 1) * 2 * rows)
            acc[...] = jnp.zeros_like(acc)
            part[...] = jnp.zeros_like(part)

            def trunk(step, masked):
                start = pl.multiple_of(step * CHUNK, CHUNK)
                weights = jnp.exp2(nt(qs[head, region], kvs[0, head, pl.ds(start, CHUNK)]) * exp2_scale)
                low, high = weights[:, :HEAD_DIM], weights[:, HEAD_DIM:]
                if masked:
                    room = places[...] + (base - start)
                    low = jnp.where(lane <= room, low, 0.0)
                    high = jnp.where(lane + HEAD_DIM <= room, high, 0.0)
                    weights = jnp.concatenate([low, high], axis=1)
                part[...] += low + high
                acc[...] += matmul(weights.astype(BF16), kvs[1, head, pl.ds(start, CHUNK)])
                return masked

            if piece == 0:
                clear = jnp.minimum(base // CHUNK, TRUNK // CHUNK)
                last = jnp.minimum((base + rows + CHUNK - 1) // CHUNK, TRUNK // CHUNK)
                lax.fori_loop(0, clear, lambda i, c: (trunk(i, False), c)[1], 0)
                lax.fori_loop(clear, last, lambda i, c: (trunk(i, True), c)[1], 0)
            else:
                lax.fori_loop(0, TRUNK // CHUNK, lambda i, c: (trunk(i, False), c)[1], 0)

            lead = jnp.maximum(base - TRUNK, 0) // SEG

            def parents_():
                gather_parents(
                    meta,
                    lead,
                    0,
                    [
                        (lambda b: kvs[0, head, TRUNK + b * SEG : TRUNK + (b + 1) * SEG], kp),
                        (lambda b: kvs[1, head, TRUNK + b * SEG : TRUNK + (b + 1) * SEG], vp),
                    ],
                )

            if piece == 0:
                pl.when(base + rows > TRUNK)(parents_)
            else:
                parents_()
            for s in range(SUBS):
                block = slice(2 * sub * s, 2 * sub * (s + 1))

                def runs():
                    row = base + s * sub - TRUNK
                    run = row // SEG
                    own = pl.multiple_of(TRUNK + run * SEG, SEG)
                    flag = jnp.minimum(meta[run] + 1, 1).astype(F32)
                    query = qs[head, piece * 2 * rows + 2 * sub * s : piece * 2 * rows + 2 * sub * (s + 1)]
                    room = places[block] + (lax.rem(row, SEG) - s * sub)
                    weights = jnp.exp2(nt(query, kvs[0, head, pl.ds(own, SEG)]) * exp2_scale)
                    weights = jnp.where(lane[block] <= room, weights, 0.0)
                    above = jnp.exp2(nt(query, kp[run - lead]) * exp2_scale) * flag
                    part[block] += weights + above
                    acc[block] += matmul(weights.astype(BF16), kvs[1, head, pl.ds(own, SEG)]) + matmul(
                        above.astype(BF16), vp[run - lead]
                    )

                if piece == 0:
                    pl.when(base + s * sub >= TRUNK)(runs)
                else:
                    runs()

            total = jnp.sum(part[...], axis=-1, keepdims=True)
            mixed = (acc[...] / total).astype(BF16)
            for s in range(SUBS):
                for h in range(2):
                    row = piece * rows + sub * s
                    mixed_ref[row : row + sub, h * HEAD_DIM : (h + 1) * HEAD_DIM] = mixed[
                        (2 * s + h) * sub : (2 * s + h + 1) * sub
                    ]
            l_ref[region] = jnp.where(lane == head, total, l_ref[region])


    pl.when(step >= PAIRS)(attend)
    for moment, steps in FORWARD_AFTER.items():
        pl.when(step == moment)(functools.partial(act, steps))

    @pl.when(step == PAIRS + KV_HEADS - 1)
    def _():
        for array in weights_[PAIRS : PAIRS + 1 + FF_FIRST]:
            for g in array:
                g.close()
        for group in range(4):
            run_all(kept(group), "wait")


def forward(sizes, meta, cosine, sine, tokens, cotangent, shards_):
    ny, nx, nz = sizes
    rows = tokens.shape[1]
    count = 2 * rows
    arrays = PAIRS + 2 + FF_FIRST
    shard_rows = shards_[0].shape[0]
    blocks = (ny, nx, nz, 2, shard_rows)
    widths = [w.shape[-1] for w in shards_]
    rounds = KeyValues.copies(sizes) + 2 * arrays * Gather.copies(sizes) + 2

    def at_head(s):
        return jnp.maximum(s - PAIRS, 0)

    results = pl.pallas_call(
        functools.partial(forward_kernel, sizes, rows),
        out_shape=[
            jax.ShapeDtypeStruct((count, QD), BF16),
            jax.ShapeDtypeStruct((2 * count, HEAD_DIM), F32),
            jax.ShapeDtypeStruct((KV_HEADS, count, 3 * HEAD_DIM), F32),
            jax.ShapeDtypeStruct((count, D), BF16),
            jax.ShapeDtypeStruct((8, D), F32),
            jax.ShapeDtypeStruct((8, HEAD_DIM), F32),
            jax.ShapeDtypeStruct(tokens.shape, BF16),
            jax.ShapeDtypeStruct(tokens.shape, BF16),
            jax.ShapeDtypeStruct((KV_HEADS, 2 * count, HEAD_DIM), BF16),
            jax.ShapeDtypeStruct((2, KV_HEADS, TREE, HEAD_DIM), BF16),
            jax.ShapeDtypeStruct((PAIRS,) + blocks + (widths[0],), BF16),
            jax.ShapeDtypeStruct(blocks + (widths[-1],), BF16),
            jax.ShapeDtypeStruct(blocks + (widths[PAIRS],), BF16),
            jax.ShapeDtypeStruct((FF_FIRST,) + blocks + (widths[PAIRS + 1],), BF16),
        ],
        grid_spec=pltpu.PrefetchScalarGridSpec(
            num_scalar_prefetch=1,
            grid=(PAIRS + KV_HEADS,),
            in_specs=[pl.BlockSpec((count, HEAD_DIM), lambda s, meta: (0, 0))] * 2 + [ANY] * (2 + arrays),
            out_specs=[
                pl.BlockSpec((count, 2 * HEAD_DIM), lambda s, meta: (0, at_head(s))),
                pl.BlockSpec((2 * count, HEAD_DIM), lambda s, meta: (0, 0)),
                pl.BlockSpec((2, count, 3 * HEAD_DIM), lambda s, meta: (jnp.minimum(s, PAIRS - 1), 0, 0)),
                pl.BlockSpec((count, D), lambda s, meta: (0, 0)),
                pl.BlockSpec((8, D), lambda s, meta: (0, 0)),
                pl.BlockSpec((8, HEAD_DIM), lambda s, meta: (0, 0)),
            ]
            + [ANY] * 8,
            scratch_shapes=[
                pltpu.VMEM((KV_HEADS, 2 * count, HEAD_DIM), BF16),
                pltpu.VMEM((2, KV_HEADS, TREE, HEAD_DIM), BF16),
                pltpu.VMEM(tokens.shape, BF16),
                pltpu.VMEM((D, widths[0]), BF16),
                pltpu.VMEM((D, widths[-1]), BF16),
                pltpu.VMEM((count, HEAD_DIM), F32),
                pltpu.VMEM((count, HEAD_DIM), F32),
                pltpu.VMEM((count, HEAD_DIM), jnp.int32),
                pltpu.VMEM((LOCAL_RUNS, SEG, HEAD_DIM), BF16),
                pltpu.VMEM((LOCAL_RUNS, SEG, HEAD_DIM), BF16),
                pltpu.SemaphoreType.DMA((rounds,)),
                pltpu.SemaphoreType.DMA((rounds,)),
                pltpu.SemaphoreType.DMA((12 + 2 * arrays,)),
            ],
        ),
        compiler_params=pltpu.CompilerParams(
            collective_id=2, has_side_effects=True, vmem_limit_bytes=56 * MIB
        ),
        name="forward",
    )(meta, cosine, sine, tokens, cotangent, *shards_)
    return results


def feed_kernel(
    sizes, rows, x_ref, mixed_ref, cot_ref, out_ref, gain_ref, first_ref, *refs,
):
    shard = refs[: FF_CHUNKS - FF_FIRST]
    refs = refs[FF_CHUNKS - FF_FIRST :]
    result_ref, hid_ref, stack_ref, delta_ref, post_ref, dout_ref, late_ref, rest_ref, early_ref = refs[:9]
    hidden, second, second_t, cot_t, total, grads, inner, gate_up, low, stack, part, wbuf = refs[9:21]
    buffers = refs[21:-3]
    send_sem, recv_sem, local_sem = refs[-3:]
    ny, nx, nz = sizes
    count = 2 * rows
    sub = rows // SUBS
    shard_rows = part.shape[5]
    width = 3 * FF_CHUNK
    tile = 256
    chunk = pl.program_id(0)
    links = Links(sizes, send_sem, recv_sem)
    _, _, _, core = links.place()
    scatters = []
    for c in range(FF_EARLY):
        for b, cols in enumerate(halves_of(width)):
            k = 4 * len(scatters)
            scatters.append(
                Scatter(
                    links,
                    (c, b),
                    part.at[c % 2],
                    ORDERS[b],
                    cols,
                    *buffers[k : k + 4],
                    part.at[c % 2, :, :, :, core, :, cols],
                    None,
                    early_ref.at[c],
                )
            )

    gathers = [
        [
            Gather(links, ("w", c, b), shard[c], rest_ref.at[c], ORDERS[b], cols, local_sem.at[8 + 2 * c + b])
            for b, cols in enumerate(halves_of(width))
        ]
        for c in range(FF_CHUNKS - FF_FIRST)
    ]

    def fetch(c):
        if c < FF_FIRST:
            pltpu.make_async_copy(first_ref.at[c], wbuf.at[c % 2], local_sem.at[6 + c % 2]).start()
        else:
            for g in gathers[c - FF_FIRST]:
                g.close()
            run_all(
                block_copies(sizes, rest_ref.at[c - FF_FIRST], wbuf.at[c % 2], local_sem.at[6 + c % 2]), "start"
            )

    def act(steps):
        for what, c in steps:
            if what == "fetch":
                fetch(c)
                continue
            if what == "send":
                for g in gathers[c[1] - FF_FIRST]:
                    if c[0] == 0:
                        g.start()
                    else:
                        g.step(c[0])
                continue
            for s in scatters[2 * c : 2 * c + 2]:
                if what == "core":
                    s.start()
                elif what == "begin":
                    s.begin()
                elif what == "finish":
                    s.finish()
                else:
                    s.middle(what)

    def rows_of(block):
        return (block // (2 * nz * nx), lax.rem(block // (2 * nz), nx), lax.rem(block // 2, nz), lax.rem(block, 2))

    def put(slot, first, cols, value):
        for k in range(value.shape[0] // shard_rows):
            y, x, z, c = rows_of(first // shard_rows + k)
            part[slot, y, x, z, c, :, cols] = value[k * shard_rows : (k + 1) * shard_rows].astype(BF16)

    def late(c):
        return pltpu.make_async_copy(part.at[c % 2], late_ref.at[c - FF_EARLY], local_sem.at[c % 2])

    @pl.when(chunk == 0)
    def _():
        links.meet()
        act(FEED_START)

        def project_out(t, carry):
            at = pl.multiple_of(t * tile, tile)
            hidden[:, pl.ds(at, tile)] = x_ref[:, pl.ds(at, tile)].astype(F32) + nt(
                mixed_ref[...], out_ref[pl.ds(at, tile), :]
            )
            return carry

        lax.fori_loop(0, D // tile, project_out, 0)
        act(FEED_NEXT)
        values = hidden[...]
        values = values * norm_factor(values) * gain_ref[1:2]
        second[...] = values.astype(BF16)
        second_t[...] = values.T.astype(BF16)
        cot_t[...] = cot_ref[...].astype(F32).T.astype(BF16)
        total[...] = jnp.zeros_like(total)
        grads[...] = jnp.zeros_like(grads)

    slot = lax.rem(chunk, 2)
    pltpu.make_async_copy(wbuf.at[slot], wbuf.at[slot], local_sem.at[6 + slot]).wait()

    def columns(t, carry):
        at = pl.multiple_of(t * tile, tile)
        gate = matmul(second[...], wbuf[slot, :, pl.ds(at, tile)])
        up = matmul(second[...], wbuf[slot, :, pl.ds(FF_CHUNK + at, tile)])
        grad = matmul(cot_ref[...], wbuf[slot, :, pl.ds(2 * FF_CHUNK + at, tile)])
        sigmoid = 1.0 / (1.0 + jnp.exp(-gate))
        active = gate * sigmoid
        inner[:, pl.ds(at, tile)] = (active * up).astype(BF16)
        gate_up[:, pl.ds(at, tile)] = (grad * up * sigmoid * (1.0 + gate * (1.0 - sigmoid))).astype(BF16)
        gate_up[:, pl.ds(FF_CHUNK + at, tile)] = (grad * active).astype(BF16)
        return carry

    lax.fori_loop(0, FF_CHUNK // tile, columns, 0)
    for moment, steps in FEED_MIDDLE.items():
        pl.when(chunk == moment)(functools.partial(act, steps))
    for c in range(FF_EARLY, FF_CHUNKS - 2):
        pl.when(chunk == c + 2)(lambda: late(c).wait())

    def model(t, carry):
        at = pl.multiple_of(t * tile, tile)
        total[:, pl.ds(at, tile)] += nt(inner[...], wbuf[slot, pl.ds(at, tile), 2 * FF_CHUNK :])
        grads[:, pl.ds(at, tile)] += nt(gate_up[...], wbuf[slot, pl.ds(at, tile), : 2 * FF_CHUNK])
        put(slot, at, slice(0, 2 * FF_CHUNK), matmul(second_t[pl.ds(at, tile)], gate_up[...]))
        put(slot, at, slice(2 * FF_CHUNK, width), matmul(cot_t[pl.ds(at, tile)], inner[...]))
        return carry

    lax.fori_loop(0, D // tile, model, 0)
    for c in range(FF_EARLY, FF_CHUNKS):
        pl.when(chunk == c)(lambda: late(c).start())
    for moment, steps in FEED_AFTER.items():
        pl.when(chunk == moment)(functools.partial(act, steps))

    @pl.when(chunk == FF_CHUNKS - 1)
    def _():
        values = hidden[...]
        low[...] = (values + total[...]).astype(BF16)
        output = pltpu.make_async_copy(low, result_ref, local_sem.at[2])
        output.start()
        factor = norm_factor(values)
        grad_in, share = norm_backward(grads[...], gain_ref[1:2], values * factor, factor)
        post_ref[...] = jnp.sum(share, axis=0, keepdims=True)
        hidden[...] = cot_ref[...].astype(F32) + grad_in
        saved = pltpu.make_async_copy(hidden, hid_ref, local_sem.at[3])
        saved.start()
        second[...] = hidden[...].astype(BF16)
        second_t[...] = hidden[...].T.astype(BF16)
        lane = lax.broadcasted_iota(jnp.int32, (count, HEAD_DIM), 1)
        dots = jnp.zeros((count, HEAD_DIM), F32)
        for h in range(KV_HEADS):
            cols = slice(2 * h * HEAD_DIM, 2 * (h + 1) * HEAD_DIM)
            grad = matmul(second[...], out_ref[:, cols]).astype(BF16)
            for g in range(2):
                one = grad[:, g * HEAD_DIM : (g + 1) * HEAD_DIM]
                for s in range(2 * SUBS):
                    stack[h, (2 * s + g) * sub : (2 * s + g + 1) * sub] = one[s * sub : (s + 1) * sub]
                head = 2 * h + g
                product = one.astype(F32) * mixed_ref[:, head * HEAD_DIM : (head + 1) * HEAD_DIM].astype(F32)
                dots = jnp.where(lane == head, jnp.sum(product, axis=-1, keepdims=True), dots)
        delta_ref[...] = dots.T
        stacked_ = pltpu.make_async_copy(stack, stack_ref, local_sem.at[4])
        stacked_.start()
        act(FEED_LAST)
        for c in range(FF_CHUNKS - 2, FF_CHUNKS):
            late(c).wait()

        def model_out(t, carry):
            at = pl.multiple_of(t * tile, tile)
            for a in range(0, QD, 2 * FF_CHUNK):
                cols = slice(a, a + 2 * FF_CHUNK)
                value = matmul(second_t[pl.ds(at, tile)], mixed_ref[:, cols])
                slot = a // (2 * FF_CHUNK)
                put(slot, at, slice(0, 2 * FF_CHUNK), value)
            return carry

        lax.fori_loop(0, D // tile, model_out, 0)
        gone = [
            pltpu.make_async_copy(
                part.at[k, :, :, :, :, :, : 2 * FF_CHUNK],
                dout_ref.at[:, :, :, :, :, 2 * FF_CHUNK * k : 2 * FF_CHUNK * (k + 1)],
                local_sem.at[k],
            )
            for k in range(2)
        ]
        run_all(gone, "start")
        for c in range(FF_EARLY):
            act([("finish", c)])
        run_all(gone + [output, saved, stacked_], "wait")


def feed(sizes, x, mixed, cot, out_t, gain, first, shards_):
    ny, nx, nz = sizes
    count = x.shape[0]
    rows = count // 2
    shard_rows = D // (ny * nx * nz * 2)
    width = 3 * FF_CHUNK
    buffers = []
    for c in range(FF_EARLY):
        for b, cols in enumerate(halves_of(width)):
            buffers += Scatter.scratch(sizes, ORDERS[b], shard_rows, cols.stop - cols.start)
    late = FF_CHUNKS - FF_FIRST
    rounds = 2 * FF_EARLY * Scatter.copies(sizes) + 2 * late * Gather.copies(sizes)

    def whole_block(shape):
        return pl.BlockSpec(shape, lambda c: (0,) * len(shape), pipeline_mode=pl.Buffered(1))

    blocks = (ny, nx, nz, 2, shard_rows)
    return pl.pallas_call(
        functools.partial(feed_kernel, sizes, rows),
        grid=(FF_CHUNKS,),
        out_shape=[
            jax.ShapeDtypeStruct((count, D), BF16),
            jax.ShapeDtypeStruct((count, D), F32),
            jax.ShapeDtypeStruct((KV_HEADS, 2 * count, HEAD_DIM), BF16),
            jax.ShapeDtypeStruct((HEAD_DIM, count), F32),
            jax.ShapeDtypeStruct((1, D), F32),
            jax.ShapeDtypeStruct(blocks + (QD,), BF16),
            jax.ShapeDtypeStruct((FF_CHUNKS - FF_EARLY,) + blocks + (width,), BF16),
            jax.ShapeDtypeStruct((late,) + blocks + (width,), BF16),
            jax.ShapeDtypeStruct((FF_EARLY, shard_rows, width), F32),
        ],
        in_specs=[
            whole_block((count, D)),
            whole_block((count, QD)),
            whole_block((count, D)),
            whole_block((D, QD)),
            whole_block((8, D)),
            ANY,
        ]
        + [ANY] * late,
        out_specs=[
            ANY,
            ANY,
            ANY,
            pl.BlockSpec((HEAD_DIM, count), lambda c: (0, 0)),
            pl.BlockSpec((1, D), lambda c: (0, 0)),
            ANY,
            ANY,
            ANY,
            pl.BlockSpec((FF_EARLY, shard_rows, width), lambda c: (0, 0, 0)),
        ],
        scratch_shapes=[
            pltpu.VMEM((count, D), F32),
            pltpu.VMEM((count, D), BF16),
            pltpu.VMEM((D, count), BF16),
            pltpu.VMEM((D, count), BF16),
            pltpu.VMEM((count, D), F32),
            pltpu.VMEM((count, D), F32),
            pltpu.VMEM((count, FF_CHUNK), BF16),
            pltpu.VMEM((count, 2 * FF_CHUNK), BF16),
            pltpu.VMEM((count, D), BF16),
            pltpu.VMEM((KV_HEADS, 2 * count, HEAD_DIM), BF16),
            pltpu.VMEM((2,) + blocks + (width,), BF16),
            pltpu.VMEM((2, D, width), BF16),
        ]
        + buffers
        + [
            pltpu.SemaphoreType.DMA((rounds,)),
            pltpu.SemaphoreType.DMA((rounds,)),
            pltpu.SemaphoreType.DMA((8 + 2 * late,)),
        ],
        compiler_params=pltpu.CompilerParams(
            collective_id=5, has_side_effects=True, vmem_limit_bytes=61 * MIB
        ),
        name="feed",
    )(x, mixed, cot, out_t, gain, first, *shards_)


def backward_kernel(sizes, rows, widths, meta, q_ref, g_ref, k_ref, v_ref, lse_ref, del_ref, late_ref, dout_ref, done_ref, *refs):
    dq_ref, dkv_ref, late_out, dout_out, done_placed = refs[:5]
    dq, dk, dv, pk, pv, kp, vp, stage, near, sums, far, last = refs[5:17]
    buffers = refs[17:-3]
    send_sem, recv_sem, local_sem = refs[-3:]
    members = sizes[2]
    chips = members // 2
    sub = rows // SUBS
    head = pl.program_id(0)
    links = Links(sizes, send_sem, recv_sem)
    scatters = []
    late = FF_CHUNKS - FF_EARLY
    for a, width in enumerate(widths):
        for b, cols in enumerate(halves_of(width)):
            k = 5 * len(scatters)
            scatters.append(
                Scatter(
                    links,
                    (a, b),
                    late_ref.at[a] if a < late else dout_ref,
                    ORDERS[b],
                    cols,
                    *buffers[k : k + 5],
                    local_sem.at[2 + len(scatters)],
                    late_out.at[a] if a < late else dout_out,
                )
            )

    swap = Exchange(links, done_ref, done_placed, local_sem.at[2 + len(scatters)])

    def each(array):
        return scatters[2 * array : 2 * array + 2]

    @pl.when(head == 0)
    def _():
        for s in scatters:
            s.load().start()
        links.meet()
        for s in scatters:
            s.start()
        swap.start()

    _, _, z, core = links.place()
    here = lax.rem(z, chips)
    mine = here * 2 + core
    dk[...] = jnp.zeros_like(dk)
    dv[...] = jnp.zeros_like(dv)
    pk[...] = jnp.zeros_like(pk)
    pv[...] = jnp.zeros_like(pv)
    for piece in range(2):
        base = rows * (piece * members + mine)
        at = piece * 2 * rows
        region = slice(at, at + 2 * rows)
        dq[...] = jnp.zeros_like(dq)

        def pair(key, value, block, mask):
            spot = slice(at + block.start, at + block.stop)
            weights = jnp.exp2(nt(key, q_ref[0, spot]) * exp2_scale - lse_ref[0, :, spot])
            if mask is not None:
                weights = mask(weights)
            grads = (weights * (nt(value, g_ref[0, spot]) - del_ref[0, :, spot])).astype(BF16)
            weights = weights.astype(BF16)
            dq[block] += contract_rows(grads, key)
            return matmul(grads, q_ref[0, spot]), matmul(weights, g_ref[0, spot])

        everything = slice(0, 2 * rows)

        def trunk(step, masked):
            start = pl.multiple_of(step * CHUNK, CHUNK)

            def mask(weights):
                shape = weights.shape
                room = row_places((1, shape[1]), 1, sub) + (base - start)
                return jnp.where(lax.broadcasted_iota(jnp.int32, shape, 0) <= room, weights, 0.0)

            key_grad, value_grad = pair(
                k_ref[0, 0, pl.ds(start, CHUNK)],
                v_ref[0, 0, pl.ds(start, CHUNK)],
                everything,
                mask if masked else None,
            )
            dk[pl.ds(start, CHUNK)] += key_grad
            dv[pl.ds(start, CHUNK)] += value_grad

        if piece == 0:
            clear = jnp.minimum(base // CHUNK, TRUNK // CHUNK)
            end = jnp.minimum((base + rows + CHUNK - 1) // CHUNK, TRUNK // CHUNK)
            lax.fori_loop(0, clear, lambda i, c: (trunk(i, False), c)[1], 0)
            lax.fori_loop(clear, end, lambda i, c: (trunk(i, True), c)[1], 0)
        else:
            lax.fori_loop(0, TRUNK // CHUNK, lambda i, c: (trunk(i, False), c)[1], 0)

        lead = jnp.maximum(base - TRUNK, 0) // SEG

        def parents_():
            gather_parents(
                meta,
                lead,
                0,
                [
                    (lambda b: k_ref[0, 0, TRUNK + b * SEG : TRUNK + (b + 1) * SEG], kp),
                    (lambda b: v_ref[0, 0, TRUNK + b * SEG : TRUNK + (b + 1) * SEG], vp),
                ],
            )

        if piece == 0:
            pl.when(base + rows > TRUNK)(parents_)
        else:
            parents_()
        for s in range(SUBS):
            block = slice(2 * sub * s, 2 * sub * (s + 1))

            def runs():
                row = base + s * sub - TRUNK
                run = row // SEG
                own = pl.multiple_of(TRUNK + run * SEG, SEG)
                flag = jnp.minimum(meta[run] + 1, 1).astype(F32)

                def mask(weights):
                    shape = (SEG, 2 * sub)
                    room = lax.broadcasted_iota(jnp.int32, shape, 1) % sub + lax.rem(row, SEG)
                    seen = lax.broadcasted_iota(jnp.int32, shape, 0) <= room
                    return jnp.concatenate(
                        [jnp.where(seen, weights[:SEG], 0.0), weights[SEG:] * flag], axis=0
                    )

                key_grad, value_grad = pair(
                    jnp.concatenate([k_ref[0, 0, pl.ds(own, SEG)], kp[run - lead]], axis=0),
                    jnp.concatenate([v_ref[0, 0, pl.ds(own, SEG)], vp[run - lead]], axis=0),
                    block,
                    mask,
                )
                dk[pl.ds(own, SEG)] += key_grad[:SEG]
                dv[pl.ds(own, SEG)] += value_grad[:SEG]
                slot = LOCAL_RUNS * piece + run - lead
                pk[slot] += key_grad[SEG:]
                pv[slot] += value_grad[SEG:]

            if piece == 0:
                pl.when(base + s * sub >= TRUNK)(runs)
            else:
                runs()

        dq_ref[0, region] = dq[...] * score_scale

        def spread():
            parents = [meta[jnp.minimum(lead + k, TREE // SEG - TRUNK // SEG - 1)] for k in range(LOCAL_RUNS)]

            def place(b, carry):
                start = pl.multiple_of(TRUNK + b * SEG, SEG)
                key_grad, value_grad = dk[pl.ds(start, SEG)], dv[pl.ds(start, SEG)]
                for k in range(LOCAL_RUNS):
                    share = (1 - jnp.minimum(jnp.abs(parents[k] - b), 1)).astype(F32)
                    key_grad += pk[LOCAL_RUNS * piece + k] * share
                    value_grad += pv[LOCAL_RUNS * piece + k] * share
                dk[pl.ds(start, SEG)] = key_grad
                dv[pl.ds(start, SEG)] = value_grad
                return carry

            lax.fori_loop(0, (TREE - TRUNK) // SEG, place, 0)

        if piece == 0:
            pl.when(base + rows > TRUNK)(spread)
        else:
            spread()

    def core_copy(h):
        return links.copy(("kv core", h), stage.at[h % 2, :, 1 - core], near.at[h % 2], links.sibling())

    def far_copies(h):
        return [
            links.copy(("kv z", h, i), sums.at[h, chip], far.at[h, i], target)
            for i, (chip, target) in enumerate(links.group())
        ]

    def pass_on(h):
        core_copy(h).wait()

        def add(i, carry):
            chip, which, piece = i // 4, lax.rem(i // 2, 2), lax.rem(i, 2)
            sums[h, chip, which, piece] = (
                stage[h % 2, chip, core, which, piece].astype(F32) + near[h % 2, chip, which, piece].astype(F32)
            ).astype(BF16)
            return carry

        lax.fori_loop(0, chips * 4, add, 0)
        run_all(far_copies(h), "start")

    for h in range(1, KV_HEADS):
        pl.when(head == h)(functools.partial(pass_on, h - 1))

    for which, grad, scale in ((0, dk, score_scale), (1, dv, 1.0)):
        for piece in range(2):
            for member in range(members):
                start = rows * (piece * members + member)
                stage[lax.rem(head, 2), member // 2, member % 2, which, piece] = (
                    grad[start : start + rows] * scale
                ).astype(BF16)
    for h in range(KV_HEADS):

        @pl.when(head == h)
        def _():
            core_copy(h).start()

    for moment, steps in BACKWARD_AFTER.items():

        @pl.when(head == moment)
        def _():
            for step, array in steps:
                for s in each(array):
                    if step == 0:
                        s.begin()
                    else:
                        s.middle(step - 1)

    def result(h):
        return pltpu.make_async_copy(last.at[h % 2], dkv_ref.at[:, h], local_sem.at[h % 2])

    @pl.when(head == KV_HEADS - 1)
    def _():
        pass_on(KV_HEADS - 1)
        for s in scatters:
            s.finish()
        for h in range(KV_HEADS):
            run_all(far_copies(h), "wait")
            if h > 1:
                result(h - 2).wait()
            for which in range(2):
                for piece in range(2):
                    total = sums[h, here, which, piece].astype(F32)
                    for i in range(chips - 1):
                        total = total + far[h, i, which, piece].astype(F32)
                    last[h % 2, which, piece] = total
            result(h).start()
        for h in (KV_HEADS - 2, KV_HEADS - 1):
            result(h).wait()
        swap.wait()


def backward(sizes, meta, queries, grads, kv_all, log_total, delta, late, dout, done):
    ny, nx, nz = sizes
    chips = nz // 2
    rows = queries.shape[1] // 4
    widths = (late.shape[-1],) * late.shape[0] + (dout.shape[-1],)
    shard_rows = dout.shape[4]
    stack = pl.BlockSpec((1, 4 * rows, HEAD_DIM), lambda h, meta: (h, 0, 0))
    line = pl.BlockSpec((1, 1, 4 * rows), lambda h, meta: (h, 0, 0))
    buffers, count = [], 0
    for w in widths:
        for b, cols in enumerate(halves_of(w)):
            buffers += Scatter.scratch(sizes, ORDERS[b], shard_rows, cols.stop - cols.start)
            buffers.append(pltpu.VMEM((ny, nx, nz, shard_rows, cols.stop - cols.start), BF16))
            count += 1
    rounds = count * Scatter.copies(sizes) + KV_HEADS * chips + 1
    late_shape = (late.shape[0], shard_rows, late.shape[-1])
    dout_shape = (shard_rows, dout.shape[-1])
    return pl.pallas_call(
        functools.partial(backward_kernel, sizes, rows, widths),
        out_shape=[
            jax.ShapeDtypeStruct((KV_HEADS, 4 * rows, HEAD_DIM), F32),
            jax.ShapeDtypeStruct((2, KV_HEADS, 2, rows, HEAD_DIM), F32),
            jax.ShapeDtypeStruct(late_shape, F32),
            jax.ShapeDtypeStruct(dout_shape, F32),
            jax.ShapeDtypeStruct(done.shape, BF16),
        ],
        grid_spec=pltpu.PrefetchScalarGridSpec(
            num_scalar_prefetch=1,
            grid=(KV_HEADS,),
            in_specs=[
                stack,
                stack,
                pl.BlockSpec((1, 1, TREE, HEAD_DIM), lambda h, meta: (0, h, 0, 0)),
                pl.BlockSpec((1, 1, TREE, HEAD_DIM), lambda h, meta: (1, h, 0, 0)),
                line,
                line,
                ANY,
                ANY,
                ANY,
            ],
            out_specs=[
                stack,
                ANY,
                pl.BlockSpec(late_shape, lambda h, meta: (0, 0, 0)),
                pl.BlockSpec(dout_shape, lambda h, meta: (0, 0)),
                ANY,
            ],
            scratch_shapes=[
                pltpu.VMEM((2 * rows, HEAD_DIM), F32),
                pltpu.VMEM((TREE, HEAD_DIM), F32),
                pltpu.VMEM((TREE, HEAD_DIM), F32),
                pltpu.VMEM((2 * LOCAL_RUNS, SEG, HEAD_DIM), F32),
                pltpu.VMEM((2 * LOCAL_RUNS, SEG, HEAD_DIM), F32),
                pltpu.VMEM((LOCAL_RUNS, SEG, HEAD_DIM), BF16),
                pltpu.VMEM((LOCAL_RUNS, SEG, HEAD_DIM), BF16),
                pltpu.VMEM((2, chips, 2, 2, 2, rows, HEAD_DIM), BF16),
                pltpu.VMEM((2, chips, 2, 2, rows, HEAD_DIM), BF16),
                pltpu.VMEM((KV_HEADS, chips, 2, 2, rows, HEAD_DIM), BF16),
                pltpu.VMEM((KV_HEADS, chips - 1, 2, 2, rows, HEAD_DIM), BF16),
                pltpu.VMEM((2, 2, 2, rows, HEAD_DIM), F32),
            ]
            + buffers
            + [
                pltpu.SemaphoreType.DMA((rounds,)),
                pltpu.SemaphoreType.DMA((rounds,)),
                pltpu.SemaphoreType.DMA((3 + count,)),
            ],
        ),
        compiler_params=pltpu.CompilerParams(
            collective_id=3, has_side_effects=True, vmem_limit_bytes=60 * MIB
        ),
        name="backward",
    )(
        meta,
        queries,
        grads,
        kv_all,
        kv_all,
        log_total.reshape(KV_HEADS, 1, 4 * rows),
        delta.reshape(KV_HEADS, 1, 4 * rows),
        late,
        dout,
        done,
    )


def finish_kernel(
    sizes, rows, dq_ref, dkv_ref, pre_ref, w_ref, normed_ref, x_ref, hid_ref, gain_ref, post_ref, qk_ref, cos_ref, sin_ref,
    q_out, k_out, v_out, g_out, dx_placed, *refs,
):
    normed_t, low, grads, qk, dx, part, part_g = refs[:7]
    buffers = refs[7:-3]
    send_sem, recv_sem, local_sem = refs[-3:]
    ny, nx, nz = sizes
    count = 2 * rows
    sub = rows // SUBS
    shard_rows = part.shape[5]
    tile = 256
    pair = pl.program_id(0)
    links = Links(sizes, send_sem, recv_sem)
    _, _, _, core = links.place()
    swap = Exchange(links, dx, dx_placed, local_sem.at[0])

    def to_query(c):
        def store(total):
            q_out[:, 4 * HEAD_DIM * c : 4 * HEAD_DIM * (c + 1)] = total

        return store

    def to_key_value(c):
        def store(total):
            k_out[:, 2 * HEAD_DIM * c : 2 * HEAD_DIM * (c + 1)] = total[:, : 2 * HEAD_DIM]
            v_out[:, 2 * HEAD_DIM * c : 2 * HEAD_DIM * (c + 1)] = total[:, 2 * HEAD_DIM :]

        return store

    scatters = []
    for c in range(PAIRS):
        for b, cols in enumerate(halves_of(8 * HEAD_DIM)):
            k = 4 * len(scatters)
            scatters.append(
                Scatter(
                    links,
                    (c, b),
                    part.at[c % 2],
                    ORDERS[b],
                    cols,
                    *buffers[k : k + 4],
                    part.at[c % 2, :, :, :, core, :, cols],
                    None,
                    to_key_value(c) if b else to_query(c),
                )
            )
    k = 4 * len(scatters)
    whole = slice(0, 3 * GAIN_COLS)
    scatters.append(
        Scatter(
            links, "gains", part_g, ORDERS[0], whole, *buffers[k : k + 4], part_g.at[:, :, :, core], None, g_out
        )
    )

    def act(steps):
        for what, c in steps:
            for s in scatters[2 * c : 2 * c + 2]:
                if what == "core":
                    s.start()
                elif what == "begin":
                    s.begin()
                elif what == "finish":
                    s.finish()
                else:
                    s.middle(what)

    def rows_of(block):
        return (block // (2 * nz * nx), lax.rem(block // (2 * nz), nx), lax.rem(block // 2, nz), lax.rem(block, 2))

    @pl.when(pair == 0)
    def _():
        links.meet()
        normed_t[...] = normed_ref[...].astype(F32).T.astype(BF16)
        grads[...] = jnp.zeros_like(grads)
        qk[...] = jnp.zeros_like(qk)

    cosine, sine = cos_ref[...], sin_ref[...]

    def back(turned_grad, pre, gain):
        grad = turned_grad * cosine - roll_half(turned_grad) * sine
        factor = norm_factor(pre)
        grad_pre, share = norm_backward(grad, gain, pre * factor, factor)
        return grad_pre.astype(BF16), jnp.sum(share, axis=0, keepdims=True)

    for hh in range(2):
        for h in range(2):
            grad = jnp.concatenate(
                [dq_ref[hh, (2 * s + h) * sub : (2 * s + h + 1) * sub] for s in range(2 * SUBS)], axis=0
            )
            value, share = back(grad, pre_ref[hh, :, h * HEAD_DIM : (h + 1) * HEAD_DIM], qk_ref[0:1])
            qk[0:1] += share
            at = 2 * hh + h
            low[:, at * HEAD_DIM : (at + 1) * HEAD_DIM] = value
        value, share = back(dkv_ref[0, hh].reshape(count, HEAD_DIM), pre_ref[hh, :, 2 * HEAD_DIM :], qk_ref[1:2])
        qk[1:2] += share
        low[:, (4 + hh) * HEAD_DIM : (5 + hh) * HEAD_DIM] = value
        low[:, (6 + hh) * HEAD_DIM : (7 + hh) * HEAD_DIM] = dkv_ref[1, hh].reshape(count, HEAD_DIM).astype(BF16)
    for moment, steps in FINISH_MIDDLE.items():
        pl.when(pair == moment)(functools.partial(act, steps))
    slot = lax.rem(pair, 2)

    def model(t, carry):
        at = pl.multiple_of(t * tile, tile)
        grads[:, pl.ds(at, tile)] += nt(low[...], w_ref[0, pl.ds(at, tile), :])
        value = matmul(normed_t[pl.ds(at, tile)], low[...])
        for k in range(tile // shard_rows):
            y, x, z, c = rows_of(at // shard_rows + k)
            part[slot, y, x, z, c] = value[k * shard_rows : (k + 1) * shard_rows].astype(BF16)
        return carry

    lax.fori_loop(0, D // tile, model, 0)
    for moment, steps in FINISH_AFTER.items():
        pl.when(pair == moment)(functools.partial(act, steps))

    @pl.when(pair == PAIRS - 1)
    def _():
        values = x_ref[...].astype(F32)
        factor = norm_factor(values)
        grad_in, share = norm_backward(grads[...], gain_ref[0:1], values * factor, factor)
        dx[...] = (hid_ref[...] + grad_in).astype(BF16).reshape(2, rows, D)
        swap.start()
        act([(0, PAIRS - 2), ("begin", PAIRS - 1)])
        lines = jnp.concatenate(
            [jnp.sum(share, axis=0, keepdims=True), post_ref[...], jnp.zeros((GAIN_COLS - 2, D), F32)], axis=0
        )
        columns = lines.T.astype(BF16)
        first = lax.broadcasted_iota(jnp.int32, (shard_rows, GAIN_COLS), 0) == 0
        query_line = jnp.where(first, qk[0:1], 0.0).astype(BF16)
        key_line = jnp.where(first, qk[1:2], 0.0).astype(BF16)
        for k in range(D // shard_rows):
            y, x, z, c = k // (2 * nz * nx), k // (2 * nz) % nx, k // 2 % nz, k % 2
            part_g[y, x, z, c, :, :GAIN_COLS] = columns[k * shard_rows : (k + 1) * shard_rows]
            part_g[y, x, z, c, :, GAIN_COLS : 2 * GAIN_COLS] = query_line
            part_g[y, x, z, c, :, 2 * GAIN_COLS :] = key_line
        act([("core", PAIRS), (1, PAIRS - 2), ("begin", PAIRS), (0, PAIRS - 1), (0, PAIRS), (1, PAIRS - 1), (1, PAIRS)])
        for c in range(PAIRS + 1):
            act([("finish", c)])
        swap.wait()


def finish(sizes, dq, dkv, pre, normed, x, grad_hidden, gain, post_part, qkv_full, qk_gain, cosine, sine):
    ny, nx, nz = sizes
    count = x.shape[0]
    rows = count // 2
    shard_rows = D // (ny * nx * nz * 2)
    blocks = (ny, nx, nz, 2, shard_rows)
    width = 8 * HEAD_DIM

    def whole_block(shape):
        return pl.BlockSpec(shape, lambda c: (0,) * len(shape), pipeline_mode=pl.Buffered(1))

    buffers = []
    for c in range(PAIRS):
        for b, cols in enumerate(halves_of(width)):
            buffers += Scatter.scratch(sizes, ORDERS[b], shard_rows, cols.stop - cols.start)
    buffers += Scatter.scratch(sizes, ORDERS[0], shard_rows, 3 * GAIN_COLS)
    rounds = (2 * PAIRS + 1) * Scatter.copies(sizes) + 1

    def out_block(n):
        return pl.BlockSpec((shard_rows, n), lambda c: (0, 0))

    return pl.pallas_call(
        functools.partial(finish_kernel, sizes, rows),
        grid=(PAIRS,),
        out_shape=[
            jax.ShapeDtypeStruct((shard_rows, QD), F32),
            jax.ShapeDtypeStruct((shard_rows, KVD), F32),
            jax.ShapeDtypeStruct((shard_rows, KVD), F32),
            jax.ShapeDtypeStruct((shard_rows, 3 * GAIN_COLS), F32),
            jax.ShapeDtypeStruct((2, rows, D), BF16),
        ],
        in_specs=[
            pl.BlockSpec((2, 2 * count, HEAD_DIM), lambda c: (c, 0, 0)),
            pl.BlockSpec((2, 2, 2, rows, HEAD_DIM), lambda c: (0, c, 0, 0, 0)),
            pl.BlockSpec((2, count, 3 * HEAD_DIM), lambda c: (c, 0, 0)),
            pl.BlockSpec((1, D, width), lambda c: (c, 0, 0)),
            whole_block((count, D)),
            whole_block((count, D)),
            whole_block((count, D)),
            whole_block((8, D)),
            whole_block((1, D)),
            whole_block((8, HEAD_DIM)),
            whole_block((count, HEAD_DIM)),
            whole_block((count, HEAD_DIM)),
        ],
        out_specs=[out_block(QD), out_block(KVD), out_block(KVD), out_block(3 * GAIN_COLS), ANY],
        scratch_shapes=[
            pltpu.VMEM((D, count), BF16),
            pltpu.VMEM((count, width), BF16),
            pltpu.VMEM((count, D), F32),
            pltpu.VMEM((8, HEAD_DIM), F32),
            pltpu.VMEM((2, rows, D), BF16),
            pltpu.VMEM((2,) + blocks + (width,), BF16),
            pltpu.VMEM(blocks + (3 * GAIN_COLS,), BF16),
        ]
        + buffers
        + [
            pltpu.SemaphoreType.DMA((rounds,)),
            pltpu.SemaphoreType.DMA((rounds,)),
            pltpu.SemaphoreType.DMA((1,)),
        ],
        compiler_params=pltpu.CompilerParams(
            collective_id=4, has_side_effects=True, vmem_limit_bytes=58 * MIB
        ),
        name="finish",
    )(dq, dkv, pre, qkv_full, normed, x, grad_hidden, gain, post_part, qk_gain, cosine, sine)


def shards(
    sizes,
    tokens,
    cotangent,
    segment_ids,
    positions,
    parents,
    input_norm,
    query_proj,
    key_proj,
    value_proj,
    query_norm,
    key_norm,
    out_proj,
    post_norm,
    gate_proj,
    up_proj,
    down_proj,
):
    nz = sizes[2]
    rows = tokens.shape[1]
    shard_rows = query_proj.shape[0]
    gain_rows = query_norm.shape[0]
    ctx = lax.axis_index("ctx")
    half = ctx // nz
    member = ctx % nz
    count = 2 * rows
    sub = rows // SUBS

    device = lax.axis_index("dp") * 2 * nz + ctx

    def spread(gain):
        line = jnp.zeros((1, HEAD_DIM), BF16)
        line = lax.dynamic_update_slice(line, gain[None, :], (0, device * gain_rows))
        return jnp.pad(line, ((0, shard_rows - 1), (0, 0)))

    gains = jnp.pad(
        jnp.stack([input_norm, post_norm], axis=1), ((0, 0), (0, GAIN_COLS - 2))
    )
    gains = jnp.concatenate([gains, spread(query_norm), spread(key_norm)], axis=1)
    qkv_shards = [
        jnp.concatenate(
            [
                query_proj[:, 4 * HEAD_DIM * c : 4 * HEAD_DIM * (c + 1)],
                key_proj[:, 2 * HEAD_DIM * c : 2 * HEAD_DIM * (c + 1)],
                value_proj[:, 2 * HEAD_DIM * c : 2 * HEAD_DIM * (c + 1)],
            ],
            axis=1,
        )
        for c in range(PAIRS)
    ]
    down_t = down_proj.T
    feed_shards = [
        jnp.concatenate(
            [w[:, c * FF_CHUNK : (c + 1) * FF_CHUNK] for w in (gate_proj, up_proj, down_t)], axis=1
        )
        for c in range(FF_CHUNKS)
    ]

    run_seg = segment_ids[half][TRUNK::SEG]
    run_parent = parents[half][run_seg]
    parent_run = jnp.argmax(run_seg[None, :] == run_parent[:, None], axis=1).astype(jnp.int32)
    meta = jnp.where(run_parent > 0, parent_run, -1)
    pos_tree = positions[half].reshape(2, nz, rows)
    pos_local = lax.dynamic_index_in_dim(pos_tree, member, 1, keepdims=False).reshape(count)
    cosine, sine = rope_tables(pos_local)

    (mixed, totals, pre, normed, gain_rows_, qk_gains, placed, cot, queries, kv_all,
     qkv_full, _, out_t, feed_whole) = forward(
        sizes, meta, cosine, sine, tokens, cotangent, qkv_shards + [out_proj.T] + feed_shards[:FF_FIRST] + [gains]
    )
    x = placed.reshape(count, D)
    cot = cot.reshape(count, D)
    qkv_full = qkv_full.reshape(PAIRS, D, -1)
    out_t = out_t.reshape(D, QD)
    feed_whole = feed_whole.reshape(FF_FIRST, D, -1)
    log_total = jnp.log2(totals[:, :KV_HEADS]).T
    result, grad_hidden, grad_stack, delta, post_part, dout, late, _, early_grad = feed(
        sizes, x, mixed, cot, out_t, gain_rows_, feed_whole, feed_shards[FF_FIRST:]
    )
    delta = delta[:HEADS].reshape(KV_HEADS, 2, 2 * SUBS, sub).transpose(0, 2, 1, 3)
    dq, dkv, late_grad, out_grad, output = backward(
        sizes, meta, queries, grad_stack, kv_all, log_total, delta, late, dout, result.reshape(2, rows, D)
    )
    feed_grad = jnp.concatenate([early_grad, late_grad], axis=0)

    def feed_columns(k):
        piece = feed_grad[:, :, k * FF_CHUNK : (k + 1) * FF_CHUNK]
        return piece.transpose(1, 0, 2).reshape(shard_rows, FF)

    query_grad, key_grad, value_grad, gain_grad, input_grad = finish(
        sizes, dq, dkv, pre, normed, x, grad_hidden, gain_rows_, post_part, qkv_full, qk_gains, cosine, sine
    )

    def own(line):
        return lax.dynamic_slice_in_dim(line, device * gain_rows, gain_rows)

    return (
        output,
        input_grad.astype(F32),
        gain_grad[:, 0],
        query_grad,
        key_grad,
        value_grad,
        own(gain_grad[0, GAIN_COLS : 2 * GAIN_COLS]),
        own(gain_grad[0, 2 * GAIN_COLS :]),
        out_grad.T,
        gain_grad[:, 1],
        feed_columns(0),
        feed_columns(1),
        feed_columns(2).T,
    )


def solution(mesh):
    dp, ctx = mesh.shape["dp"], mesh.shape["ctx"]
    sizes = (2, dp // 2, ctx // 2)
    return jax.shard_map(
        functools.partial(shards, sizes),
        mesh=mesh,
        in_specs=(
            P("dp", "ctx", None),
            P("dp", "ctx", None),
            P("dp", None),
            P("dp", None),
            P("dp", None),
            P(("dp", "ctx")),
            P(("dp", "ctx"), None),
            P(("dp", "ctx"), None),
            P(("dp", "ctx"), None),
            P(("dp", "ctx")),
            P(("dp", "ctx")),
            P(None, ("dp", "ctx")),
            P(("dp", "ctx")),
            P(("dp", "ctx"), None),
            P(("dp", "ctx"), None),
            P(None, ("dp", "ctx")),
        ),
        out_specs=(
            P("dp", "ctx", None),
            P("dp", "ctx", None),
            P(("dp", "ctx")),
            P(("dp", "ctx"), None),
            P(("dp", "ctx"), None),
            P(("dp", "ctx"), None),
            P(("dp", "ctx")),
            P(("dp", "ctx")),
            P(None, ("dp", "ctx")),
            P(("dp", "ctx")),
            P(("dp", "ctx"), None),
            P(("dp", "ctx"), None),
            P(None, ("dp", "ctx")),
        ),
        check_vma=False,
    )
```

```python
import functools
import math

import jax
import jax.numpy as jnp
from jax import lax
from jax.experimental import pallas as pl
from jax.experimental.pallas import tpu as pltpu
from jax.sharding import PartitionSpec as P

D = 1024
HEADS = 16
KV_HEADS = 8
HEAD_DIM = 128
FF = 3072
TRUNK = 1024
SEG = 128
TREE = 2560
QD = HEADS * HEAD_DIM
KVD = KV_HEADS * HEAD_DIM
SUBS = 5
CHUNK = 256
GAIN_COLS = 128
FF_CHUNK = 512
PAIRS = KV_HEADS // 2
FF_CHUNKS = FF // FF_CHUNK
FF_EARLY = 2
FF_FIRST = 4
LOCAL_RUNS = 3
MIB = 1024 * 1024

eps_norm = 1e-06
rope_base = 1000000.0
exp2_scale = math.log2(math.e) / math.sqrt(HEAD_DIM)
score_scale = HEAD_DIM ** (-0.5)

MESH = pl.DeviceIdType.MESH
ANY = pl.BlockSpec(memory_space=pl.ANY)
F32 = jnp.float32
BF16 = jnp.bfloat16


def matmul(left_side, right_side):
    return jnp.dot(left_side, right_side, preferred_element_type=F32)


def nt(left_side, right_side):
    return lax.dot_general(
        left_side, right_side, (((1,), (1,)), ((), ())), preferred_element_type=F32
    )


def contract_rows(left_side, right_side):
    return lax.dot_general(
        left_side, right_side, (((0,), (0,)), ((), ())), preferred_element_type=F32
    )


def norm_factor(values):
    return lax.rsqrt(jnp.mean(values * values, axis=-1, keepdims=True) + eps_norm)


def norm_backward(grad_out, weight, normed, factor):
    weighted = grad_out * weight
    grad_in = factor * (weighted - normed * jnp.mean(weighted * normed, axis=-1, keepdims=True))
    return (grad_in, grad_out * normed)


def rope_tables(positions):
    steps_half = jnp.arange(HEAD_DIM // 2, dtype=F32)
    inverse = rope_base ** (-(steps_half * 2.0 / HEAD_DIM))
    angles = positions.astype(F32)[:, None] * inverse[None, :]
    cosine, sine = jnp.cos(angles), jnp.sin(angles)
    return jnp.concatenate([cosine, cosine], axis=-1), jnp.concatenate([-sine, sine], axis=-1)


class Links:
    def __init__(self, sizes, send_sem, recv_sem):
        self.sizes = sizes
        self.send_sem = send_sem
        self.recv_sem = recv_sem
        self.index = {}

    def place(self):
        _, nx, _ = self.sizes
        dp, ctx = lax.axis_index("dp"), lax.axis_index("ctx")
        return dp // nx, lax.rem(dp, nx), ctx // 2, lax.rem(ctx, 2)

    def device(self, y, x, z, core):
        return (y * self.sizes[1] + x, z * 2 + core)

    def peers(self, axis, back=False):
        y, x, z, core = self.place()
        at = {"y": y, "x": x, "z": z}
        n = self.sizes["yxz".index(axis)]
        found = []
        for s in range(1, n):
            moved = dict(at)
            moved[axis] = lax.rem(at[axis] + (n - s if back else s), n)
            found.append((moved["y"], moved["x"], moved["z"], core))
        return found

    def sibling(self):
        y, x, z, core = self.place()
        return self.device(y, x, z, 1 - core)

    def across(self):
        y, x, z, core = self.place()
        nz = self.sizes[2]
        return self.device(y, x, lax.rem(z + nz // 2, nz), core)

    def group(self, back=False):
        y, x, z, core = self.place()
        chips = self.sizes[2] // 2
        base = (z // chips) * chips
        here = z - base
        chosen = [lax.rem(here + (chips - s if back else s), chips) for s in range(1, chips)]
        return [(chip, self.device(y, x, base + chip, core)) for chip in chosen]

    def meet(self):
        barrier = pltpu.get_barrier_semaphore()
        partners = [self.device(*p) for a in "zxy" for p in self.peers(a)] + [self.sibling()]
        for partner in partners:
            pl.semaphore_signal(barrier, inc=1, device_id=partner, device_id_type=MESH)
        pl.semaphore_wait(barrier, len(partners))

    def copy(self, key, src, dst, target):
        k = self.index.setdefault(key, len(self.index))
        return pltpu.make_async_remote_copy(
            src_ref=src,
            dst_ref=dst,
            send_sem=self.send_sem.at[k],
            recv_sem=self.recv_sem.at[k],
            device_id=target,
            device_id_type=MESH,
        )


class Exchange:
    def __init__(self, links, source, placed, local_sem, tag="swap"):
        self.tag = tag
        self.links = links
        self.source = source
        self.placed = placed
        self.local_sem = local_sem

    def copies_(self):
        _, _, z, _ = self.links.place()
        half = z // (self.links.sizes[2] // 2)
        return [
            self.links.copy(self.tag, self.source.at[1 - half], self.placed.at[half], self.links.across()),
            pltpu.make_async_copy(self.source.at[half], self.placed.at[half], self.local_sem),
        ]

    def start(self):
        for copy in self.copies_():
            copy.start()

    def wait(self):
        for copy in self.copies_():
            copy.wait()


class Gather:
    def __init__(self, links, tag, shard, whole, order, cols, local_sem):
        self.links = links
        self.tag = tag
        self.shard = shard
        self.whole = whole
        self.order = order
        self.cols = cols
        self.local_sem = local_sem

    def own(self):
        y, x, z, core = self.links.place()
        return self.whole.at[y, x, z, core, :, self.cols]

    def slab(self, stage, at):
        y, x, z, core = at
        if stage == 0:
            return self.whole.at[y, x, z, core, :, self.cols]
        if stage == 1:
            return self.whole.at[y, x, :, core, :, self.cols]
        if self.order[0] == "x":
            return self.whole.at[y, :, :, core, :, self.cols]
        return self.whole.at[:, x, :, core, :, self.cols]

    def axis(self, stage):
        return ("z",) + tuple(self.order)[0:2] if stage is None else ("z", self.order[0], self.order[1])[stage]

    def send(self, stage):
        me = self.links.place()
        src = self.shard.at[:, self.cols] if stage == 0 else self.slab(stage, me)
        dst = self.slab(stage, me)
        return [
            self.links.copy((self.tag, stage, i), src, dst, self.links.device(*p))
            for i, p in enumerate(self.links.peers(self.axis(stage)))
        ]

    def forward(self, stage):
        sibling = self.links.sibling()
        if stage < 0:
            return [self.links.copy((self.tag, "own"), self.shard.at[:, self.cols], self.own(), sibling)]
        return [
            self.links.copy((self.tag, "pass", stage, i), self.slab(stage, p), self.slab(stage, p), sibling)
            for i, p in enumerate(self.links.peers(self.axis(stage), back=True))
        ]

    def local(self):
        return pltpu.make_async_copy(self.shard.at[:, self.cols], self.own(), self.local_sem)

    def start(self):
        self.local().start()
        for copy in self.send(0) + self.forward(-1):
            copy.start()

    def step(self, stage):
        if stage == 1:
            self.local().wait()
        for copy in self.send(stage - 1):
            copy.wait()
        if stage < 3:
            for copy in self.send(stage):
                copy.start()
        for copy in self.forward(stage - 1):
            copy.start()

    def close(self):
        for stage in range(-1, 3):
            for copy in self.forward(stage):
                copy.wait()

    @staticmethod
    def copies(sizes):
        return 2 * sum(n - 1 for n in sizes) + 1


class Scatter:
    def __init__(self, links, tag, part, order, cols, halves, firsts, seconds, thirds, temp, temp_sem, out):
        self.links = links
        self.tag = tag
        self.part = part
        self.order = order
        self.cols = cols
        self.sums = halves
        self.got = (firsts, seconds, thirds)
        self.temp = temp
        self.temp_sem = temp_sem
        self.out = out

    def first(self):
        _, _, _, core = self.links.place()
        return self.links.copy(
            (self.tag, "core"), self.part.at[:, :, :, 1 - core, :, self.cols], self.sums, self.links.sibling()
        )

    def load(self):
        _, _, _, core = self.links.place()
        return pltpu.make_async_copy(
            self.part.at[:, :, :, core, :, self.cols], self.temp, self.temp_sem
        )

    def axis(self, stage):
        return (self.order[0], self.order[1], "z")[stage]

    def at(self, stage, place, rest=None):
        y, x, z, _ = place
        if stage == 0:
            return (y,) if self.order[0] == "y" else (slice(None), x)
        if stage == 1:
            return (y, x)
        return (y, x, z)

    def send(self, stage):
        me = self.links.place()
        found = []
        for i, p in enumerate(self.links.peers(self.axis(stage))):
            index = self.at(stage, p)
            found.append(
                self.links.copy(
                    (self.tag, stage, i), self.sums.at[index], self.got[stage].at[i], self.links.device(*p)
                )
            )
        return found

    def start(self):
        self.first().start()

    def begin(self):
        self.first().wait()
        if self.temp_sem is not None:
            self.load().wait()
        ny, nx, nz = self.links.sizes

        def add(i, carry):
            a, b, c = i // (nx * nz), lax.rem(i // nz, nx), lax.rem(i, nz)
            self.sums[a, b, c] = (
                self.sums[a, b, c].astype(F32) + self.temp[a, b, c].astype(F32)
            ).astype(BF16)
            return carry

        lax.fori_loop(0, ny * nx * nz, add, 0)
        for copy in self.send(0):
            copy.start()

    def middle(self, stage):
        for copy in self.send(stage):
            copy.wait()
        y, x, z, _ = self.links.place()
        _, _, nz = self.links.sizes
        got = self.got[stage]
        peers = got.shape[0]
        if stage == 0:
            other = got.shape[1]

            def add(i, carry):
                b, c = i // nz, lax.rem(i, nz)
                index = (y, b, c) if self.order[0] == "y" else (b, x, c)
                total = self.sums[index].astype(F32)
                for p in range(peers):
                    total = total + got[p, b, c].astype(F32)
                self.sums[index] = total.astype(BF16)
                return carry

            lax.fori_loop(0, other * nz, add, 0)
        else:

            def add(c, carry):
                total = self.sums[y, x, c].astype(F32)
                for p in range(peers):
                    total = total + got[p, c].astype(F32)
                self.sums[y, x, c] = total.astype(BF16)
                return carry

            lax.fori_loop(0, nz, add, 0)
        for copy in self.send(stage + 1):
            copy.start()

    def finish(self):
        for copy in self.send(2):
            copy.wait()
        y, x, z, _ = self.links.place()
        total = self.sums[y, x, z].astype(F32)
        for p in range(self.got[2].shape[0]):
            total = total + self.got[2][p].astype(F32)
        if callable(self.out):
            self.out(total)
        else:
            self.out[:, self.cols] = total

    @staticmethod
    def copies(sizes):
        return sum(n - 1 for n in sizes) + 1

    @staticmethod
    def scratch(sizes, order, rows, width):
        ny, nx, nz = sizes
        na, nb = (ny, nx) if order[0] == "y" else (nx, ny)
        return [
            pltpu.VMEM((ny, nx, nz, rows, width), BF16),
            pltpu.VMEM((na - 1, nb, nz, rows, width), BF16),
            pltpu.VMEM((nb - 1, nz, rows, width), BF16),
            pltpu.VMEM((nz - 1, rows, width), BF16),
        ]


ORDERS = ("xy", "yx")

FORWARD_START = [
    ("swap", "tokens"), (0, 9), (0, 0), (1, 9), (1, 0), (2, 9), (2, 0), (0, 1), (0, 2), (3, 9), (4, 9), (3, 0),
    (1, 1), (1, 2), (0, 3), (2, 1), (0, 4), ("swapped", "tokens"),
]
FORWARD_AFTER = {
    0: [("kv", 0), (2, 2), (1, 3), (3, 1), (1, 4), (0, 5)],
    1: [("kv", 1), (3, 2), (2, 3), (2, 4), (1, 5)],
    2: [("use", 0), (3, 3), (3, 4), (2, 5), (0, 6), ("kv", 2)],
    3: [("got", 0), (1, 6), (0, 7), (3, 5)],
    4: [("use", 1), ("got", 1), ("kv", 3), (2, 6), (1, 7)],
    5: [(3, 6), (2, 7), (0, 8)],
    6: [("use", 2), ("swap", "cot"), (1, 8)],
    7: [("got", 2), (3, 7), (2, 8)],
    8: [("use", 3)],
    9: [("got", 3), (3, 8)],
    11: [("swapped", "cot")],
}
FEED_START = [("fetch", 0), ("send", (0, 4)), ("fetch", 1)]
FEED_NEXT = [("send", (1, 4)), ("send", (0, 5))]
FEED_MIDDLE = {
    0: [("send", (2, 4))],
    1: [("send", (3, 4)), ("send", (2, 5)), ("fetch", 2)],
    2: [("send", (3, 5)), ("fetch", 3)],
    3: [("fetch", 4)],
    4: [("fetch", 5)],
    5: [(1, 1)],
}
FEED_AFTER = {
    0: [("send", (1, 5)), ("core", 0)],
    1: [("begin", 0), ("core", 1)],
    2: [("begin", 1)],
    3: [(0, 0), (0, 1)],
    4: [(1, 0)],
}
FEED_LAST = []
FINISH_MIDDLE = {
    1: [("begin", 0)],
    2: [("begin", 1), (1, 0)],
    3: [("begin", 2), (1, 1)],
}
FINISH_AFTER = {
    0: [("core", 0)],
    1: [("core", 1), (0, 0)],
    2: [("core", 2), (0, 1)],
    3: [("core", 3)],
}
BACKWARD_AFTER = {
    0: [(0, 0)],
    1: [(1, 0), (0, 1)],
    2: [(2, 0), (1, 1), (0, 2)],
    3: [(2, 1), (1, 2), (0, 3)],
    4: [(2, 2), (1, 3), (0, 4)],
    5: [(2, 3), (1, 4)],
    6: [(2, 4)],
}


def halves_of(width):
    return (slice(0, width // 2), slice(width // 2, width)) if width >= 512 else (slice(0, width),)


def roll_half(values):
    return pltpu.roll(values, HEAD_DIM // 2, 1)


class KeyValues:
    def __init__(self, links, rows, held):
        self.links = links
        self.rows = rows
        self.held = held

    def slab(self, group, piece, member):
        members = self.links.sizes[2]
        start = pl.multiple_of(self.rows * (piece * members + member), self.rows)
        return self.held.at[:, 2 * group : 2 * group + 2, pl.ds(start, self.rows)]

    def mine(self):
        _, _, z, core = self.links.place()
        return lax.rem(z, self.links.sizes[2] // 2) * 2 + core

    def across(self, group):
        found = []
        for piece in range(2):
            slab = self.slab(group, piece, self.mine())
            for i, (_, target) in enumerate(self.links.group()):
                found.append(self.links.copy(("kv", group, piece, i), slab, slab, target))
        return found

    def near(self, group):
        found = []
        for piece in range(2):
            slab = self.slab(group, piece, self.mine())
            found.append(self.links.copy(("kv own", group, piece), slab, slab, self.links.sibling()))
        return found

    def forward(self, group):
        _, _, _, core = self.links.place()
        found = []
        for piece in range(2):
            for i, (chip, _) in enumerate(self.links.group(back=True)):
                slab = self.slab(group, piece, chip * 2 + core)
                found.append(
                    self.links.copy(("kv pass", group, piece, i), slab, slab, self.links.sibling())
                )
        return found

    @staticmethod
    def copies(sizes):
        return 4 * 2 * (2 * (sizes[2] // 2 - 1) + 1)


def run_all(copies, act):
    for copy in copies:
        if act == "start":
            copy.start()
        else:
            copy.wait()


def row_places(shape, dim, sub):
    t = lax.broadcasted_iota(jnp.int32, shape, dim)
    return (t // (2 * sub)) * sub + t % sub


def block_copies(sizes, src, dst, sem):
    ny, nx, nz = sizes
    shard_rows = src.shape[-2]
    found = []
    for i in range(ny * nx * nz * 2):
        block = src.at[i // (nx * nz * 2), i // (nz * 2) % nx, i // 2 % nz, i % 2]
        found.append(pltpu.make_async_copy(block, dst.at[i * shard_rows : (i + 1) * shard_rows], sem))
    return found


def gather_parents(meta, lead, slot, pairs):
    runs = (TREE - TRUNK) // SEG
    for k in range(LOCAL_RUNS):
        parent = meta[jnp.minimum(lead + k, runs - 1)]
        for read, out in pairs:
            total = None
            for b in range(runs):
                share = (1 - jnp.minimum(jnp.abs(parent - b), 1)).astype(F32).astype(BF16)
                term = read(b) * share
                total = term if total is None else total + term
            out[slot + k] = total


def forward_kernel(sizes, rows, meta, cos_ref, sin_ref, tok_ref, cot_ref, *refs):
    arrays = PAIRS + 2 + FF_FIRST
    qkv_width, feed_width = 8 * HEAD_DIM, 3 * FF_CHUNK
    shard = (
        tuple(refs[0].at[:, qkv_width * c : qkv_width * (c + 1)] for c in range(PAIRS))
        + (refs[1],)
        + tuple(refs[2].at[:, feed_width * c : feed_width * (c + 1)] for c in range(FF_FIRST))
        + (refs[3],)
    )
    refs = refs[4:]
    (mixed_ref, l_ref, pre_ref, normed_ref, gains_ref, qk_ref,
     placed, cot_placed, q_all, kv_all, qkv_whole, gain_whole, out_whole, feed_whole) = refs[:14]
    whole = (
        tuple(qkv_whole.at[c] for c in range(PAIRS))
        + (out_whole,)
        + tuple(feed_whole.at[c] for c in range(FF_FIRST))
        + (gain_whole,)
    )
    (qs, kvs, xs, ws, gs, acc, part, places, kp, vp, send_sem, recv_sem, local_sem) = refs[14:]
    members = sizes[2]
    sub = rows // SUBS
    count = 2 * rows
    step = pl.program_id(0)
    head = jnp.maximum(step - PAIRS, 0)
    links = Links(sizes, send_sem, recv_sem)
    kv = KeyValues(links, rows, kvs)
    swaps = {
        "tokens": Exchange(links, tok_ref, placed, local_sem.at[0], "tokens"),
        "cot": Exchange(links, cot_ref, cot_placed, local_sem.at[1], "cot"),
    }
    weights_ = [
        [
            Gather(links, (a, b), shard[a], whole[a], ORDERS[b], cols, local_sem.at[12 + 2 * a + b])
            for b, cols in enumerate(halves_of(shard[a].shape[-1]))
        ]
        for a in range(arrays)
    ]
    _, _, z, core = links.place()
    mine = lax.rem(z, members // 2) * 2 + core

    def kept(group):
        pair = slice(2 * group, 2 * group + 2)
        return [
            pltpu.make_async_copy(kvs.at[:, pair], kv_all.at[:, pair], local_sem.at[2 + group]),
            pltpu.make_async_copy(qs.at[pair], q_all.at[pair], local_sem.at[6 + group]),
        ]

    def act(steps):
        for what, a in steps:
            if what == "swap":
                swaps[a].start()
            elif what == "swapped":
                swaps[a].wait()
            elif what == "kv":
                run_all(kv.across(a), "start")
                run_all(kv.near(a), "start")
            elif what == "use":
                run_all(kv.across(a), "wait")
                run_all(kv.forward(a), "start")
            elif what == "got":
                run_all(kv.near(a), "wait")
                run_all(kv.forward(a), "wait")
                run_all(kept(a), "start")
            else:
                for g in weights_[a]:
                    if what == 0:
                        g.start()
                    elif what == 4:
                        g.close()
                    else:
                        g.step(what)

    @pl.when(step == 0)
    def _():
        links.meet()
        act(FORWARD_START)
        l_ref[...] = jnp.zeros_like(l_ref)
        places[...] = row_places(places.shape, 0, sub)
        run_all(block_copies(sizes, gain_whole, gs, local_sem.at[10]), "start")
        pltpu.make_async_copy(gs, gs, local_sem.at[10]).wait()
        loaded = pltpu.make_async_copy(placed, xs, local_sem.at[11])
        loaded.start()
        gains_ref[...] = gs[:, :GAIN_COLS].astype(F32).T[:8]
        qk_ref[0:1] = jnp.sum(gs[:, GAIN_COLS : 2 * GAIN_COLS].astype(F32), axis=0, keepdims=True)
        qk_ref[1:2] = jnp.sum(gs[:, 2 * GAIN_COLS :].astype(F32), axis=0, keepdims=True)
        loaded.wait()
        values = xs[...].reshape(count, D).astype(F32)
        normed_ref[...] = (values * norm_factor(values) * gains_ref[0:1]).astype(BF16)

    for c in range(PAIRS):

        @pl.when(step == c)
        def _():
            act([(4, c)])
            run_all(block_copies(sizes, qkv_whole.at[c], ws, local_sem.at[10]), "start")
            pltpu.make_async_copy(ws, ws, local_sem.at[10]).wait()

    @pl.when(step < PAIRS)
    def _():
        normed = normed_ref[...]
        cosine, sine = cos_ref[...], sin_ref[...]

        def turned(pre, gain):
            values = pre * norm_factor(pre) * gain
            return (values * cosine + roll_half(values) * sine).astype(BF16)

        for hh in range(2):
            at = 2 * step + hh
            query = matmul(normed, ws[:, 2 * hh * HEAD_DIM : 2 * (hh + 1) * HEAD_DIM])
            for h in range(2):
                pre = query[:, h * HEAD_DIM : (h + 1) * HEAD_DIM]
                pre_ref[hh, :, h * HEAD_DIM : (h + 1) * HEAD_DIM] = pre
                low = turned(pre, qk_ref[0:1])
                for s in range(2 * SUBS):
                    qs[at, (2 * s + h) * sub : (2 * s + h + 1) * sub] = low[s * sub : (s + 1) * sub]
            pre = matmul(normed, ws[:, (4 + hh) * HEAD_DIM : (5 + hh) * HEAD_DIM])
            pre_ref[hh, :, 2 * HEAD_DIM :] = pre
            low = turned(pre, qk_ref[1:2])
            value = matmul(normed, ws[:, (6 + hh) * HEAD_DIM : (7 + hh) * HEAD_DIM]).astype(BF16)
            for piece in range(2):
                start = pl.multiple_of(rows * (piece * members + mine), rows)
                kvs[0, at, pl.ds(start, rows)] = low[piece * rows : (piece + 1) * rows]
                kvs[1, at, pl.ds(start, rows)] = value[piece * rows : (piece + 1) * rows]

    def attend():
        lane = lax.broadcasted_iota(jnp.int32, (2 * rows, HEAD_DIM), 1)
        for piece in range(2):
            base = rows * (piece * members + mine)
            region = slice(piece * 2 * rows, (piece + 1) * 2 * rows)
            acc[...] = jnp.zeros_like(acc)
            part[...] = jnp.zeros_like(part)

            def trunk(step, masked):
                start = pl.multiple_of(step * CHUNK, CHUNK)
                weights = jnp.exp2(nt(qs[head, region], kvs[0, head, pl.ds(start, CHUNK)]) * exp2_scale)
                low, high = weights[:, :HEAD_DIM], weights[:, HEAD_DIM:]
                if masked:
                    room = places[...] + (base - start)
                    low = jnp.where(lane <= room, low, 0.0)
                    high = jnp.where(lane + HEAD_DIM <= room, high, 0.0)
                    weights = jnp.concatenate([low, high], axis=1)
                part[...] += low + high
                acc[...] += matmul(weights.astype(BF16), kvs[1, head, pl.ds(start, CHUNK)])
                return masked

            if piece == 0:
                clear = jnp.minimum(base // CHUNK, TRUNK // CHUNK)
                last = jnp.minimum((base + rows + CHUNK - 1) // CHUNK, TRUNK // CHUNK)
                lax.fori_loop(0, clear, lambda i, c: (trunk(i, False), c)[1], 0)
                lax.fori_loop(clear, last, lambda i, c: (trunk(i, True), c)[1], 0)
            else:
                lax.fori_loop(0, TRUNK // CHUNK, lambda i, c: (trunk(i, False), c)[1], 0)

            lead = jnp.maximum(base - TRUNK, 0) // SEG

            def parents_():
                gather_parents(
                    meta,
                    lead,
                    0,
                    [
                        (lambda b: kvs[0, head, TRUNK + b * SEG : TRUNK + (b + 1) * SEG], kp),
                        (lambda b: kvs[1, head, TRUNK + b * SEG : TRUNK + (b + 1) * SEG], vp),
                    ],
                )

            if piece == 0:
                pl.when(base + rows > TRUNK)(parents_)
            else:
                parents_()
            for s in range(SUBS):
                block = slice(2 * sub * s, 2 * sub * (s + 1))

                def runs():
                    row = base + s * sub - TRUNK
                    run = row // SEG
                    own = pl.multiple_of(TRUNK + run * SEG, SEG)
                    flag = jnp.minimum(meta[run] + 1, 1).astype(F32)
                    query = qs[head, piece * 2 * rows + 2 * sub * s : piece * 2 * rows + 2 * sub * (s + 1)]
                    room = places[block] + (lax.rem(row, SEG) - s * sub)
                    weights = jnp.exp2(nt(query, kvs[0, head, pl.ds(own, SEG)]) * exp2_scale)
                    weights = jnp.where(lane[block] <= room, weights, 0.0)
                    above = jnp.exp2(nt(query, kp[run - lead]) * exp2_scale) * flag
                    part[block] += weights + above
                    acc[block] += matmul(weights.astype(BF16), kvs[1, head, pl.ds(own, SEG)]) + matmul(
                        above.astype(BF16), vp[run - lead]
                    )

                if piece == 0:
                    pl.when(base + s * sub >= TRUNK)(runs)
                else:
                    runs()

            total = jnp.sum(part[...], axis=-1, keepdims=True)
            mixed = (acc[...] / total).astype(BF16)
            for s in range(SUBS):
                for h in range(2):
                    row = piece * rows + sub * s
                    mixed_ref[row : row + sub, h * HEAD_DIM : (h + 1) * HEAD_DIM] = mixed[
                        (2 * s + h) * sub : (2 * s + h + 1) * sub
                    ]
            l_ref[region] = jnp.where(lane == head, total, l_ref[region])


    pl.when(step >= PAIRS)(attend)
    for moment, steps in FORWARD_AFTER.items():
        pl.when(step == moment)(functools.partial(act, steps))

    @pl.when(step == PAIRS + KV_HEADS - 1)
    def _():
        for array in weights_[PAIRS : PAIRS + 1 + FF_FIRST]:
            for g in array:
                g.close()
        for group in range(4):
            run_all(kept(group), "wait")


def forward(sizes, meta, cosine, sine, tokens, cotangent, shards_):
    ny, nx, nz = sizes
    rows = tokens.shape[1]
    count = 2 * rows
    arrays = PAIRS + 2 + FF_FIRST
    shard_rows = shards_[0].shape[0]
    blocks = (ny, nx, nz, 2, shard_rows)
    widths = [8 * HEAD_DIM] * PAIRS + [QD] + [3 * FF_CHUNK] * FF_FIRST + [3 * GAIN_COLS]
    rounds = KeyValues.copies(sizes) + 2 * arrays * Gather.copies(sizes) + 2

    def at_head(s):
        return jnp.maximum(s - PAIRS, 0)

    results = pl.pallas_call(
        functools.partial(forward_kernel, sizes, rows),
        out_shape=[
            jax.ShapeDtypeStruct((count, QD), BF16),
            jax.ShapeDtypeStruct((2 * count, HEAD_DIM), F32),
            jax.ShapeDtypeStruct((KV_HEADS, count, 3 * HEAD_DIM), F32),
            jax.ShapeDtypeStruct((count, D), BF16),
            jax.ShapeDtypeStruct((8, D), F32),
            jax.ShapeDtypeStruct((8, HEAD_DIM), F32),
            jax.ShapeDtypeStruct(tokens.shape, BF16),
            jax.ShapeDtypeStruct(tokens.shape, BF16),
            jax.ShapeDtypeStruct((KV_HEADS, 2 * count, HEAD_DIM), BF16),
            jax.ShapeDtypeStruct((2, KV_HEADS, TREE, HEAD_DIM), BF16),
            jax.ShapeDtypeStruct((PAIRS,) + blocks + (widths[0],), BF16),
            jax.ShapeDtypeStruct(blocks + (widths[-1],), BF16),
            jax.ShapeDtypeStruct(blocks + (widths[PAIRS],), BF16),
            jax.ShapeDtypeStruct((FF_FIRST,) + blocks + (widths[PAIRS + 1],), BF16),
        ],
        grid_spec=pltpu.PrefetchScalarGridSpec(
            num_scalar_prefetch=1,
            grid=(PAIRS + KV_HEADS,),
            in_specs=[pl.BlockSpec((count, HEAD_DIM), lambda s, meta: (0, 0))] * 2 + [ANY] * 6,
            out_specs=[
                pl.BlockSpec((count, 2 * HEAD_DIM), lambda s, meta: (0, at_head(s))),
                pl.BlockSpec((2 * count, HEAD_DIM), lambda s, meta: (0, 0)),
                pl.BlockSpec((2, count, 3 * HEAD_DIM), lambda s, meta: (jnp.minimum(s, PAIRS - 1), 0, 0)),
                pl.BlockSpec((count, D), lambda s, meta: (0, 0)),
                pl.BlockSpec((8, D), lambda s, meta: (0, 0)),
                pl.BlockSpec((8, HEAD_DIM), lambda s, meta: (0, 0)),
            ]
            + [ANY] * 8,
            scratch_shapes=[
                pltpu.VMEM((KV_HEADS, 2 * count, HEAD_DIM), BF16),
                pltpu.VMEM((2, KV_HEADS, TREE, HEAD_DIM), BF16),
                pltpu.VMEM(tokens.shape, BF16),
                pltpu.VMEM((D, widths[0]), BF16),
                pltpu.VMEM((D, widths[-1]), BF16),
                pltpu.VMEM((count, HEAD_DIM), F32),
                pltpu.VMEM((count, HEAD_DIM), F32),
                pltpu.VMEM((count, HEAD_DIM), jnp.int32),
                pltpu.VMEM((LOCAL_RUNS, SEG, HEAD_DIM), BF16),
                pltpu.VMEM((LOCAL_RUNS, SEG, HEAD_DIM), BF16),
                pltpu.SemaphoreType.DMA((rounds,)),
                pltpu.SemaphoreType.DMA((rounds,)),
                pltpu.SemaphoreType.DMA((12 + 2 * arrays,)),
            ],
        ),
        compiler_params=pltpu.CompilerParams(
            collective_id=2, has_side_effects=True, vmem_limit_bytes=56 * MIB
        ),
        name="forward",
    )(meta, cosine, sine, tokens, cotangent, *shards_)
    return results


def feed_kernel(
    sizes, rows, x_ref, mixed_ref, cot_ref, out_ref, gain_ref, first_ref, *refs,
):
    shard = refs[: FF_CHUNKS - FF_FIRST]
    refs = refs[FF_CHUNKS - FF_FIRST :]
    result_ref, hid_ref, stack_ref, delta_ref, post_ref, dout_ref, late_ref, rest_ref, early_ref = refs[:9]
    hidden, second, second_t, cot_t, total, grads, inner, gate_up, low, stack, part, wbuf = refs[9:21]
    buffers = refs[21:-3]
    send_sem, recv_sem, local_sem = refs[-3:]
    ny, nx, nz = sizes
    count = 2 * rows
    sub = rows // SUBS
    shard_rows = part.shape[5]
    width = 3 * FF_CHUNK
    tile = 256
    chunk = pl.program_id(0)
    links = Links(sizes, send_sem, recv_sem)
    _, _, _, core = links.place()
    scatters = []
    for c in range(FF_EARLY):
        for b, cols in enumerate(halves_of(width)):
            k = 4 * len(scatters)
            scatters.append(
                Scatter(
                    links,
                    (c, b),
                    part.at[c % 2],
                    ORDERS[b],
                    cols,
                    *buffers[k : k + 4],
                    part.at[c % 2, :, :, :, core, :, cols],
                    None,
                    early_ref.at[c],
                )
            )

    gathers = [
        [
            Gather(links, ("w", c, b), shard[c], rest_ref.at[c], ORDERS[b], cols, local_sem.at[8 + 2 * c + b])
            for b, cols in enumerate(halves_of(width))
        ]
        for c in range(FF_CHUNKS - FF_FIRST)
    ]

    def fetch(c):
        if c < FF_FIRST:
            pltpu.make_async_copy(first_ref.at[c], wbuf.at[c % 2], local_sem.at[6 + c % 2]).start()
        else:
            for g in gathers[c - FF_FIRST]:
                g.close()
            run_all(
                block_copies(sizes, rest_ref.at[c - FF_FIRST], wbuf.at[c % 2], local_sem.at[6 + c % 2]), "start"
            )

    def act(steps):
        for what, c in steps:
            if what == "fetch":
                fetch(c)
                continue
            if what == "send":
                for g in gathers[c[1] - FF_FIRST]:
                    if c[0] == 0:
                        g.start()
                    else:
                        g.step(c[0])
                continue
            for s in scatters[2 * c : 2 * c + 2]:
                if what == "core":
                    s.start()
                elif what == "begin":
                    s.begin()
                elif what == "finish":
                    s.finish()
                else:
                    s.middle(what)

    def rows_of(block):
        return (block // (2 * nz * nx), lax.rem(block // (2 * nz), nx), lax.rem(block // 2, nz), lax.rem(block, 2))

    def put(slot, first, cols, value):
        for k in range(value.shape[0] // shard_rows):
            y, x, z, c = rows_of(first // shard_rows + k)
            part[slot, y, x, z, c, :, cols] = value[k * shard_rows : (k + 1) * shard_rows].astype(BF16)

    def late(c):
        return pltpu.make_async_copy(part.at[c % 2], late_ref.at[c - FF_EARLY], local_sem.at[c % 2])

    @pl.when(chunk == 0)
    def _():
        links.meet()
        act(FEED_START)

        def project_out(t, carry):
            at = pl.multiple_of(t * tile, tile)
            hidden[:, pl.ds(at, tile)] = x_ref[:, pl.ds(at, tile)].astype(F32) + nt(
                mixed_ref[...], out_ref[pl.ds(at, tile), :]
            )
            return carry

        lax.fori_loop(0, D // tile, project_out, 0)
        act(FEED_NEXT)
        values = hidden[...]
        values = values * norm_factor(values) * gain_ref[1:2]
        second[...] = values.astype(BF16)
        second_t[...] = values.T.astype(BF16)
        cot_t[...] = cot_ref[...].astype(F32).T.astype(BF16)
        total[...] = jnp.zeros_like(total)
        grads[...] = jnp.zeros_like(grads)

    slot = lax.rem(chunk, 2)
    pltpu.make_async_copy(wbuf.at[slot], wbuf.at[slot], local_sem.at[6 + slot]).wait()

    def columns(t, carry):
        at = pl.multiple_of(t * tile, tile)
        gate = matmul(second[...], wbuf[slot, :, pl.ds(at, tile)])
        up = matmul(second[...], wbuf[slot, :, pl.ds(FF_CHUNK + at, tile)])
        grad = matmul(cot_ref[...], wbuf[slot, :, pl.ds(2 * FF_CHUNK + at, tile)])
        sigmoid = 1.0 / (1.0 + jnp.exp(-gate))
        active = gate * sigmoid
        inner[:, pl.ds(at, tile)] = (active * up).astype(BF16)
        gate_up[:, pl.ds(at, tile)] = (grad * up * sigmoid * (1.0 + gate * (1.0 - sigmoid))).astype(BF16)
        gate_up[:, pl.ds(FF_CHUNK + at, tile)] = (grad * active).astype(BF16)
        return carry

    lax.fori_loop(0, FF_CHUNK // tile, columns, 0)
    for moment, steps in FEED_MIDDLE.items():
        pl.when(chunk == moment)(functools.partial(act, steps))
    for c in range(FF_EARLY, FF_CHUNKS - 2):
        pl.when(chunk == c + 2)(lambda: late(c).wait())

    def model(t, carry):
        at = pl.multiple_of(t * tile, tile)
        total[:, pl.ds(at, tile)] += nt(inner[...], wbuf[slot, pl.ds(at, tile), 2 * FF_CHUNK :])
        grads[:, pl.ds(at, tile)] += nt(gate_up[...], wbuf[slot, pl.ds(at, tile), : 2 * FF_CHUNK])
        put(slot, at, slice(0, 2 * FF_CHUNK), matmul(second_t[pl.ds(at, tile)], gate_up[...]))
        put(slot, at, slice(2 * FF_CHUNK, width), matmul(cot_t[pl.ds(at, tile)], inner[...]))
        return carry

    lax.fori_loop(0, D // tile, model, 0)
    for c in range(FF_EARLY, FF_CHUNKS):
        pl.when(chunk == c)(lambda: late(c).start())
    for moment, steps in FEED_AFTER.items():
        pl.when(chunk == moment)(functools.partial(act, steps))

    @pl.when(chunk == FF_CHUNKS - 1)
    def _():
        values = hidden[...]
        low[...] = (values + total[...]).astype(BF16)
        output = pltpu.make_async_copy(low, result_ref, local_sem.at[2])
        output.start()
        factor = norm_factor(values)
        grad_in, share = norm_backward(grads[...], gain_ref[1:2], values * factor, factor)
        post_ref[...] = jnp.sum(share, axis=0, keepdims=True)
        hidden[...] = cot_ref[...].astype(F32) + grad_in
        saved = pltpu.make_async_copy(hidden, hid_ref, local_sem.at[3])
        saved.start()
        second[...] = hidden[...].astype(BF16)
        second_t[...] = hidden[...].T.astype(BF16)
        lane = lax.broadcasted_iota(jnp.int32, (count, HEAD_DIM), 1)
        dots = jnp.zeros((count, HEAD_DIM), F32)
        for h in range(KV_HEADS):
            cols = slice(2 * h * HEAD_DIM, 2 * (h + 1) * HEAD_DIM)
            grad = matmul(second[...], out_ref[:, cols]).astype(BF16)
            for g in range(2):
                one = grad[:, g * HEAD_DIM : (g + 1) * HEAD_DIM]
                for s in range(2 * SUBS):
                    stack[h, (2 * s + g) * sub : (2 * s + g + 1) * sub] = one[s * sub : (s + 1) * sub]
                head = 2 * h + g
                product = one.astype(F32) * mixed_ref[:, head * HEAD_DIM : (head + 1) * HEAD_DIM].astype(F32)
                dots = jnp.where(lane == head, jnp.sum(product, axis=-1, keepdims=True), dots)
        delta_ref[...] = dots.T
        stacked_ = pltpu.make_async_copy(stack, stack_ref, local_sem.at[4])
        stacked_.start()
        act(FEED_LAST)
        for c in range(FF_CHUNKS - 2, FF_CHUNKS):
            late(c).wait()

        def model_out(t, carry):
            at = pl.multiple_of(t * tile, tile)
            for a in range(0, QD, 2 * FF_CHUNK):
                cols = slice(a, a + 2 * FF_CHUNK)
                value = matmul(second_t[pl.ds(at, tile)], mixed_ref[:, cols])
                slot = a // (2 * FF_CHUNK)
                put(slot, at, slice(0, 2 * FF_CHUNK), value)
            return carry

        lax.fori_loop(0, D // tile, model_out, 0)
        gone = [
            pltpu.make_async_copy(
                part.at[k, :, :, :, :, :, : 2 * FF_CHUNK],
                dout_ref.at[:, :, :, :, :, 2 * FF_CHUNK * k : 2 * FF_CHUNK * (k + 1)],
                local_sem.at[k],
            )
            for k in range(2)
        ]
        run_all(gone, "start")
        for c in range(FF_EARLY):
            act([("finish", c)])
        run_all(gone + [output, saved, stacked_], "wait")


def feed(sizes, x, mixed, cot, out_t, gain, first, shards_):
    ny, nx, nz = sizes
    count = x.shape[0]
    rows = count // 2
    shard_rows = D // (ny * nx * nz * 2)
    width = 3 * FF_CHUNK
    buffers = []
    for c in range(FF_EARLY):
        for b, cols in enumerate(halves_of(width)):
            buffers += Scatter.scratch(sizes, ORDERS[b], shard_rows, cols.stop - cols.start)
    late = FF_CHUNKS - FF_FIRST
    rounds = 2 * FF_EARLY * Scatter.copies(sizes) + 2 * late * Gather.copies(sizes)

    def whole_block(shape):
        return pl.BlockSpec(shape, lambda c: (0,) * len(shape), pipeline_mode=pl.Buffered(1))

    blocks = (ny, nx, nz, 2, shard_rows)
    return pl.pallas_call(
        functools.partial(feed_kernel, sizes, rows),
        grid=(FF_CHUNKS,),
        out_shape=[
            jax.ShapeDtypeStruct((count, D), BF16),
            jax.ShapeDtypeStruct((count, D), F32),
            jax.ShapeDtypeStruct((KV_HEADS, 2 * count, HEAD_DIM), BF16),
            jax.ShapeDtypeStruct((HEAD_DIM, count), F32),
            jax.ShapeDtypeStruct((1, D), F32),
            jax.ShapeDtypeStruct(blocks + (QD,), BF16),
            jax.ShapeDtypeStruct((FF_CHUNKS - FF_EARLY,) + blocks + (width,), BF16),
            jax.ShapeDtypeStruct((late,) + blocks + (width,), BF16),
            jax.ShapeDtypeStruct((FF_EARLY, shard_rows, width), F32),
        ],
        in_specs=[
            whole_block((count, D)),
            whole_block((count, QD)),
            whole_block((count, D)),
            whole_block((D, QD)),
            whole_block((8, D)),
            ANY,
        ]
        + [ANY] * late,
        out_specs=[
            ANY,
            ANY,
            ANY,
            pl.BlockSpec((HEAD_DIM, count), lambda c: (0, 0)),
            pl.BlockSpec((1, D), lambda c: (0, 0)),
            ANY,
            ANY,
            ANY,
            pl.BlockSpec((FF_EARLY, shard_rows, width), lambda c: (0, 0, 0)),
        ],
        scratch_shapes=[
            pltpu.VMEM((count, D), F32),
            pltpu.VMEM((count, D), BF16),
            pltpu.VMEM((D, count), BF16),
            pltpu.VMEM((D, count), BF16),
            pltpu.VMEM((count, D), F32),
            pltpu.VMEM((count, D), F32),
            pltpu.VMEM((count, FF_CHUNK), BF16),
            pltpu.VMEM((count, 2 * FF_CHUNK), BF16),
            pltpu.VMEM((count, D), BF16),
            pltpu.VMEM((KV_HEADS, 2 * count, HEAD_DIM), BF16),
            pltpu.VMEM((2,) + blocks + (width,), BF16),
            pltpu.VMEM((2, D, width), BF16),
        ]
        + buffers
        + [
            pltpu.SemaphoreType.DMA((rounds,)),
            pltpu.SemaphoreType.DMA((rounds,)),
            pltpu.SemaphoreType.DMA((8 + 2 * late,)),
        ],
        compiler_params=pltpu.CompilerParams(
            collective_id=5, has_side_effects=True, vmem_limit_bytes=61 * MIB
        ),
        name="feed",
    )(x, mixed, cot, out_t, gain, first, *shards_)


def backward_kernel(sizes, rows, widths, meta, q_ref, g_ref, k_ref, v_ref, lse_ref, del_ref, late_ref, dout_ref, done_ref, *refs):
    dq_ref, dkv_ref, late_out, dout_out, done_placed = refs[:5]
    dq, dk, dv, pk, pv, kp, vp, stage, near, sums, far, last = refs[5:17]
    buffers = refs[17:-3]
    send_sem, recv_sem, local_sem = refs[-3:]
    members = sizes[2]
    chips = members // 2
    sub = rows // SUBS
    head = pl.program_id(0)
    links = Links(sizes, send_sem, recv_sem)
    scatters = []
    late = FF_CHUNKS - FF_EARLY
    for a, width in enumerate(widths):
        for b, cols in enumerate(halves_of(width)):
            k = 5 * len(scatters)
            scatters.append(
                Scatter(
                    links,
                    (a, b),
                    late_ref.at[a] if a < late else dout_ref,
                    ORDERS[b],
                    cols,
                    *buffers[k : k + 5],
                    local_sem.at[2 + len(scatters)],
                    late_out.at[a] if a < late else dout_out,
                )
            )

    swap = Exchange(links, done_ref, done_placed, local_sem.at[2 + len(scatters)])

    def each(array):
        return scatters[2 * array : 2 * array + 2]

    @pl.when(head == 0)
    def _():
        for s in scatters:
            s.load().start()
        links.meet()
        for s in scatters:
            s.start()
        swap.start()

    _, _, z, core = links.place()
    here = lax.rem(z, chips)
    mine = here * 2 + core
    dk[...] = jnp.zeros_like(dk)
    dv[...] = jnp.zeros_like(dv)
    pk[...] = jnp.zeros_like(pk)
    pv[...] = jnp.zeros_like(pv)
    for piece in range(2):
        base = rows * (piece * members + mine)
        at = piece * 2 * rows
        region = slice(at, at + 2 * rows)
        dq[...] = jnp.zeros_like(dq)

        def pair(key, value, block, mask):
            spot = slice(at + block.start, at + block.stop)
            weights = jnp.exp2(nt(key, q_ref[0, spot]) * exp2_scale - lse_ref[0, :, spot])
            if mask is not None:
                weights = mask(weights)
            grads = (weights * (nt(value, g_ref[0, spot]) - del_ref[0, :, spot])).astype(BF16)
            weights = weights.astype(BF16)
            dq[block] += contract_rows(grads, key)
            return matmul(grads, q_ref[0, spot]), matmul(weights, g_ref[0, spot])

        everything = slice(0, 2 * rows)

        def trunk(step, masked):
            start = pl.multiple_of(step * CHUNK, CHUNK)

            def mask(weights):
                shape = weights.shape
                room = row_places((1, shape[1]), 1, sub) + (base - start)
                return jnp.where(lax.broadcasted_iota(jnp.int32, shape, 0) <= room, weights, 0.0)

            key_grad, value_grad = pair(
                k_ref[0, 0, pl.ds(start, CHUNK)],
                v_ref[0, 0, pl.ds(start, CHUNK)],
                everything,
                mask if masked else None,
            )
            dk[pl.ds(start, CHUNK)] += key_grad
            dv[pl.ds(start, CHUNK)] += value_grad

        if piece == 0:
            clear = jnp.minimum(base // CHUNK, TRUNK // CHUNK)
            end = jnp.minimum((base + rows + CHUNK - 1) // CHUNK, TRUNK // CHUNK)
            lax.fori_loop(0, clear, lambda i, c: (trunk(i, False), c)[1], 0)
            lax.fori_loop(clear, end, lambda i, c: (trunk(i, True), c)[1], 0)
        else:
            lax.fori_loop(0, TRUNK // CHUNK, lambda i, c: (trunk(i, False), c)[1], 0)

        lead = jnp.maximum(base - TRUNK, 0) // SEG

        def parents_():
            gather_parents(
                meta,
                lead,
                0,
                [
                    (lambda b: k_ref[0, 0, TRUNK + b * SEG : TRUNK + (b + 1) * SEG], kp),
                    (lambda b: v_ref[0, 0, TRUNK + b * SEG : TRUNK + (b + 1) * SEG], vp),
                ],
            )

        if piece == 0:
            pl.when(base + rows > TRUNK)(parents_)
        else:
            parents_()
        for s in range(SUBS):
            block = slice(2 * sub * s, 2 * sub * (s + 1))

            def runs():
                row = base + s * sub - TRUNK
                run = row // SEG
                own = pl.multiple_of(TRUNK + run * SEG, SEG)
                flag = jnp.minimum(meta[run] + 1, 1).astype(F32)

                def mask(weights):
                    shape = (SEG, 2 * sub)
                    room = lax.broadcasted_iota(jnp.int32, shape, 1) % sub + lax.rem(row, SEG)
                    seen = lax.broadcasted_iota(jnp.int32, shape, 0) <= room
                    return jnp.concatenate(
                        [jnp.where(seen, weights[:SEG], 0.0), weights[SEG:] * flag], axis=0
                    )

                key_grad, value_grad = pair(
                    jnp.concatenate([k_ref[0, 0, pl.ds(own, SEG)], kp[run - lead]], axis=0),
                    jnp.concatenate([v_ref[0, 0, pl.ds(own, SEG)], vp[run - lead]], axis=0),
                    block,
                    mask,
                )
                dk[pl.ds(own, SEG)] += key_grad[:SEG]
                dv[pl.ds(own, SEG)] += value_grad[:SEG]
                slot = LOCAL_RUNS * piece + run - lead
                pk[slot] += key_grad[SEG:]
                pv[slot] += value_grad[SEG:]

            if piece == 0:
                pl.when(base + s * sub >= TRUNK)(runs)
            else:
                runs()

        dq_ref[0, region] = dq[...] * score_scale

        def spread():
            parents = [meta[jnp.minimum(lead + k, TREE // SEG - TRUNK // SEG - 1)] for k in range(LOCAL_RUNS)]

            def place(b, carry):
                start = pl.multiple_of(TRUNK + b * SEG, SEG)
                key_grad, value_grad = dk[pl.ds(start, SEG)], dv[pl.ds(start, SEG)]
                for k in range(LOCAL_RUNS):
                    share = (1 - jnp.minimum(jnp.abs(parents[k] - b), 1)).astype(F32)
                    key_grad += pk[LOCAL_RUNS * piece + k] * share
                    value_grad += pv[LOCAL_RUNS * piece + k] * share
                dk[pl.ds(start, SEG)] = key_grad
                dv[pl.ds(start, SEG)] = value_grad
                return carry

            lax.fori_loop(0, (TREE - TRUNK) // SEG, place, 0)

        if piece == 0:
            pl.when(base + rows > TRUNK)(spread)
        else:
            spread()

    def core_copy(h):
        return links.copy(("kv core", h), stage.at[h % 2, :, 1 - core], near.at[h % 2], links.sibling())

    def far_copies(h):
        return [
            links.copy(("kv z", h, i), sums.at[h, chip], far.at[h, i], target)
            for i, (chip, target) in enumerate(links.group())
        ]

    def pass_on(h):
        core_copy(h).wait()

        def add(i, carry):
            chip, which, piece = i // 4, lax.rem(i // 2, 2), lax.rem(i, 2)
            sums[h, chip, which, piece] = (
                stage[h % 2, chip, core, which, piece].astype(F32) + near[h % 2, chip, which, piece].astype(F32)
            ).astype(BF16)
            return carry

        lax.fori_loop(0, chips * 4, add, 0)
        run_all(far_copies(h), "start")

    for h in range(1, KV_HEADS):
        pl.when(head == h)(functools.partial(pass_on, h - 1))

    for which, grad, scale in ((0, dk, score_scale), (1, dv, 1.0)):
        for piece in range(2):
            for member in range(members):
                start = rows * (piece * members + member)
                stage[lax.rem(head, 2), member // 2, member % 2, which, piece] = (
                    grad[start : start + rows] * scale
                ).astype(BF16)
    for h in range(KV_HEADS):

        @pl.when(head == h)
        def _():
            core_copy(h).start()

    for moment, steps in BACKWARD_AFTER.items():

        @pl.when(head == moment)
        def _():
            for step, array in steps:
                for s in each(array):
                    if step == 0:
                        s.begin()
                    else:
                        s.middle(step - 1)

    def result(h):
        return pltpu.make_async_copy(last.at[h % 2], dkv_ref.at[:, h], local_sem.at[h % 2])

    @pl.when(head == KV_HEADS - 1)
    def _():
        pass_on(KV_HEADS - 1)
        for s in scatters:
            s.finish()
        for h in range(KV_HEADS):
            run_all(far_copies(h), "wait")
            if h > 1:
                result(h - 2).wait()
            for which in range(2):
                for piece in range(2):
                    total = sums[h, here, which, piece].astype(F32)
                    for i in range(chips - 1):
                        total = total + far[h, i, which, piece].astype(F32)
                    last[h % 2, which, piece] = total
            result(h).start()
        for h in (KV_HEADS - 2, KV_HEADS - 1):
            result(h).wait()
        swap.wait()


def backward(sizes, meta, queries, grads, kv_all, log_total, delta, late, dout, done):
    ny, nx, nz = sizes
    chips = nz // 2
    rows = queries.shape[1] // 4
    widths = (late.shape[-1],) * late.shape[0] + (dout.shape[-1],)
    shard_rows = dout.shape[4]
    stack = pl.BlockSpec((1, 4 * rows, HEAD_DIM), lambda h, meta: (h, 0, 0))
    line = pl.BlockSpec((1, 1, 4 * rows), lambda h, meta: (h, 0, 0))
    buffers, count = [], 0
    for w in widths:
        for b, cols in enumerate(halves_of(w)):
            buffers += Scatter.scratch(sizes, ORDERS[b], shard_rows, cols.stop - cols.start)
            buffers.append(pltpu.VMEM((ny, nx, nz, shard_rows, cols.stop - cols.start), BF16))
            count += 1
    rounds = count * Scatter.copies(sizes) + KV_HEADS * chips + 1
    late_shape = (late.shape[0], shard_rows, late.shape[-1])
    dout_shape = (shard_rows, dout.shape[-1])
    return pl.pallas_call(
        functools.partial(backward_kernel, sizes, rows, widths),
        out_shape=[
            jax.ShapeDtypeStruct((KV_HEADS, 4 * rows, HEAD_DIM), F32),
            jax.ShapeDtypeStruct((2, KV_HEADS, 2, rows, HEAD_DIM), F32),
            jax.ShapeDtypeStruct(late_shape, F32),
            jax.ShapeDtypeStruct(dout_shape, F32),
            jax.ShapeDtypeStruct(done.shape, BF16),
        ],
        grid_spec=pltpu.PrefetchScalarGridSpec(
            num_scalar_prefetch=1,
            grid=(KV_HEADS,),
            in_specs=[
                stack,
                stack,
                pl.BlockSpec((1, 1, TREE, HEAD_DIM), lambda h, meta: (0, h, 0, 0)),
                pl.BlockSpec((1, 1, TREE, HEAD_DIM), lambda h, meta: (1, h, 0, 0)),
                line,
                line,
                ANY,
                ANY,
                ANY,
            ],
            out_specs=[
                stack,
                ANY,
                pl.BlockSpec(late_shape, lambda h, meta: (0, 0, 0)),
                pl.BlockSpec(dout_shape, lambda h, meta: (0, 0)),
                ANY,
            ],
            scratch_shapes=[
                pltpu.VMEM((2 * rows, HEAD_DIM), F32),
                pltpu.VMEM((TREE, HEAD_DIM), F32),
                pltpu.VMEM((TREE, HEAD_DIM), F32),
                pltpu.VMEM((2 * LOCAL_RUNS, SEG, HEAD_DIM), F32),
                pltpu.VMEM((2 * LOCAL_RUNS, SEG, HEAD_DIM), F32),
                pltpu.VMEM((LOCAL_RUNS, SEG, HEAD_DIM), BF16),
                pltpu.VMEM((LOCAL_RUNS, SEG, HEAD_DIM), BF16),
                pltpu.VMEM((2, chips, 2, 2, 2, rows, HEAD_DIM), BF16),
                pltpu.VMEM((2, chips, 2, 2, rows, HEAD_DIM), BF16),
                pltpu.VMEM((KV_HEADS, chips, 2, 2, rows, HEAD_DIM), BF16),
                pltpu.VMEM((KV_HEADS, chips - 1, 2, 2, rows, HEAD_DIM), BF16),
                pltpu.VMEM((2, 2, 2, rows, HEAD_DIM), F32),
            ]
            + buffers
            + [
                pltpu.SemaphoreType.DMA((rounds,)),
                pltpu.SemaphoreType.DMA((rounds,)),
                pltpu.SemaphoreType.DMA((3 + count,)),
            ],
        ),
        compiler_params=pltpu.CompilerParams(
            collective_id=3, has_side_effects=True, vmem_limit_bytes=60 * MIB
        ),
        name="backward",
    )(
        meta,
        queries,
        grads,
        kv_all,
        kv_all,
        log_total.reshape(KV_HEADS, 1, 4 * rows),
        delta.reshape(KV_HEADS, 1, 4 * rows),
        late,
        dout,
        done,
    )


def finish_kernel(
    sizes, rows, dq_ref, dkv_ref, pre_ref, w_ref, normed_ref, x_ref, hid_ref, gain_ref, post_ref, qk_ref, cos_ref, sin_ref,
    q_out, k_out, v_out, g_out, dx_placed, *refs,
):
    normed_t, low, grads, qk, dx, part, part_g = refs[:7]
    buffers = refs[7:-3]
    send_sem, recv_sem, local_sem = refs[-3:]
    ny, nx, nz = sizes
    count = 2 * rows
    sub = rows // SUBS
    shard_rows = part.shape[5]
    tile = 256
    pair = pl.program_id(0)
    links = Links(sizes, send_sem, recv_sem)
    _, _, _, core = links.place()
    swap = Exchange(links, dx, dx_placed, local_sem.at[0])

    def to_query(c):
        def store(total):
            q_out[:, 4 * HEAD_DIM * c : 4 * HEAD_DIM * (c + 1)] = total

        return store

    def to_key_value(c):
        def store(total):
            k_out[:, 2 * HEAD_DIM * c : 2 * HEAD_DIM * (c + 1)] = total[:, : 2 * HEAD_DIM]
            v_out[:, 2 * HEAD_DIM * c : 2 * HEAD_DIM * (c + 1)] = total[:, 2 * HEAD_DIM :]

        return store

    scatters = []
    for c in range(PAIRS):
        for b, cols in enumerate(halves_of(8 * HEAD_DIM)):
            k = 4 * len(scatters)
            scatters.append(
                Scatter(
                    links,
                    (c, b),
                    part.at[c % 2],
                    ORDERS[b],
                    cols,
                    *buffers[k : k + 4],
                    part.at[c % 2, :, :, :, core, :, cols],
                    None,
                    to_key_value(c) if b else to_query(c),
                )
            )
    k = 4 * len(scatters)
    whole = slice(0, 3 * GAIN_COLS)
    scatters.append(
        Scatter(
            links, "gains", part_g, ORDERS[0], whole, *buffers[k : k + 4], part_g.at[:, :, :, core], None, g_out
        )
    )

    def act(steps):
        for what, c in steps:
            for s in scatters[2 * c : 2 * c + 2]:
                if what == "core":
                    s.start()
                elif what == "begin":
                    s.begin()
                elif what == "finish":
                    s.finish()
                else:
                    s.middle(what)

    def rows_of(block):
        return (block // (2 * nz * nx), lax.rem(block // (2 * nz), nx), lax.rem(block // 2, nz), lax.rem(block, 2))

    @pl.when(pair == 0)
    def _():
        links.meet()
        normed_t[...] = normed_ref[...].astype(F32).T.astype(BF16)
        grads[...] = jnp.zeros_like(grads)
        qk[...] = jnp.zeros_like(qk)

    cosine, sine = cos_ref[...], sin_ref[...]

    def back(turned_grad, pre, gain):
        grad = turned_grad * cosine - roll_half(turned_grad) * sine
        factor = norm_factor(pre)
        grad_pre, share = norm_backward(grad, gain, pre * factor, factor)
        return grad_pre.astype(BF16), jnp.sum(share, axis=0, keepdims=True)

    for hh in range(2):
        for h in range(2):
            grad = jnp.concatenate(
                [dq_ref[hh, (2 * s + h) * sub : (2 * s + h + 1) * sub] for s in range(2 * SUBS)], axis=0
            )
            value, share = back(grad, pre_ref[hh, :, h * HEAD_DIM : (h + 1) * HEAD_DIM], qk_ref[0:1])
            qk[0:1] += share
            at = 2 * hh + h
            low[:, at * HEAD_DIM : (at + 1) * HEAD_DIM] = value
        value, share = back(dkv_ref[0, hh].reshape(count, HEAD_DIM), pre_ref[hh, :, 2 * HEAD_DIM :], qk_ref[1:2])
        qk[1:2] += share
        low[:, (4 + hh) * HEAD_DIM : (5 + hh) * HEAD_DIM] = value
        low[:, (6 + hh) * HEAD_DIM : (7 + hh) * HEAD_DIM] = dkv_ref[1, hh].reshape(count, HEAD_DIM).astype(BF16)
    for moment, steps in FINISH_MIDDLE.items():
        pl.when(pair == moment)(functools.partial(act, steps))
    slot = lax.rem(pair, 2)

    def model(t, carry):
        at = pl.multiple_of(t * tile, tile)
        grads[:, pl.ds(at, tile)] += nt(low[...], w_ref[0, pl.ds(at, tile), :])
        value = matmul(normed_t[pl.ds(at, tile)], low[...])
        for k in range(tile // shard_rows):
            y, x, z, c = rows_of(at // shard_rows + k)
            part[slot, y, x, z, c] = value[k * shard_rows : (k + 1) * shard_rows].astype(BF16)
        return carry

    lax.fori_loop(0, D // tile, model, 0)
    for moment, steps in FINISH_AFTER.items():
        pl.when(pair == moment)(functools.partial(act, steps))

    @pl.when(pair == PAIRS - 1)
    def _():
        values = x_ref[...].astype(F32)
        factor = norm_factor(values)
        grad_in, share = norm_backward(grads[...], gain_ref[0:1], values * factor, factor)
        dx[...] = (hid_ref[...] + grad_in).astype(BF16).reshape(2, rows, D)
        swap.start()
        act([(0, PAIRS - 2), ("begin", PAIRS - 1)])
        lines = jnp.concatenate(
            [jnp.sum(share, axis=0, keepdims=True), post_ref[...], jnp.zeros((GAIN_COLS - 2, D), F32)], axis=0
        )
        columns = lines.T.astype(BF16)
        first = lax.broadcasted_iota(jnp.int32, (shard_rows, GAIN_COLS), 0) == 0
        query_line = jnp.where(first, qk[0:1], 0.0).astype(BF16)
        key_line = jnp.where(first, qk[1:2], 0.0).astype(BF16)
        for k in range(D // shard_rows):
            y, x, z, c = k // (2 * nz * nx), k // (2 * nz) % nx, k // 2 % nz, k % 2
            part_g[y, x, z, c, :, :GAIN_COLS] = columns[k * shard_rows : (k + 1) * shard_rows]
            part_g[y, x, z, c, :, GAIN_COLS : 2 * GAIN_COLS] = query_line
            part_g[y, x, z, c, :, 2 * GAIN_COLS :] = key_line
        act([("core", PAIRS), (1, PAIRS - 2), ("begin", PAIRS), (0, PAIRS - 1), (0, PAIRS), (1, PAIRS - 1), (1, PAIRS)])
        for c in range(PAIRS + 1):
            act([("finish", c)])
        swap.wait()


def finish(sizes, dq, dkv, pre, normed, x, grad_hidden, gain, post_part, qkv_full, qk_gain, cosine, sine):
    ny, nx, nz = sizes
    count = x.shape[0]
    rows = count // 2
    shard_rows = D // (ny * nx * nz * 2)
    blocks = (ny, nx, nz, 2, shard_rows)
    width = 8 * HEAD_DIM

    def whole_block(shape):
        return pl.BlockSpec(shape, lambda c: (0,) * len(shape), pipeline_mode=pl.Buffered(1))

    buffers = []
    for c in range(PAIRS):
        for b, cols in enumerate(halves_of(width)):
            buffers += Scatter.scratch(sizes, ORDERS[b], shard_rows, cols.stop - cols.start)
    buffers += Scatter.scratch(sizes, ORDERS[0], shard_rows, 3 * GAIN_COLS)
    rounds = (2 * PAIRS + 1) * Scatter.copies(sizes) + 1

    def out_block(n):
        return pl.BlockSpec((shard_rows, n), lambda c: (0, 0))

    return pl.pallas_call(
        functools.partial(finish_kernel, sizes, rows),
        grid=(PAIRS,),
        out_shape=[
            jax.ShapeDtypeStruct((shard_rows, QD), F32),
            jax.ShapeDtypeStruct((shard_rows, KVD), F32),
            jax.ShapeDtypeStruct((shard_rows, KVD), F32),
            jax.ShapeDtypeStruct((shard_rows, 3 * GAIN_COLS), F32),
            jax.ShapeDtypeStruct((2, rows, D), BF16),
        ],
        in_specs=[
            pl.BlockSpec((2, 2 * count, HEAD_DIM), lambda c: (c, 0, 0)),
            pl.BlockSpec((2, 2, 2, rows, HEAD_DIM), lambda c: (0, c, 0, 0, 0)),
            pl.BlockSpec((2, count, 3 * HEAD_DIM), lambda c: (c, 0, 0)),
            pl.BlockSpec((1, D, width), lambda c: (c, 0, 0)),
            whole_block((count, D)),
            whole_block((count, D)),
            whole_block((count, D)),
            whole_block((8, D)),
            whole_block((1, D)),
            whole_block((8, HEAD_DIM)),
            whole_block((count, HEAD_DIM)),
            whole_block((count, HEAD_DIM)),
        ],
        out_specs=[out_block(QD), out_block(KVD), out_block(KVD), out_block(3 * GAIN_COLS), ANY],
        scratch_shapes=[
            pltpu.VMEM((D, count), BF16),
            pltpu.VMEM((count, width), BF16),
            pltpu.VMEM((count, D), F32),
            pltpu.VMEM((8, HEAD_DIM), F32),
            pltpu.VMEM((2, rows, D), BF16),
            pltpu.VMEM((2,) + blocks + (width,), BF16),
            pltpu.VMEM(blocks + (3 * GAIN_COLS,), BF16),
        ]
        + buffers
        + [
            pltpu.SemaphoreType.DMA((rounds,)),
            pltpu.SemaphoreType.DMA((rounds,)),
            pltpu.SemaphoreType.DMA((1,)),
        ],
        compiler_params=pltpu.CompilerParams(
            collective_id=4, has_side_effects=True, vmem_limit_bytes=58 * MIB
        ),
        name="finish",
    )(dq, dkv, pre, qkv_full, normed, x, grad_hidden, gain, post_part, qk_gain, cosine, sine)


def shards(
    sizes,
    tokens,
    cotangent,
    segment_ids,
    positions,
    parents,
    input_norm,
    query_proj,
    key_proj,
    value_proj,
    query_norm,
    key_norm,
    out_proj,
    post_norm,
    gate_proj,
    up_proj,
    down_proj,
):
    nz = sizes[2]
    rows = tokens.shape[1]
    shard_rows = query_proj.shape[0]
    gain_rows = query_norm.shape[0]
    ctx = lax.axis_index("ctx")
    half = ctx // nz
    member = ctx % nz
    count = 2 * rows
    sub = rows // SUBS

    device = lax.axis_index("dp") * 2 * nz + ctx

    def spread(gain):
        line = jnp.zeros((1, HEAD_DIM), BF16)
        line = lax.dynamic_update_slice(line, gain[None, :], (0, device * gain_rows))
        return jnp.pad(line, ((0, shard_rows - 1), (0, 0)))

    gains = jnp.pad(
        jnp.stack([input_norm, post_norm], axis=1), ((0, 0), (0, GAIN_COLS - 2))
    )
    gains = jnp.concatenate([gains, spread(query_norm), spread(key_norm)], axis=1)
    qkv_shard = jnp.concatenate(
        [
            w[:, n * HEAD_DIM * c : n * HEAD_DIM * (c + 1)]
            for c in range(PAIRS)
            for w, n in ((query_proj, 4), (key_proj, 2), (value_proj, 2))
        ],
        axis=1,
    )
    down_t = down_proj.T

    def feed_shard(chunks):
        return jnp.concatenate(
            [w[:, c * FF_CHUNK : (c + 1) * FF_CHUNK] for c in chunks for w in (gate_proj, up_proj, down_t)], axis=1
        )

    run_seg = segment_ids[half][TRUNK::SEG]
    run_parent = parents[half][run_seg]
    parent_run = jnp.argmax(run_seg[None, :] == run_parent[:, None], axis=1).astype(jnp.int32)
    meta = jnp.where(run_parent > 0, parent_run, -1)
    pos_tree = positions[half].reshape(2, nz, rows)
    pos_local = lax.dynamic_index_in_dim(pos_tree, member, 1, keepdims=False).reshape(count)
    cosine, sine = rope_tables(pos_local)

    (mixed, totals, pre, normed, gain_rows_, qk_gains, placed, cot, queries, kv_all,
     qkv_full, _, out_t, feed_whole) = forward(
        sizes, meta, cosine, sine, tokens, cotangent, [qkv_shard, out_proj.T, feed_shard(range(FF_FIRST)), gains]
    )
    x = placed.reshape(count, D)
    cot = cot.reshape(count, D)
    qkv_full = qkv_full.reshape(PAIRS, D, -1)
    out_t = out_t.reshape(D, QD)
    feed_whole = feed_whole.reshape(FF_FIRST, D, -1)
    log_total = jnp.log2(totals[:, :KV_HEADS]).T
    result, grad_hidden, grad_stack, delta, post_part, dout, late, _, early_grad = feed(
        sizes, x, mixed, cot, out_t, gain_rows_, feed_whole, [feed_shard([c]) for c in range(FF_FIRST, FF_CHUNKS)]
    )
    delta = delta[:HEADS].reshape(KV_HEADS, 2, 2 * SUBS, sub).transpose(0, 2, 1, 3)
    dq, dkv, late_grad, out_grad, output = backward(
        sizes, meta, queries, grad_stack, kv_all, log_total, delta, late, dout, result.reshape(2, rows, D)
    )
    feed_grad = jnp.concatenate([early_grad, late_grad], axis=0)

    def feed_columns(k):
        piece = feed_grad[:, :, k * FF_CHUNK : (k + 1) * FF_CHUNK]
        return piece.transpose(1, 0, 2).reshape(shard_rows, FF)

    query_grad, key_grad, value_grad, gain_grad, input_grad = finish(
        sizes, dq, dkv, pre, normed, x, grad_hidden, gain_rows_, post_part, qkv_full, qk_gains, cosine, sine
    )

    def own(line):
        return lax.dynamic_slice_in_dim(line, device * gain_rows, gain_rows)

    return (
        output,
        input_grad.astype(F32),
        gain_grad[:, 0],
        query_grad,
        key_grad,
        value_grad,
        own(gain_grad[0, GAIN_COLS : 2 * GAIN_COLS]),
        own(gain_grad[0, 2 * GAIN_COLS :]),
        out_grad.T,
        gain_grad[:, 1],
        feed_columns(0),
        feed_columns(1),
        feed_columns(2).T,
    )


def solution(mesh):
    dp, ctx = mesh.shape["dp"], mesh.shape["ctx"]
    sizes = (2, dp // 2, ctx // 2)
    return jax.shard_map(
        functools.partial(shards, sizes),
        mesh=mesh,
        in_specs=(
            P("dp", "ctx", None),
            P("dp", "ctx", None),
            P("dp", None),
            P("dp", None),
            P("dp", None),
            P(("dp", "ctx")),
            P(("dp", "ctx"), None),
            P(("dp", "ctx"), None),
            P(("dp", "ctx"), None),
            P(("dp", "ctx")),
            P(("dp", "ctx")),
            P(None, ("dp", "ctx")),
            P(("dp", "ctx")),
            P(("dp", "ctx"), None),
            P(("dp", "ctx"), None),
            P(None, ("dp", "ctx")),
        ),
        out_specs=(
            P("dp", "ctx", None),
            P("dp", "ctx", None),
            P(("dp", "ctx")),
            P(("dp", "ctx"), None),
            P(("dp", "ctx"), None),
            P(("dp", "ctx"), None),
            P(("dp", "ctx")),
            P(("dp", "ctx")),
            P(None, ("dp", "ctx")),
            P(("dp", "ctx")),
            P(("dp", "ctx"), None),
            P(("dp", "ctx"), None),
            P(None, ("dp", "ctx")),
        ),
        check_vma=False,
    )
```
